32 devices in a mesh: dp: 4 (over y, x), seq: 8 (over z, core).
Axes of the slice: x: 2, y: 2, z: 4, core: 2. Of those that a mesh axis runs over, the one named last changes fastest.
Arguments:
- inputs: bfloat16 [8, 1536, 768], P('dp', 'seq'), may hold values from -6 to 6
- segments: int32 [8, 1536], P('dp'), may hold values from 0 to 5, never falling along the last dimension, each value on 1 to 1152 neighbouring positions
- rand_blocks: int32 [8, 24, 12, 3], P('dp'), may hold values from 0 to 23, as said below
- w_qkv: bfloat16 [768, 2304], P('dp'), may hold values from -0.21875 to 0.21875
- w_out: bfloat16 [768, 768], P('dp'), may hold values from -1.75 to 1.75
- w_up: bfloat16 [768, 3072], P('dp'), may hold values from -0.21875 to 0.21875
- w_down: bfloat16 [3072, 768], P('dp'), may hold values from -0.109375 to 0.109375
- norm_gain: float32 [2, 768], replicated, may hold values from 0.5 to 1.5
- norm_bias: float32 [2, 768], replicated, may hold values from -3 to 3
- out_grad: bfloat16 [8, 1536, 768], P('dp', 'seq'), may hold values from -6 to 6
Outputs:
- output: bfloat16 [8, 1536, 768], P('dp', 'seq')
- input_grad: float32 [8, 1536, 768], P('dp', 'seq')
- w_qkv_grad: float32 [768, 2304], P(('dp', 'seq'))
- w_out_grad: float32 [768, 768], P(('dp', 'seq'))
- w_up_grad: float32 [768, 3072], P(('dp', 'seq'))
- w_down_grad: float32 [3072, 768], P(('dp', 'seq'))
- norm_gain_grad: float32 [2, 768], P(None, ('dp', 'seq'))
- norm_bias_grad: float32 [2, 768], P(None, ('dp', 'seq'))
The draws below stay inside these ranges and needn't reach their ends.
Inputs may be any that keep to these rules, and one draw needn't show every extreme that they name: `rand_blocks`: for every sequence and every index t of seq, among the 108 entries of the query blocks t * 3 .. (t + 1) * 3 - 1, at most 14 name key blocks held by one index of seq (key block // 3), and some index is named exactly 14 times.
All inputs are finite; a program needn't handle non-finite values.
Results may differ from the reference program's by a relative error of at most 0.013.
Values may be sent and summed in bfloat16 or wider, within the bound.
A program may use at most 192 MiB of HBM per device.

```python
import math
import jax
import jax.numpy as jnp
import numpy as np
from jax import lax

D = 768
H = 12
HEAD = 64
FF = 3072
BLOCK = 64
R = 3
BLK_DEV = 3
SEQUENCES = 8
LENGTH = 1536
NB = 24
CAP = 14
DOCS = 6
DOC_MOST = 1152
N_SEQ = 8


def draw_rand_blocks(key, part):
    entries = BLK_DEV * H * R
    pool_size = N_SEQ * CAP
    groups = SEQUENCES * N_SEQ
    owner_pool = jnp.repeat(jnp.arange(N_SEQ, dtype=jnp.int32), CAP)

    def one_group(group_key):
        sub_keys = jax.random.split(group_key, 4)
        forced = jax.random.randint(sub_keys[0], (), 0, N_SEQ, dtype=jnp.int32)
        order_score = jax.random.permutation(sub_keys[1], pool_size).astype(jnp.int32)
        order_score = jnp.where(owner_pool == forced, order_score - pool_size, order_score)
        chosen = owner_pool[jnp.argsort(order_score, stable=True)][:entries]
        chosen = chosen[jax.random.permutation(sub_keys[2], entries)]
        local_block = jax.random.randint(sub_keys[3], (entries,), 0, BLK_DEV, dtype=jnp.int32)
        return chosen * BLK_DEV + local_block
    drawn_table = jax.vmap(one_group)(jax.random.split(key, groups))
    return drawn_table.reshape(SEQUENCES, NB, H, R)


def level_of(own_key, dims, cuts, smallest, high):
    def one(axis_at, shards_of):
        heights = jax.random.uniform(jax.random.fold_in(jax.random.fold_in(own_key, 6), axis_at), (shards_of,), jnp.float32, smallest / len(cuts), high / len(cuts))
        return jnp.repeat(jnp.exp(heights), dims[axis_at] // shards_of).reshape((-1,) + (1,) * (len(dims) - axis_at - 1))

    factor_of = one(*cuts[0])
    for cut in cuts[1:]:
        factor_of = factor_of * one(*cut)
    return factor_of


def profile(number_of, total, limit, lean):
    portions = [(1 << 20) // math.isqrt(grade ** lean) + 1 for grade in range(2, number_of + 1)]
    spare, counts = total - limit - (number_of - 1), [1] * (number_of - 1)
    while spare > 0:
        candidates = [i for i in range(number_of - 1) if counts[i] < limit]
        whole, remaining = sum([portions[i] for i in candidates]), spare
        for i in candidates:
            extra = min(limit - counts[i], max(1, remaining * portions[i] // whole), spare)
            counts[i] = counts[i] + extra
            spare = spare - extra
    return np.array([limit] + counts)


def uneven_parts(stream_key, count, total, most, skew):
    if count == 2:
        one = jax.random.randint(stream_key, (), max(1, total - most), min(most, total - 1) + 1)
        return jnp.stack([one, total - one])
    lengths = jnp.asarray(profile(count, total, most, skew), jnp.int32)
    twos = (count - 1) // 2
    source_of, taker = lengths[1:1 + 2 * twos:2], lengths[2:2 + 2 * twos:2]
    margin = jnp.minimum(source_of - 1, most - taker)
    shifted = jax.random.randint(jax.random.fold_in(stream_key, 1), (twos,), 0, 1 << 20) % (margin + 1)
    lengths = lengths.at[1:1 + 2 * twos:2].set(source_of - shifted).at[2:2 + 2 * twos:2].set(taker + shifted)
    return lengths[jax.random.permutation(jax.random.fold_in(stream_key, 2), count)]


def noise(own_key, extent, scale, bound, cuts=(), kind=jnp.bfloat16):
    values = jax.random.normal(own_key, extent, jnp.float32) * scale
    if len(cuts) > 0:
        values = level_of(own_key, extent, cuts, -0.22, 0.18) * values
    return jnp.clip(values, min=-bound, max=bound).astype(kind)


def setup_inputs(seed: int = 0) -> dict:
    key_of = jax.random.split(jax.random.key(seed), 11)
    inputs = noise(key_of[0], (SEQUENCES, LENGTH, D), 1.0, 6.0, ((0, 4), (1, 8)))
    segments = jax.vmap(lambda own: jnp.searchsorted(jnp.cumsum(uneven_parts(own, DOCS, LENGTH, DOC_MOST, 2)), jnp.arange(LENGTH), side="right"))(jax.random.split(key_of[1], SEQUENCES)).reshape((SEQUENCES, LENGTH)).astype(jnp.int32)
    rand_blocks = draw_rand_blocks(jax.random.fold_in(key_of[10], 71), 0)
    w_qkv = noise(key_of[3], (D, 3 * D), D ** -0.5, 0.21875, ((0, 4),))
    w_out = noise(key_of[4], (D, D), (D // 64) ** -0.5, 1.75, ((0, 4),))
    w_up = noise(key_of[5], (D, FF), D ** -0.5, 0.21875, ((0, 4),))
    w_down = noise(key_of[6], (FF, D), FF ** -0.5, 0.109375, ((0, 4),))
    norm_gain = jnp.clip(1.0 + 0.1 * jax.random.normal(key_of[7], (2, D), jnp.float32), 0.5, 1.5)
    norm_bias = noise(key_of[8], (2, D), 0.5, 3.0, (), jnp.float32)
    out_grad = noise(key_of[9], (SEQUENCES, LENGTH, D), 1.0, 6.0, ((0, 4), (1, 8)))
    return {"inputs": inputs, "segments": segments, "rand_blocks": rand_blocks, "w_qkv": w_qkv, "w_out": w_out, "w_up": w_up, "w_down": w_down, "norm_gain": norm_gain, "norm_bias": norm_bias, "out_grad": out_grad}


@jax.custom_vjp
def low(v):
    return lax.optimization_barrier(v.astype(jnp.bfloat16)).astype(jnp.float32)

@jax.custom_vjp
def low_back(v):
    return v

def low_keep(v):
    return (low(v), None)

def low_pass(kept, grad):
    return (grad,)

def back_keep(v):
    return (v, None)

def back_low(kept, grad):
    return (low(grad),)
low.defvjp(low_keep, low_pass)
low_back.defvjp(back_keep, back_low)
norm_eps = 1e-05
masked_score = -1e+30
highest = lax.Precision.HIGHEST

def matmul(left_side, right_side):
    return jnp.dot(left_side, right_side, precision=highest)

def softmax_rows(scores):
    row_max = lax.optimization_barrier(jnp.max(scores, axis=-1, keepdims=True))
    exp_terms = jnp.exp(scores - row_max)
    return exp_terms / lax.optimization_barrier(jnp.sum(exp_terms, axis=-1, keepdims=True))

def layer_norm(residual, gain_row, shift_row):
    mean_row = lax.optimization_barrier(jnp.mean(residual, axis=-1, keepdims=True))
    centred = residual - mean_row
    variance = lax.optimization_barrier(jnp.mean(centred * centred, axis=-1, keepdims=True))
    return centred * lax.rsqrt(variance + norm_eps) * gain_row + shift_row

def gelu_exact(pre_act):
    return 0.5 * pre_act * (1.0 + lax.erf(pre_act * 0.7071067811865476))

def attend(queries, keys_in, values_in, seg_ids, random_ids):
    length = queries.shape[0]
    block_count = length // BLOCK
    scale_factor = HEAD ** (-0.5)
    query_heads = queries.reshape(block_count, BLOCK, H, HEAD)
    key_heads = keys_in.reshape(block_count, BLOCK, H, HEAD)
    value_heads = values_in.reshape(block_count, BLOCK, H, HEAD)
    seg_blocks = seg_ids.reshape(block_count, BLOCK)
    blocks = jnp.arange(block_count).astype(jnp.int32)
    window = blocks[:, None] + jnp.arange(-1, 2).astype(jnp.int32)[None, :]
    inside = (window >= 0) & (window < block_count)
    window = jnp.clip(window, 0, block_count - 1).astype(jnp.int32)
    glob_ids = jnp.broadcast_to(jnp.arange(2).astype(jnp.int32)[None, :], (block_count, 2))
    shared = jnp.concatenate([window, glob_ids], axis=1)
    key_shared = key_heads[shared].reshape(block_count, 5 * BLOCK, H, HEAD)
    value_shared = value_heads[shared].reshape(block_count, 5 * BLOCK, H, HEAD)
    window_seg = seg_blocks[window].reshape(block_count, 3 * BLOCK)
    window_ok = (seg_blocks[:, :, None] == window_seg[:, None, :]) & jnp.repeat(inside, BLOCK, axis=1)[:, None, :]
    shared_ok = jnp.concatenate([window_ok, jnp.ones((block_count, BLOCK, 2 * BLOCK), bool)], axis=2)
    head_ids = jnp.arange(H).astype(jnp.int32)[None, :, None]
    key_by_head = jnp.transpose(key_heads, (0, 2, 1, 3))
    value_by_head = jnp.transpose(value_heads, (0, 2, 1, 3))
    key_random = key_by_head[random_ids, head_ids].reshape(block_count, H, R * BLOCK, HEAD)
    value_random = value_by_head[random_ids, head_ids].reshape(block_count, H, R * BLOCK, HEAD)
    random_seg = seg_blocks[random_ids].reshape(block_count, H, R * BLOCK)
    random_ok = seg_blocks[:, None, :, None] == random_seg[:, :, None, :]
    part_shared = jnp.einsum('bqhd,bkhd->bhqk', query_heads, key_shared, precision=highest)
    part_random = jnp.einsum('bqhd,bhkd->bhqk', query_heads, key_random, precision=highest)
    scores = low_back(jnp.concatenate([part_shared, part_random], axis=-1) * scale_factor)
    allowed = jnp.concatenate([jnp.broadcast_to(shared_ok[:, None], part_shared.shape), random_ok], axis=-1)
    weights = low(softmax_rows(jnp.where(allowed, scores, masked_score)))
    local_out = jnp.einsum('bhqk,bkhd->bqhd', weights[..., :5 * BLOCK], value_shared, precision=highest)
    local_out = local_out + jnp.einsum('bhqk,bhkd->bqhd', weights[..., 5 * BLOCK:], value_random, precision=highest)
    local_out = local_out.reshape(length, H * HEAD)
    glob_query = queries[:2 * BLOCK].reshape(2 * BLOCK, H, HEAD)
    glob_scores = low_back(jnp.einsum('qhd,khd->hqk', glob_query, keys_in.reshape(length, H, HEAD), precision=highest) * scale_factor)
    glob_weights = low(softmax_rows(glob_scores))
    glob_out = jnp.einsum('hqk,khd->qhd', glob_weights, values_in.reshape(length, H, HEAD), precision=highest)
    return jnp.concatenate([glob_out.reshape(2 * BLOCK, H * HEAD), local_out[2 * BLOCK:]], axis=0)

def layer_forward(tokens, seg_ids, random_ids, mat_qkv, mat_out, mat_up, mat_down, gain_rows, shift_rows):
    features = tokens.shape[1]
    qkv = low(low_back(matmul(tokens, mat_qkv)))
    attention = low(low_back(attend(qkv[:, :features], qkv[:, features:2 * features], qkv[:, 2 * features:], seg_ids, random_ids)))
    residual = tokens + low_back(matmul(attention, mat_out))
    hidden = layer_norm(residual, gain_rows[0], shift_rows[0])
    pre_act = low_back(matmul(low(hidden), mat_up))
    branch = low_back(matmul(low(gelu_exact(pre_act)), mat_down))
    return layer_norm(hidden + branch, gain_rows[1], shift_rows[1])

def reference(inputs, segments, rand_blocks, w_qkv, w_out, w_up, w_down, norm_gain, norm_bias, out_grad):
    matrices = (w_qkv.astype(jnp.float32), w_out.astype(jnp.float32), w_up.astype(jnp.float32), w_down.astype(jnp.float32))

    def per_sequence(running, sequence_item):
        tokens, seg_ids, random_ids, cotangent = sequence_item

        def forward(token_rows, mat_qkv, mat_out, mat_up, mat_down, gain_rows, shift_rows):
            return layer_forward(token_rows, seg_ids, random_ids, mat_qkv, mat_out, mat_up, mat_down, gain_rows, shift_rows)
        result, pullback = jax.vjp(forward, tokens.astype(jnp.float32), *matrices, norm_gain, norm_bias)
        gradients = pullback(cotangent.astype(jnp.float32))
        running = tuple((acc + piece for acc, piece in zip(running, gradients[1:])))
        return (running, (result.astype(jnp.bfloat16), gradients[0]))
    initial = tuple((jnp.zeros(matrix.shape, jnp.float32) for matrix in matrices))
    initial = initial + (jnp.zeros(norm_gain.shape, jnp.float32), jnp.zeros(norm_bias.shape, jnp.float32))
    totals, (outputs, input_grads) = lax.scan(per_sequence, initial, (inputs, segments, rand_blocks, out_grad))
    return (outputs, input_grads, totals[0], totals[1], totals[2], totals[3], totals[4], totals[5])
```

```python
import jax
import jax.numpy as jnp
import numpy as np
from jax import lax
from jax.experimental import pallas as pl
from jax.experimental.pallas import tpu as pltpu
from jax.sharding import PartitionSpec as P

H = 12
HEAD = 64
BLOCK = 64
R = 3
MICRO = 2


norm_eps = 1e-05
masked_score = -1e30
root_half = 0.7071067811865476
inv_root_two_pi = 0.3989422804014327


def padded(cells, sides, width):
    for axis, dim in sides:
        count = lax.axis_size(axis)
        ends = count - 1
        head = lax.slice_in_dim(cells, 0, width, axis=dim)
        tail = lax.slice_in_dim(cells, cells.shape[dim] - width, cells.shape[dim], axis=dim)
        cells = jnp.concatenate(
            [
                lax.ppermute(tail, axis, [(i, (i + 1) % count) for i in range(ends)]),
                cells,
                lax.ppermute(head, axis, [((i + 1) % count, i) for i in range(ends)]),
            ],
            axis=dim,
        )
    return cells


def from_root(x, axis, root):
    mine = lax.axis_index(axis) == root
    return lax.psum(jnp.where(mine, x, jnp.zeros_like(x)), axis)


def merged(x, axis, combine):
    everything = jax.tree.map(lambda part: lax.all_gather(part, axis), x)
    initial = jax.tree.map(lambda part: part[0], everything)

    def step(k, so_far):
        return combine(so_far, jax.tree.map(lambda part: part[k], everything))

    return lax.fori_loop(1, lax.axis_size(axis), step, initial)


def product(left_side, right_side):
    return jnp.dot(left_side, right_side, preferred_element_type=jnp.float32)


def product_tn(left_side, right_side):
    return lax.dot_general(
        left_side, right_side, (((0,), (0,)), ((), ())), preferred_element_type=jnp.float32
    )


def product_nt(left_side, right_side):
    return lax.dot_general(
        left_side, right_side, (((1,), (1,)), ((), ())), preferred_element_type=jnp.float32
    )


def gelu_value(pre_act):
    return 0.5 * pre_act * (1.0 + lax.erf(pre_act * root_half))


def gelu_slope(pre_act):
    return (
        0.5 * (1.0 + lax.erf(pre_act * root_half))
        + pre_act * jnp.exp(-0.5 * pre_act * pre_act) * inv_root_two_pi
    )


def norm_forward(residual, gain_row, shift_row):
    mean_row = jnp.mean(residual, axis=-1, keepdims=True)
    centred = residual - mean_row
    variance = jnp.mean(centred * centred, axis=-1, keepdims=True)
    inv_std = lax.rsqrt(variance + norm_eps)
    normed = centred * inv_std
    return (normed * gain_row + shift_row, normed, inv_std)


def norm_backward(grad_rows, normed, inv_std, gain_row):
    scaled = grad_rows * gain_row
    back_rows = inv_std * (
        scaled
        - jnp.mean(scaled, axis=-1, keepdims=True)
        - normed * jnp.mean(scaled * normed, axis=-1, keepdims=True)
    )
    return (back_rows, jnp.sum(grad_rows * normed, axis=0), jnp.sum(grad_rows, axis=0))


def merge_stats(first_pair, second_pair):
    joint_max = jnp.maximum(first_pair[0], second_pair[0])
    joint_sum = first_pair[1] * jnp.exp(first_pair[0] - joint_max) + second_pair[1] * jnp.exp(
        second_pair[0] - joint_max
    )
    return (joint_max, joint_sum)


def local_scores(query_heads, shared_keys, random_keys, shared_ok, random_ok, scale_factor):
    part_shared = jnp.einsum(
        "sbqhd,sbkhd->sbhqk", query_heads, shared_keys, preferred_element_type=jnp.float32
    )
    part_random = jnp.einsum(
        "sbqhd,sbhkd->sbhqk", query_heads, random_keys, preferred_element_type=jnp.float32
    )
    scores = jnp.concatenate([part_shared, part_random], axis=4) * scale_factor
    allowed = jnp.concatenate(
        [jnp.broadcast_to(shared_ok[:, :, None], part_shared.shape), random_ok], axis=4
    )
    return jnp.where(allowed, scores, masked_score)


def per_device(
    inputs, segments, rand_blocks, w_qkv, w_out, w_up, w_down, norm_gain, norm_bias, out_grad
):
    seq_total, tok_dev, features = inputs.shape
    devices = lax.axis_size("seq")
    my_index = lax.axis_index("seq")
    blocks_dev = tok_dev // BLOCK
    blocks_all = blocks_dev * devices
    entries = blocks_dev * H * R
    capacity = max(2, entries // devices + 1)
    per_micro = seq_total // MICRO
    glob_rows = 2 * BLOCK
    shared_count = 5 * BLOCK
    scale_factor = HEAD ** (-0.5)
    token_rows = per_micro * tok_dev
    owner_flag = (my_index == 0).astype(jnp.float32)
    row_global = my_index * tok_dev + jnp.arange(tok_dev, dtype=jnp.int32) < glob_rows
    window_index = np.arange(blocks_dev)[:, None] + np.arange(3)[None, :]
    win_blocks = (
        my_index * blocks_dev
        + jnp.arange(blocks_dev, dtype=jnp.int32)[:, None]
        + jnp.arange(-1, 2, dtype=jnp.int32)[None, :]
    )
    win_inside = (win_blocks >= 0) & (win_blocks < blocks_all)
    win_clipped = jnp.clip(win_blocks, 0, blocks_all - 1)
    entry_heads = jnp.arange(entries, dtype=jnp.int32) // R % H
    slot_ids = jnp.arange(capacity, dtype=jnp.int32)
    earlier = jnp.arange(entries)[None, :] < jnp.arange(entries)[:, None]
    seq_ids = jnp.arange(per_micro, dtype=jnp.int32)
    grad_qkv_w = jnp.zeros((features, 3 * features), jnp.float32)
    grad_out_w = jnp.zeros((features, features), jnp.float32)
    grad_up_w = jnp.zeros((features, w_up.shape[1]), jnp.float32)
    grad_down_w = jnp.zeros((w_down.shape[0] * lax.axis_size("dp"), features), jnp.float32)
    gain_acc = jnp.zeros((2, features), jnp.float32)
    shift_acc = jnp.zeros((2, features), jnp.float32)
    output_parts = []
    input_parts = []
    for micro_step in range(MICRO):
        start_seq = micro_step * per_micro
        tokens_in = inputs[start_seq : start_seq + per_micro]
        seg_micro = segments[start_seq : start_seq + per_micro]
        rand_micro = rand_blocks[start_seq : start_seq + per_micro]
        cotangent = out_grad[start_seq : start_seq + per_micro]
        full_qkv, full_out, full_up, full_down = (
            lax.all_gather(w_qkv, "dp", axis=0, tiled=True),
            lax.all_gather(w_out, "dp", axis=0, tiled=True),
            lax.all_gather(w_up, "dp", axis=0, tiled=True),
            lax.all_gather(w_down, "dp", axis=0, tiled=True),
        )
        tokens_flat = tokens_in.reshape(token_rows, features)
        qkv_rows = (
            product(tokens_flat, full_qkv)
            .astype(jnp.bfloat16)
            .reshape(per_micro, tok_dev, 3 * features)
        )
        queries = qkv_rows[..., :features]
        keyvals = qkv_rows[..., features:]
        extended = padded(keyvals, (("seq", 1),), BLOCK)
        global_block = from_root(qkv_rows[:, :glob_rows], "seq", 0)
        requests = rand_micro.reshape(per_micro, devices, entries)
        owners = requests // blocks_dev
        local_block = requests % blocks_dev
        same_owner = owners[:, :, :, None] == owners[:, :, None, :]
        slot_rank = jnp.sum(same_owner & earlier[None, None], axis=3)
        slot_hit = ((owners == my_index)[..., None] & (slot_rank[..., None] == slot_ids)).astype(
            jnp.int32
        )
        slot_live = jnp.sum(slot_hit, axis=2)
        slot_piece = jnp.sum(slot_hit * (local_block * H + entry_heads)[..., None], axis=2)
        piece_index = jnp.transpose(slot_piece, (1, 2, 0))
        live_mask = jnp.transpose(slot_live, (1, 2, 0))
        pieces = (
            keyvals.reshape(per_micro, blocks_dev, BLOCK, 2, H, HEAD)
            .transpose(0, 1, 4, 2, 3, 5)
            .reshape(per_micro, blocks_dev * H, BLOCK, 2 * HEAD)
        )
        outgoing = pieces[seq_ids[None, None, :], piece_index]
        outgoing = jnp.where(live_mask[..., None, None] > 0, outgoing, jnp.zeros((), jnp.bfloat16))
        outgoing = outgoing.reshape(devices * capacity, per_micro, BLOCK, 2 * HEAD)
        incoming = lax.all_to_all(outgoing, "seq", split_axis=0, concat_axis=0, tiled=True)
        my_owner = jnp.take(owners, my_index, axis=1)
        my_rank = jnp.take(slot_rank, my_index, axis=1)
        my_request = jnp.take(requests, my_index, axis=1)
        positions = my_owner * capacity + my_rank
        fetched = incoming[positions, seq_ids[:, None]].reshape(
            per_micro, blocks_dev, H, R, BLOCK, 2, HEAD
        )
        random_keys = fetched[..., 0, :].reshape(per_micro, blocks_dev, H, R * BLOCK, HEAD)
        random_vals = fetched[..., 1, :].reshape(per_micro, blocks_dev, H, R * BLOCK, HEAD)
        seg_blocks = seg_micro.reshape(per_micro, blocks_all, BLOCK)
        query_seg = lax.dynamic_slice_in_dim(seg_micro, my_index * tok_dev, tok_dev, 1).reshape(
            per_micro, blocks_dev, BLOCK
        )
        window_seg = seg_blocks[:, win_clipped].reshape(per_micro, blocks_dev, 3 * BLOCK)
        window_ok = (query_seg[..., :, None] == window_seg[:, :, None, :]) & jnp.repeat(
            win_inside, BLOCK, axis=1
        )[None, :, None, :]
        shared_ok = jnp.concatenate(
            [window_ok, jnp.ones((per_micro, blocks_dev, BLOCK, glob_rows), bool)], axis=3
        )
        random_seg = seg_blocks[seq_ids[:, None], my_request].reshape(
            per_micro, blocks_dev, H, R * BLOCK
        )
        random_ok = query_seg[:, :, None, :, None] == random_seg[:, :, :, None, :]
        ext_blocks = extended.reshape(per_micro, blocks_dev + 2, BLOCK, 2 * features)
        window_kv = ext_blocks[:, window_index].reshape(
            per_micro, blocks_dev, 3 * BLOCK, 2 * features
        )
        glob_kv = jnp.broadcast_to(
            global_block[:, None, :, features:], (per_micro, blocks_dev, glob_rows, 2 * features)
        )
        shared_kv = jnp.concatenate([window_kv, glob_kv], axis=2)
        shared_keys = shared_kv[..., :features].reshape(
            per_micro, blocks_dev, shared_count, H, HEAD
        )
        shared_vals = shared_kv[..., features:].reshape(
            per_micro, blocks_dev, shared_count, H, HEAD
        )
        query_heads = queries.reshape(per_micro, blocks_dev, BLOCK, H, HEAD)
        scores = local_scores(
            query_heads, shared_keys, random_keys, shared_ok, random_ok, scale_factor
        )
        row_max = jnp.max(scores, axis=4, keepdims=True)
        exp_terms = jnp.exp(scores - row_max)
        row_sum = jnp.sum(exp_terms, axis=4, keepdims=True)
        local_probs = exp_terms / row_sum
        log_norm = row_max + jnp.log(row_sum)
        local_weights = local_probs.astype(jnp.bfloat16)
        local_att = jnp.einsum(
            "sbhqk,sbkhd->sbqhd",
            local_weights[..., :shared_count],
            shared_vals,
            preferred_element_type=jnp.float32,
        )
        local_att = local_att + jnp.einsum(
            "sbhqk,sbhkd->sbqhd",
            local_weights[..., shared_count:],
            random_vals,
            preferred_element_type=jnp.float32,
        )
        local_att = local_att.reshape(per_micro, tok_dev, features)
        glob_query = global_block[..., :features].reshape(per_micro, glob_rows, H, HEAD)
        local_keys = keyvals[..., :features].reshape(per_micro, tok_dev, H, HEAD)
        local_vals = keyvals[..., features:].reshape(per_micro, tok_dev, H, HEAD)
        glob_scores = (
            jnp.einsum(
                "sqhd,skhd->shqk", glob_query, local_keys, preferred_element_type=jnp.float32
            )
            * scale_factor
        )
        part_max = jnp.max(glob_scores, axis=3)
        part_sum = jnp.sum(jnp.exp(glob_scores - part_max[..., None]), axis=3)
        glob_max, glob_sum = merged((part_max, part_sum), "seq", merge_stats)
        glob_lse = glob_max + jnp.log(glob_sum)
        glob_probs = jnp.exp(glob_scores - glob_lse[..., None])
        glob_weights = glob_probs.astype(jnp.bfloat16)
        glob_part = jnp.einsum(
            "shqk,skhd->sqhd", glob_weights, local_vals, preferred_element_type=jnp.float32
        ).reshape(per_micro, glob_rows, features)
        glob_out = lax.psum(glob_part, "seq")
        glob_full = jnp.concatenate(
            [glob_out, jnp.zeros((per_micro, tok_dev - glob_rows, features), jnp.float32)], axis=1
        )
        attention = jnp.where(row_global[None, :, None], glob_full, local_att).astype(jnp.bfloat16)
        att_flat = attention.reshape(token_rows, features)
        resid_one = tokens_flat.astype(jnp.float32) + product(att_flat, full_out)
        hidden_one, normed_one, inv_one = norm_forward(resid_one, norm_gain[0], norm_bias[0])
        hidden_low = hidden_one.astype(jnp.bfloat16)
        pre_act = product(hidden_low, full_up)
        activated = gelu_value(pre_act).astype(jnp.bfloat16)
        resid_two = hidden_one + product(activated, full_down)
        result, normed_two, inv_two = norm_forward(resid_two, norm_gain[1], norm_bias[1])
        output_parts.append(result.astype(jnp.bfloat16).reshape(per_micro, tok_dev, features))
        grad_rows = cotangent.reshape(token_rows, features).astype(jnp.float32)
        grad_resid_two, gain_two, shift_two = norm_backward(
            grad_rows, normed_two, inv_two, norm_gain[1]
        )
        grad_branch = grad_resid_two.astype(jnp.bfloat16)
        grad_down_w = grad_down_w + product_tn(activated, grad_branch)
        grad_pre = (product_nt(grad_branch, full_down) * gelu_slope(pre_act)).astype(jnp.bfloat16)
        grad_up_w = grad_up_w + product_tn(hidden_low, grad_pre)
        grad_hidden = grad_resid_two + product_nt(grad_pre, full_up)
        grad_resid_one, gain_one, shift_one = norm_backward(
            grad_hidden, normed_one, inv_one, norm_gain[0]
        )
        grad_mix = grad_resid_one.astype(jnp.bfloat16)
        grad_out_w = grad_out_w + product_tn(att_flat, grad_mix)
        grad_att = (
            product_nt(grad_mix, full_out)
            .astype(jnp.bfloat16)
            .reshape(per_micro, tok_dev, features)
        )
        gain_acc = gain_acc + jnp.stack([gain_one, gain_two])
        shift_acc = shift_acc + jnp.stack([shift_one, shift_two])
        grad_local = jnp.where(
            row_global[None, :, None], jnp.zeros((), jnp.bfloat16), grad_att
        ).reshape(per_micro, blocks_dev, BLOCK, H, HEAD)
        scores = local_scores(
            query_heads, shared_keys, random_keys, shared_ok, random_ok, scale_factor
        )
        local_probs = jnp.exp(scores - log_norm)
        local_weights = local_probs.astype(jnp.bfloat16)
        grad_prob = jnp.concatenate(
            [
                jnp.einsum(
                    "sbqhd,sbkhd->sbhqk",
                    grad_local,
                    shared_vals,
                    preferred_element_type=jnp.float32,
                ),
                jnp.einsum(
                    "sbqhd,sbhkd->sbhqk",
                    grad_local,
                    random_vals,
                    preferred_element_type=jnp.float32,
                ),
            ],
            axis=4,
        )
        row_delta = jnp.sum(local_probs * grad_prob, axis=4, keepdims=True)
        grad_score = (local_probs * (grad_prob - row_delta)).astype(jnp.bfloat16)
        grad_query = jnp.einsum(
            "sbhqk,sbkhd->sbqhd",
            grad_score[..., :shared_count],
            shared_keys,
            preferred_element_type=jnp.float32,
        )
        grad_query = (
            grad_query
            + jnp.einsum(
                "sbhqk,sbhkd->sbqhd",
                grad_score[..., shared_count:],
                random_keys,
                preferred_element_type=jnp.float32,
            )
        ) * scale_factor
        grad_key_shared = (
            jnp.einsum(
                "sbhqk,sbqhd->sbkhd",
                grad_score[..., :shared_count],
                query_heads,
                preferred_element_type=jnp.float32,
            )
            * scale_factor
        )
        grad_val_shared = jnp.einsum(
            "sbhqk,sbqhd->sbkhd",
            local_weights[..., :shared_count],
            grad_local,
            preferred_element_type=jnp.float32,
        )
        grad_key_random = (
            jnp.einsum(
                "sbhqk,sbqhd->sbhkd",
                grad_score[..., shared_count:],
                query_heads,
                preferred_element_type=jnp.float32,
            )
            * scale_factor
        )
        grad_val_random = jnp.einsum(
            "sbhqk,sbqhd->sbhkd",
            local_weights[..., shared_count:],
            grad_local,
            preferred_element_type=jnp.float32,
        )
        grad_shared = jnp.concatenate(
            [
                grad_key_shared.reshape(per_micro, blocks_dev, shared_count, features),
                grad_val_shared.reshape(per_micro, blocks_dev, shared_count, features),
            ],
            axis=3,
        )
        grad_window = grad_shared[:, :, : 3 * BLOCK].reshape(
            per_micro, blocks_dev, 3, BLOCK, 2 * features
        )
        ext_grad = jnp.zeros((per_micro, blocks_dev + 2, BLOCK, 2 * features), jnp.float32)
        for offset in range(3):
            ext_grad = ext_grad.at[:, offset : offset + blocks_dev].add(grad_window[:, :, offset])
        grad_glob_keys = jnp.sum(grad_shared[:, :, 3 * BLOCK :], axis=1)
        grad_random = jnp.stack([grad_key_random, grad_val_random], axis=4).reshape(
            per_micro, entries, BLOCK, 2 * HEAD
        )
        returned = (
            jnp.zeros((devices * capacity, per_micro, BLOCK, 2 * HEAD), jnp.float32)
            .at[positions, seq_ids[:, None]]
            .set(grad_random)
        )
        arrived = lax.all_to_all(
            returned.astype(jnp.bfloat16), "seq", split_axis=0, concat_axis=0, tiled=True
        ).astype(returned.dtype)
        arrived = arrived.reshape(devices, capacity, per_micro, BLOCK, 2 * HEAD) * live_mask[
            ..., None, None
        ].astype(jnp.float32)
        piece_grad = (
            jnp.zeros((per_micro, blocks_dev * H, BLOCK, 2 * HEAD), jnp.float32)
            .at[seq_ids[None, None, :], piece_index]
            .add(arrived)
        )
        piece_grad = (
            piece_grad.reshape(per_micro, blocks_dev, H, BLOCK, 2, HEAD)
            .transpose(0, 1, 3, 4, 2, 5)
            .reshape(per_micro, tok_dev, 2 * features)
        )
        rim_pair = jnp.concatenate([ext_grad[:, 0], ext_grad[:, blocks_dev + 1]], axis=1)
        rim_back = padded(rim_pair.astype(jnp.bfloat16), (("seq", 1),), BLOCK).astype(
            rim_pair.dtype
        )
        grad_kv = (
            ext_grad[:, 1 : blocks_dev + 1].reshape(per_micro, tok_dev, 2 * features) + piece_grad
        )
        grad_kv = grad_kv.at[:, :BLOCK].add(rim_back[:, :BLOCK])
        grad_kv = grad_kv.at[:, tok_dev - BLOCK :].add(rim_back[:, 3 * BLOCK :])
        grad_glob = from_root(grad_att[:, :glob_rows], "seq", 0)
        grad_glob_heads = grad_glob.reshape(per_micro, glob_rows, H, HEAD)
        glob_scores = (
            jnp.einsum(
                "sqhd,skhd->shqk", glob_query, local_keys, preferred_element_type=jnp.float32
            )
            * scale_factor
        )
        glob_probs = jnp.exp(glob_scores - glob_lse[..., None])
        glob_weights = glob_probs.astype(jnp.bfloat16)
        glob_grad_prob = jnp.einsum(
            "sqhd,skhd->shqk", grad_glob_heads, local_vals, preferred_element_type=jnp.float32
        )
        glob_delta = lax.psum(jnp.sum(glob_probs * glob_grad_prob, axis=3), "seq")
        glob_grad_score = (glob_probs * (glob_grad_prob - glob_delta[..., None])).astype(
            jnp.bfloat16
        )
        glob_grad_query = (
            jnp.einsum(
                "shqk,skhd->sqhd", glob_grad_score, local_keys, preferred_element_type=jnp.float32
            )
            * scale_factor
        )
        glob_grad_key = (
            jnp.einsum(
                "shqk,sqhd->skhd", glob_grad_score, glob_query, preferred_element_type=jnp.float32
            )
            * scale_factor
        )
        glob_grad_val = jnp.einsum(
            "shqk,sqhd->skhd", glob_weights, grad_glob_heads, preferred_element_type=jnp.float32
        )
        grad_kv = grad_kv + jnp.concatenate(
            [
                glob_grad_key.reshape(per_micro, tok_dev, features),
                glob_grad_val.reshape(per_micro, tok_dev, features),
            ],
            axis=2,
        )
        summed_query, summed_keys = lax.psum(
            (glob_grad_query.reshape(per_micro, glob_rows, features), grad_glob_keys), "seq"
        )
        grad_kv = grad_kv.at[:, :glob_rows].add(owner_flag * summed_keys)
        grad_queries = (
            grad_query.reshape(per_micro, tok_dev, features)
            .at[:, :glob_rows]
            .add(owner_flag * summed_query)
        )
        grad_qkv_rows = (
            jnp.concatenate([grad_queries, grad_kv], axis=2)
            .astype(jnp.bfloat16)
            .reshape(token_rows, 3 * features)
        )
        grad_qkv_w = grad_qkv_w + product_tn(tokens_flat, grad_qkv_rows)
        input_rows = grad_resid_one + product_nt(grad_qkv_rows, full_qkv)
        input_parts.append(input_rows.reshape(per_micro, tok_dev, features))
    summed = (
        lax.psum_scatter(grad_qkv_w, ("dp", "seq"), scatter_dimension=0, tiled=True),
        lax.psum_scatter(grad_out_w, ("dp", "seq"), scatter_dimension=0, tiled=True),
        lax.psum_scatter(grad_up_w, ("dp", "seq"), scatter_dimension=0, tiled=True),
        lax.psum_scatter(grad_down_w, ("dp", "seq"), scatter_dimension=0, tiled=True),
        lax.psum_scatter(gain_acc, ("dp", "seq"), scatter_dimension=1, tiled=True),
        lax.psum_scatter(shift_acc, ("dp", "seq"), scatter_dimension=1, tiled=True),
    )
    return (
        jnp.concatenate(output_parts, axis=0),
        jnp.concatenate(input_parts, axis=0),
        summed[0],
        summed[1],
        summed[2],
        summed[3],
        summed[4],
        summed[5],
    )


TILE = 128
NH = 3
CH = 256
LOG2E = 1.4426950408889634
SCALE2 = HEAD ** (-0.5) * LOG2E
NEG = -1e30
F32 = jnp.float32
BF16 = jnp.bfloat16


def nt(a, b):
    return lax.dot_general(a, b, (((1,), (1,)), ((), ())), preferred_element_type=F32)


def nn(a, b):
    return jnp.dot(a, b, preferred_element_type=F32)


def biased(s, mask, b1_ref, b0_ref, first_block):
    rows = []
    for j in range(s.shape[0] // BLOCK):
        kb = first_block + j
        m3 = jnp.concatenate([mask[BLOCK * j : BLOCK * (j + 1)]] * NH, axis=1)
        on = b1_ref[0, kb : kb + 1, :]
        off = jnp.concatenate([b0_ref[0, kb : kb + 1, :]] * NH, axis=1)
        rows.append(s[BLOCK * j : BLOCK * (j + 1)] * SCALE2 + jnp.where(m3, on, off))
    return jnp.concatenate(rows, axis=0)


def forward_kernel(
    xs, wg, b1, b0, segk, segq, att, otile, lse, qn, kn, vn, qt, kt, vt, q3, tbuf
):
    step = pl.program_id(0)
    length = xs.shape[0]
    chunks = length // CH

    @pl.when(step == 0)
    def _():
        q3[...] = jnp.zeros_like(q3)
        for j in range(chunks):
            rows = slice(CH * j, CH * (j + 1))
            both = nn(xs[rows, :], wg[...])
            qf, kf, vf = both[:, :256], both[:, 256:512], both[:, 512:]
            qn[rows, :] = qf.astype(BF16)
            kn[rows, :] = kf.astype(BF16)
            vn[rows, :] = vf.astype(BF16)
            qt[:, rows] = qf.T.astype(BF16)
            kt[:, rows] = kf.T.astype(BF16)
            vt[:, rows] = vf.T.astype(BF16)

    cols = pl.ds(pl.multiple_of(step * TILE, TILE), TILE)
    for h in range(NH):
        q3[HEAD * h : HEAD * (h + 1), TILE * h : TILE * (h + 1)] = qt[
            HEAD * h : HEAD * (h + 1), cols
        ]
    top = jnp.full((8, NH * TILE), NEG, F32)
    for j in range(chunks):
        rows = slice(CH * j, CH * (j + 1))
        s = nn(kn[rows, :], q3[...])
        t = biased(s, segk[rows, :] == segq[0], b1, b0, CH // BLOCK * j)
        tbuf[rows, :] = t
        top = jnp.maximum(top, jnp.max(t.reshape(CH // 8, 8, NH * TILE), axis=0))
    peak = jnp.max(top, axis=0, keepdims=True)
    total = jnp.zeros((8, NH * TILE), F32)
    out = jnp.zeros((256, NH * TILE), F32)
    for j in range(chunks):
        rows = slice(CH * j, CH * (j + 1))
        p = jnp.exp2(tbuf[rows, :] - peak)
        total = total + jnp.sum(p.reshape(CH // 8, 8, NH * TILE), axis=0)
        out = out + nn(vt[:, rows], p.astype(BF16))
    weight = jnp.sum(total, axis=0, keepdims=True)
    lse[0] = peak + jnp.log2(weight)
    inv = 1.0 / weight
    heads = [
        out[HEAD * h : HEAD * (h + 1), TILE * h : TILE * (h + 1)] * inv[:, TILE * h : TILE * (h + 1)]
        for h in range(NH)
    ]
    merged = jnp.concatenate(heads, axis=0)
    otile[0] = merged
    att[...] = merged.T.astype(BF16)


def attend_forward(xs, wg, b1, b0, segk, segq):
    length = xs.shape[0]
    steps = length // TILE
    blocks = length // BLOCK
    whole = lambda *shape: pl.BlockSpec(shape, lambda i: (0,) * len(shape))
    per = lambda *shape: pl.BlockSpec((1,) + shape, lambda i: (i,) + (0,) * len(shape))
    nat = jax.ShapeDtypeStruct((length, 256), BF16)
    tra = jax.ShapeDtypeStruct((256, length), BF16)
    return pl.pallas_call(
        forward_kernel,
        grid=(steps,),
        in_specs=[
            whole(*xs.shape), whole(*wg.shape), per(blocks, NH * TILE), per(blocks, TILE),
            whole(*segk.shape), per(1, TILE),
        ],
        out_specs=[
            pl.BlockSpec((TILE, NH * HEAD), lambda i: (i, 0)), per(NH * HEAD, TILE), per(1, NH * TILE),
            whole(length, 256), whole(length, 256), whole(length, 256),
            whole(256, length), whole(256, length),
        ],
        out_shape=[
            jax.ShapeDtypeStruct((length, NH * HEAD), BF16),
            jax.ShapeDtypeStruct((steps, NH * HEAD, TILE), F32),
            jax.ShapeDtypeStruct((steps, 1, NH * TILE), F32),
            nat, nat, nat, tra, tra,
        ],
        scratch_shapes=[
            pltpu.VMEM((256, length), BF16),
            pltpu.VMEM((256, NH * TILE), BF16),
            pltpu.VMEM((length, NH * TILE), F32),
        ],
        name="attend_forward",
    )(xs, wg, b1, b0, segk, segq)


def backward_kernel(
    dat, qn, qt, otile, lse, b1, b0, segk, segq, kn, vn, kt, dqkv, q3t, d3t, q3, d3, dk, dv
):
    step = pl.program_id(0)
    steps = pl.num_programs(0)
    length = kn.shape[0]
    chunks = length // CH

    @pl.when(step == 0)
    def _():
        q3t[...] = jnp.zeros_like(q3t)
        d3t[...] = jnp.zeros_like(d3t)
        dk[...] = jnp.zeros_like(dk)
        dv[...] = jnp.zeros_like(dv)

    dat_f = dat[...].astype(F32)
    dat_t = dat_f.T
    lane = lax.broadcasted_iota(jnp.int32, (TILE, NH * HEAD), 1) // HEAD
    qblk = qn[:, : NH * HEAD].astype(F32)
    delta = []
    for h in range(NH):
        hr = slice(HEAD * h, HEAD * (h + 1))
        hc = slice(TILE * h, TILE * (h + 1))
        q3t[hr, hc] = qt[hr, :]
        d3t[hr, hc] = dat_t[hr].astype(BF16)
        q3[hc, :] = jnp.where(lane == h, qblk, 0.0).astype(BF16)
        d3[hc, :] = jnp.where(lane == h, dat_f, 0.0).astype(BF16)
        delta.append(jnp.sum(dat_t[hr] * otile[0, hr, :], axis=0, keepdims=True))
    delta = jnp.concatenate(delta, axis=1)
    norm = lse[0]
    dq = jnp.zeros((256, NH * TILE), F32)
    for j in range(chunks):
        rows = slice(CH * j, CH * (j + 1))
        s = nn(kn[rows, :], q3t[...])
        dp = nn(vn[rows, :], d3t[...])
        t = biased(s, segk[rows, :] == segq[0], b1, b0, CH // BLOCK * j)
        p = jnp.exp2(t - norm)
        ds = (p * (dp - delta)).astype(BF16)
        dv[rows, :] += nn(p.astype(BF16), d3[...])
        dk[rows, :] += nn(ds, q3[...])
        dq = dq + nn(kt[:, rows], ds)
    heads = [dq[HEAD * h : HEAD * (h + 1), TILE * h : TILE * (h + 1)] for h in range(NH)]
    merged = jnp.concatenate(heads, axis=0).T * HEAD ** (-0.5)
    here = pl.ds(pl.multiple_of(step * TILE, TILE), TILE)
    dqkv[here, : NH * HEAD] = merged.astype(BF16)

    @pl.when(step == steps - 1)
    def _():
        gap = jnp.zeros((length, 256 - NH * HEAD), BF16)
        for g in range(3):
            dqkv[:, 256 * g + NH * HEAD : 256 * (g + 1)] = gap
        dqkv[:, 256 : 256 + NH * HEAD] = (dk[...] * HEAD ** (-0.5)).astype(BF16)
        dqkv[:, 512 : 512 + NH * HEAD] = dv[...].astype(BF16)


def attend_backward(dat, qn, qt, otile, lse, b1, b0, segk, segq, kn, vn, kt):
    length = kn.shape[0]
    steps = length // TILE
    blocks = length // BLOCK
    whole = lambda *shape: pl.BlockSpec(shape, lambda i: (0,) * len(shape))
    per = lambda *shape: pl.BlockSpec((1,) + shape, lambda i: (i,) + (0,) * len(shape))
    return pl.pallas_call(
        backward_kernel,
        grid=(steps,),
        in_specs=[
            pl.BlockSpec((TILE, NH * HEAD), lambda i: (i, 0)),
            pl.BlockSpec((TILE, 256), lambda i: (i, 0)),
            pl.BlockSpec((256, TILE), lambda i: (0, i)),
            per(NH * HEAD, TILE), per(1, NH * TILE),
            per(blocks, NH * TILE), per(blocks, TILE),
            whole(*segk.shape), per(1, TILE),
            whole(*kn.shape), whole(*vn.shape), whole(*kt.shape),
        ],
        out_specs=whole(length, 768),
        out_shape=jax.ShapeDtypeStruct((length, 768), BF16),
        scratch_shapes=[
            pltpu.VMEM((256, NH * TILE), BF16),
            pltpu.VMEM((256, NH * TILE), BF16),
            pltpu.VMEM((NH * TILE, NH * HEAD), BF16),
            pltpu.VMEM((NH * TILE, NH * HEAD), BF16),
            pltpu.VMEM((length, NH * HEAD), F32),
            pltpu.VMEM((length, NH * HEAD), F32),
        ],
        name="attend_backward",
    )(dat, qn, qt, otile, lse, b1, b0, segk, segq, kn, vn, kt)


def tables(rand, seg):
    blocks = rand.shape[0]
    qb = jnp.arange(blocks, dtype=jnp.int32)
    near = (jnp.abs(qb[:, None] - qb[None, :]) <= 1).astype(jnp.int32)
    hits = jnp.sum((rand[:, None, :, :] == qb[None, :, None, None]).astype(jnp.int32), axis=3)
    local = (qb >= 2).astype(jnp.int32)
    listed = (near[:, :, None] + hits) * local[:, None, None]
    fixed = ((qb[:, None] < 2) | (qb[None, :] < 2)).astype(jnp.int32)
    log_of = lambda n: jnp.where(n > 0, jnp.log2(jnp.maximum(n, 1).astype(F32)), NEG)
    b1 = log_of(listed + fixed[:, :, None])
    b0 = log_of(fixed)
    steps = blocks // 2
    b1 = b1.reshape(steps, 2, blocks, NH).transpose(0, 2, 3, 1)
    b1 = jnp.broadcast_to(b1[..., None], (steps, blocks, NH, 2, BLOCK)).reshape(steps, blocks, NH * TILE)
    b0 = b0.reshape(steps, 2, blocks).transpose(0, 2, 1)
    b0 = jnp.broadcast_to(b0[..., None], (steps, blocks, 2, BLOCK)).reshape(steps, blocks, TILE)
    segk = jnp.broadcast_to(seg[:, None], (seg.shape[0], TILE))
    segq = seg.reshape(steps, 1, TILE)
    return b1, b0, segk, segq


MESH = pl.DeviceIdType.MESH
ANYSPACE = pl.BlockSpec(memory_space=pl.ANY)
VMEMSPACE = pl.BlockSpec(memory_space=pltpu.VMEM)


class Copies:
    def __init__(self, send, recv):
        self.send = send
        self.recv = recv
        self.used = 0

    def to(self, src, dst, device):
        index = self.used
        self.used += 1
        return pltpu.make_async_remote_copy(
            src_ref=src, dst_ref=dst, send_sem=self.send.at[index], recv_sem=self.recv.at[index],
            device_id=device, device_id_type=MESH,
        )


class Place:
    def __init__(self):
        self.d = lax.axis_index("dp")
        self.t = lax.axis_index("seq")
        self.x = lax.rem(self.d, 2)
        self.y = self.d // 2
        self.c = lax.rem(self.t, 2)
        self.z = self.t // 2
        self.half = self.z // 2
        self.xn = self.d + 1 - 2 * self.x
        self.yn = self.d + 2 - 4 * self.y
        self.diag = 3 - self.d
        self.pair_z = self.z + 1 - 2 * lax.rem(self.z, 2)
        self.across_x = (self.xn, self.t)
        self.across_y = (self.yn, self.t)
        self.partner = (self.d, self.t + 1 - 2 * self.c)

    def at_z(self, z):
        return (self.d, 2 * z + self.c)


def meet(devices):
    barrier = pltpu.get_barrier_semaphore()
    for device in devices:
        pl.semaphore_signal(barrier, inc=1, device_id=device, device_id_type=MESH)
    pl.semaphore_wait(barrier, len(devices))


def gather_kernel(x, wg, wo, wu, wd, xs, wgf, wof, wuf, wdf, send, recv, xsend, xrecv, local):
    me = Place()
    d, t, c, z = me.d, me.t, me.c, me.z
    mine, other = me.half, 1 - me.half
    middle = 1 + me.half
    is_middle = z == middle
    z_step = [me.at_z(lax.rem(z + k, 4)) for k in (1, 2, 3)]
    meet([me.across_x, me.across_y, me.partner] + z_step)
    cps = Copies(send, recv)

    wg_x = cps.to(wg, wgf.at[d], me.across_x)
    wg_y = cps.to(wg, wgf.at[d], me.across_y)
    wg_x.start()
    wg_y.start()
    near = cps.to(x.at[mine], xs.at[t], me.at_z(me.pair_z))
    near.start()
    row = lax.rem(z, 2)
    far = pltpu.make_async_remote_copy(
        src_ref=x.at[other], dst_ref=xs.at[t], send_sem=xsend.at[0], recv_sem=xrecv.at[row],
        device_id=me.at_z(2 - me.half), device_id_type=MESH,
    )
    far.start()
    give = cps.to(x.at[mine], xs.at[t], me.partner)
    give.start()
    keeps = [
        pltpu.make_async_copy(x.at[mine], xs.at[t], local.at[0]),
        pltpu.make_async_copy(wg, wgf.at[d], local.at[1]),
        pltpu.make_async_copy(wo, wof.at[d], local.at[2]),
        pltpu.make_async_copy(wu, wuf.at[d], local.at[3]),
        pltpu.make_async_copy(wd, wdf.at[d], local.at[4]),
    ]
    for keep in keeps:
        keep.start()
    heavy = []
    for w, full in ((wo, wof), (wu, wuf), (wd, wdf)):
        rows = w.shape[0] // 2
        part = pl.ds(pl.multiple_of(c * rows, rows), rows)
        to_x = cps.to(w.at[part], full.at[d, part], me.across_x)
        to_y = cps.to(w.at[part], full.at[d, part], me.across_y)
        to_x.start()
        to_y.start()
        heavy.append((full, rows, to_x, to_y))

    half = wg.shape[0] // 2
    lo, hi = pl.ds(0, half), pl.ds(half, half)
    wg_x.wait_recv()
    wg_dy = cps.to(wgf.at[me.xn, lo], wgf.at[me.xn, lo], me.across_y)
    wg_dy.start()
    wg_y.wait_recv()
    wg_dx = cps.to(wgf.at[me.yn, hi], wgf.at[me.yn, hi], me.across_x)
    wg_dx.start()

    near.wait_recv()
    near_t = 2 * me.pair_z + c
    pass_near = cps.to(xs.at[near_t], xs.at[near_t], me.partner)
    pass_near.start()
    passes = []
    for j in range(2):
        src_t = 2 * (2 * other + j) + c
        relay = pltpu.make_async_remote_copy(
            src_ref=xs.at[src_t], dst_ref=xs.at[src_t], send_sem=xsend.at[1 + j],
            recv_sem=xrecv.at[j], device_id=me.at_z(me.pair_z), device_id_type=MESH,
        )
        relay.wait_recv()

        @pl.when(is_middle)
        def _():
            relay.start()

        onward = cps.to(xs.at[src_t], xs.at[src_t], me.partner)
        onward.start()
        passes.append((relay, onward))

    tail = []
    for full, rows, to_x, to_y in heavy:
        part = pl.ds(pl.multiple_of(c * rows, rows), rows)
        quarter = rows // 2
        lo = pl.ds(pl.multiple_of(c * rows, quarter), quarter)
        hi = pl.ds(pl.multiple_of(c * rows + quarter, quarter), quarter)
        to_x.wait_recv()
        dy = cps.to(full.at[me.xn, lo], full.at[me.xn, lo], me.across_y)
        px = cps.to(full.at[me.xn, part], full.at[me.xn, part], me.partner)
        dy.start()
        px.start()
        to_y.wait_recv()
        dx = cps.to(full.at[me.yn, hi], full.at[me.yn, hi], me.across_x)
        py = cps.to(full.at[me.yn, part], full.at[me.yn, part], me.partner)
        dx.start()
        py.start()
        tail.append((full, part, lo, hi, dy, dx, px, py, to_x, to_y))
    ends = []
    for full, part, lo, hi, dy, dx, px, py, to_x, to_y in tail:
        dy.wait_recv()
        dx.wait_recv()
        pd = cps.to(full.at[me.diag, part], full.at[me.diag, part], me.partner)
        pd.start()
        ends.append(pd)

    wg_dy.wait_recv()
    wg_dx.wait_recv()
    give.wait_recv()
    pass_near.wait_recv()
    for relay, onward in passes:
        onward.wait()

        @pl.when(is_middle)
        def _():
            relay.wait_send()

    for pd in ends:
        pd.wait()
    for full, part, lo, hi, dy, dx, px, py, to_x, to_y in tail:
        px.wait()
        py.wait()
        for cp in (dy, dx, to_x, to_y):
            cp.wait_send()
    for cp in (wg_x, wg_y, wg_dx, wg_dy, near, far, give, pass_near):
        cp.wait_send()
    for keep in keeps:
        keep.wait()


def gather(x, wg, wo, wu, wd):
    dp = lax.axis_size("dp")
    seq = lax.axis_size("seq")
    shapes = [(seq,) + x.shape[1:]] + [(dp,) + w.shape for w in (wg, wo, wu, wd)]
    return pl.pallas_call(
        gather_kernel,
        in_specs=[VMEMSPACE] * 5,
        out_specs=[ANYSPACE] * 5,
        out_shape=[jax.ShapeDtypeStruct(shape, BF16) for shape in shapes],
        scratch_shapes=[
            pltpu.SemaphoreType.DMA((40,)),
            pltpu.SemaphoreType.DMA((40,)),
            pltpu.SemaphoreType.DMA((3,)),
            pltpu.SemaphoreType.DMA((2,)),
            pltpu.SemaphoreType.DMA((5,)),
        ],
        compiler_params=pltpu.CompilerParams(collective_id=0, has_side_effects=True),
        name="gather",
    )(x, wg, wo, wu, wd)


def swap_kernel(src, dst, send, recv, local):
    d = lax.axis_index("dp")
    t = lax.axis_index("seq")
    count = src.shape[0]
    peers = [lax.rem(t + k, count) for k in range(1, count)]
    meet([(d, peer) for peer in peers])
    cps = Copies(send, recv)
    moves = [cps.to(src.at[peer], dst.at[t], (d, peer)) for peer in peers]
    for move in moves:
        move.start()
    keep = pltpu.make_async_copy(src.at[t], dst.at[t], local.at[0])
    keep.start()
    for move in moves:
        move.wait()
    keep.wait()


def swap(src, number):
    count = src.shape[0]
    return pl.pallas_call(
        swap_kernel,
        in_specs=[VMEMSPACE],
        out_specs=ANYSPACE,
        out_shape=jax.ShapeDtypeStruct(src.shape, src.dtype),
        scratch_shapes=[
            pltpu.SemaphoreType.DMA((count,)),
            pltpu.SemaphoreType.DMA((count,)),
            pltpu.SemaphoreType.DMA((1,)),
        ],
        compiler_params=pltpu.CompilerParams(collective_id=number, has_side_effects=True),
        name="swap",
    )(src)


def each(count, body):
    def run(i, carry):
        body(i)
        return carry

    lax.fori_loop(0, count, run, 0)


def plus(a, b):
    return a.astype(F32) + b.astype(F32)


def reduce_kernel(*refs):
    (g0, g1, g2, stats), refs = refs[:4], refs[4:]
    (o0, o1, o2, stats_out), refs = refs[:4], refs[4:]
    bufs, refs = refs[:18], refs[18:]
    nsend, nrecv, send, recv, local = refs
    me = Place()
    c, z, x, y = me.c, me.z, me.x, me.y
    z_step = [lax.rem(z + k, 4) for k in (1, 2, 3)]
    meet([me.across_x, me.across_y, me.partner] + [me.at_z(k) for k in z_step])
    cps = Copies(send, recv)
    works = []
    for i, (g, o) in enumerate(((g2, o2), (g1, o1), (g0, o0))):
        own, ra, rb1, rb2, rc, rd = bufs[6 * i : 6 * i + 6]
        swap_core = cps.to(g.at[:, :, :, 1 - c], ra, me.partner)
        swap_core.start()
        load = pltpu.make_async_copy(g.at[:, :, :, c], own, local.at[i])
        load.start()
        works.append((o, own, ra, rb1, rb2, rc, rd, swap_core, load))
    stat_to = [me.partner, me.across_x, me.across_y, me.at_z(me.pair_z), me.at_z(lax.rem(z + 2, 4))]
    nsend[0] = stats[...]
    stat = cps.to(nsend.at[0], nrecv.at[0], stat_to[0])
    stat.start()
    stat_all = [stat]
    stage_b = []
    for o, own, ra, rb1, rb2, rc, rd, swap_core, load in works:
        load.wait()
        swap_core.wait_recv()

        def fold(i):
            yy, xx, zz = i // 8, lax.rem(i // 4, 2), lax.rem(i, 4)
            own[yy, xx, zz] = plus(own[yy, xx, zz], ra[yy, xx, zz]).astype(BF16)

        each(16, fold)
        bx = cps.to(own.at[:, 1 - x, 0:2], rb1, me.across_x)
        by = cps.to(own.at[1 - y, :, 2:4], rb2, me.across_y)
        bx.start()
        by.start()
        stage_b.append((bx, by))
        k = len(stat_all)
        stat_all[-1].wait_recv()
        nsend[k] = nsend[k - 1] + nrecv[k - 1]
        stat = cps.to(nsend.at[k], nrecv.at[k], stat_to[k])
        stat.start()
        stat_all.append(stat)
    stage_c = []
    for (o, own, ra, rb1, rb2, rc, rd, swap_core, load), (bx, by) in zip(works, stage_b):
        bx.wait_recv()

        def fold_x(i):
            yy, zz = i // 2, lax.rem(i, 2)
            rb1[yy, zz] = plus(own[yy, x, zz], rb1[yy, zz]).astype(BF16)

        each(4, fold_x)
        cy = cps.to(rb1.at[1 - y], rc.at[0:2], me.across_y)
        cy.start()
        by.wait_recv()

        def fold_y(i):
            xx, zz = i // 2, lax.rem(i, 2)
            rb2[xx, zz] = plus(own[y, xx, 2 + zz], rb2[xx, zz]).astype(BF16)

        each(4, fold_y)
        cx = cps.to(rb2.at[1 - x], rc.at[2:4], me.across_x)
        cx.start()
        stage_c.append((cy, cx))
        if len(stat_all) < 5:
            k = len(stat_all)
            stat_all[-1].wait_recv()
            nsend[k] = nsend[k - 1] + nrecv[k - 1]
            stat = cps.to(nsend.at[k], nrecv.at[k], stat_to[k])
            stat.start()
            stat_all.append(stat)
    stage_d = []
    for (o, own, ra, rb1, rb2, rc, rd, swap_core, load), (cy, cx) in zip(works, stage_c):
        cy.wait_recv()
        cx.wait_recv()
        for zz in range(2):
            rc[zz] = plus(rb1[y, zz], rc[zz]).astype(BF16)
            rc[2 + zz] = plus(rb2[x, zz], rc[2 + zz]).astype(BF16)
        ds = [cps.to(rc.at[k], rd.at[j], me.at_z(k)) for j, k in enumerate(z_step)]
        for cp in ds:
            cp.start()
        stage_d.append(ds)
    stat_all[-1].wait_recv()
    stats_out[...] = nsend[4] + nrecv[4]
    for (o, own, ra, rb1, rb2, rc, rd, swap_core, load), ds in zip(works, stage_d):
        for cp in ds:
            cp.wait_recv()
        o[...] = plus(rc[z], rd[0]) + plus(rd[1], rd[2])
    for cp in stat_all:
        cp.wait_send()
    for work, bs, cs, ds in zip(works, stage_b, stage_c, stage_d):
        for cp in (work[7],) + bs + cs + tuple(ds):
            cp.wait_send()


def reduce_grads(grads, stats):
    dims = [g.shape[-2:] for g in grads]
    bufs = []
    for rows, cols in dims[::-1]:
        bufs += [
            pltpu.VMEM((2, 2, 4, rows, cols), BF16),
            pltpu.VMEM((2, 2, 4, rows, cols), BF16),
            pltpu.VMEM((2, 2, rows, cols), BF16),
            pltpu.VMEM((2, 2, rows, cols), BF16),
            pltpu.VMEM((4, rows, cols), BF16),
            pltpu.VMEM((3, rows, cols), BF16),
        ]
    return pl.pallas_call(
        reduce_kernel,
        in_specs=[ANYSPACE] * 3 + [VMEMSPACE],
        out_specs=[VMEMSPACE] * 4,
        out_shape=[jax.ShapeDtypeStruct(dim, F32) for dim in dims]
        + [jax.ShapeDtypeStruct(stats.shape, F32)],
        scratch_shapes=bufs
        + [
            pltpu.VMEM((5,) + stats.shape, F32),
            pltpu.VMEM((5,) + stats.shape, F32),
            pltpu.SemaphoreType.DMA((29,)),
            pltpu.SemaphoreType.DMA((29,)),
            pltpu.SemaphoreType.DMA((3,)),
        ],
        compiler_params=pltpu.CompilerParams(collective_id=3, has_side_effects=True),
        name="reduce_grads",
    )(*grads, stats)


def finish_kernel(
    part, dwg, ig, wq, own, rp, ra, rb, ro, wb1, wb2, wc, wr, send, recv, local
):
    me = Place()
    c, z, x, y, t = me.c, me.z, me.x, me.y, me.t
    mine, other = me.half, 1 - me.half
    is_middle = z == 1 + me.half
    z_step = [lax.rem(z + k, 4) for k in (1, 2, 3)]
    peers = [lax.rem(t + k, 8) for k in range(1, 8)]
    meet([me.across_x, me.across_y] + [(me.d, peer) for peer in peers])
    cps = Copies(send, recv)
    core = cps.to(part.at[:, 1 - c], rp, me.partner)
    core.start()
    bx = cps.to(dwg.at[:, 1 - x, 0:4], wb1, me.across_x)
    by = cps.to(dwg.at[1 - y, :, 4:8], wb2, me.across_y)
    bx.start()
    by.start()
    core.wait_recv()

    def fold(i):
        own[i] = plus(part[i, c], rp[i]).astype(BF16)

    each(4, fold)
    near = cps.to(own.at[me.pair_z], ra, me.at_z(me.pair_z))
    near.start()
    middle_t = me.at_z(me.pair_z)
    up = [cps.to(own.at[2 * other + j], rb.at[j], middle_t) for j in range(2)]
    down = [
        pltpu.make_async_remote_copy(
            src_ref=own.at[2 * other + j], dst_ref=ro, send_sem=send.at[cps.used + j],
            recv_sem=recv.at[cps.used], device_id=me.at_z(2 * other + j), device_id_type=MESH,
        )
        for j in range(2)
    ]
    cps.used += 2

    @pl.when(z != 1 + me.half)
    def _():
        for cp in up:
            cp.start()

    bx.wait_recv()

    def fold_x(i):
        yy, tt = i // 4, lax.rem(i, 4)
        wb1[yy, tt] = plus(dwg[yy, x, tt], wb1[yy, tt]).astype(BF16)

    each(8, fold_x)
    cy = cps.to(wb1.at[1 - y], wc.at[0:4], me.across_y)
    cy.start()
    by.wait_recv()

    def fold_y(i):
        xx, tt = i // 4, lax.rem(i, 4)
        wb2[xx, tt] = plus(dwg[y, xx, 4 + tt], wb2[xx, tt]).astype(BF16)

    each(8, fold_y)
    cx = cps.to(wb2.at[1 - x], wc.at[4:8], me.across_x)
    cx.start()

    @pl.when(is_middle)
    def _():
        for j in range(2):
            up[j].wait_recv()
            own[2 * other + j] = plus(own[2 * other + j], rb[j]).astype(BF16)
            down[j].start()

    cy.wait_recv()
    cx.wait_recv()

    def fold_c(i):
        wc[i] = plus(wb1[y, i], wc[i]).astype(BF16)
        wc[4 + i] = plus(wb2[x, i], wc[4 + i]).astype(BF16)

    each(4, fold_c)
    moves = [cps.to(wc.at[peer], wr.at[t], (me.d, peer)) for peer in peers]
    for move in moves:
        move.start()
    near.wait_recv()
    ig[mine] = plus(own[z], ra[...])
    down[0].wait_recv()
    ig[other] = ro[...].astype(F32)
    wr[t] = wc[t]
    for move in moves:
        move.wait_recv()
    for g in range(4):
        wq[g] = plus(wr[g], wr[4 + g])
    for cp in [core, bx, by, near, cy, cx] + moves:
        cp.wait_send()

    @pl.when(z != 1 + me.half)
    def _():
        for cp in up:
            cp.wait_send()

    @pl.when(is_middle)
    def _():
        for cp in down:
            cp.wait_send()


def finish(part, dwg):
    rows, cols = part.shape[-2:]
    wrows, wcols = dwg.shape[-2:]
    return pl.pallas_call(
        finish_kernel,
        in_specs=[VMEMSPACE] * 2,
        out_specs=[VMEMSPACE] * 2,
        out_shape=[
            jax.ShapeDtypeStruct((2, rows, cols), F32),
            jax.ShapeDtypeStruct((4, wrows, wcols), F32),
        ],
        scratch_shapes=[
            pltpu.VMEM((4, rows, cols), BF16),
            pltpu.VMEM((4, rows, cols), BF16),
            pltpu.VMEM((rows, cols), BF16),
            pltpu.VMEM((2, rows, cols), BF16),
            pltpu.VMEM((rows, cols), BF16),
            pltpu.VMEM((2, 4, wrows, wcols), BF16),
            pltpu.VMEM((2, 4, wrows, wcols), BF16),
            pltpu.VMEM((8, wrows, wcols), BF16),
            pltpu.VMEM((8, wrows, wcols), BF16),
            pltpu.SemaphoreType.DMA((20,)),
            pltpu.SemaphoreType.DMA((20,)),
            pltpu.SemaphoreType.DMA((1,)),
        ],
        compiler_params=pltpu.CompilerParams(collective_id=4, has_side_effects=True),
        name="finish",
    )(part, dwg)


def head_layout(
    inputs, segments, rand_blocks, w_qkv, w_out, w_up, w_down, norm_gain, norm_bias, out_grad
):
    seqs, tok, features = inputs.shape
    seq = lax.axis_size("seq")
    t = lax.axis_index("seq")
    groups = seq // seqs
    my_seq, my_group = t // groups, lax.rem(t, groups)
    width = features // groups
    shard = w_qkv.reshape(w_qkv.shape[0], 3, groups, width)
    shard = lax.dynamic_index_in_dim(shard, my_group, 2, keepdims=False)
    shard = jnp.pad(shard, ((0, 0), (0, 0), (0, 256 - width))).reshape(w_qkv.shape[0], 768)
    rand = lax.dynamic_slice_in_dim(
        lax.dynamic_index_in_dim(rand_blocks, my_seq, 0, keepdims=False), my_group * NH, NH, 1
    )
    seg = lax.dynamic_index_in_dim(segments, my_seq, 0, keepdims=False)
    b1, b0, segk, segq = tables(rand, seg)
    xs, wgf, wof, wuf, wdf = gather(inputs, shard, w_out, w_up, w_down)
    xs = xs.reshape(seq * tok, features)
    wgf = wgf.reshape(features, 768)
    full_out = wof.reshape(features, features)
    full_up = wuf.reshape(features, -1)
    full_down = wdf.reshape(-1, features)
    att, otile, lse, qn, kn, vn, qt, kt = attend_forward(xs, wgf, b1, b0, segk, segq)
    att_home = swap(att.reshape(seq, tok, width), 1)
    att_flat = (
        att_home.reshape(seqs, groups, tok, width).transpose(0, 2, 1, 3).reshape(seqs * tok, features)
    )
    tokens_flat = inputs.reshape(seqs * tok, features)
    resid_one = tokens_flat.astype(F32) + product(att_flat, full_out)
    hidden_one, normed_one, inv_one = norm_forward(resid_one, norm_gain[0], norm_bias[0])
    hidden_low = hidden_one.astype(BF16)
    pre_act = product(hidden_low, full_up)
    activated = gelu_value(pre_act).astype(BF16)
    resid_two = hidden_one + product(activated, full_down)
    result, normed_two, inv_two = norm_forward(resid_two, norm_gain[1], norm_bias[1])
    grad_rows = out_grad.reshape(seqs * tok, features).astype(F32)
    grad_resid_two, gain_two, shift_two = norm_backward(
        grad_rows, normed_two, inv_two, norm_gain[1]
    )
    grad_branch = grad_resid_two.astype(BF16)
    grad_down_w = product_tn(activated, grad_branch).astype(BF16)
    grad_pre = (product_nt(grad_branch, full_down) * gelu_slope(pre_act)).astype(BF16)
    grad_up_w = product_tn(hidden_low, grad_pre).astype(BF16)
    grad_hidden = grad_resid_two + product_nt(grad_pre, full_up)
    grad_resid_one, gain_one, shift_one = norm_backward(
        grad_hidden, normed_one, inv_one, norm_gain[0]
    )
    grad_mix = grad_resid_one.astype(BF16)
    grad_out_w = product_tn(att_flat, grad_mix).astype(BF16)
    grad_att = product_nt(grad_mix, full_out).astype(BF16)
    grad_att = grad_att.reshape(seqs, tok, groups, width).transpose(0, 2, 1, 3)
    dat = swap(grad_att.reshape(seq, tok, width), 2).reshape(seq * tok, width)
    stats = jnp.stack([gain_one, gain_two, shift_one, shift_two])
    cut = lambda g: g.reshape(2, 2, 4, 2, g.shape[0] // 32, g.shape[1])
    out_sum, up_sum, down_sum, stats = reduce_grads(
        [cut(grad_out_w), cut(grad_up_w), cut(grad_down_w)], stats
    )
    dqkv = attend_backward(dat, qn, qt, otile, lse, b1, b0, segk, segq, kn, vn, kt)
    part = product_nt(dqkv, wgf).astype(BF16).reshape(4, 2, tok, features)
    dwg = product_tn(xs, dqkv).astype(BF16).reshape(2, 2, 8, features // 32, 768)
    ig, wq = finish(part, dwg)
    wq = wq.reshape(groups, features // 32, 3, 256)[..., :width].transpose(1, 2, 0, 3)
    mine = lax.axis_index("dp") * seq + t
    stats = lax.dynamic_slice_in_dim(stats, mine * (features // 32), features // 32, 1)
    return (
        result.astype(BF16).reshape(seqs, tok, features),
        ig + grad_resid_one.reshape(seqs, tok, features),
        wq.reshape(features // 32, 3 * features),
        out_sum,
        up_sum,
        down_sum,
        stats[:2],
        stats[2:],
    )


def solution(mesh):
    in_specs = (
        P("dp", "seq", None),
        P("dp", None),
        P("dp", None, None, None),
        P("dp", None),
        P("dp", None),
        P("dp", None),
        P("dp", None),
        P(),
        P(),
        P("dp", "seq", None),
    )
    out_specs = (
        P("dp", "seq", None),
        P("dp", "seq", None),
        P(("dp", "seq"), None),
        P(("dp", "seq"), None),
        P(("dp", "seq"), None),
        P(("dp", "seq"), None),
        P(None, ("dp", "seq")),
        P(None, ("dp", "seq")),
    )
    fits = mesh.shape["dp"] == 4 and mesh.shape["seq"] == 8
    return jax.shard_map(
        head_layout if fits else per_device, mesh=mesh, in_specs=in_specs, out_specs=out_specs, check_vma=False
    )
```

```python
import jax
import jax.numpy as jnp
import numpy as np
from jax import lax
from jax.experimental import pallas as pl
from jax.experimental.pallas import tpu as pltpu
from jax.sharding import PartitionSpec as P

H = 12
HEAD = 64
BLOCK = 64
R = 3
MICRO = 2


norm_eps = 1e-05
masked_score = -1e30
root_half = 0.7071067811865476
inv_root_two_pi = 0.3989422804014327


def padded(cells, sides, width):
    for axis, dim in sides:
        count = lax.axis_size(axis)
        ends = count - 1
        head = lax.slice_in_dim(cells, 0, width, axis=dim)
        tail = lax.slice_in_dim(cells, cells.shape[dim] - width, cells.shape[dim], axis=dim)
        cells = jnp.concatenate(
            [
                lax.ppermute(tail, axis, [(i, (i + 1) % count) for i in range(ends)]),
                cells,
                lax.ppermute(head, axis, [((i + 1) % count, i) for i in range(ends)]),
            ],
            axis=dim,
        )
    return cells


def from_root(x, axis, root):
    mine = lax.axis_index(axis) == root
    return lax.psum(jnp.where(mine, x, jnp.zeros_like(x)), axis)


def merged(x, axis, combine):
    everything = jax.tree.map(lambda part: lax.all_gather(part, axis), x)
    initial = jax.tree.map(lambda part: part[0], everything)

    def step(k, so_far):
        return combine(so_far, jax.tree.map(lambda part: part[k], everything))

    return lax.fori_loop(1, lax.axis_size(axis), step, initial)


def product(left_side, right_side):
    return jnp.dot(left_side, right_side, preferred_element_type=jnp.float32)


def product_tn(left_side, right_side):
    return lax.dot_general(
        left_side, right_side, (((0,), (0,)), ((), ())), preferred_element_type=jnp.float32
    )


def product_nt(left_side, right_side):
    return lax.dot_general(
        left_side, right_side, (((1,), (1,)), ((), ())), preferred_element_type=jnp.float32
    )


def gelu_value(pre_act):
    return 0.5 * pre_act * (1.0 + lax.erf(pre_act * root_half))


def gelu_slope(pre_act):
    return (
        0.5 * (1.0 + lax.erf(pre_act * root_half))
        + pre_act * jnp.exp(-0.5 * pre_act * pre_act) * inv_root_two_pi
    )


def norm_forward(residual, gain_row, shift_row):
    mean_row = jnp.mean(residual, axis=-1, keepdims=True)
    centred = residual - mean_row
    variance = jnp.mean(centred * centred, axis=-1, keepdims=True)
    inv_std = lax.rsqrt(variance + norm_eps)
    normed = centred * inv_std
    return (normed * gain_row + shift_row, normed, inv_std)


def norm_backward(grad_rows, normed, inv_std, gain_row):
    scaled = grad_rows * gain_row
    back_rows = inv_std * (
        scaled
        - jnp.mean(scaled, axis=-1, keepdims=True)
        - normed * jnp.mean(scaled * normed, axis=-1, keepdims=True)
    )
    return (back_rows, jnp.sum(grad_rows * normed, axis=0), jnp.sum(grad_rows, axis=0))


def merge_stats(first_pair, second_pair):
    joint_max = jnp.maximum(first_pair[0], second_pair[0])
    joint_sum = first_pair[1] * jnp.exp(first_pair[0] - joint_max) + second_pair[1] * jnp.exp(
        second_pair[0] - joint_max
    )
    return (joint_max, joint_sum)


def local_scores(query_heads, shared_keys, random_keys, shared_ok, random_ok, scale_factor):
    part_shared = jnp.einsum(
        "sbqhd,sbkhd->sbhqk", query_heads, shared_keys, preferred_element_type=jnp.float32
    )
    part_random = jnp.einsum(
        "sbqhd,sbhkd->sbhqk", query_heads, random_keys, preferred_element_type=jnp.float32
    )
    scores = jnp.concatenate([part_shared, part_random], axis=4) * scale_factor
    allowed = jnp.concatenate(
        [jnp.broadcast_to(shared_ok[:, :, None], part_shared.shape), random_ok], axis=4
    )
    return jnp.where(allowed, scores, masked_score)


def per_device(
    inputs, segments, rand_blocks, w_qkv, w_out, w_up, w_down, norm_gain, norm_bias, out_grad
):
    seq_total, tok_dev, features = inputs.shape
    devices = lax.axis_size("seq")
    my_index = lax.axis_index("seq")
    blocks_dev = tok_dev // BLOCK
    blocks_all = blocks_dev * devices
    entries = blocks_dev * H * R
    capacity = max(2, entries // devices + 1)
    per_micro = seq_total // MICRO
    glob_rows = 2 * BLOCK
    shared_count = 5 * BLOCK
    scale_factor = HEAD ** (-0.5)
    token_rows = per_micro * tok_dev
    owner_flag = (my_index == 0).astype(jnp.float32)
    row_global = my_index * tok_dev + jnp.arange(tok_dev, dtype=jnp.int32) < glob_rows
    window_index = np.arange(blocks_dev)[:, None] + np.arange(3)[None, :]
    win_blocks = (
        my_index * blocks_dev
        + jnp.arange(blocks_dev, dtype=jnp.int32)[:, None]
        + jnp.arange(-1, 2, dtype=jnp.int32)[None, :]
    )
    win_inside = (win_blocks >= 0) & (win_blocks < blocks_all)
    win_clipped = jnp.clip(win_blocks, 0, blocks_all - 1)
    entry_heads = jnp.arange(entries, dtype=jnp.int32) // R % H
    slot_ids = jnp.arange(capacity, dtype=jnp.int32)
    earlier = jnp.arange(entries)[None, :] < jnp.arange(entries)[:, None]
    seq_ids = jnp.arange(per_micro, dtype=jnp.int32)
    grad_qkv_w = jnp.zeros((features, 3 * features), jnp.float32)
    grad_out_w = jnp.zeros((features, features), jnp.float32)
    grad_up_w = jnp.zeros((features, w_up.shape[1]), jnp.float32)
    grad_down_w = jnp.zeros((w_down.shape[0] * lax.axis_size("dp"), features), jnp.float32)
    gain_acc = jnp.zeros((2, features), jnp.float32)
    shift_acc = jnp.zeros((2, features), jnp.float32)
    output_parts = []
    input_parts = []
    for micro_step in range(MICRO):
        start_seq = micro_step * per_micro
        tokens_in = inputs[start_seq : start_seq + per_micro]
        seg_micro = segments[start_seq : start_seq + per_micro]
        rand_micro = rand_blocks[start_seq : start_seq + per_micro]
        cotangent = out_grad[start_seq : start_seq + per_micro]
        full_qkv, full_out, full_up, full_down = (
            lax.all_gather(w_qkv, "dp", axis=0, tiled=True),
            lax.all_gather(w_out, "dp", axis=0, tiled=True),
            lax.all_gather(w_up, "dp", axis=0, tiled=True),
            lax.all_gather(w_down, "dp", axis=0, tiled=True),
        )
        tokens_flat = tokens_in.reshape(token_rows, features)
        qkv_rows = (
            product(tokens_flat, full_qkv)
            .astype(jnp.bfloat16)
            .reshape(per_micro, tok_dev, 3 * features)
        )
        queries = qkv_rows[..., :features]
        keyvals = qkv_rows[..., features:]
        extended = padded(keyvals, (("seq", 1),), BLOCK)
        global_block = from_root(qkv_rows[:, :glob_rows], "seq", 0)
        requests = rand_micro.reshape(per_micro, devices, entries)
        owners = requests // blocks_dev
        local_block = requests % blocks_dev
        same_owner = owners[:, :, :, None] == owners[:, :, None, :]
        slot_rank = jnp.sum(same_owner & earlier[None, None], axis=3)
        slot_hit = ((owners == my_index)[..., None] & (slot_rank[..., None] == slot_ids)).astype(
            jnp.int32
        )
        slot_live = jnp.sum(slot_hit, axis=2)
        slot_piece = jnp.sum(slot_hit * (local_block * H + entry_heads)[..., None], axis=2)
        piece_index = jnp.transpose(slot_piece, (1, 2, 0))
        live_mask = jnp.transpose(slot_live, (1, 2, 0))
        pieces = (
            keyvals.reshape(per_micro, blocks_dev, BLOCK, 2, H, HEAD)
            .transpose(0, 1, 4, 2, 3, 5)
            .reshape(per_micro, blocks_dev * H, BLOCK, 2 * HEAD)
        )
        outgoing = pieces[seq_ids[None, None, :], piece_index]
        outgoing = jnp.where(live_mask[..., None, None] > 0, outgoing, jnp.zeros((), jnp.bfloat16))
        outgoing = outgoing.reshape(devices * capacity, per_micro, BLOCK, 2 * HEAD)
        incoming = lax.all_to_all(outgoing, "seq", split_axis=0, concat_axis=0, tiled=True)
        my_owner = jnp.take(owners, my_index, axis=1)
        my_rank = jnp.take(slot_rank, my_index, axis=1)
        my_request = jnp.take(requests, my_index, axis=1)
        positions = my_owner * capacity + my_rank
        fetched = incoming[positions, seq_ids[:, None]].reshape(
            per_micro, blocks_dev, H, R, BLOCK, 2, HEAD
        )
        random_keys = fetched[..., 0, :].reshape(per_micro, blocks_dev, H, R * BLOCK, HEAD)
        random_vals = fetched[..., 1, :].reshape(per_micro, blocks_dev, H, R * BLOCK, HEAD)
        seg_blocks = seg_micro.reshape(per_micro, blocks_all, BLOCK)
        query_seg = lax.dynamic_slice_in_dim(seg_micro, my_index * tok_dev, tok_dev, 1).reshape(
            per_micro, blocks_dev, BLOCK
        )
        window_seg = seg_blocks[:, win_clipped].reshape(per_micro, blocks_dev, 3 * BLOCK)
        window_ok = (query_seg[..., :, None] == window_seg[:, :, None, :]) & jnp.repeat(
            win_inside, BLOCK, axis=1
        )[None, :, None, :]
        shared_ok = jnp.concatenate(
            [window_ok, jnp.ones((per_micro, blocks_dev, BLOCK, glob_rows), bool)], axis=3
        )
        random_seg = seg_blocks[seq_ids[:, None], my_request].reshape(
            per_micro, blocks_dev, H, R * BLOCK
        )
        random_ok = query_seg[:, :, None, :, None] == random_seg[:, :, :, None, :]
        ext_blocks = extended.reshape(per_micro, blocks_dev + 2, BLOCK, 2 * features)
        window_kv = ext_blocks[:, window_index].reshape(
            per_micro, blocks_dev, 3 * BLOCK, 2 * features
        )
        glob_kv = jnp.broadcast_to(
            global_block[:, None, :, features:], (per_micro, blocks_dev, glob_rows, 2 * features)
        )
        shared_kv = jnp.concatenate([window_kv, glob_kv], axis=2)
        shared_keys = shared_kv[..., :features].reshape(
            per_micro, blocks_dev, shared_count, H, HEAD
        )
        shared_vals = shared_kv[..., features:].reshape(
            per_micro, blocks_dev, shared_count, H, HEAD
        )
        query_heads = queries.reshape(per_micro, blocks_dev, BLOCK, H, HEAD)
        scores = local_scores(
            query_heads, shared_keys, random_keys, shared_ok, random_ok, scale_factor
        )
        row_max = jnp.max(scores, axis=4, keepdims=True)
        exp_terms = jnp.exp(scores - row_max)
        row_sum = jnp.sum(exp_terms, axis=4, keepdims=True)
        local_probs = exp_terms / row_sum
        log_norm = row_max + jnp.log(row_sum)
        local_weights = local_probs.astype(jnp.bfloat16)
        local_att = jnp.einsum(
            "sbhqk,sbkhd->sbqhd",
            local_weights[..., :shared_count],
            shared_vals,
            preferred_element_type=jnp.float32,
        )
        local_att = local_att + jnp.einsum(
            "sbhqk,sbhkd->sbqhd",
            local_weights[..., shared_count:],
            random_vals,
            preferred_element_type=jnp.float32,
        )
        local_att = local_att.reshape(per_micro, tok_dev, features)
        glob_query = global_block[..., :features].reshape(per_micro, glob_rows, H, HEAD)
        local_keys = keyvals[..., :features].reshape(per_micro, tok_dev, H, HEAD)
        local_vals = keyvals[..., features:].reshape(per_micro, tok_dev, H, HEAD)
        glob_scores = (
            jnp.einsum(
                "sqhd,skhd->shqk", glob_query, local_keys, preferred_element_type=jnp.float32
            )
            * scale_factor
        )
        part_max = jnp.max(glob_scores, axis=3)
        part_sum = jnp.sum(jnp.exp(glob_scores - part_max[..., None]), axis=3)
        glob_max, glob_sum = merged((part_max, part_sum), "seq", merge_stats)
        glob_lse = glob_max + jnp.log(glob_sum)
        glob_probs = jnp.exp(glob_scores - glob_lse[..., None])
        glob_weights = glob_probs.astype(jnp.bfloat16)
        glob_part = jnp.einsum(
            "shqk,skhd->sqhd", glob_weights, local_vals, preferred_element_type=jnp.float32
        ).reshape(per_micro, glob_rows, features)
        glob_out = lax.psum(glob_part, "seq")
        glob_full = jnp.concatenate(
            [glob_out, jnp.zeros((per_micro, tok_dev - glob_rows, features), jnp.float32)], axis=1
        )
        attention = jnp.where(row_global[None, :, None], glob_full, local_att).astype(jnp.bfloat16)
        att_flat = attention.reshape(token_rows, features)
        resid_one = tokens_flat.astype(jnp.float32) + product(att_flat, full_out)
        hidden_one, normed_one, inv_one = norm_forward(resid_one, norm_gain[0], norm_bias[0])
        hidden_low = hidden_one.astype(jnp.bfloat16)
        pre_act = product(hidden_low, full_up)
        activated = gelu_value(pre_act).astype(jnp.bfloat16)
        resid_two = hidden_one + product(activated, full_down)
        result, normed_two, inv_two = norm_forward(resid_two, norm_gain[1], norm_bias[1])
        output_parts.append(result.astype(jnp.bfloat16).reshape(per_micro, tok_dev, features))
        grad_rows = cotangent.reshape(token_rows, features).astype(jnp.float32)
        grad_resid_two, gain_two, shift_two = norm_backward(
            grad_rows, normed_two, inv_two, norm_gain[1]
        )
        grad_branch = grad_resid_two.astype(jnp.bfloat16)
        grad_down_w = grad_down_w + product_tn(activated, grad_branch)
        grad_pre = (product_nt(grad_branch, full_down) * gelu_slope(pre_act)).astype(jnp.bfloat16)
        grad_up_w = grad_up_w + product_tn(hidden_low, grad_pre)
        grad_hidden = grad_resid_two + product_nt(grad_pre, full_up)
        grad_resid_one, gain_one, shift_one = norm_backward(
            grad_hidden, normed_one, inv_one, norm_gain[0]
        )
        grad_mix = grad_resid_one.astype(jnp.bfloat16)
        grad_out_w = grad_out_w + product_tn(att_flat, grad_mix)
        grad_att = (
            product_nt(grad_mix, full_out)
            .astype(jnp.bfloat16)
            .reshape(per_micro, tok_dev, features)
        )
        gain_acc = gain_acc + jnp.stack([gain_one, gain_two])
        shift_acc = shift_acc + jnp.stack([shift_one, shift_two])
        grad_local = jnp.where(
            row_global[None, :, None], jnp.zeros((), jnp.bfloat16), grad_att
        ).reshape(per_micro, blocks_dev, BLOCK, H, HEAD)
        scores = local_scores(
            query_heads, shared_keys, random_keys, shared_ok, random_ok, scale_factor
        )
        local_probs = jnp.exp(scores - log_norm)
        local_weights = local_probs.astype(jnp.bfloat16)
        grad_prob = jnp.concatenate(
            [
                jnp.einsum(
                    "sbqhd,sbkhd->sbhqk",
                    grad_local,
                    shared_vals,
                    preferred_element_type=jnp.float32,
                ),
                jnp.einsum(
                    "sbqhd,sbhkd->sbhqk",
                    grad_local,
                    random_vals,
                    preferred_element_type=jnp.float32,
                ),
            ],
            axis=4,
        )
        row_delta = jnp.sum(local_probs * grad_prob, axis=4, keepdims=True)
        grad_score = (local_probs * (grad_prob - row_delta)).astype(jnp.bfloat16)
        grad_query = jnp.einsum(
            "sbhqk,sbkhd->sbqhd",
            grad_score[..., :shared_count],
            shared_keys,
            preferred_element_type=jnp.float32,
        )
        grad_query = (
            grad_query
            + jnp.einsum(
                "sbhqk,sbhkd->sbqhd",
                grad_score[..., shared_count:],
                random_keys,
                preferred_element_type=jnp.float32,
            )
        ) * scale_factor
        grad_key_shared = (
            jnp.einsum(
                "sbhqk,sbqhd->sbkhd",
                grad_score[..., :shared_count],
                query_heads,
                preferred_element_type=jnp.float32,
            )
            * scale_factor
        )
        grad_val_shared = jnp.einsum(
            "sbhqk,sbqhd->sbkhd",
            local_weights[..., :shared_count],
            grad_local,
            preferred_element_type=jnp.float32,
        )
        grad_key_random = (
            jnp.einsum(
                "sbhqk,sbqhd->sbhkd",
                grad_score[..., shared_count:],
                query_heads,
                preferred_element_type=jnp.float32,
            )
            * scale_factor
        )
        grad_val_random = jnp.einsum(
            "sbhqk,sbqhd->sbhkd",
            local_weights[..., shared_count:],
            grad_local,
            preferred_element_type=jnp.float32,
        )
        grad_shared = jnp.concatenate(
            [
                grad_key_shared.reshape(per_micro, blocks_dev, shared_count, features),
                grad_val_shared.reshape(per_micro, blocks_dev, shared_count, features),
            ],
            axis=3,
        )
        grad_window = grad_shared[:, :, : 3 * BLOCK].reshape(
            per_micro, blocks_dev, 3, BLOCK, 2 * features
        )
        ext_grad = jnp.zeros((per_micro, blocks_dev + 2, BLOCK, 2 * features), jnp.float32)
        for offset in range(3):
            ext_grad = ext_grad.at[:, offset : offset + blocks_dev].add(grad_window[:, :, offset])
        grad_glob_keys = jnp.sum(grad_shared[:, :, 3 * BLOCK :], axis=1)
        grad_random = jnp.stack([grad_key_random, grad_val_random], axis=4).reshape(
            per_micro, entries, BLOCK, 2 * HEAD
        )
        returned = (
            jnp.zeros((devices * capacity, per_micro, BLOCK, 2 * HEAD), jnp.float32)
            .at[positions, seq_ids[:, None]]
            .set(grad_random)
        )
        arrived = lax.all_to_all(
            returned.astype(jnp.bfloat16), "seq", split_axis=0, concat_axis=0, tiled=True
        ).astype(returned.dtype)
        arrived = arrived.reshape(devices, capacity, per_micro, BLOCK, 2 * HEAD) * live_mask[
            ..., None, None
        ].astype(jnp.float32)
        piece_grad = (
            jnp.zeros((per_micro, blocks_dev * H, BLOCK, 2 * HEAD), jnp.float32)
            .at[seq_ids[None, None, :], piece_index]
            .add(arrived)
        )
        piece_grad = (
            piece_grad.reshape(per_micro, blocks_dev, H, BLOCK, 2, HEAD)
            .transpose(0, 1, 3, 4, 2, 5)
            .reshape(per_micro, tok_dev, 2 * features)
        )
        rim_pair = jnp.concatenate([ext_grad[:, 0], ext_grad[:, blocks_dev + 1]], axis=1)
        rim_back = padded(rim_pair.astype(jnp.bfloat16), (("seq", 1),), BLOCK).astype(
            rim_pair.dtype
        )
        grad_kv = (
            ext_grad[:, 1 : blocks_dev + 1].reshape(per_micro, tok_dev, 2 * features) + piece_grad
        )
        grad_kv = grad_kv.at[:, :BLOCK].add(rim_back[:, :BLOCK])
        grad_kv = grad_kv.at[:, tok_dev - BLOCK :].add(rim_back[:, 3 * BLOCK :])
        grad_glob = from_root(grad_att[:, :glob_rows], "seq", 0)
        grad_glob_heads = grad_glob.reshape(per_micro, glob_rows, H, HEAD)
        glob_scores = (
            jnp.einsum(
                "sqhd,skhd->shqk", glob_query, local_keys, preferred_element_type=jnp.float32
            )
            * scale_factor
        )
        glob_probs = jnp.exp(glob_scores - glob_lse[..., None])
        glob_weights = glob_probs.astype(jnp.bfloat16)
        glob_grad_prob = jnp.einsum(
            "sqhd,skhd->shqk", grad_glob_heads, local_vals, preferred_element_type=jnp.float32
        )
        glob_delta = lax.psum(jnp.sum(glob_probs * glob_grad_prob, axis=3), "seq")
        glob_grad_score = (glob_probs * (glob_grad_prob - glob_delta[..., None])).astype(
            jnp.bfloat16
        )
        glob_grad_query = (
            jnp.einsum(
                "shqk,skhd->sqhd", glob_grad_score, local_keys, preferred_element_type=jnp.float32
            )
            * scale_factor
        )
        glob_grad_key = (
            jnp.einsum(
                "shqk,sqhd->skhd", glob_grad_score, glob_query, preferred_element_type=jnp.float32
            )
            * scale_factor
        )
        glob_grad_val = jnp.einsum(
            "shqk,sqhd->skhd", glob_weights, grad_glob_heads, preferred_element_type=jnp.float32
        )
        grad_kv = grad_kv + jnp.concatenate(
            [
                glob_grad_key.reshape(per_micro, tok_dev, features),
                glob_grad_val.reshape(per_micro, tok_dev, features),
            ],
            axis=2,
        )
        summed_query, summed_keys = lax.psum(
            (glob_grad_query.reshape(per_micro, glob_rows, features), grad_glob_keys), "seq"
        )
        grad_kv = grad_kv.at[:, :glob_rows].add(owner_flag * summed_keys)
        grad_queries = (
            grad_query.reshape(per_micro, tok_dev, features)
            .at[:, :glob_rows]
            .add(owner_flag * summed_query)
        )
        grad_qkv_rows = (
            jnp.concatenate([grad_queries, grad_kv], axis=2)
            .astype(jnp.bfloat16)
            .reshape(token_rows, 3 * features)
        )
        grad_qkv_w = grad_qkv_w + product_tn(tokens_flat, grad_qkv_rows)
        input_rows = grad_resid_one + product_nt(grad_qkv_rows, full_qkv)
        input_parts.append(input_rows.reshape(per_micro, tok_dev, features))
    summed = (
        lax.psum_scatter(grad_qkv_w, ("dp", "seq"), scatter_dimension=0, tiled=True),
        lax.psum_scatter(grad_out_w, ("dp", "seq"), scatter_dimension=0, tiled=True),
        lax.psum_scatter(grad_up_w, ("dp", "seq"), scatter_dimension=0, tiled=True),
        lax.psum_scatter(grad_down_w, ("dp", "seq"), scatter_dimension=0, tiled=True),
        lax.psum_scatter(gain_acc, ("dp", "seq"), scatter_dimension=1, tiled=True),
        lax.psum_scatter(shift_acc, ("dp", "seq"), scatter_dimension=1, tiled=True),
    )
    return (
        jnp.concatenate(output_parts, axis=0),
        jnp.concatenate(input_parts, axis=0),
        summed[0],
        summed[1],
        summed[2],
        summed[3],
        summed[4],
        summed[5],
    )


TILE = 128
NH = 3
CH = 256
LOG2E = 1.4426950408889634
SCALE2 = HEAD ** (-0.5) * LOG2E
NEG = -1e30
F32 = jnp.float32
BF16 = jnp.bfloat16


def nt(a, b):
    return lax.dot_general(a, b, (((1,), (1,)), ((), ())), preferred_element_type=F32)


def nn(a, b):
    return jnp.dot(a, b, preferred_element_type=F32)


def biased(s, mask, b1_ref, b0_ref, tile, first_block):
    rows = []
    for j in range(s.shape[0] // BLOCK):
        kb = first_block + j
        m3 = jnp.concatenate([mask[BLOCK * j : BLOCK * (j + 1)]] * NH, axis=1)
        on = b1_ref[tile, kb : kb + 1, :]
        off = jnp.concatenate([b0_ref[tile, kb : kb + 1, :]] * NH, axis=1)
        rows.append(s[BLOCK * j : BLOCK * (j + 1)] * SCALE2 + jnp.where(m3, on, off))
    return jnp.concatenate(rows, axis=0)


def forward_kernel(
    xs, wg, b1, b0, segk, segq, att, otile, lse, qn, kn, vn, qt, kt, vt, q3, tbuf
):
    step = pl.program_id(0)
    length = xs.shape[0]
    chunks = length // CH

    @pl.when(step == 0)
    def _():
        q3[...] = jnp.zeros_like(q3)
        for j in range(chunks):
            rows = slice(CH * j, CH * (j + 1))
            both = nn(xs[rows, :], wg[...])
            qf, kf, vf = both[:, :256], both[:, 256:512], both[:, 512:]
            qn[rows, :] = qf.astype(BF16)
            kn[rows, :] = kf.astype(BF16)
            vn[rows, :] = vf.astype(BF16)
            qt[:, rows] = qf.T.astype(BF16)
            kt[:, rows] = kf.T.astype(BF16)
            vt[:, rows] = vf.T.astype(BF16)

    cols = pl.ds(pl.multiple_of(step * TILE, TILE), TILE)
    for h in range(NH):
        q3[HEAD * h : HEAD * (h + 1), TILE * h : TILE * (h + 1)] = qt[
            HEAD * h : HEAD * (h + 1), cols
        ]
    top = jnp.full((8, NH * TILE), NEG, F32)
    for j in range(chunks):
        rows = slice(CH * j, CH * (j + 1))
        s = nn(kn[rows, :], q3[...])
        t = biased(s, segk[rows, :] == segq[0], b1, b0, 0, CH // BLOCK * j)
        tbuf[rows, :] = t
        top = jnp.maximum(top, jnp.max(t.reshape(CH // 8, 8, NH * TILE), axis=0))
    peak = jnp.max(top, axis=0, keepdims=True)
    total = jnp.zeros((8, NH * TILE), F32)
    out = jnp.zeros((256, NH * TILE), F32)
    for j in range(chunks):
        rows = slice(CH * j, CH * (j + 1))
        p = jnp.exp2(tbuf[rows, :] - peak)
        total = total + jnp.sum(p.reshape(CH // 8, 8, NH * TILE), axis=0)
        out = out + nn(vt[:, rows], p.astype(BF16))
    weight = jnp.sum(total, axis=0, keepdims=True)
    lse[0] = peak + jnp.log2(weight)
    inv = 1.0 / weight
    heads = [
        out[HEAD * h : HEAD * (h + 1), TILE * h : TILE * (h + 1)] * inv[:, TILE * h : TILE * (h + 1)]
        for h in range(NH)
    ]
    merged = jnp.concatenate(heads, axis=0)
    otile[0] = merged
    att[...] = merged.T.astype(BF16)


def attend_forward(xs, wg, b1, b0, segk, segq):
    length = xs.shape[0]
    steps = length // TILE
    blocks = length // BLOCK
    whole = lambda *shape: pl.BlockSpec(shape, lambda i: (0,) * len(shape))
    per = lambda *shape: pl.BlockSpec((1,) + shape, lambda i: (i,) + (0,) * len(shape))
    nat = jax.ShapeDtypeStruct((length, 256), BF16)
    tra = jax.ShapeDtypeStruct((256, length), BF16)
    return pl.pallas_call(
        forward_kernel,
        grid=(steps,),
        in_specs=[
            whole(*xs.shape), whole(*wg.shape), per(blocks, NH * TILE), per(blocks, TILE),
            whole(*segk.shape), per(1, TILE),
        ],
        out_specs=[
            pl.BlockSpec((TILE, NH * HEAD), lambda i: (i, 0)), per(NH * HEAD, TILE), per(1, NH * TILE),
            whole(length, 256), whole(length, 256), whole(length, 256),
            whole(256, length), whole(256, length),
        ],
        out_shape=[
            jax.ShapeDtypeStruct((length, NH * HEAD), BF16),
            jax.ShapeDtypeStruct((steps, NH * HEAD, TILE), F32),
            jax.ShapeDtypeStruct((steps, 1, NH * TILE), F32),
            nat, nat, nat, tra, tra,
        ],
        scratch_shapes=[
            pltpu.VMEM((256, length), BF16),
            pltpu.VMEM((256, NH * TILE), BF16),
            pltpu.VMEM((length, NH * TILE), F32),
        ],
        name="attend_forward",
    )(xs, wg, b1, b0, segk, segq)


def tables(rand, seg):
    blocks = rand.shape[0]
    qb = jnp.arange(blocks, dtype=jnp.int32)
    near = (jnp.abs(qb[:, None] - qb[None, :]) <= 1).astype(jnp.int32)
    hits = jnp.sum((rand[:, None, :, :] == qb[None, :, None, None]).astype(jnp.int32), axis=3)
    local = (qb >= 2).astype(jnp.int32)
    listed = (near[:, :, None] + hits) * local[:, None, None]
    fixed = ((qb[:, None] < 2) | (qb[None, :] < 2)).astype(jnp.int32)
    log_of = lambda n: jnp.where(n > 0, jnp.log2(jnp.maximum(n, 1).astype(F32)), NEG)
    b1 = log_of(listed + fixed[:, :, None])
    b0 = log_of(fixed)
    steps = blocks // 2
    b1 = b1.reshape(steps, 2, blocks, NH).transpose(0, 2, 3, 1)
    b1 = jnp.broadcast_to(b1[..., None], (steps, blocks, NH, 2, BLOCK)).reshape(steps, blocks, NH * TILE)
    b0 = b0.reshape(steps, 2, blocks).transpose(0, 2, 1)
    b0 = jnp.broadcast_to(b0[..., None], (steps, blocks, 2, BLOCK)).reshape(steps, blocks, TILE)
    segk = jnp.broadcast_to(seg[:, None], (seg.shape[0], TILE))
    segq = seg.reshape(steps, 1, TILE)
    return b1, b0, segk, segq


MESH = pl.DeviceIdType.MESH
ANYSPACE = pl.BlockSpec(memory_space=pl.ANY)
VMEMSPACE = pl.BlockSpec(memory_space=pltpu.VMEM)


class Copies:
    def __init__(self, send, recv):
        self.send = send
        self.recv = recv
        self.used = 0

    def to(self, src, dst, device):
        index = self.used
        self.used += 1
        return pltpu.make_async_remote_copy(
            src_ref=src, dst_ref=dst, send_sem=self.send.at[index], recv_sem=self.recv.at[index],
            device_id=device, device_id_type=MESH,
        )


class Place:
    def __init__(self):
        self.d = lax.axis_index("dp")
        self.t = lax.axis_index("seq")
        self.x = lax.rem(self.d, 2)
        self.y = self.d // 2
        self.c = lax.rem(self.t, 2)
        self.z = self.t // 2
        self.half = self.z // 2
        self.xn = self.d + 1 - 2 * self.x
        self.yn = self.d + 2 - 4 * self.y
        self.diag = 3 - self.d
        self.pair_z = self.z + 1 - 2 * lax.rem(self.z, 2)
        self.across_x = (self.xn, self.t)
        self.across_y = (self.yn, self.t)
        self.partner = (self.d, self.t + 1 - 2 * self.c)

    def at_z(self, z):
        return (self.d, 2 * z + self.c)


def meet(devices):
    barrier = pltpu.get_barrier_semaphore()
    for device in devices:
        pl.semaphore_signal(barrier, inc=1, device_id=device, device_id_type=MESH)
    pl.semaphore_wait(barrier, len(devices))


def gather_kernel(x, wg, wo, wu, wd, xs, wgf, wof, wuf, wdf, send, recv, xsend, xrecv, local):
    me = Place()
    d, t, c, z = me.d, me.t, me.c, me.z
    mine, other = me.half, 1 - me.half
    middle = 1 + me.half
    is_middle = z == middle
    z_step = [me.at_z(lax.rem(z + k, 4)) for k in (1, 2, 3)]
    meet([me.across_x, me.across_y, me.partner] + z_step)
    cps = Copies(send, recv)

    wg_x = cps.to(wg, wgf.at[d], me.across_x)
    wg_y = cps.to(wg, wgf.at[d], me.across_y)
    wg_x.start()
    wg_y.start()
    near = cps.to(x.at[mine], xs.at[t], me.at_z(me.pair_z))
    near.start()
    row = lax.rem(z, 2)
    far = pltpu.make_async_remote_copy(
        src_ref=x.at[other], dst_ref=xs.at[t], send_sem=xsend.at[0], recv_sem=xrecv.at[row],
        device_id=me.at_z(2 - me.half), device_id_type=MESH,
    )
    far.start()
    give = cps.to(x.at[mine], xs.at[t], me.partner)
    give.start()
    keeps = [
        pltpu.make_async_copy(x.at[mine], xs.at[t], local.at[0]),
        pltpu.make_async_copy(wg, wgf.at[d], local.at[1]),
        pltpu.make_async_copy(wo, wof.at[d], local.at[2]),
        pltpu.make_async_copy(wu, wuf.at[d], local.at[3]),
        pltpu.make_async_copy(wd, wdf.at[d], local.at[4]),
    ]
    for keep in keeps:
        keep.start()
    heavy = []
    for w, full in ((wo, wof), (wu, wuf), (wd, wdf)):
        rows = w.shape[0] // 2
        part = pl.ds(pl.multiple_of(c * rows, rows), rows)
        to_x = cps.to(w.at[part], full.at[d, part], me.across_x)
        to_y = cps.to(w.at[part], full.at[d, part], me.across_y)
        to_x.start()
        to_y.start()
        heavy.append((full, rows, to_x, to_y))

    half = wg.shape[0] // 2
    lo, hi = pl.ds(0, half), pl.ds(half, half)
    wg_x.wait_recv()
    wg_dy = cps.to(wgf.at[me.xn, lo], wgf.at[me.xn, lo], me.across_y)
    wg_dy.start()
    wg_y.wait_recv()
    wg_dx = cps.to(wgf.at[me.yn, hi], wgf.at[me.yn, hi], me.across_x)
    wg_dx.start()

    near.wait_recv()
    near_t = 2 * me.pair_z + c
    pass_near = cps.to(xs.at[near_t], xs.at[near_t], me.partner)
    pass_near.start()
    passes = []
    for j in range(2):
        src_t = 2 * (2 * other + j) + c
        relay = pltpu.make_async_remote_copy(
            src_ref=xs.at[src_t], dst_ref=xs.at[src_t], send_sem=xsend.at[1 + j],
            recv_sem=xrecv.at[j], device_id=me.at_z(me.pair_z), device_id_type=MESH,
        )
        relay.wait_recv()

        @pl.when(is_middle)
        def _():
            relay.start()

        onward = cps.to(xs.at[src_t], xs.at[src_t], me.partner)
        onward.start()
        passes.append((relay, onward))

    tail = []
    for full, rows, to_x, to_y in heavy:
        part = pl.ds(pl.multiple_of(c * rows, rows), rows)
        quarter = rows // 2
        lo = pl.ds(pl.multiple_of(c * rows, quarter), quarter)
        hi = pl.ds(pl.multiple_of(c * rows + quarter, quarter), quarter)
        to_x.wait_recv()
        dy = cps.to(full.at[me.xn, lo], full.at[me.xn, lo], me.across_y)
        px = cps.to(full.at[me.xn, part], full.at[me.xn, part], me.partner)
        dy.start()
        px.start()
        to_y.wait_recv()
        dx = cps.to(full.at[me.yn, hi], full.at[me.yn, hi], me.across_x)
        py = cps.to(full.at[me.yn, part], full.at[me.yn, part], me.partner)
        dx.start()
        py.start()
        tail.append((full, part, lo, hi, dy, dx, px, py, to_x, to_y))
    ends = []
    for full, part, lo, hi, dy, dx, px, py, to_x, to_y in tail:
        dy.wait_recv()
        dx.wait_recv()
        pd = cps.to(full.at[me.diag, part], full.at[me.diag, part], me.partner)
        pd.start()
        ends.append(pd)

    wg_dy.wait_recv()
    wg_dx.wait_recv()
    give.wait_recv()
    pass_near.wait_recv()
    for relay, onward in passes:
        onward.wait()

        @pl.when(is_middle)
        def _():
            relay.wait_send()

    for pd in ends:
        pd.wait()
    for full, part, lo, hi, dy, dx, px, py, to_x, to_y in tail:
        px.wait()
        py.wait()
        for cp in (dy, dx, to_x, to_y):
            cp.wait_send()
    for cp in (wg_x, wg_y, wg_dx, wg_dy, near, far, give, pass_near):
        cp.wait_send()
    for keep in keeps:
        keep.wait()


def gather(x, wg, wo, wu, wd):
    dp = lax.axis_size("dp")
    seq = lax.axis_size("seq")
    shapes = [(seq,) + x.shape[1:]] + [(dp,) + w.shape for w in (wg, wo, wu, wd)]
    return pl.pallas_call(
        gather_kernel,
        in_specs=[VMEMSPACE] * 5,
        out_specs=[ANYSPACE] * 5,
        out_shape=[jax.ShapeDtypeStruct(shape, BF16) for shape in shapes],
        scratch_shapes=[
            pltpu.SemaphoreType.DMA((40,)),
            pltpu.SemaphoreType.DMA((40,)),
            pltpu.SemaphoreType.DMA((3,)),
            pltpu.SemaphoreType.DMA((2,)),
            pltpu.SemaphoreType.DMA((5,)),
        ],
        compiler_params=pltpu.CompilerParams(collective_id=0, has_side_effects=True),
        name="gather",
    )(x, wg, wo, wu, wd)


def swap_kernel(src, dst, send, recv, local):
    d = lax.axis_index("dp")
    t = lax.axis_index("seq")
    count = src.shape[0]
    peers = [lax.rem(t + k, count) for k in range(1, count)]
    meet([(d, peer) for peer in peers])
    cps = Copies(send, recv)
    moves = [cps.to(src.at[peer], dst.at[t], (d, peer)) for peer in peers]
    for move in moves:
        move.start()
    keep = pltpu.make_async_copy(src.at[t], dst.at[t], local.at[0])
    keep.start()
    for move in moves:
        move.wait()
    keep.wait()


def swap(src, number):
    count = src.shape[0]
    return pl.pallas_call(
        swap_kernel,
        in_specs=[VMEMSPACE],
        out_specs=ANYSPACE,
        out_shape=jax.ShapeDtypeStruct(src.shape, src.dtype),
        scratch_shapes=[
            pltpu.SemaphoreType.DMA((count,)),
            pltpu.SemaphoreType.DMA((count,)),
            pltpu.SemaphoreType.DMA((1,)),
        ],
        compiler_params=pltpu.CompilerParams(collective_id=number, has_side_effects=True),
        name="swap",
    )(src)


def each(count, body):
    def run(i, carry):
        body(i)
        return carry

    lax.fori_loop(0, count, run, 0)


def plus(a, b):
    return a.astype(F32) + b.astype(F32)


def backward_tile(
    tile, dat, qn, qt, otile, lse, b1, b0, segk, segq, kn, vn, kt, dqkv, q3t, d3t, q3, d3, dk, dv
):
    chunks = kn.shape[0] // CH
    here = pl.ds(pl.multiple_of(tile * TILE, TILE), TILE)
    dat_f = dat[here, :].astype(F32)
    dat_t = dat_f.T
    lane = lax.broadcasted_iota(jnp.int32, (TILE, NH * HEAD), 1) // HEAD
    qblk = qn[here, : NH * HEAD].astype(F32)
    delta = []
    for h in range(NH):
        hr = slice(HEAD * h, HEAD * (h + 1))
        hc = slice(TILE * h, TILE * (h + 1))
        q3t[hr, hc] = qt[hr, here]
        d3t[hr, hc] = dat_t[hr].astype(BF16)
        q3[hc, :] = jnp.where(lane == h, qblk, 0.0).astype(BF16)
        d3[hc, :] = jnp.where(lane == h, dat_f, 0.0).astype(BF16)
        delta.append(jnp.sum(dat_t[hr] * otile[tile, hr, :], axis=0, keepdims=True))
    delta = jnp.concatenate(delta, axis=1)
    norm = lse[tile]
    dq = jnp.zeros((256, NH * TILE), F32)
    for j in range(chunks):
        rows = slice(CH * j, CH * (j + 1))
        s = nn(kn[rows, :], q3t[...])
        dp = nn(vn[rows, :], d3t[...])
        t = biased(s, segk[rows, :] == segq[tile], b1, b0, tile, CH // BLOCK * j)
        p = jnp.exp2(t - norm)
        ds = (p * (dp - delta)).astype(BF16)
        dv[rows, :] += nn(p.astype(BF16), d3[...])
        dk[rows, :] += nn(ds, q3[...])
        dq = dq + nn(kt[:, rows], ds)
    heads = [dq[HEAD * h : HEAD * (h + 1), TILE * h : TILE * (h + 1)] for h in range(NH)]
    merged = jnp.concatenate(heads, axis=0).T * HEAD ** (-0.5)
    dqkv[here, : NH * HEAD] = merged.astype(BF16)


def backward_kernel(*refs):
    (src, stats, g0, g1, g2), refs = refs[:5], refs[5:]
    (qn, qt, otile, lse, b1, b0, segk, segq, kn, vn, kt, xs, wg), refs = refs[:13], refs[13:]
    (o0, o1, o2, stats_out, ig, wq), refs = refs[:6], refs[6:]
    bufs, refs = refs[:18], refs[18:]
    (dat, dqkv, q3t, d3t, q3, d3, dk, dv), refs = refs[:8], refs[8:]
    (part, own_p, rp, ra_p, rb_p, ro, dwg, wb1, wb2, wc, wr), refs = refs[:11], refs[11:]
    nsend, nrecv, send, recv, local = refs
    me = Place()
    c, z, x, y, t = me.c, me.z, me.x, me.y, me.t
    mine, other = me.half, 1 - me.half
    is_middle = z == 1 + me.half
    is_outer = z != 1 + me.half
    z_step = [lax.rem(z + k, 4) for k in (1, 2, 3)]
    tok = src.shape[1]
    units = [z, me.pair_z, 2 * other, 2 * other + 1]
    meet([me.across_x, me.across_y] + [(me.d, lax.rem(t + k, 8)) for k in range(1, 8)])
    cps = Copies(send, recv)

    def rows_of(index):
        return pl.ds(pl.multiple_of(index * tok, tok), tok)

    far_base = 80
    def dat_copy(to, send_slot, recv_slot):
        return pltpu.make_async_remote_copy(
            src_ref=src.at[to], dst_ref=dat.at[rows_of(t)], send_sem=send.at[send_slot],
            recv_sem=recv.at[recv_slot], device_id=(me.d, to), device_id_type=MESH,
        )

    core_of = [c, 1 - c]
    dat_send = []
    dat_wait = [[], [], [], []]
    for u, o in [(0, 1), (1, 0), (1, 1), (2, 0), (2, 1), (3, 0), (3, 1)]:
        to = 2 * units[u] + core_of[o]
        slot = far_base + 2 * u + o
        if u < 2:
            move = dat_copy(to, slot, slot)
            arrival = move
        else:
            move = dat_copy(to, slot, far_base + 4 + 2 * lax.rem(z, 2) + o)
            arrival = dat_copy(to, slot, slot)
        move.start()
        dat_send.append(move)
        dat_wait[u].append(arrival)
    keep = pltpu.make_async_copy(src.at[t], dat.at[rows_of(t)], local.at[3])
    keep.start()

    works = []
    for i, (g, o) in enumerate(((g2, o2), (g1, o1), (g0, o0))):
        own, ra, rb1, rb2, rc, rd = bufs[6 * i : 6 * i + 6]
        swap_core = cps.to(g.at[:, :, :, 1 - c], ra, me.partner)
        swap_core.start()
        load = pltpu.make_async_copy(g.at[:, :, :, c], own, local.at[i])
        load.start()
        works.append((o, own, ra, rb1, rb2, rc, rd, swap_core, load))
    stat_to = [me.partner, me.across_x, me.across_y, me.at_z(me.pair_z), me.at_z(lax.rem(z + 2, 4))]
    stat_all = []

    def stat_step():
        k = len(stat_all)
        if k == 0:
            nsend[0] = stats[...]
        else:
            stat_all[-1].wait_recv()
            nsend[k] = nsend[k - 1] + nrecv[k - 1]
        stat = cps.to(nsend.at[k], nrecv.at[k], stat_to[k])
        stat.start()
        stat_all.append(stat)

    sent = []

    def begin(*copies):
        for cp in copies:
            cp.start()
            sent.append(cp)

    def stage_a(work):
        o, own, ra, rb1, rb2, rc, rd, swap_core, load = work
        load.wait()
        swap_core.wait_recv()

        def fold(i):
            yy, xx, zz = i // 8, lax.rem(i // 4, 2), lax.rem(i, 4)
            own[yy, xx, zz] = plus(own[yy, xx, zz], ra[yy, xx, zz]).astype(BF16)

        each(16, fold)
        bx = cps.to(own.at[:, 1 - x, 0:2], rb1, me.across_x)
        by = cps.to(own.at[1 - y, :, 2:4], rb2, me.across_y)
        begin(bx, by)
        return bx, by

    def stage_b(work, bs):
        o, own, ra, rb1, rb2, rc, rd, swap_core, load = work
        bs[0].wait_recv()

        def fold_x(i):
            yy, zz = i // 2, lax.rem(i, 2)
            rb1[yy, zz] = plus(own[yy, x, zz], rb1[yy, zz]).astype(BF16)

        each(4, fold_x)
        cy = cps.to(rb1.at[1 - y], rc.at[0:2], me.across_y)
        begin(cy)
        bs[1].wait_recv()

        def fold_y(i):
            xx, zz = i // 2, lax.rem(i, 2)
            rb2[xx, zz] = plus(own[y, xx, 2 + zz], rb2[xx, zz]).astype(BF16)

        each(4, fold_y)
        cx = cps.to(rb2.at[1 - x], rc.at[2:4], me.across_x)
        begin(cx)
        return cy, cx

    def stage_c(work, cs):
        o, own, ra, rb1, rb2, rc, rd, swap_core, load = work
        for cp in cs:
            cp.wait_recv()
        for zz in range(2):
            rc[zz] = plus(rb1[y, zz], rc[zz]).astype(BF16)
            rc[2 + zz] = plus(rb2[x, zz], rc[2 + zz]).astype(BF16)
        ds = [cps.to(rc.at[k], rd.at[j], me.at_z(k)) for j, k in enumerate(z_step)]
        begin(*ds)
        return ds

    def stage_d(work, ds):
        o, own, ra, rb1, rb2, rc, rd, swap_core, load = work
        for cp in ds:
            cp.wait_recv()
        o[...] = plus(rc[z], rd[0]) + plus(rd[1], rd[2])

    q3t[...] = jnp.zeros_like(q3t)
    d3t[...] = jnp.zeros_like(d3t)
    dk[...] = jnp.zeros_like(dk)
    dv[...] = jnp.zeros_like(dv)
    gap = jnp.zeros((dqkv.shape[0], 256 - NH * HEAD), BF16)
    for g in range(3):
        dqkv[:, 256 * g + NH * HEAD : 256 * (g + 1)] = gap
    stat_step()
    keep.wait()

    def unit(u):
        for arrival in dat_wait[u]:
            arrival.wait_recv()
        first = units[u] * (2 * tok // TILE)
        each(
            2 * tok // TILE,
            lambda i: backward_tile(
                first + i, dat, qn, qt, otile, lse, b1, b0, segk, segq, kn, vn, kt, dqkv,
                q3t, d3t, q3, d3, dk, dv,
            ),
        )

    unit(0)
    b_of = [stage_a(work) for work in works]
    stat_step()
    unit(1)
    stat_step()
    unit(2)
    c_of = [stage_b(works[0], b_of[0])]
    stat_step()
    unit(3)
    c_of += [stage_b(works[1], b_of[1]), stage_b(works[2], b_of[2])]
    stat_step()

    dqkv[:, 256 : 256 + NH * HEAD] = (dk[...] * HEAD ** (-0.5)).astype(BF16)
    dqkv[:, 512 : 512 + NH * HEAD] = dv[...].astype(BF16)
    order = [units[2], units[3], units[1], units[0]]
    cores = []
    for zz in order:
        rows = pl.ds(pl.multiple_of(zz * 2 * tok, 2 * tok), 2 * tok)
        grad = nt(dqkv[rows, :], wg[...]).astype(BF16)
        part[zz, 0] = grad[:tok]
        part[zz, 1] = grad[tok:]
        core = cps.to(part.at[zz, 1 - c], rp.at[zz], me.partner)
        begin(core)
        cores.append(core)
    d_of = [stage_c(works[0], c_of[0])]

    up = [cps.to(own_p.at[2 * other + j], rb_p.at[j], me.at_z(me.pair_z)) for j in range(2)]
    near = cps.to(own_p.at[me.pair_z], ra_p, me.at_z(me.pair_z))
    for k, zz in enumerate(order):
        cores[k].wait_recv()
        own_p[zz] = plus(part[zz, c], rp[zz]).astype(BF16)
        if k < 2:
            pl.when(is_outer)(up[k].start)
        if k == 2:
            begin(near)
    half_rows = xs.shape[1] // 2
    for yy in range(2):
        grad = lax.dot_general(
            xs[:, half_rows * yy : half_rows * (yy + 1)], dqkv[...], (((0,), (0,)), ((), ())),
            preferred_element_type=F32,
        ).astype(BF16)
        dwg[yy] = grad.reshape(dwg.shape[1:])
    bx = cps.to(dwg.at[:, 1 - x, 0:4], wb1, me.across_x)
    by = cps.to(dwg.at[1 - y, :, 4:8], wb2, me.across_y)
    begin(bx, by)
    down_send, down_recv = cps.used, cps.used
    cps.used += 2
    down = [
        pltpu.make_async_remote_copy(
            src_ref=own_p.at[2 * other + j], dst_ref=ro, send_sem=send.at[down_send + j],
            recv_sem=recv.at[down_recv], device_id=me.at_z(2 * other + j), device_id_type=MESH,
        )
        for j in range(2)
    ]

    @pl.when(is_middle)
    def _():
        for j in range(2):
            up[j].wait_recv()
            own_p[2 * other + j] = plus(own_p[2 * other + j], rb_p[j]).astype(BF16)
            down[j].start()

    d_of += [stage_c(works[1], c_of[1]), stage_c(works[2], c_of[2])]
    bx.wait_recv()

    def fold_x(i):
        yy, tt = i // 4, lax.rem(i, 4)
        wb1[yy, tt] = plus(dwg[yy, x, tt], wb1[yy, tt]).astype(BF16)

    each(8, fold_x)
    cy = cps.to(wb1.at[1 - y], wc.at[0:4], me.across_y)
    begin(cy)
    by.wait_recv()

    def fold_y(i):
        xx, tt = i // 4, lax.rem(i, 4)
        wb2[xx, tt] = plus(dwg[y, xx, 4 + tt], wb2[xx, tt]).astype(BF16)

    each(8, fold_y)
    cx = cps.to(wb2.at[1 - x], wc.at[4:8], me.across_x)
    begin(cx)
    stat_all[-1].wait_recv()
    stats_out[...] = nsend[4] + nrecv[4]
    cy.wait_recv()
    cx.wait_recv()

    def fold_c(i):
        wc[i] = plus(wb1[y, i], wc[i]).astype(BF16)
        wc[4 + i] = plus(wb2[x, i], wc[4 + i]).astype(BF16)

    each(4, fold_c)
    moves = []
    for k in range(1, 8):
        peer = lax.rem(t + k, 8)
        moves.append(cps.to(wc.at[peer], wr.at[t], (me.d, peer)))
    begin(*moves)
    near.wait_recv()
    ig[mine] = plus(own_p[z], ra_p[...])
    down[0].wait_recv()
    ig[other] = ro[...].astype(F32)
    for work, ds in zip(works, d_of):
        stage_d(work, ds)
    wr[t] = wc[t]
    for move in moves:
        move.wait_recv()
    for g in range(4):
        wq[g] = plus(wr[g], wr[4 + g])
    for cp in sent + stat_all + dat_send + [work[7] for work in works]:
        cp.wait_send()

    @pl.when(is_outer)
    def _():
        for cp in up:
            cp.wait_send()

    @pl.when(is_middle)
    def _():
        for cp in down:
            cp.wait_send()


def backward_half(src, stats, grads, saved, tabs, xs, wg):
    dims = [g.shape[-2:] for g in grads]
    qn, qt, otile, lse, kn, vn, kt = saved
    b1, b0, segk, segq = tabs
    tok = src.shape[1]
    length, features = xs.shape
    bufs = []
    for rows, cols in dims[::-1]:
        bufs += [
            pltpu.VMEM((2, 2, 4, rows, cols), BF16),
            pltpu.VMEM((2, 2, 4, rows, cols), BF16),
            pltpu.VMEM((2, 2, rows, cols), BF16),
            pltpu.VMEM((2, 2, rows, cols), BF16),
            pltpu.VMEM((4, rows, cols), BF16),
            pltpu.VMEM((3, rows, cols), BF16),
        ]
    wrows = features // 32
    return pl.pallas_call(
        backward_kernel,
        in_specs=[VMEMSPACE] * 2 + [ANYSPACE] * 3 + [VMEMSPACE] * 13,
        out_specs=[VMEMSPACE] * 6,
        out_shape=[jax.ShapeDtypeStruct(dim, F32) for dim in dims]
        + [
            jax.ShapeDtypeStruct(stats.shape, F32),
            jax.ShapeDtypeStruct((2, tok, features), F32),
            jax.ShapeDtypeStruct((4, wrows, wg.shape[1]), F32),
        ],
        scratch_shapes=bufs
        + [
            pltpu.VMEM((length, NH * HEAD), BF16),
            pltpu.VMEM((length, 768), BF16),
            pltpu.VMEM((256, NH * TILE), BF16),
            pltpu.VMEM((256, NH * TILE), BF16),
            pltpu.VMEM((NH * TILE, NH * HEAD), BF16),
            pltpu.VMEM((NH * TILE, NH * HEAD), BF16),
            pltpu.VMEM((length, NH * HEAD), F32),
            pltpu.VMEM((length, NH * HEAD), F32),
            pltpu.VMEM((4, 2, tok, features), BF16),
            pltpu.VMEM((4, tok, features), BF16),
            pltpu.VMEM((4, tok, features), BF16),
            pltpu.VMEM((tok, features), BF16),
            pltpu.VMEM((2, tok, features), BF16),
            pltpu.VMEM((tok, features), BF16),
            pltpu.VMEM((2, 2, 8, wrows, 768), BF16),
            pltpu.VMEM((2, 4, wrows, 768), BF16),
            pltpu.VMEM((2, 4, wrows, 768), BF16),
            pltpu.VMEM((8, wrows, 768), BF16),
            pltpu.VMEM((8, wrows, 768), BF16),
            pltpu.VMEM((5,) + stats.shape, F32),
            pltpu.VMEM((5,) + stats.shape, F32),
            pltpu.SemaphoreType.DMA((90,)),
            pltpu.SemaphoreType.DMA((90,)),
            pltpu.SemaphoreType.DMA((4,)),
        ],
        compiler_params=pltpu.CompilerParams(
            collective_id=3, has_side_effects=True, vmem_limit_bytes=62 * 1024 * 1024
        ),
        name="backward_half",
    )(src, stats, *grads, qn, qt, otile, lse, b1, b0, segk, segq, kn, vn, kt, xs, wg)


def head_layout(
    inputs, segments, rand_blocks, w_qkv, w_out, w_up, w_down, norm_gain, norm_bias, out_grad
):
    seqs, tok, features = inputs.shape
    seq = lax.axis_size("seq")
    t = lax.axis_index("seq")
    groups = seq // seqs
    my_seq, my_group = t // groups, lax.rem(t, groups)
    width = features // groups
    shard = w_qkv.reshape(w_qkv.shape[0], 3, groups, width)
    shard = lax.dynamic_index_in_dim(shard, my_group, 2, keepdims=False)
    shard = jnp.pad(shard, ((0, 0), (0, 0), (0, 256 - width))).reshape(w_qkv.shape[0], 768)
    rand = lax.dynamic_slice_in_dim(
        lax.dynamic_index_in_dim(rand_blocks, my_seq, 0, keepdims=False), my_group * NH, NH, 1
    )
    seg = lax.dynamic_index_in_dim(segments, my_seq, 0, keepdims=False)
    b1, b0, segk, segq = tables(rand, seg)
    xs, wgf, wof, wuf, wdf = gather(inputs, shard, w_out, w_up, w_down)
    xs = xs.reshape(seq * tok, features)
    wgf = wgf.reshape(features, 768)
    full_out = wof.reshape(features, features)
    full_up = wuf.reshape(features, -1)
    full_down = wdf.reshape(-1, features)
    att, otile, lse, qn, kn, vn, qt, kt = attend_forward(xs, wgf, b1, b0, segk, segq)
    att_home = swap(att.reshape(seq, tok, width), 1)
    att_flat = (
        att_home.reshape(seqs, groups, tok, width).transpose(0, 2, 1, 3).reshape(seqs * tok, features)
    )
    tokens_flat = inputs.reshape(seqs * tok, features)
    resid_one = tokens_flat.astype(F32) + product(att_flat, full_out)
    hidden_one, normed_one, inv_one = norm_forward(resid_one, norm_gain[0], norm_bias[0])
    hidden_low = hidden_one.astype(BF16)
    pre_act = product(hidden_low, full_up)
    activated = gelu_value(pre_act).astype(BF16)
    resid_two = hidden_one + product(activated, full_down)
    result, normed_two, inv_two = norm_forward(resid_two, norm_gain[1], norm_bias[1])
    grad_rows = out_grad.reshape(seqs * tok, features).astype(F32)
    grad_resid_two, gain_two, shift_two = norm_backward(
        grad_rows, normed_two, inv_two, norm_gain[1]
    )
    grad_branch = grad_resid_two.astype(BF16)
    grad_down_w = product_tn(activated, grad_branch).astype(BF16)
    grad_pre = (product_nt(grad_branch, full_down) * gelu_slope(pre_act)).astype(BF16)
    grad_up_w = product_tn(hidden_low, grad_pre).astype(BF16)
    grad_hidden = grad_resid_two + product_nt(grad_pre, full_up)
    grad_resid_one, gain_one, shift_one = norm_backward(
        grad_hidden, normed_one, inv_one, norm_gain[0]
    )
    grad_mix = grad_resid_one.astype(BF16)
    grad_out_w = product_tn(att_flat, grad_mix).astype(BF16)
    grad_att = product_nt(grad_mix, full_out).astype(BF16)
    grad_att = grad_att.reshape(seqs, tok, groups, width).transpose(0, 2, 1, 3)
    src = grad_att.reshape(seq, tok, width)
    stats = jnp.stack([gain_one, gain_two, shift_one, shift_two])
    cut = lambda g: g.reshape(2, 2, 4, 2, g.shape[0] // 32, g.shape[1])
    out_sum, up_sum, down_sum, stats, ig, wq = backward_half(
        src, stats, [cut(grad_out_w), cut(grad_up_w), cut(grad_down_w)],
        (qn, qt, otile, lse, kn, vn, kt), (b1, b0, segk, segq), xs, wgf,
    )
    wq = wq.reshape(groups, features // 32, 3, 256)[..., :width].transpose(1, 2, 0, 3)
    mine = lax.axis_index("dp") * seq + t
    stats = lax.dynamic_slice_in_dim(stats, mine * (features // 32), features // 32, 1)
    return (
        result.astype(BF16).reshape(seqs, tok, features),
        ig + grad_resid_one.reshape(seqs, tok, features),
        wq.reshape(features // 32, 3 * features),
        out_sum,
        up_sum,
        down_sum,
        stats[:2],
        stats[2:],
    )


def solution(mesh):
    in_specs = (
        P("dp", "seq", None),
        P("dp", None),
        P("dp", None, None, None),
        P("dp", None),
        P("dp", None),
        P("dp", None),
        P("dp", None),
        P(),
        P(),
        P("dp", "seq", None),
    )
    out_specs = (
        P("dp", "seq", None),
        P("dp", "seq", None),
        P(("dp", "seq"), None),
        P(("dp", "seq"), None),
        P(("dp", "seq"), None),
        P(("dp", "seq"), None),
        P(None, ("dp", "seq")),
        P(None, ("dp", "seq")),
    )
    fits = mesh.shape["dp"] == 4 and mesh.shape["seq"] == 8
    return jax.shard_map(
        head_layout if fits else per_device, mesh=mesh, in_specs=in_specs, out_specs=out_specs, check_vma=False
    )
```

```python
import functools
import jax
import jax.numpy as jnp
import numpy as np
from jax import lax
from jax.experimental import pallas as pl
from jax.experimental.pallas import tpu as pltpu
from jax.sharding import PartitionSpec as P

H = 12
HEAD = 64
BLOCK = 64
R = 3
MICRO = 2


norm_eps = 1e-05
masked_score = -1e30
root_half = 0.7071067811865476
inv_root_two_pi = 0.3989422804014327


def padded(cells, sides, width):
    for axis, dim in sides:
        count = lax.axis_size(axis)
        ends = count - 1
        head = lax.slice_in_dim(cells, 0, width, axis=dim)
        tail = lax.slice_in_dim(cells, cells.shape[dim] - width, cells.shape[dim], axis=dim)
        cells = jnp.concatenate(
            [
                lax.ppermute(tail, axis, [(i, (i + 1) % count) for i in range(ends)]),
                cells,
                lax.ppermute(head, axis, [((i + 1) % count, i) for i in range(ends)]),
            ],
            axis=dim,
        )
    return cells


def from_root(x, axis, root):
    mine = lax.axis_index(axis) == root
    return lax.psum(jnp.where(mine, x, jnp.zeros_like(x)), axis)


def merged(x, axis, combine):
    everything = jax.tree.map(lambda part: lax.all_gather(part, axis), x)
    initial = jax.tree.map(lambda part: part[0], everything)

    def step(k, so_far):
        return combine(so_far, jax.tree.map(lambda part: part[k], everything))

    return lax.fori_loop(1, lax.axis_size(axis), step, initial)


def product(left_side, right_side):
    return jnp.dot(left_side, right_side, preferred_element_type=jnp.float32)


def product_tn(left_side, right_side):
    return lax.dot_general(
        left_side, right_side, (((0,), (0,)), ((), ())), preferred_element_type=jnp.float32
    )


def product_nt(left_side, right_side):
    return lax.dot_general(
        left_side, right_side, (((1,), (1,)), ((), ())), preferred_element_type=jnp.float32
    )


def gelu_value(pre_act):
    return 0.5 * pre_act * (1.0 + lax.erf(pre_act * root_half))


def gelu_slope(pre_act):
    return (
        0.5 * (1.0 + lax.erf(pre_act * root_half))
        + pre_act * jnp.exp(-0.5 * pre_act * pre_act) * inv_root_two_pi
    )


def norm_forward(residual, gain_row, shift_row):
    mean_row = jnp.mean(residual, axis=-1, keepdims=True)
    centred = residual - mean_row
    variance = jnp.mean(centred * centred, axis=-1, keepdims=True)
    inv_std = lax.rsqrt(variance + norm_eps)
    normed = centred * inv_std
    return (normed * gain_row + shift_row, normed, inv_std)


def norm_backward(grad_rows, normed, inv_std, gain_row):
    scaled = grad_rows * gain_row
    back_rows = inv_std * (
        scaled
        - jnp.mean(scaled, axis=-1, keepdims=True)
        - normed * jnp.mean(scaled * normed, axis=-1, keepdims=True)
    )
    return (back_rows, jnp.sum(grad_rows * normed, axis=0), jnp.sum(grad_rows, axis=0))


def merge_stats(first_pair, second_pair):
    joint_max = jnp.maximum(first_pair[0], second_pair[0])
    joint_sum = first_pair[1] * jnp.exp(first_pair[0] - joint_max) + second_pair[1] * jnp.exp(
        second_pair[0] - joint_max
    )
    return (joint_max, joint_sum)


def local_scores(query_heads, shared_keys, random_keys, shared_ok, random_ok, scale_factor):
    part_shared = jnp.einsum(
        "sbqhd,sbkhd->sbhqk", query_heads, shared_keys, preferred_element_type=jnp.float32
    )
    part_random = jnp.einsum(
        "sbqhd,sbhkd->sbhqk", query_heads, random_keys, preferred_element_type=jnp.float32
    )
    scores = jnp.concatenate([part_shared, part_random], axis=4) * scale_factor
    allowed = jnp.concatenate(
        [jnp.broadcast_to(shared_ok[:, :, None], part_shared.shape), random_ok], axis=4
    )
    return jnp.where(allowed, scores, masked_score)


def per_device(
    inputs, segments, rand_blocks, w_qkv, w_out, w_up, w_down, norm_gain, norm_bias, out_grad
):
    seq_total, tok_dev, features = inputs.shape
    devices = lax.axis_size("seq")
    my_index = lax.axis_index("seq")
    blocks_dev = tok_dev // BLOCK
    blocks_all = blocks_dev * devices
    entries = blocks_dev * H * R
    capacity = max(2, entries // devices + 1)
    per_micro = seq_total // MICRO
    glob_rows = 2 * BLOCK
    shared_count = 5 * BLOCK
    scale_factor = HEAD ** (-0.5)
    token_rows = per_micro * tok_dev
    owner_flag = (my_index == 0).astype(jnp.float32)
    row_global = my_index * tok_dev + jnp.arange(tok_dev, dtype=jnp.int32) < glob_rows
    window_index = np.arange(blocks_dev)[:, None] + np.arange(3)[None, :]
    win_blocks = (
        my_index * blocks_dev
        + jnp.arange(blocks_dev, dtype=jnp.int32)[:, None]
        + jnp.arange(-1, 2, dtype=jnp.int32)[None, :]
    )
    win_inside = (win_blocks >= 0) & (win_blocks < blocks_all)
    win_clipped = jnp.clip(win_blocks, 0, blocks_all - 1)
    entry_heads = jnp.arange(entries, dtype=jnp.int32) // R % H
    slot_ids = jnp.arange(capacity, dtype=jnp.int32)
    earlier = jnp.arange(entries)[None, :] < jnp.arange(entries)[:, None]
    seq_ids = jnp.arange(per_micro, dtype=jnp.int32)
    grad_qkv_w = jnp.zeros((features, 3 * features), jnp.float32)
    grad_out_w = jnp.zeros((features, features), jnp.float32)
    grad_up_w = jnp.zeros((features, w_up.shape[1]), jnp.float32)
    grad_down_w = jnp.zeros((w_down.shape[0] * lax.axis_size("dp"), features), jnp.float32)
    gain_acc = jnp.zeros((2, features), jnp.float32)
    shift_acc = jnp.zeros((2, features), jnp.float32)
    output_parts = []
    input_parts = []
    for micro_step in range(MICRO):
        start_seq = micro_step * per_micro
        tokens_in = inputs[start_seq : start_seq + per_micro]
        seg_micro = segments[start_seq : start_seq + per_micro]
        rand_micro = rand_blocks[start_seq : start_seq + per_micro]
        cotangent = out_grad[start_seq : start_seq + per_micro]
        full_qkv, full_out, full_up, full_down = (
            lax.all_gather(w_qkv, "dp", axis=0, tiled=True),
            lax.all_gather(w_out, "dp", axis=0, tiled=True),
            lax.all_gather(w_up, "dp", axis=0, tiled=True),
            lax.all_gather(w_down, "dp", axis=0, tiled=True),
        )
        tokens_flat = tokens_in.reshape(token_rows, features)
        qkv_rows = (
            product(tokens_flat, full_qkv)
            .astype(jnp.bfloat16)
            .reshape(per_micro, tok_dev, 3 * features)
        )
        queries = qkv_rows[..., :features]
        keyvals = qkv_rows[..., features:]
        extended = padded(keyvals, (("seq", 1),), BLOCK)
        global_block = from_root(qkv_rows[:, :glob_rows], "seq", 0)
        requests = rand_micro.reshape(per_micro, devices, entries)
        owners = requests // blocks_dev
        local_block = requests % blocks_dev
        same_owner = owners[:, :, :, None] == owners[:, :, None, :]
        slot_rank = jnp.sum(same_owner & earlier[None, None], axis=3)
        slot_hit = ((owners == my_index)[..., None] & (slot_rank[..., None] == slot_ids)).astype(
            jnp.int32
        )
        slot_live = jnp.sum(slot_hit, axis=2)
        slot_piece = jnp.sum(slot_hit * (local_block * H + entry_heads)[..., None], axis=2)
        piece_index = jnp.transpose(slot_piece, (1, 2, 0))
        live_mask = jnp.transpose(slot_live, (1, 2, 0))
        pieces = (
            keyvals.reshape(per_micro, blocks_dev, BLOCK, 2, H, HEAD)
            .transpose(0, 1, 4, 2, 3, 5)
            .reshape(per_micro, blocks_dev * H, BLOCK, 2 * HEAD)
        )
        outgoing = pieces[seq_ids[None, None, :], piece_index]
        outgoing = jnp.where(live_mask[..., None, None] > 0, outgoing, jnp.zeros((), jnp.bfloat16))
        outgoing = outgoing.reshape(devices * capacity, per_micro, BLOCK, 2 * HEAD)
        incoming = lax.all_to_all(outgoing, "seq", split_axis=0, concat_axis=0, tiled=True)
        my_owner = jnp.take(owners, my_index, axis=1)
        my_rank = jnp.take(slot_rank, my_index, axis=1)
        my_request = jnp.take(requests, my_index, axis=1)
        positions = my_owner * capacity + my_rank
        fetched = incoming[positions, seq_ids[:, None]].reshape(
            per_micro, blocks_dev, H, R, BLOCK, 2, HEAD
        )
        random_keys = fetched[..., 0, :].reshape(per_micro, blocks_dev, H, R * BLOCK, HEAD)
        random_vals = fetched[..., 1, :].reshape(per_micro, blocks_dev, H, R * BLOCK, HEAD)
        seg_blocks = seg_micro.reshape(per_micro, blocks_all, BLOCK)
        query_seg = lax.dynamic_slice_in_dim(seg_micro, my_index * tok_dev, tok_dev, 1).reshape(
            per_micro, blocks_dev, BLOCK
        )
        window_seg = seg_blocks[:, win_clipped].reshape(per_micro, blocks_dev, 3 * BLOCK)
        window_ok = (query_seg[..., :, None] == window_seg[:, :, None, :]) & jnp.repeat(
            win_inside, BLOCK, axis=1
        )[None, :, None, :]
        shared_ok = jnp.concatenate(
            [window_ok, jnp.ones((per_micro, blocks_dev, BLOCK, glob_rows), bool)], axis=3
        )
        random_seg = seg_blocks[seq_ids[:, None], my_request].reshape(
            per_micro, blocks_dev, H, R * BLOCK
        )
        random_ok = query_seg[:, :, None, :, None] == random_seg[:, :, :, None, :]
        ext_blocks = extended.reshape(per_micro, blocks_dev + 2, BLOCK, 2 * features)
        window_kv = ext_blocks[:, window_index].reshape(
            per_micro, blocks_dev, 3 * BLOCK, 2 * features
        )
        glob_kv = jnp.broadcast_to(
            global_block[:, None, :, features:], (per_micro, blocks_dev, glob_rows, 2 * features)
        )
        shared_kv = jnp.concatenate([window_kv, glob_kv], axis=2)
        shared_keys = shared_kv[..., :features].reshape(
            per_micro, blocks_dev, shared_count, H, HEAD
        )
        shared_vals = shared_kv[..., features:].reshape(
            per_micro, blocks_dev, shared_count, H, HEAD
        )
        query_heads = queries.reshape(per_micro, blocks_dev, BLOCK, H, HEAD)
        scores = local_scores(
            query_heads, shared_keys, random_keys, shared_ok, random_ok, scale_factor
        )
        row_max = jnp.max(scores, axis=4, keepdims=True)
        exp_terms = jnp.exp(scores - row_max)
        row_sum = jnp.sum(exp_terms, axis=4, keepdims=True)
        local_probs = exp_terms / row_sum
        log_norm = row_max + jnp.log(row_sum)
        local_weights = local_probs.astype(jnp.bfloat16)
        local_att = jnp.einsum(
            "sbhqk,sbkhd->sbqhd",
            local_weights[..., :shared_count],
            shared_vals,
            preferred_element_type=jnp.float32,
        )
        local_att = local_att + jnp.einsum(
            "sbhqk,sbhkd->sbqhd",
            local_weights[..., shared_count:],
            random_vals,
            preferred_element_type=jnp.float32,
        )
        local_att = local_att.reshape(per_micro, tok_dev, features)
        glob_query = global_block[..., :features].reshape(per_micro, glob_rows, H, HEAD)
        local_keys = keyvals[..., :features].reshape(per_micro, tok_dev, H, HEAD)
        local_vals = keyvals[..., features:].reshape(per_micro, tok_dev, H, HEAD)
        glob_scores = (
            jnp.einsum(
                "sqhd,skhd->shqk", glob_query, local_keys, preferred_element_type=jnp.float32
            )
            * scale_factor
        )
        part_max = jnp.max(glob_scores, axis=3)
        part_sum = jnp.sum(jnp.exp(glob_scores - part_max[..., None]), axis=3)
        glob_max, glob_sum = merged((part_max, part_sum), "seq", merge_stats)
        glob_lse = glob_max + jnp.log(glob_sum)
        glob_probs = jnp.exp(glob_scores - glob_lse[..., None])
        glob_weights = glob_probs.astype(jnp.bfloat16)
        glob_part = jnp.einsum(
            "shqk,skhd->sqhd", glob_weights, local_vals, preferred_element_type=jnp.float32
        ).reshape(per_micro, glob_rows, features)
        glob_out = lax.psum(glob_part, "seq")
        glob_full = jnp.concatenate(
            [glob_out, jnp.zeros((per_micro, tok_dev - glob_rows, features), jnp.float32)], axis=1
        )
        attention = jnp.where(row_global[None, :, None], glob_full, local_att).astype(jnp.bfloat16)
        att_flat = attention.reshape(token_rows, features)
        resid_one = tokens_flat.astype(jnp.float32) + product(att_flat, full_out)
        hidden_one, normed_one, inv_one = norm_forward(resid_one, norm_gain[0], norm_bias[0])
        hidden_low = hidden_one.astype(jnp.bfloat16)
        pre_act = product(hidden_low, full_up)
        activated = gelu_value(pre_act).astype(jnp.bfloat16)
        resid_two = hidden_one + product(activated, full_down)
        result, normed_two, inv_two = norm_forward(resid_two, norm_gain[1], norm_bias[1])
        output_parts.append(result.astype(jnp.bfloat16).reshape(per_micro, tok_dev, features))
        grad_rows = cotangent.reshape(token_rows, features).astype(jnp.float32)
        grad_resid_two, gain_two, shift_two = norm_backward(
            grad_rows, normed_two, inv_two, norm_gain[1]
        )
        grad_branch = grad_resid_two.astype(jnp.bfloat16)
        grad_down_w = grad_down_w + product_tn(activated, grad_branch)
        grad_pre = (product_nt(grad_branch, full_down) * gelu_slope(pre_act)).astype(jnp.bfloat16)
        grad_up_w = grad_up_w + product_tn(hidden_low, grad_pre)
        grad_hidden = grad_resid_two + product_nt(grad_pre, full_up)
        grad_resid_one, gain_one, shift_one = norm_backward(
            grad_hidden, normed_one, inv_one, norm_gain[0]
        )
        grad_mix = grad_resid_one.astype(jnp.bfloat16)
        grad_out_w = grad_out_w + product_tn(att_flat, grad_mix)
        grad_att = (
            product_nt(grad_mix, full_out)
            .astype(jnp.bfloat16)
            .reshape(per_micro, tok_dev, features)
        )
        gain_acc = gain_acc + jnp.stack([gain_one, gain_two])
        shift_acc = shift_acc + jnp.stack([shift_one, shift_two])
        grad_local = jnp.where(
            row_global[None, :, None], jnp.zeros((), jnp.bfloat16), grad_att
        ).reshape(per_micro, blocks_dev, BLOCK, H, HEAD)
        scores = local_scores(
            query_heads, shared_keys, random_keys, shared_ok, random_ok, scale_factor
        )
        local_probs = jnp.exp(scores - log_norm)
        local_weights = local_probs.astype(jnp.bfloat16)
        grad_prob = jnp.concatenate(
            [
                jnp.einsum(
                    "sbqhd,sbkhd->sbhqk",
                    grad_local,
                    shared_vals,
                    preferred_element_type=jnp.float32,
                ),
                jnp.einsum(
                    "sbqhd,sbhkd->sbhqk",
                    grad_local,
                    random_vals,
                    preferred_element_type=jnp.float32,
                ),
            ],
            axis=4,
        )
        row_delta = jnp.sum(local_probs * grad_prob, axis=4, keepdims=True)
        grad_score = (local_probs * (grad_prob - row_delta)).astype(jnp.bfloat16)
        grad_query = jnp.einsum(
            "sbhqk,sbkhd->sbqhd",
            grad_score[..., :shared_count],
            shared_keys,
            preferred_element_type=jnp.float32,
        )
        grad_query = (
            grad_query
            + jnp.einsum(
                "sbhqk,sbhkd->sbqhd",
                grad_score[..., shared_count:],
                random_keys,
                preferred_element_type=jnp.float32,
            )
        ) * scale_factor
        grad_key_shared = (
            jnp.einsum(
                "sbhqk,sbqhd->sbkhd",
                grad_score[..., :shared_count],
                query_heads,
                preferred_element_type=jnp.float32,
            )
            * scale_factor
        )
        grad_val_shared = jnp.einsum(
            "sbhqk,sbqhd->sbkhd",
            local_weights[..., :shared_count],
            grad_local,
            preferred_element_type=jnp.float32,
        )
        grad_key_random = (
            jnp.einsum(
                "sbhqk,sbqhd->sbhkd",
                grad_score[..., shared_count:],
                query_heads,
                preferred_element_type=jnp.float32,
            )
            * scale_factor
        )
        grad_val_random = jnp.einsum(
            "sbhqk,sbqhd->sbhkd",
            local_weights[..., shared_count:],
            grad_local,
            preferred_element_type=jnp.float32,
        )
        grad_shared = jnp.concatenate(
            [
                grad_key_shared.reshape(per_micro, blocks_dev, shared_count, features),
                grad_val_shared.reshape(per_micro, blocks_dev, shared_count, features),
            ],
            axis=3,
        )
        grad_window = grad_shared[:, :, : 3 * BLOCK].reshape(
            per_micro, blocks_dev, 3, BLOCK, 2 * features
        )
        ext_grad = jnp.zeros((per_micro, blocks_dev + 2, BLOCK, 2 * features), jnp.float32)
        for offset in range(3):
            ext_grad = ext_grad.at[:, offset : offset + blocks_dev].add(grad_window[:, :, offset])
        grad_glob_keys = jnp.sum(grad_shared[:, :, 3 * BLOCK :], axis=1)
        grad_random = jnp.stack([grad_key_random, grad_val_random], axis=4).reshape(
            per_micro, entries, BLOCK, 2 * HEAD
        )
        returned = (
            jnp.zeros((devices * capacity, per_micro, BLOCK, 2 * HEAD), jnp.float32)
            .at[positions, seq_ids[:, None]]
            .set(grad_random)
        )
        arrived = lax.all_to_all(
            returned.astype(jnp.bfloat16), "seq", split_axis=0, concat_axis=0, tiled=True
        ).astype(returned.dtype)
        arrived = arrived.reshape(devices, capacity, per_micro, BLOCK, 2 * HEAD) * live_mask[
            ..., None, None
        ].astype(jnp.float32)
        piece_grad = (
            jnp.zeros((per_micro, blocks_dev * H, BLOCK, 2 * HEAD), jnp.float32)
            .at[seq_ids[None, None, :], piece_index]
            .add(arrived)
        )
        piece_grad = (
            piece_grad.reshape(per_micro, blocks_dev, H, BLOCK, 2, HEAD)
            .transpose(0, 1, 3, 4, 2, 5)
            .reshape(per_micro, tok_dev, 2 * features)
        )
        rim_pair = jnp.concatenate([ext_grad[:, 0], ext_grad[:, blocks_dev + 1]], axis=1)
        rim_back = padded(rim_pair.astype(jnp.bfloat16), (("seq", 1),), BLOCK).astype(
            rim_pair.dtype
        )
        grad_kv = (
            ext_grad[:, 1 : blocks_dev + 1].reshape(per_micro, tok_dev, 2 * features) + piece_grad
        )
        grad_kv = grad_kv.at[:, :BLOCK].add(rim_back[:, :BLOCK])
        grad_kv = grad_kv.at[:, tok_dev - BLOCK :].add(rim_back[:, 3 * BLOCK :])
        grad_glob = from_root(grad_att[:, :glob_rows], "seq", 0)
        grad_glob_heads = grad_glob.reshape(per_micro, glob_rows, H, HEAD)
        glob_scores = (
            jnp.einsum(
                "sqhd,skhd->shqk", glob_query, local_keys, preferred_element_type=jnp.float32
            )
            * scale_factor
        )
        glob_probs = jnp.exp(glob_scores - glob_lse[..., None])
        glob_weights = glob_probs.astype(jnp.bfloat16)
        glob_grad_prob = jnp.einsum(
            "sqhd,skhd->shqk", grad_glob_heads, local_vals, preferred_element_type=jnp.float32
        )
        glob_delta = lax.psum(jnp.sum(glob_probs * glob_grad_prob, axis=3), "seq")
        glob_grad_score = (glob_probs * (glob_grad_prob - glob_delta[..., None])).astype(
            jnp.bfloat16
        )
        glob_grad_query = (
            jnp.einsum(
                "shqk,skhd->sqhd", glob_grad_score, local_keys, preferred_element_type=jnp.float32
            )
            * scale_factor
        )
        glob_grad_key = (
            jnp.einsum(
                "shqk,sqhd->skhd", glob_grad_score, glob_query, preferred_element_type=jnp.float32
            )
            * scale_factor
        )
        glob_grad_val = jnp.einsum(
            "shqk,sqhd->skhd", glob_weights, grad_glob_heads, preferred_element_type=jnp.float32
        )
        grad_kv = grad_kv + jnp.concatenate(
            [
                glob_grad_key.reshape(per_micro, tok_dev, features),
                glob_grad_val.reshape(per_micro, tok_dev, features),
            ],
            axis=2,
        )
        summed_query, summed_keys = lax.psum(
            (glob_grad_query.reshape(per_micro, glob_rows, features), grad_glob_keys), "seq"
        )
        grad_kv = grad_kv.at[:, :glob_rows].add(owner_flag * summed_keys)
        grad_queries = (
            grad_query.reshape(per_micro, tok_dev, features)
            .at[:, :glob_rows]
            .add(owner_flag * summed_query)
        )
        grad_qkv_rows = (
            jnp.concatenate([grad_queries, grad_kv], axis=2)
            .astype(jnp.bfloat16)
            .reshape(token_rows, 3 * features)
        )
        grad_qkv_w = grad_qkv_w + product_tn(tokens_flat, grad_qkv_rows)
        input_rows = grad_resid_one + product_nt(grad_qkv_rows, full_qkv)
        input_parts.append(input_rows.reshape(per_micro, tok_dev, features))
    summed = (
        lax.psum_scatter(grad_qkv_w, ("dp", "seq"), scatter_dimension=0, tiled=True),
        lax.psum_scatter(grad_out_w, ("dp", "seq"), scatter_dimension=0, tiled=True),
        lax.psum_scatter(grad_up_w, ("dp", "seq"), scatter_dimension=0, tiled=True),
        lax.psum_scatter(grad_down_w, ("dp", "seq"), scatter_dimension=0, tiled=True),
        lax.psum_scatter(gain_acc, ("dp", "seq"), scatter_dimension=1, tiled=True),
        lax.psum_scatter(shift_acc, ("dp", "seq"), scatter_dimension=1, tiled=True),
    )
    return (
        jnp.concatenate(output_parts, axis=0),
        jnp.concatenate(input_parts, axis=0),
        summed[0],
        summed[1],
        summed[2],
        summed[3],
        summed[4],
        summed[5],
    )


TILE = 128
NH = 3
CH = 256
LOG2E = 1.4426950408889634
SCALE2 = HEAD ** (-0.5) * LOG2E
NEG = -1e30
F32 = jnp.float32
BF16 = jnp.bfloat16


def nt(a, b):
    return lax.dot_general(a, b, (((1,), (1,)), ((), ())), preferred_element_type=F32)


def nn(a, b):
    return jnp.dot(a, b, preferred_element_type=F32)


MESH = pl.DeviceIdType.MESH
ANYSPACE = pl.BlockSpec(memory_space=pl.ANY)
VMEMSPACE = pl.BlockSpec(memory_space=pltpu.VMEM)


class Copies:
    def __init__(self, send, recv):
        self.send = send
        self.recv = recv
        self.used = 0

    def to(self, src, dst, device):
        index = self.used
        self.used += 1
        return pltpu.make_async_remote_copy(
            src_ref=src, dst_ref=dst, send_sem=self.send.at[index], recv_sem=self.recv.at[index],
            device_id=device, device_id_type=MESH,
        )


class Place:
    def __init__(self):
        self.d = lax.axis_index("dp")
        self.t = lax.axis_index("seq")
        self.x = lax.rem(self.d, 2)
        self.y = self.d // 2
        self.c = lax.rem(self.t, 2)
        self.z = self.t // 2
        self.half = self.z // 2
        self.xn = self.d + 1 - 2 * self.x
        self.yn = self.d + 2 - 4 * self.y
        self.diag = 3 - self.d
        self.pair_z = self.z + 1 - 2 * lax.rem(self.z, 2)
        self.across_x = (self.xn, self.t)
        self.across_y = (self.yn, self.t)
        self.partner = (self.d, self.t + 1 - 2 * self.c)

    def at_z(self, z):
        return (self.d, 2 * z + self.c)


def meet(devices):
    barrier = pltpu.get_barrier_semaphore()
    for device in devices:
        pl.semaphore_signal(barrier, inc=1, device_id=device, device_id_type=MESH)
    pl.semaphore_wait(barrier, len(devices))


def tile_tables(tile, rand_ref, segq_ref, blocks):
    wide = NH * TILE
    key = lax.broadcasted_iota(jnp.int32, (blocks, wide), 0)
    lane = lax.broadcasted_iota(jnp.int32, (blocks, wide), 1)
    query = tile * (TILE // BLOCK) + lax.rem(lane, TILE) // BLOCK
    near = (key - query) * (key - query) <= 1
    hits = near.astype(F32)
    for r in range(rand_ref.shape[1]):
        hits = hits + (rand_ref[tile, r : r + 1, :] == key).astype(F32)
    fixed = jnp.logical_or(query < 2, key < 2)
    count = jnp.where(query < 2, 0.0, hits) + fixed.astype(F32)
    on = jnp.where(count > 0.0, jnp.log2(jnp.maximum(count, 1.0)), NEG)
    off = jnp.where(fixed, 0.0, NEG)
    return on, off, segq_ref[tile]


def biased(s, mask, on, off, first_block):
    rows = []
    for j in range(s.shape[0] // BLOCK):
        kb = first_block + j
        m3 = jnp.concatenate([mask[BLOCK * j : BLOCK * (j + 1)]] * NH, axis=1)
        bias = jnp.where(m3, on[kb : kb + 1, :], off[kb : kb + 1, :])
        rows.append(s[BLOCK * j : BLOCK * (j + 1)] * SCALE2 + bias)
    return jnp.concatenate(rows, axis=0)


def fill_segments(segq, segk):
    steps = segq.shape[0]
    for i in range(steps):
        column = jnp.broadcast_to(segq[i].astype(F32), (8, TILE)).T[:, :1]
        segk[TILE * i : TILE * (i + 1), :] = jnp.broadcast_to(column, (TILE, TILE)).astype(jnp.int32)


def forward_tile(tile, rand, segq, segk, qt, kn, vt, q3, tbuf, att, otile, lse):
    length = kn.shape[0]
    chunks = length // CH
    here = pl.ds(pl.multiple_of(tile * TILE, TILE), TILE)
    on, off, seg = tile_tables(tile, rand, segq, length // BLOCK)
    for h in range(NH):
        q3[HEAD * h : HEAD * (h + 1), TILE * h : TILE * (h + 1)] = qt[
            HEAD * h : HEAD * (h + 1), here
        ]
    top = jnp.full((8, NH * TILE), NEG, F32)
    for j in range(chunks):
        rows = slice(CH * j, CH * (j + 1))
        s = nn(kn[rows, :], q3[...])
        t = biased(s, segk[rows, :] == seg, on, off, CH // BLOCK * j)
        tbuf[rows, :] = t
        top = jnp.maximum(top, jnp.max(t.reshape(CH // 8, 8, NH * TILE), axis=0))
    peak = jnp.max(top, axis=0, keepdims=True)
    total = jnp.zeros((8, NH * TILE), F32)
    out = jnp.zeros((256, NH * TILE), F32)
    for j in range(chunks):
        rows = slice(CH * j, CH * (j + 1))
        p = jnp.exp2(tbuf[rows, :] - peak)
        total = total + jnp.sum(p.reshape(CH // 8, 8, NH * TILE), axis=0)
        out = out + nn(vt[:, rows], p.astype(BF16))
    weight = jnp.sum(total, axis=0, keepdims=True)
    lse[tile] = peak + jnp.log2(weight)
    inv = 1.0 / weight
    heads = [
        out[HEAD * h : HEAD * (h + 1), TILE * h : TILE * (h + 1)] * inv[:, TILE * h : TILE * (h + 1)]
        for h in range(NH)
    ]
    merged = jnp.concatenate(heads, axis=0)
    otile[tile] = merged
    att[here, :] = merged.T.astype(BF16)


def unit_place(me, u):
    low = lax.rem(me.z, 2)
    return 2 * lax.rem(me.half + 1 + u // 2, 2) + lax.rem(low + 1 + u, 2)


def forward_kernel(*refs):
    (x, wg, wo, wu, wd, rand, segq), refs = refs[:7], refs[7:]
    outs, refs = refs[:14], refs[14:]
    wof, wuf, wdf, att_out, otile_o, lse_o, segk_o, qn_o, kn_o, vn_o, qt_o, kt_o, xst_o, wgf_o = outs
    (xs, wgf, bo, bu, bd, att, home, otile, lse, segk), refs = refs[:10], refs[10:]
    (qn, kn, vn, qt, kt, vt, xst, q3, tbuf), refs = refs[:9], refs[9:]
    send, recv, xsend, xrecv, local = refs
    me = Place()
    d, t, c, z = me.d, me.t, me.c, me.z
    mine, other = me.half, 1 - me.half
    is_middle = z == 1 + me.half
    tok = x.shape[1]
    length = xs.shape[0]
    steps = length // TILE
    per_unit = 2 * tok // TILE
    loads = [
        pltpu.make_async_copy(src, dst, local.at[i])
        for i, (src, dst) in enumerate(((wo, bo), (wu, bu), (wd, bd)))
    ]
    for load in loads:
        load.start()
    meet([me.across_x, me.across_y] + [(d, lax.rem(t + k, 8)) for k in range(1, 8)])
    cps = Copies(send, recv)
    sent = []

    def begin(*copies):
        for cp in copies:
            cp.start()
            sent.append(cp)

    def rows_of(index):
        return pl.ds(pl.multiple_of(index * tok, tok), tok)

    shard = wg.shape[0]
    wrows = lambda index, start, size: pl.ds(pl.multiple_of(index * shard + start, size), size)
    wg_x = cps.to(wg, wgf.at[wrows(d, 0, shard)], me.across_x)
    wg_y = cps.to(wg, wgf.at[wrows(d, 0, shard)], me.across_y)
    near = cps.to(x.at[mine], xs.at[rows_of(t)], me.at_z(me.pair_z))
    give = cps.to(x.at[mine], xs.at[rows_of(t)], me.partner)
    far = pltpu.make_async_remote_copy(
        src_ref=x.at[other], dst_ref=xs.at[rows_of(t)], send_sem=xsend.at[0],
        recv_sem=xrecv.at[lax.rem(z, 2)], device_id=me.at_z(2 - me.half), device_id_type=MESH,
    )
    begin(wg_x, wg_y, far, near, give)
    heavy = []
    for w, full in ((wo, wof), (wu, wuf), (wd, wdf)):
        rows = w.shape[0] // 2
        part = pl.ds(pl.multiple_of(c * rows, rows), rows)
        to_x = cps.to(w.at[part], full.at[d, part], me.across_x)
        to_y = cps.to(w.at[part], full.at[d, part], me.across_y)
        begin(to_x, to_y)
        heavy.append((full, rows, part, to_x, to_y))

    xs[rows_of(t), :] = x[mine]
    wgf[wrows(d, 0, shard), :] = wg[...]
    q3[...] = jnp.zeros_like(q3)
    fill_segments(segq, segk)
    keeps = []
    for i, (load, buf, full) in enumerate(zip(loads, (bo, bu, bd), (wof, wuf, wdf))):
        load.wait()
        keep = pltpu.make_async_copy(buf, full.at[d], local.at[3 + i])
        keep.start()
        keeps.append(keep)

    half = shard // 2
    wg_x.wait_recv()
    lo = wrows(me.xn, 0, half)
    wg_dy = cps.to(wgf.at[lo], wgf.at[lo], me.across_y)
    begin(wg_dy)
    wg_y.wait_recv()
    hi = wrows(me.yn, half, half)
    wg_dx = cps.to(wgf.at[hi], wgf.at[hi], me.across_x)
    begin(wg_dx)

    def project(unit):
        rows = pl.ds(pl.multiple_of(unit * 2 * tok, 2 * tok), 2 * tok)
        both = nn(xs[rows, :], wgf[...])
        qf, kf, vf = both[:, :256], both[:, 256:512], both[:, 512:]
        qn[rows, :] = qf.astype(BF16)
        kn[rows, :] = kf.astype(BF16)
        vn[rows, :] = vf.astype(BF16)
        qt[:, rows] = qf.T.astype(BF16)
        kt[:, rows] = kf.T.astype(BF16)
        vt[:, rows] = vf.T.astype(BF16)
        xst[:, rows] = xs[rows, :].astype(F32).T.astype(BF16)

    wg_dy.wait_recv()
    wg_dx.wait_recv()
    give.wait_recv()
    near.wait_recv()
    near_rows = rows_of(2 * me.pair_z + c)
    pass_near = cps.to(xs.at[near_rows], xs.at[near_rows], me.partner)
    begin(pass_near)
    relays, onwards = [], []
    for j in range(2):
        src_rows = rows_of(2 * (2 * other + j) + c)
        relays.append(
            pltpu.make_async_remote_copy(
                src_ref=xs.at[src_rows], dst_ref=xs.at[src_rows], send_sem=xsend.at[1 + j],
                recv_sem=xrecv.at[j], device_id=me.at_z(me.pair_z), device_id_type=MESH,
            )
        )
        onwards.append(cps.to(xs.at[src_rows], xs.at[src_rows], me.partner))

    def forward_x(j):
        relays[j].wait_recv()
        pl.when(is_middle)(relays[j].start)
        begin(onwards[j])

    def arrive(k):
        if k == 0:
            forward_x(0)
        if k == 1:
            forward_x(1)
            pass_near.wait_recv()
        if k == 2:
            onwards[0].wait_recv()
        if k == 3:
            onwards[1].wait_recv()

    def project_step(k, carry):
        for i in range(4):
            pl.when(k == i)(functools.partial(arrive, i))
        unit = jnp.where(k < 2, 2 * mine + lax.rem(lax.rem(z, 2) + k, 2), 2 * other + k - 2)
        project(unit)
        return carry

    lax.fori_loop(0, 4, project_step, 0)
    saves = [
        pltpu.make_async_copy(src, dst, local.at[6 + i])
        for i, (src, dst) in enumerate(
            ((segk, segk_o), (qn, qn_o), (kn, kn_o), (vn, vn_o), (qt, qt_o), (kt, kt_o), (xst, xst_o), (wgf, wgf_o))
        )
    ]
    for save in saves:
        save.start()

    tail = []
    for full, rows, part, to_x, to_y in heavy:
        quarter = rows // 2
        lo = pl.ds(pl.multiple_of(c * rows, quarter), quarter)
        hi = pl.ds(pl.multiple_of(c * rows + quarter, quarter), quarter)
        tail.append(
            (
                to_x, to_y,
                cps.to(full.at[me.xn, lo], full.at[me.xn, lo], me.across_y),
                cps.to(full.at[me.xn, part], full.at[me.xn, part], me.partner),
                cps.to(full.at[me.yn, hi], full.at[me.yn, hi], me.across_x),
                cps.to(full.at[me.yn, part], full.at[me.yn, part], me.partner),
                cps.to(full.at[me.diag, part], full.at[me.diag, part], me.partner),
            )
        )

    def relay_weights(k):
        to_x, to_y, dy, px, dx, py, pd = tail[k]
        to_x.wait_recv()
        begin(dy, px)
        to_y.wait_recv()
        begin(dx, py)

    def relay_diag(k):
        to_x, to_y, dy, px, dx, py, pd = tail[k]
        dy.wait_recv()
        dx.wait_recv()
        begin(pd)

    homes = []
    for u in range(4):
        unit = unit_place(me, u)
        for o in range(1 if u == 3 else 0, 2):
            to = 2 * unit + (c if o == 0 else 1 - c)
            homes.append((u, cps.to(att.at[rows_of(to)], home.at[t], (d, to))))

    def send_home(u):
        for v, move in homes:
            if u == v:
                move.start()

    def between(i):
        if i == 0:
            relay_weights(0)
        if i == per_unit:
            send_home(0)
            relay_weights(1)
        if i == 2 * per_unit:
            send_home(1)
            relay_diag(0)
        if i == 3 * per_unit:
            send_home(2)
            relay_weights(2)
            relay_diag(1)

    def tile_step(i, carry):
        for point in range(0, steps, per_unit):
            pl.when(i == point)(functools.partial(between, point))
        tile = unit_place(me, i // per_unit) * per_unit + lax.rem(i, per_unit)
        forward_tile(tile, rand, segq, segk, qt, kn, vt, q3, tbuf, att, otile, lse)
        return carry

    lax.fori_loop(0, steps, tile_step, 0)
    send_home(3)
    last = [
        pltpu.make_async_copy(src, dst, local.at[14 + i])
        for i, (src, dst) in enumerate(((otile, otile_o), (lse, lse_o)))
    ]
    for save in last:
        save.start()
    home[t] = att[rows_of(t), :]
    relay_diag(2)
    for u, move in homes:
        move.wait()
    for s in range(2):
        pieces = [home[4 * s + g].astype(F32) for g in range(4)]
        att_out[tok * s : tok * (s + 1), :] = jnp.concatenate(pieces, axis=1).astype(BF16)
    for to_x, to_y, dy, px, dx, py, pd in tail:
        px.wait_recv()
        py.wait_recv()
        pd.wait_recv()
    for cp in sent:
        cp.wait_send()

    @pl.when(is_middle)
    def _():
        for relay in relays:
            relay.wait_send()

    for copy in keeps + saves + last:
        copy.wait()


def forward_half(x, wg, wo, wu, wd, rand, segq):
    dp = lax.axis_size("dp")
    seq = lax.axis_size("seq")
    tok, features = x.shape[1:]
    length = seq * tok
    steps = length // TILE
    nat, tra = (length, 256), (256, length)
    stacked = lambda w: jax.ShapeDtypeStruct((dp,) + w.shape, BF16)
    low = lambda *shape: jax.ShapeDtypeStruct(shape, BF16)
    full = lambda *shape: jax.ShapeDtypeStruct(shape, F32)
    return pl.pallas_call(
        forward_kernel,
        in_specs=[VMEMSPACE] * 2 + [ANYSPACE] * 3 + [VMEMSPACE] * 2,
        out_specs=[ANYSPACE] * 3 + [VMEMSPACE] + [ANYSPACE] * 10,
        out_shape=[
            stacked(wo), stacked(wu), stacked(wd), low(2 * tok, features),
            full(steps, NH * HEAD, TILE), full(steps, 1, NH * TILE),
            jax.ShapeDtypeStruct((length, TILE), jnp.int32),
            low(*nat), low(*nat), low(*nat), low(*tra), low(*tra),
            low(features, length), low(features, 768),
        ],
        scratch_shapes=[
            pltpu.VMEM((length, features), BF16),
            pltpu.VMEM((features, 768), BF16),
            pltpu.VMEM(wo.shape, BF16),
            pltpu.VMEM(wu.shape, BF16),
            pltpu.VMEM(wd.shape, BF16),
            pltpu.VMEM((length, NH * HEAD), BF16),
            pltpu.VMEM((seq, tok, NH * HEAD), BF16),
            pltpu.VMEM((steps, NH * HEAD, TILE), F32),
            pltpu.VMEM((steps, 1, NH * TILE), F32),
            pltpu.VMEM((length, TILE), jnp.int32),
            pltpu.VMEM(nat, BF16),
            pltpu.VMEM(nat, BF16),
            pltpu.VMEM(nat, BF16),
            pltpu.VMEM(tra, BF16),
            pltpu.VMEM(tra, BF16),
            pltpu.VMEM(tra, BF16),
            pltpu.VMEM((features, length), BF16),
            pltpu.VMEM((256, NH * TILE), BF16),
            pltpu.VMEM((length, NH * TILE), F32),
            pltpu.SemaphoreType.DMA((90,)),
            pltpu.SemaphoreType.DMA((90,)),
            pltpu.SemaphoreType.DMA((3,)),
            pltpu.SemaphoreType.DMA((2,)),
            pltpu.SemaphoreType.DMA((16,)),
        ],
        compiler_params=pltpu.CompilerParams(
            collective_id=0, has_side_effects=True, vmem_limit_bytes=62 * 1024 * 1024
        ),
        name="forward_half",
    )(x, wg, wo, wu, wd, rand, segq)


def each(count, body):
    def run(i, carry):
        body(i)
        return carry

    lax.fori_loop(0, count, run, 0)


def plus(a, b):
    return a.astype(F32) + b.astype(F32)


def backward_tile(
    tile, dat, qn, qt, otile, lse, rand, segq, segk, kn, vn, kt, dqkv, q3t, d3t, q3, d3, dk, dv
):
    chunks = kn.shape[0] // CH
    on, off, seg = tile_tables(tile, rand, segq, kn.shape[0] // BLOCK)
    here = pl.ds(pl.multiple_of(tile * TILE, TILE), TILE)
    dat_f = dat[here, :].astype(F32)
    dat_t = dat_f.T
    lane = lax.broadcasted_iota(jnp.int32, (TILE, NH * HEAD), 1) // HEAD
    qblk = qn[here, : NH * HEAD].astype(F32)
    delta = []
    for h in range(NH):
        hr = slice(HEAD * h, HEAD * (h + 1))
        hc = slice(TILE * h, TILE * (h + 1))
        q3t[hr, hc] = qt[hr, here]
        d3t[hr, hc] = dat_t[hr].astype(BF16)
        q3[hc, :] = jnp.where(lane == h, qblk, 0.0).astype(BF16)
        d3[hc, :] = jnp.where(lane == h, dat_f, 0.0).astype(BF16)
        delta.append(jnp.sum(dat_t[hr] * otile[tile, hr, :], axis=0, keepdims=True))
    delta = jnp.concatenate(delta, axis=1)
    norm = lse[tile]
    dq = jnp.zeros((256, NH * TILE), F32)
    for j in range(chunks):
        rows = slice(CH * j, CH * (j + 1))
        s = nn(kn[rows, :], q3t[...])
        dp = nn(vn[rows, :], d3t[...])
        t = biased(s, segk[rows, :] == seg, on, off, CH // BLOCK * j)
        p = jnp.exp2(t - norm)
        ds = (p * (dp - delta)).astype(BF16)
        dv[rows, :] += nn(p.astype(BF16), d3[...])
        dk[rows, :] += nn(ds, q3[...])
        dq = dq + nn(kt[:, rows], ds)
    heads = [dq[HEAD * h : HEAD * (h + 1), TILE * h : TILE * (h + 1)] for h in range(NH)]
    merged = jnp.concatenate(heads, axis=0).T * HEAD ** (-0.5)
    dqkv[here, : NH * HEAD] = merged.astype(BF16)


def backward_kernel(*refs):
    (src, stats, g0, g1, g2), refs = refs[:5], refs[5:]
    (rand, segq), refs = refs[:2], refs[2:]
    saved, refs = refs[:10], refs[10:]
    (o0, o1, o2, stats_out, ig, wq), refs = refs[:6], refs[6:]
    bufs, refs = refs[:18], refs[18:]
    held, refs = refs[:10], refs[10:]
    kn, vn, kt, segk, qn, qt, otile, lse, xst, wg = held
    (dat, dqkv, q3t, d3t, q3, d3, dk, dv), refs = refs[:8], refs[8:]
    (part, own_p, rp, ra_p, rb_p, ro, dwg, wb1, wb2, wc, wr), refs = refs[:11], refs[11:]
    nsend, nrecv, send, recv, local = refs
    me = Place()
    c, z, x, y, t = me.c, me.z, me.x, me.y, me.t
    mine, other = me.half, 1 - me.half
    is_middle = z == 1 + me.half
    is_outer = z != 1 + me.half
    z_step = [lax.rem(z + k, 4) for k in (1, 2, 3)]
    tok = src.shape[1]
    loads = [
        pltpu.make_async_copy(from_hbm, to_vmem, local.at[4 + i])
        for i, (from_hbm, to_vmem) in enumerate(zip(saved, held))
    ]
    for load in loads:
        load.start()
    meet([me.across_x, me.across_y] + [(me.d, lax.rem(t + k, 8)) for k in range(1, 8)])
    cps = Copies(send, recv)

    def rows_of(index):
        return pl.ds(pl.multiple_of(index * tok, tok), tok)

    dat_moves = []
    for u in range(4):
        place = unit_place(me, 3 - u)
        for o in range(1 if u == 0 else 0, 2):
            to = 2 * place + (c if o == 0 else 1 - c)
            dat_moves.append((u, cps.to(src.at[to], dat.at[rows_of(t)], (me.d, to))))
    for u, move in dat_moves:
        move.start()
    keep = pltpu.make_async_copy(src.at[t], dat.at[rows_of(t)], local.at[3])
    keep.start()

    works = []
    for i, (g, o) in enumerate(((g2, o2), (g1, o1), (g0, o0))):
        own, ra, rb1, rb2, rc, rd = bufs[6 * i : 6 * i + 6]
        swap_core = cps.to(g.at[:, :, :, 1 - c], ra, me.partner)
        swap_core.start()
        load = pltpu.make_async_copy(g.at[:, :, :, c], own, local.at[i])
        load.start()
        moves = (
            swap_core,
            load,
            cps.to(own.at[:, 1 - x, 0:2], rb1, me.across_x),
            cps.to(own.at[1 - y, :, 2:4], rb2, me.across_y),
            cps.to(rb1.at[1 - y], rc.at[0:2], me.across_y),
            cps.to(rb2.at[1 - x], rc.at[2:4], me.across_x),
            [cps.to(rc.at[k], rd.at[j], me.at_z(k)) for j, k in enumerate(z_step)],
        )
        works.append(((o, own, ra, rb1, rb2, rc, rd), moves))
    stat_to = [me.partner, me.across_x, me.across_y, me.at_z(me.pair_z), me.at_z(lax.rem(z + 2, 4))]
    stat_all = [cps.to(nsend.at[k], nrecv.at[k], stat_to[k]) for k in range(5)]

    def stat_step(k):
        if k == 0:
            nsend[0] = stats[...]
        else:
            stat_all[k - 1].wait_recv()
            nsend[k] = nsend[k - 1] + nrecv[k - 1]
        stat_all[k].start()

    sent = []

    def begin(*copies):
        for cp in copies:
            cp.start()
            sent.append(cp)

    def stage_a(work):
        (o, own, ra, rb1, rb2, rc, rd), (swap_core, load, bx, by, cy, cx, ds) = work
        load.wait()
        swap_core.wait_recv()

        def fold(i):
            yy, xx, zz = i // 8, lax.rem(i // 4, 2), lax.rem(i, 4)
            own[yy, xx, zz] = plus(own[yy, xx, zz], ra[yy, xx, zz]).astype(BF16)

        each(16, fold)
        begin(bx, by)

    def stage_b(work):
        (o, own, ra, rb1, rb2, rc, rd), (swap_core, load, bx, by, cy, cx, ds) = work
        bx.wait_recv()

        def fold_x(i):
            yy, zz = i // 2, lax.rem(i, 2)
            rb1[yy, zz] = plus(own[yy, x, zz], rb1[yy, zz]).astype(BF16)

        each(4, fold_x)
        begin(cy)
        by.wait_recv()

        def fold_y(i):
            xx, zz = i // 2, lax.rem(i, 2)
            rb2[xx, zz] = plus(own[y, xx, 2 + zz], rb2[xx, zz]).astype(BF16)

        each(4, fold_y)
        begin(cx)

    def stage_c(work):
        (o, own, ra, rb1, rb2, rc, rd), (swap_core, load, bx, by, cy, cx, ds) = work
        cy.wait_recv()
        cx.wait_recv()
        for zz in range(2):
            rc[zz] = plus(rb1[y, zz], rc[zz]).astype(BF16)
            rc[2 + zz] = plus(rb2[x, zz], rc[2 + zz]).astype(BF16)
        begin(*ds)

    def stage_d(work):
        (o, own, ra, rb1, rb2, rc, rd), (swap_core, load, bx, by, cy, cx, ds) = work
        for cp in ds:
            cp.wait_recv()
        o[...] = plus(rc[z], rd[0]) + plus(rd[1], rd[2])

    q3t[...] = jnp.zeros_like(q3t)
    d3t[...] = jnp.zeros_like(d3t)
    dk[...] = jnp.zeros_like(dk)
    dv[...] = jnp.zeros_like(dv)
    gap = jnp.zeros((dqkv.shape[0], 256 - NH * HEAD), BF16)
    for g in range(3):
        dqkv[:, 256 * g + NH * HEAD : 256 * (g + 1)] = gap
    stat_step(0)
    for load in loads[:8]:
        load.wait()
    keep.wait()
    per_unit = 2 * tok // TILE
    steps = dqkv.shape[0] // TILE

    def before_unit(u):
        for v, move in dat_moves:
            if u == v:
                move.wait_recv()
        if u == 1:
            for work in works:
                stage_a(work)
            stat_step(1)
        if u == 2:
            stat_step(2)
        if u == 3:
            stage_b(works[0])
            stat_step(3)

    def tile_step(i, carry):
        for u in range(4):
            pl.when(i == u * per_unit)(functools.partial(before_unit, u))
        tile = unit_place(me, 3 - i // per_unit) * per_unit + lax.rem(i, per_unit)
        backward_tile(
            tile, dat, qn, qt, otile, lse, rand, segq, segk, kn, vn, kt, dqkv,
            q3t, d3t, q3, d3, dk, dv,
        )
        return carry

    lax.fori_loop(0, steps, tile_step, 0)
    stage_b(works[1])
    stage_b(works[2])
    stat_step(4)
    loads[9].wait()

    dqkv[:, 256 : 256 + NH * HEAD] = (dk[...] * HEAD ** (-0.5)).astype(BF16)
    dqkv[:, 512 : 512 + NH * HEAD] = dv[...].astype(BF16)
    order = [2 * other, 2 * other + 1, me.pair_z, z]
    cores = []
    for zz in order:
        rows = pl.ds(pl.multiple_of(zz * 2 * tok, 2 * tok), 2 * tok)
        grad = nt(dqkv[rows, :], wg[...]).astype(BF16)
        part[zz, 0] = grad[:tok]
        part[zz, 1] = grad[tok:]
        core = cps.to(part.at[zz, 1 - c], rp.at[zz], me.partner)
        begin(core)
        cores.append(core)
    stage_c(works[0])

    up = [cps.to(own_p.at[2 * other + j], rb_p.at[j], me.at_z(me.pair_z)) for j in range(2)]
    near = cps.to(own_p.at[me.pair_z], ra_p, me.at_z(me.pair_z))
    for k, zz in enumerate(order):
        cores[k].wait_recv()
        own_p[zz] = plus(part[zz, c], rp[zz]).astype(BF16)
        if k < 2:
            pl.when(is_outer)(up[k].start)
        if k == 2:
            begin(near)
    loads[8].wait()
    half_rows = xst.shape[0] // 2
    for yy in range(2):
        grad = nn(xst[half_rows * yy : half_rows * (yy + 1), :], dqkv[...]).astype(BF16)
        dwg[yy] = grad.reshape(dwg.shape[1:])
    bx = cps.to(dwg.at[:, 1 - x, 0:4], wb1, me.across_x)
    by = cps.to(dwg.at[1 - y, :, 4:8], wb2, me.across_y)
    begin(bx, by)
    down_send, down_recv = cps.used, cps.used
    cps.used += 2
    down = [
        pltpu.make_async_remote_copy(
            src_ref=own_p.at[2 * other + j], dst_ref=ro, send_sem=send.at[down_send + j],
            recv_sem=recv.at[down_recv], device_id=me.at_z(2 * other + j), device_id_type=MESH,
        )
        for j in range(2)
    ]

    @pl.when(is_middle)
    def _():
        for j in range(2):
            up[j].wait_recv()
            own_p[2 * other + j] = plus(own_p[2 * other + j], rb_p[j]).astype(BF16)
            down[j].start()

    stage_c(works[1])
    stage_c(works[2])
    bx.wait_recv()

    def fold_x(i):
        yy, tt = i // 4, lax.rem(i, 4)
        wb1[yy, tt] = plus(dwg[yy, x, tt], wb1[yy, tt]).astype(BF16)

    each(8, fold_x)
    cy = cps.to(wb1.at[1 - y], wc.at[0:4], me.across_y)
    begin(cy)
    by.wait_recv()

    def fold_y(i):
        xx, tt = i // 4, lax.rem(i, 4)
        wb2[xx, tt] = plus(dwg[y, xx, 4 + tt], wb2[xx, tt]).astype(BF16)

    each(8, fold_y)
    cx = cps.to(wb2.at[1 - x], wc.at[4:8], me.across_x)
    begin(cx)
    stat_all[-1].wait_recv()
    stats_out[...] = nsend[4] + nrecv[4]
    cy.wait_recv()
    cx.wait_recv()

    def fold_c(i):
        wc[i] = plus(wb1[y, i], wc[i]).astype(BF16)
        wc[4 + i] = plus(wb2[x, i], wc[4 + i]).astype(BF16)

    each(4, fold_c)
    moves = []
    for k in range(1, 8):
        peer = lax.rem(t + k, 8)
        moves.append(cps.to(wc.at[peer], wr.at[t], (me.d, peer)))
    begin(*moves)
    near.wait_recv()
    ig[mine] = plus(own_p[z], ra_p[...])
    down[0].wait_recv()
    ig[other] = ro[...].astype(F32)
    for work in works:
        stage_d(work)
    wr[t] = wc[t]
    for move in moves:
        move.wait_recv()
    for g in range(4):
        wq[g] = plus(wr[g], wr[4 + g])
    for cp in sent + stat_all + [move for u, move in dat_moves] + [moves[0] for refs, moves in works]:
        cp.wait_send()

    @pl.when(is_outer)
    def _():
        for cp in up:
            cp.wait_send()

    @pl.when(is_middle)
    def _():
        for cp in down:
            cp.wait_send()


def backward_half(src, stats, grads, rand, segq, saved):
    dims = [g.shape[-2:] for g in grads]
    tok = src.shape[1]
    features, length = saved[8].shape
    bufs = []
    for rows, cols in dims[::-1]:
        bufs += [
            pltpu.VMEM((2, 2, 4, rows, cols), BF16),
            pltpu.VMEM((2, 2, 4, rows, cols), BF16),
            pltpu.VMEM((2, 2, rows, cols), BF16),
            pltpu.VMEM((2, 2, rows, cols), BF16),
            pltpu.VMEM((4, rows, cols), BF16),
            pltpu.VMEM((3, rows, cols), BF16),
        ]
    wrows = features // 32
    return pl.pallas_call(
        backward_kernel,
        in_specs=[VMEMSPACE] * 2 + [ANYSPACE] * 3 + [VMEMSPACE] * 2 + [ANYSPACE] * 10,
        out_specs=[VMEMSPACE] * 6,
        out_shape=[jax.ShapeDtypeStruct(dim, F32) for dim in dims]
        + [
            jax.ShapeDtypeStruct(stats.shape, F32),
            jax.ShapeDtypeStruct((2, tok, features), F32),
            jax.ShapeDtypeStruct((4, wrows, 768), F32),
        ],
        scratch_shapes=bufs
        + [pltpu.VMEM(a.shape, a.dtype) for a in saved]
        + [
            pltpu.VMEM((length, NH * HEAD), BF16),
            pltpu.VMEM((length, 768), BF16),
            pltpu.VMEM((256, NH * TILE), BF16),
            pltpu.VMEM((256, NH * TILE), BF16),
            pltpu.VMEM((NH * TILE, NH * HEAD), BF16),
            pltpu.VMEM((NH * TILE, NH * HEAD), BF16),
            pltpu.VMEM((length, NH * HEAD), F32),
            pltpu.VMEM((length, NH * HEAD), F32),
            pltpu.VMEM((4, 2, tok, features), BF16),
            pltpu.VMEM((4, tok, features), BF16),
            pltpu.VMEM((4, tok, features), BF16),
            pltpu.VMEM((tok, features), BF16),
            pltpu.VMEM((2, tok, features), BF16),
            pltpu.VMEM((tok, features), BF16),
            pltpu.VMEM((2, 2, 8, wrows, 768), BF16),
            pltpu.VMEM((2, 4, wrows, 768), BF16),
            pltpu.VMEM((2, 4, wrows, 768), BF16),
            pltpu.VMEM((8, wrows, 768), BF16),
            pltpu.VMEM((8, wrows, 768), BF16),
            pltpu.VMEM((5,) + stats.shape, F32),
            pltpu.VMEM((5,) + stats.shape, F32),
            pltpu.SemaphoreType.DMA((90,)),
            pltpu.SemaphoreType.DMA((90,)),
            pltpu.SemaphoreType.DMA((14,)),
        ],
        compiler_params=pltpu.CompilerParams(
            collective_id=3, has_side_effects=True, vmem_limit_bytes=62 * 1024 * 1024
        ),
        name="backward_half",
    )(src, stats, *grads, rand, segq, *saved)


def head_layout(
    inputs, segments, rand_blocks, w_qkv, w_out, w_up, w_down, norm_gain, norm_bias, out_grad
):
    seqs, tok, features = inputs.shape
    seq = lax.axis_size("seq")
    t = lax.axis_index("seq")
    groups = seq // seqs
    my_seq, my_group = t // groups, lax.rem(t, groups)
    width = features // groups
    shard = w_qkv.reshape(w_qkv.shape[0], 3, groups, width)
    shard = lax.dynamic_index_in_dim(shard, my_group, 2, keepdims=False)
    shard = jnp.pad(shard, ((0, 0), (0, 0), (0, 256 - width))).reshape(w_qkv.shape[0], 768)
    steps = seq * tok // TILE
    rand = lax.dynamic_slice_in_dim(
        lax.dynamic_index_in_dim(rand_blocks, my_seq, 0, keepdims=False), my_group * NH, NH, 1
    )
    rand = rand.reshape(steps, TILE // BLOCK, NH, 3).transpose(0, 3, 2, 1)
    rand = jnp.broadcast_to(rand[..., None], rand.shape + (BLOCK,)).reshape(steps, 3, NH * TILE)
    seg = lax.dynamic_index_in_dim(segments, my_seq, 0, keepdims=False)
    segq = seg.reshape(steps, 1, TILE)
    wof, wuf, wdf, att_flat, otile, lse, segk, qn, kn, vn, qt, kt, xst, wgf = forward_half(
        inputs, shard, w_out, w_up, w_down, rand, segq
    )
    full_out = wof.reshape(features, features)
    full_up = wuf.reshape(features, -1)
    full_down = wdf.reshape(-1, features)
    tokens_flat = inputs.reshape(seqs * tok, features)
    resid_one = tokens_flat.astype(F32) + product(att_flat, full_out)
    hidden_one, normed_one, inv_one = norm_forward(resid_one, norm_gain[0], norm_bias[0])
    hidden_low = hidden_one.astype(BF16)
    pre_act = product(hidden_low, full_up)
    activated = gelu_value(pre_act).astype(BF16)
    resid_two = hidden_one + product(activated, full_down)
    result, normed_two, inv_two = norm_forward(resid_two, norm_gain[1], norm_bias[1])
    grad_rows = out_grad.reshape(seqs * tok, features).astype(F32)
    grad_resid_two, gain_two, shift_two = norm_backward(
        grad_rows, normed_two, inv_two, norm_gain[1]
    )
    grad_branch = grad_resid_two.astype(BF16)
    grad_down_w = product_tn(activated, grad_branch).astype(BF16)
    grad_pre = (product_nt(grad_branch, full_down) * gelu_slope(pre_act)).astype(BF16)
    grad_up_w = product_tn(hidden_low, grad_pre).astype(BF16)
    grad_hidden = grad_resid_two + product_nt(grad_pre, full_up)
    grad_resid_one, gain_one, shift_one = norm_backward(
        grad_hidden, normed_one, inv_one, norm_gain[0]
    )
    grad_mix = grad_resid_one.astype(BF16)
    grad_out_w = product_tn(att_flat, grad_mix).astype(BF16)
    grad_att = product_nt(grad_mix, full_out).astype(BF16)
    grad_att = grad_att.reshape(seqs, tok, groups, width).transpose(0, 2, 1, 3)
    src = grad_att.reshape(seq, tok, width)
    stats = jnp.stack([gain_one, gain_two, shift_one, shift_two])
    cut = lambda g: g.reshape(2, 2, 4, 2, g.shape[0] // 32, g.shape[1])
    out_sum, up_sum, down_sum, stats, ig, wq = backward_half(
        src, stats, [cut(grad_out_w), cut(grad_up_w), cut(grad_down_w)], rand, segq,
        (kn, vn, kt, segk, qn, qt, otile, lse, xst, wgf),
    )
    wq = wq.reshape(groups, features // 32, 3, 256)[..., :width].transpose(1, 2, 0, 3)
    mine = lax.axis_index("dp") * seq + t
    stats = lax.dynamic_slice_in_dim(stats, mine * (features // 32), features // 32, 1)
    return (
        result.astype(BF16).reshape(seqs, tok, features),
        ig + grad_resid_one.reshape(seqs, tok, features),
        wq.reshape(features // 32, 3 * features),
        out_sum,
        up_sum,
        down_sum,
        stats[:2],
        stats[2:],
    )


def solution(mesh):
    in_specs = (
        P("dp", "seq", None),
        P("dp", None),
        P("dp", None, None, None),
        P("dp", None),
        P("dp", None),
        P("dp", None),
        P("dp", None),
        P(),
        P(),
        P("dp", "seq", None),
    )
    out_specs = (
        P("dp", "seq", None),
        P("dp", "seq", None),
        P(("dp", "seq"), None),
        P(("dp", "seq"), None),
        P(("dp", "seq"), None),
        P(("dp", "seq"), None),
        P(None, ("dp", "seq")),
        P(None, ("dp", "seq")),
    )
    fits = mesh.shape["dp"] == 4 and mesh.shape["seq"] == 8
    return jax.shard_map(
        head_layout if fits else per_device, mesh=mesh, in_specs=in_specs, out_specs=out_specs, check_vma=False
    )
```

```python
import functools
import jax
import jax.numpy as jnp
import numpy as np
from jax import lax
from jax.experimental import pallas as pl
from jax.experimental.pallas import tpu as pltpu
from jax.sharding import PartitionSpec as P

H = 12
HEAD = 64
BLOCK = 64
R = 3
MICRO = 2


norm_eps = 1e-05
masked_score = -1e30
root_half = 0.7071067811865476
inv_root_two_pi = 0.3989422804014327


def padded(cells, sides, width):
    for axis, dim in sides:
        count = lax.axis_size(axis)
        ends = count - 1
        head = lax.slice_in_dim(cells, 0, width, axis=dim)
        tail = lax.slice_in_dim(cells, cells.shape[dim] - width, cells.shape[dim], axis=dim)
        cells = jnp.concatenate(
            [
                lax.ppermute(tail, axis, [(i, (i + 1) % count) for i in range(ends)]),
                cells,
                lax.ppermute(head, axis, [((i + 1) % count, i) for i in range(ends)]),
            ],
            axis=dim,
        )
    return cells


def from_root(x, axis, root):
    mine = lax.axis_index(axis) == root
    return lax.psum(jnp.where(mine, x, jnp.zeros_like(x)), axis)


def merged(x, axis, combine):
    everything = jax.tree.map(lambda part: lax.all_gather(part, axis), x)
    initial = jax.tree.map(lambda part: part[0], everything)

    def step(k, so_far):
        return combine(so_far, jax.tree.map(lambda part: part[k], everything))

    return lax.fori_loop(1, lax.axis_size(axis), step, initial)


def product(left_side, right_side):
    return jnp.dot(left_side, right_side, preferred_element_type=jnp.float32)


def product_tn(left_side, right_side):
    return lax.dot_general(
        left_side, right_side, (((0,), (0,)), ((), ())), preferred_element_type=jnp.float32
    )


def product_nt(left_side, right_side):
    return lax.dot_general(
        left_side, right_side, (((1,), (1,)), ((), ())), preferred_element_type=jnp.float32
    )


def gelu_value(pre_act):
    return 0.5 * pre_act * (1.0 + lax.erf(pre_act * root_half))


def gelu_slope(pre_act):
    return (
        0.5 * (1.0 + lax.erf(pre_act * root_half))
        + pre_act * jnp.exp(-0.5 * pre_act * pre_act) * inv_root_two_pi
    )


def norm_forward(residual, gain_row, shift_row):
    mean_row = jnp.mean(residual, axis=-1, keepdims=True)
    centred = residual - mean_row
    variance = jnp.mean(centred * centred, axis=-1, keepdims=True)
    inv_std = lax.rsqrt(variance + norm_eps)
    normed = centred * inv_std
    return (normed * gain_row + shift_row, normed, inv_std)


def norm_backward(grad_rows, normed, inv_std, gain_row):
    scaled = grad_rows * gain_row
    back_rows = inv_std * (
        scaled
        - jnp.mean(scaled, axis=-1, keepdims=True)
        - normed * jnp.mean(scaled * normed, axis=-1, keepdims=True)
    )
    return (back_rows, jnp.sum(grad_rows * normed, axis=0), jnp.sum(grad_rows, axis=0))


def merge_stats(first_pair, second_pair):
    joint_max = jnp.maximum(first_pair[0], second_pair[0])
    joint_sum = first_pair[1] * jnp.exp(first_pair[0] - joint_max) + second_pair[1] * jnp.exp(
        second_pair[0] - joint_max
    )
    return (joint_max, joint_sum)


def local_scores(query_heads, shared_keys, random_keys, shared_ok, random_ok, scale_factor):
    part_shared = jnp.einsum(
        "sbqhd,sbkhd->sbhqk", query_heads, shared_keys, preferred_element_type=jnp.float32
    )
    part_random = jnp.einsum(
        "sbqhd,sbhkd->sbhqk", query_heads, random_keys, preferred_element_type=jnp.float32
    )
    scores = jnp.concatenate([part_shared, part_random], axis=4) * scale_factor
    allowed = jnp.concatenate(
        [jnp.broadcast_to(shared_ok[:, :, None], part_shared.shape), random_ok], axis=4
    )
    return jnp.where(allowed, scores, masked_score)


def per_device(
    inputs, segments, rand_blocks, w_qkv, w_out, w_up, w_down, norm_gain, norm_bias, out_grad
):
    seq_total, tok_dev, features = inputs.shape
    devices = lax.axis_size("seq")
    my_index = lax.axis_index("seq")
    blocks_dev = tok_dev // BLOCK
    blocks_all = blocks_dev * devices
    entries = blocks_dev * H * R
    capacity = max(2, entries // devices + 1)
    per_micro = seq_total // MICRO
    glob_rows = 2 * BLOCK
    shared_count = 5 * BLOCK
    scale_factor = HEAD ** (-0.5)
    token_rows = per_micro * tok_dev
    owner_flag = (my_index == 0).astype(jnp.float32)
    row_global = my_index * tok_dev + jnp.arange(tok_dev, dtype=jnp.int32) < glob_rows
    window_index = np.arange(blocks_dev)[:, None] + np.arange(3)[None, :]
    win_blocks = (
        my_index * blocks_dev
        + jnp.arange(blocks_dev, dtype=jnp.int32)[:, None]
        + jnp.arange(-1, 2, dtype=jnp.int32)[None, :]
    )
    win_inside = (win_blocks >= 0) & (win_blocks < blocks_all)
    win_clipped = jnp.clip(win_blocks, 0, blocks_all - 1)
    entry_heads = jnp.arange(entries, dtype=jnp.int32) // R % H
    slot_ids = jnp.arange(capacity, dtype=jnp.int32)
    earlier = jnp.arange(entries)[None, :] < jnp.arange(entries)[:, None]
    seq_ids = jnp.arange(per_micro, dtype=jnp.int32)
    grad_qkv_w = jnp.zeros((features, 3 * features), jnp.float32)
    grad_out_w = jnp.zeros((features, features), jnp.float32)
    grad_up_w = jnp.zeros((features, w_up.shape[1]), jnp.float32)
    grad_down_w = jnp.zeros((w_down.shape[0] * lax.axis_size("dp"), features), jnp.float32)
    gain_acc = jnp.zeros((2, features), jnp.float32)
    shift_acc = jnp.zeros((2, features), jnp.float32)
    output_parts = []
    input_parts = []
    for micro_step in range(MICRO):
        start_seq = micro_step * per_micro
        tokens_in = inputs[start_seq : start_seq + per_micro]
        seg_micro = segments[start_seq : start_seq + per_micro]
        rand_micro = rand_blocks[start_seq : start_seq + per_micro]
        cotangent = out_grad[start_seq : start_seq + per_micro]
        full_qkv, full_out, full_up, full_down = (
            lax.all_gather(w_qkv, "dp", axis=0, tiled=True),
            lax.all_gather(w_out, "dp", axis=0, tiled=True),
            lax.all_gather(w_up, "dp", axis=0, tiled=True),
            lax.all_gather(w_down, "dp", axis=0, tiled=True),
        )
        tokens_flat = tokens_in.reshape(token_rows, features)
        qkv_rows = (
            product(tokens_flat, full_qkv)
            .astype(jnp.bfloat16)
            .reshape(per_micro, tok_dev, 3 * features)
        )
        queries = qkv_rows[..., :features]
        keyvals = qkv_rows[..., features:]
        extended = padded(keyvals, (("seq", 1),), BLOCK)
        global_block = from_root(qkv_rows[:, :glob_rows], "seq", 0)
        requests = rand_micro.reshape(per_micro, devices, entries)
        owners = requests // blocks_dev
        local_block = requests % blocks_dev
        same_owner = owners[:, :, :, None] == owners[:, :, None, :]
        slot_rank = jnp.sum(same_owner & earlier[None, None], axis=3)
        slot_hit = ((owners == my_index)[..., None] & (slot_rank[..., None] == slot_ids)).astype(
            jnp.int32
        )
        slot_live = jnp.sum(slot_hit, axis=2)
        slot_piece = jnp.sum(slot_hit * (local_block * H + entry_heads)[..., None], axis=2)
        piece_index = jnp.transpose(slot_piece, (1, 2, 0))
        live_mask = jnp.transpose(slot_live, (1, 2, 0))
        pieces = (
            keyvals.reshape(per_micro, blocks_dev, BLOCK, 2, H, HEAD)
            .transpose(0, 1, 4, 2, 3, 5)
            .reshape(per_micro, blocks_dev * H, BLOCK, 2 * HEAD)
        )
        outgoing = pieces[seq_ids[None, None, :], piece_index]
        outgoing = jnp.where(live_mask[..., None, None] > 0, outgoing, jnp.zeros((), jnp.bfloat16))
        outgoing = outgoing.reshape(devices * capacity, per_micro, BLOCK, 2 * HEAD)
        incoming = lax.all_to_all(outgoing, "seq", split_axis=0, concat_axis=0, tiled=True)
        my_owner = jnp.take(owners, my_index, axis=1)
        my_rank = jnp.take(slot_rank, my_index, axis=1)
        my_request = jnp.take(requests, my_index, axis=1)
        positions = my_owner * capacity + my_rank
        fetched = incoming[positions, seq_ids[:, None]].reshape(
            per_micro, blocks_dev, H, R, BLOCK, 2, HEAD
        )
        random_keys = fetched[..., 0, :].reshape(per_micro, blocks_dev, H, R * BLOCK, HEAD)
        random_vals = fetched[..., 1, :].reshape(per_micro, blocks_dev, H, R * BLOCK, HEAD)
        seg_blocks = seg_micro.reshape(per_micro, blocks_all, BLOCK)
        query_seg = lax.dynamic_slice_in_dim(seg_micro, my_index * tok_dev, tok_dev, 1).reshape(
            per_micro, blocks_dev, BLOCK
        )
        window_seg = seg_blocks[:, win_clipped].reshape(per_micro, blocks_dev, 3 * BLOCK)
        window_ok = (query_seg[..., :, None] == window_seg[:, :, None, :]) & jnp.repeat(
            win_inside, BLOCK, axis=1
        )[None, :, None, :]
        shared_ok = jnp.concatenate(
            [window_ok, jnp.ones((per_micro, blocks_dev, BLOCK, glob_rows), bool)], axis=3
        )
        random_seg = seg_blocks[seq_ids[:, None], my_request].reshape(
            per_micro, blocks_dev, H, R * BLOCK
        )
        random_ok = query_seg[:, :, None, :, None] == random_seg[:, :, :, None, :]
        ext_blocks = extended.reshape(per_micro, blocks_dev + 2, BLOCK, 2 * features)
        window_kv = ext_blocks[:, window_index].reshape(
            per_micro, blocks_dev, 3 * BLOCK, 2 * features
        )
        glob_kv = jnp.broadcast_to(
            global_block[:, None, :, features:], (per_micro, blocks_dev, glob_rows, 2 * features)
        )
        shared_kv = jnp.concatenate([window_kv, glob_kv], axis=2)
        shared_keys = shared_kv[..., :features].reshape(
            per_micro, blocks_dev, shared_count, H, HEAD
        )
        shared_vals = shared_kv[..., features:].reshape(
            per_micro, blocks_dev, shared_count, H, HEAD
        )
        query_heads = queries.reshape(per_micro, blocks_dev, BLOCK, H, HEAD)
        scores = local_scores(
            query_heads, shared_keys, random_keys, shared_ok, random_ok, scale_factor
        )
        row_max = jnp.max(scores, axis=4, keepdims=True)
        exp_terms = jnp.exp(scores - row_max)
        row_sum = jnp.sum(exp_terms, axis=4, keepdims=True)
        local_probs = exp_terms / row_sum
        log_norm = row_max + jnp.log(row_sum)
        local_weights = local_probs.astype(jnp.bfloat16)
        local_att = jnp.einsum(
            "sbhqk,sbkhd->sbqhd",
            local_weights[..., :shared_count],
            shared_vals,
            preferred_element_type=jnp.float32,
        )
        local_att = local_att + jnp.einsum(
            "sbhqk,sbhkd->sbqhd",
            local_weights[..., shared_count:],
            random_vals,
            preferred_element_type=jnp.float32,
        )
        local_att = local_att.reshape(per_micro, tok_dev, features)
        glob_query = global_block[..., :features].reshape(per_micro, glob_rows, H, HEAD)
        local_keys = keyvals[..., :features].reshape(per_micro, tok_dev, H, HEAD)
        local_vals = keyvals[..., features:].reshape(per_micro, tok_dev, H, HEAD)
        glob_scores = (
            jnp.einsum(
                "sqhd,skhd->shqk", glob_query, local_keys, preferred_element_type=jnp.float32
            )
            * scale_factor
        )
        part_max = jnp.max(glob_scores, axis=3)
        part_sum = jnp.sum(jnp.exp(glob_scores - part_max[..., None]), axis=3)
        glob_max, glob_sum = merged((part_max, part_sum), "seq", merge_stats)
        glob_lse = glob_max + jnp.log(glob_sum)
        glob_probs = jnp.exp(glob_scores - glob_lse[..., None])
        glob_weights = glob_probs.astype(jnp.bfloat16)
        glob_part = jnp.einsum(
            "shqk,skhd->sqhd", glob_weights, local_vals, preferred_element_type=jnp.float32
        ).reshape(per_micro, glob_rows, features)
        glob_out = lax.psum(glob_part, "seq")
        glob_full = jnp.concatenate(
            [glob_out, jnp.zeros((per_micro, tok_dev - glob_rows, features), jnp.float32)], axis=1
        )
        attention = jnp.where(row_global[None, :, None], glob_full, local_att).astype(jnp.bfloat16)
        att_flat = attention.reshape(token_rows, features)
        resid_one = tokens_flat.astype(jnp.float32) + product(att_flat, full_out)
        hidden_one, normed_one, inv_one = norm_forward(resid_one, norm_gain[0], norm_bias[0])
        hidden_low = hidden_one.astype(jnp.bfloat16)
        pre_act = product(hidden_low, full_up)
        activated = gelu_value(pre_act).astype(jnp.bfloat16)
        resid_two = hidden_one + product(activated, full_down)
        result, normed_two, inv_two = norm_forward(resid_two, norm_gain[1], norm_bias[1])
        output_parts.append(result.astype(jnp.bfloat16).reshape(per_micro, tok_dev, features))
        grad_rows = cotangent.reshape(token_rows, features).astype(jnp.float32)
        grad_resid_two, gain_two, shift_two = norm_backward(
            grad_rows, normed_two, inv_two, norm_gain[1]
        )
        grad_branch = grad_resid_two.astype(jnp.bfloat16)
        grad_down_w = grad_down_w + product_tn(activated, grad_branch)
        grad_pre = (product_nt(grad_branch, full_down) * gelu_slope(pre_act)).astype(jnp.bfloat16)
        grad_up_w = grad_up_w + product_tn(hidden_low, grad_pre)
        grad_hidden = grad_resid_two + product_nt(grad_pre, full_up)
        grad_resid_one, gain_one, shift_one = norm_backward(
            grad_hidden, normed_one, inv_one, norm_gain[0]
        )
        grad_mix = grad_resid_one.astype(jnp.bfloat16)
        grad_out_w = grad_out_w + product_tn(att_flat, grad_mix)
        grad_att = (
            product_nt(grad_mix, full_out)
            .astype(jnp.bfloat16)
            .reshape(per_micro, tok_dev, features)
        )
        gain_acc = gain_acc + jnp.stack([gain_one, gain_two])
        shift_acc = shift_acc + jnp.stack([shift_one, shift_two])
        grad_local = jnp.where(
            row_global[None, :, None], jnp.zeros((), jnp.bfloat16), grad_att
        ).reshape(per_micro, blocks_dev, BLOCK, H, HEAD)
        scores = local_scores(
            query_heads, shared_keys, random_keys, shared_ok, random_ok, scale_factor
        )
        local_probs = jnp.exp(scores - log_norm)
        local_weights = local_probs.astype(jnp.bfloat16)
        grad_prob = jnp.concatenate(
            [
                jnp.einsum(
                    "sbqhd,sbkhd->sbhqk",
                    grad_local,
                    shared_vals,
                    preferred_element_type=jnp.float32,
                ),
                jnp.einsum(
                    "sbqhd,sbhkd->sbhqk",
                    grad_local,
                    random_vals,
                    preferred_element_type=jnp.float32,
                ),
            ],
            axis=4,
        )
        row_delta = jnp.sum(local_probs * grad_prob, axis=4, keepdims=True)
        grad_score = (local_probs * (grad_prob - row_delta)).astype(jnp.bfloat16)
        grad_query = jnp.einsum(
            "sbhqk,sbkhd->sbqhd",
            grad_score[..., :shared_count],
            shared_keys,
            preferred_element_type=jnp.float32,
        )
        grad_query = (
            grad_query
            + jnp.einsum(
                "sbhqk,sbhkd->sbqhd",
                grad_score[..., shared_count:],
                random_keys,
                preferred_element_type=jnp.float32,
            )
        ) * scale_factor
        grad_key_shared = (
            jnp.einsum(
                "sbhqk,sbqhd->sbkhd",
                grad_score[..., :shared_count],
                query_heads,
                preferred_element_type=jnp.float32,
            )
            * scale_factor
        )
        grad_val_shared = jnp.einsum(
            "sbhqk,sbqhd->sbkhd",
            local_weights[..., :shared_count],
            grad_local,
            preferred_element_type=jnp.float32,
        )
        grad_key_random = (
            jnp.einsum(
                "sbhqk,sbqhd->sbhkd",
                grad_score[..., shared_count:],
                query_heads,
                preferred_element_type=jnp.float32,
            )
            * scale_factor
        )
        grad_val_random = jnp.einsum(
            "sbhqk,sbqhd->sbhkd",
            local_weights[..., shared_count:],
            grad_local,
            preferred_element_type=jnp.float32,
        )
        grad_shared = jnp.concatenate(
            [
                grad_key_shared.reshape(per_micro, blocks_dev, shared_count, features),
                grad_val_shared.reshape(per_micro, blocks_dev, shared_count, features),
            ],
            axis=3,
        )
        grad_window = grad_shared[:, :, : 3 * BLOCK].reshape(
            per_micro, blocks_dev, 3, BLOCK, 2 * features
        )
        ext_grad = jnp.zeros((per_micro, blocks_dev + 2, BLOCK, 2 * features), jnp.float32)
        for offset in range(3):
            ext_grad = ext_grad.at[:, offset : offset + blocks_dev].add(grad_window[:, :, offset])
        grad_glob_keys = jnp.sum(grad_shared[:, :, 3 * BLOCK :], axis=1)
        grad_random = jnp.stack([grad_key_random, grad_val_random], axis=4).reshape(
            per_micro, entries, BLOCK, 2 * HEAD
        )
        returned = (
            jnp.zeros((devices * capacity, per_micro, BLOCK, 2 * HEAD), jnp.float32)
            .at[positions, seq_ids[:, None]]
            .set(grad_random)
        )
        arrived = lax.all_to_all(
            returned.astype(jnp.bfloat16), "seq", split_axis=0, concat_axis=0, tiled=True
        ).astype(returned.dtype)
        arrived = arrived.reshape(devices, capacity, per_micro, BLOCK, 2 * HEAD) * live_mask[
            ..., None, None
        ].astype(jnp.float32)
        piece_grad = (
            jnp.zeros((per_micro, blocks_dev * H, BLOCK, 2 * HEAD), jnp.float32)
            .at[seq_ids[None, None, :], piece_index]
            .add(arrived)
        )
        piece_grad = (
            piece_grad.reshape(per_micro, blocks_dev, H, BLOCK, 2, HEAD)
            .transpose(0, 1, 3, 4, 2, 5)
            .reshape(per_micro, tok_dev, 2 * features)
        )
        rim_pair = jnp.concatenate([ext_grad[:, 0], ext_grad[:, blocks_dev + 1]], axis=1)
        rim_back = padded(rim_pair.astype(jnp.bfloat16), (("seq", 1),), BLOCK).astype(
            rim_pair.dtype
        )
        grad_kv = (
            ext_grad[:, 1 : blocks_dev + 1].reshape(per_micro, tok_dev, 2 * features) + piece_grad
        )
        grad_kv = grad_kv.at[:, :BLOCK].add(rim_back[:, :BLOCK])
        grad_kv = grad_kv.at[:, tok_dev - BLOCK :].add(rim_back[:, 3 * BLOCK :])
        grad_glob = from_root(grad_att[:, :glob_rows], "seq", 0)
        grad_glob_heads = grad_glob.reshape(per_micro, glob_rows, H, HEAD)
        glob_scores = (
            jnp.einsum(
                "sqhd,skhd->shqk", glob_query, local_keys, preferred_element_type=jnp.float32
            )
            * scale_factor
        )
        glob_probs = jnp.exp(glob_scores - glob_lse[..., None])
        glob_weights = glob_probs.astype(jnp.bfloat16)
        glob_grad_prob = jnp.einsum(
            "sqhd,skhd->shqk", grad_glob_heads, local_vals, preferred_element_type=jnp.float32
        )
        glob_delta = lax.psum(jnp.sum(glob_probs * glob_grad_prob, axis=3), "seq")
        glob_grad_score = (glob_probs * (glob_grad_prob - glob_delta[..., None])).astype(
            jnp.bfloat16
        )
        glob_grad_query = (
            jnp.einsum(
                "shqk,skhd->sqhd", glob_grad_score, local_keys, preferred_element_type=jnp.float32
            )
            * scale_factor
        )
        glob_grad_key = (
            jnp.einsum(
                "shqk,sqhd->skhd", glob_grad_score, glob_query, preferred_element_type=jnp.float32
            )
            * scale_factor
        )
        glob_grad_val = jnp.einsum(
            "shqk,sqhd->skhd", glob_weights, grad_glob_heads, preferred_element_type=jnp.float32
        )
        grad_kv = grad_kv + jnp.concatenate(
            [
                glob_grad_key.reshape(per_micro, tok_dev, features),
                glob_grad_val.reshape(per_micro, tok_dev, features),
            ],
            axis=2,
        )
        summed_query, summed_keys = lax.psum(
            (glob_grad_query.reshape(per_micro, glob_rows, features), grad_glob_keys), "seq"
        )
        grad_kv = grad_kv.at[:, :glob_rows].add(owner_flag * summed_keys)
        grad_queries = (
            grad_query.reshape(per_micro, tok_dev, features)
            .at[:, :glob_rows]
            .add(owner_flag * summed_query)
        )
        grad_qkv_rows = (
            jnp.concatenate([grad_queries, grad_kv], axis=2)
            .astype(jnp.bfloat16)
            .reshape(token_rows, 3 * features)
        )
        grad_qkv_w = grad_qkv_w + product_tn(tokens_flat, grad_qkv_rows)
        input_rows = grad_resid_one + product_nt(grad_qkv_rows, full_qkv)
        input_parts.append(input_rows.reshape(per_micro, tok_dev, features))
    summed = (
        lax.psum_scatter(grad_qkv_w, ("dp", "seq"), scatter_dimension=0, tiled=True),
        lax.psum_scatter(grad_out_w, ("dp", "seq"), scatter_dimension=0, tiled=True),
        lax.psum_scatter(grad_up_w, ("dp", "seq"), scatter_dimension=0, tiled=True),
        lax.psum_scatter(grad_down_w, ("dp", "seq"), scatter_dimension=0, tiled=True),
        lax.psum_scatter(gain_acc, ("dp", "seq"), scatter_dimension=1, tiled=True),
        lax.psum_scatter(shift_acc, ("dp", "seq"), scatter_dimension=1, tiled=True),
    )
    return (
        jnp.concatenate(output_parts, axis=0),
        jnp.concatenate(input_parts, axis=0),
        summed[0],
        summed[1],
        summed[2],
        summed[3],
        summed[4],
        summed[5],
    )


TILE = 128
NH = 3
CH = 256
LOG2E = 1.4426950408889634
SCALE2 = HEAD ** (-0.5) * LOG2E
NEG = -1e30
F32 = jnp.float32
BF16 = jnp.bfloat16


def nt(a, b):
    return lax.dot_general(a, b, (((1,), (1,)), ((), ())), preferred_element_type=F32)


def nn(a, b):
    return jnp.dot(a, b, preferred_element_type=F32)


MESH = pl.DeviceIdType.MESH
ANYSPACE = pl.BlockSpec(memory_space=pl.ANY)
VMEMSPACE = pl.BlockSpec(memory_space=pltpu.VMEM)


class Copies:
    def __init__(self, send, recv):
        self.send = send
        self.recv = recv
        self.used = 0

    def to(self, src, dst, device):
        index = self.used
        self.used += 1
        return pltpu.make_async_remote_copy(
            src_ref=src, dst_ref=dst, send_sem=self.send.at[index], recv_sem=self.recv.at[index],
            device_id=device, device_id_type=MESH,
        )


class Place:
    def __init__(self):
        self.d = lax.axis_index("dp")
        self.t = lax.axis_index("seq")
        self.x = lax.rem(self.d, 2)
        self.y = self.d // 2
        self.c = lax.rem(self.t, 2)
        self.z = self.t // 2
        self.half = self.z // 2
        self.xn = self.d + 1 - 2 * self.x
        self.yn = self.d + 2 - 4 * self.y
        self.diag = 3 - self.d
        self.pair_z = self.z + 1 - 2 * lax.rem(self.z, 2)
        self.across_x = (self.xn, self.t)
        self.across_y = (self.yn, self.t)
        self.partner = (self.d, self.t + 1 - 2 * self.c)

    def at_z(self, z):
        return (self.d, 2 * z + self.c)


def meet(devices):
    barrier = pltpu.get_barrier_semaphore()
    for device in devices:
        pl.semaphore_signal(barrier, inc=1, device_id=device, device_id_type=MESH)
    pl.semaphore_wait(barrier, len(devices))


def tile_tables(tile, rand_ref, segq_ref, blocks):
    wide = NH * TILE
    key = lax.broadcasted_iota(jnp.int32, (blocks, wide), 0)
    lane = lax.broadcasted_iota(jnp.int32, (blocks, wide), 1)
    query = tile * (TILE // BLOCK) + lax.rem(lane, TILE) // BLOCK
    near = (key - query) * (key - query) <= 1
    hits = near.astype(F32)
    for r in range(rand_ref.shape[1]):
        hits = hits + (rand_ref[tile, r : r + 1, :] == key).astype(F32)
    fixed = jnp.logical_or(query < 2, key < 2)
    count = jnp.where(query < 2, 0.0, hits) + fixed.astype(F32)
    on = jnp.where(count > 0.0, jnp.log2(jnp.maximum(count, 1.0)), NEG)
    off = jnp.where(fixed, 0.0, NEG)
    return on, off, segq_ref[tile]


def biased(s, mask, on, off, first_block):
    rows = []
    for j in range(s.shape[0] // BLOCK):
        kb = first_block + j
        m3 = jnp.concatenate([mask[BLOCK * j : BLOCK * (j + 1)]] * NH, axis=1)
        bias = jnp.where(m3, on[kb : kb + 1, :], off[kb : kb + 1, :])
        rows.append(s[BLOCK * j : BLOCK * (j + 1)] * SCALE2 + bias)
    return jnp.concatenate(rows, axis=0)


def fill_segments(segq, segk):
    steps = segq.shape[0]
    for i in range(steps):
        column = jnp.broadcast_to(segq[i].astype(F32), (8, TILE)).T[:, :1]
        segk[TILE * i : TILE * (i + 1), :] = jnp.broadcast_to(column, (TILE, TILE)).astype(jnp.int32)


def forward_tile(tile, rand, segq, segk, qt, kn, vt, q3, tbuf, att, otile, lse):
    length = kn.shape[0]
    chunks = length // CH
    here = pl.ds(pl.multiple_of(tile * TILE, TILE), TILE)
    on, off, seg = tile_tables(tile, rand, segq, length // BLOCK)
    for h in range(NH):
        q3[HEAD * h : HEAD * (h + 1), TILE * h : TILE * (h + 1)] = qt[
            HEAD * h : HEAD * (h + 1), here
        ]
    top = jnp.full((8, NH * TILE), NEG, F32)
    for j in range(chunks):
        rows = slice(CH * j, CH * (j + 1))
        s = nn(kn[rows, :], q3[...])
        t = biased(s, segk[rows, :] == seg, on, off, CH // BLOCK * j)
        tbuf[rows, :] = t
        top = jnp.maximum(top, jnp.max(t.reshape(CH // 8, 8, NH * TILE), axis=0))
    peak = jnp.max(top, axis=0, keepdims=True)
    total = jnp.zeros((8, NH * TILE), F32)
    out = jnp.zeros((256, NH * TILE), F32)
    for j in range(chunks):
        rows = slice(CH * j, CH * (j + 1))
        p = jnp.exp2(tbuf[rows, :] - peak)
        total = total + jnp.sum(p.reshape(CH // 8, 8, NH * TILE), axis=0)
        out = out + nn(vt[:, rows], p.astype(BF16))
    weight = jnp.sum(total, axis=0, keepdims=True)
    lse[tile] = peak + jnp.log2(weight)
    inv = 1.0 / weight
    heads = [
        out[HEAD * h : HEAD * (h + 1), TILE * h : TILE * (h + 1)] * inv[:, TILE * h : TILE * (h + 1)]
        for h in range(NH)
    ]
    merged = jnp.concatenate(heads, axis=0)
    otile[tile] = merged
    att[here, :] = merged.T.astype(BF16)


def unit_place(me, u):
    low = lax.rem(me.z, 2)
    return 2 * lax.rem(me.half + 1 + u // 2, 2) + lax.rem(low + 1 + u, 2)


def forward_kernel(*refs):
    (x, wg, wo, wu, wd, rand, segq), refs = refs[:7], refs[7:]
    outs, refs = refs[:14], refs[14:]
    wof, wuf, wdf, att_out, otile_o, lse_o, segk_o, qn_o, kn_o, vn_o, qt_o, kt_o, xst_o, wgf_o = outs
    (xs, wgf, bo, bu, bd, att, home, otile, lse, segk), refs = refs[:10], refs[10:]
    (qn, kn, vn, qt, kt, vt, xst, q3, tbuf), refs = refs[:9], refs[9:]
    send, recv, xsend, xrecv, local = refs
    me = Place()
    d, t, c, z = me.d, me.t, me.c, me.z
    mine, other = me.half, 1 - me.half
    is_middle = z == 1 + me.half
    tok = x.shape[1]
    length = xs.shape[0]
    steps = length // TILE
    per_unit = 2 * tok // TILE
    loads = [
        pltpu.make_async_copy(src, dst, local.at[i])
        for i, (src, dst) in enumerate(((wo, bo), (wu, bu), (wd, bd)))
    ]
    for load in loads:
        load.start()
    meet([me.across_x, me.across_y] + [(d, lax.rem(t + k, 8)) for k in range(1, 8)])
    cps = Copies(send, recv)
    sent = []

    def begin(*copies):
        for cp in copies:
            cp.start()
            sent.append(cp)

    def rows_of(index):
        return pl.ds(pl.multiple_of(index * tok, tok), tok)

    shard = wg.shape[0]
    wrows = lambda index, start, size: pl.ds(pl.multiple_of(index * shard + start, size), size)
    half = shard // 2
    top_half, low_half = pl.ds(0, half), pl.ds(half, half)
    my_top, my_low = wrows(d, 0, half), wrows(d, half, half)
    wg_x0 = cps.to(wg.at[top_half], wgf.at[my_top], me.across_x)
    wg_x1 = cps.to(wg.at[low_half], wgf.at[my_low], me.across_x)
    wg_y0 = cps.to(wg.at[low_half], wgf.at[my_low], me.across_y)
    wg_y1 = cps.to(wg.at[top_half], wgf.at[my_top], me.across_y)
    near = cps.to(x.at[mine], xs.at[rows_of(t)], me.at_z(me.pair_z))
    give = cps.to(x.at[mine], xs.at[rows_of(t)], me.partner)
    far = pltpu.make_async_remote_copy(
        src_ref=x.at[other], dst_ref=xs.at[rows_of(t)], send_sem=xsend.at[0],
        recv_sem=xrecv.at[lax.rem(z, 2)], device_id=me.at_z(2 - me.half), device_id_type=MESH,
    )
    begin(wg_x0, wg_y0, far, wg_x1, wg_y1, near, give)
    heavy = []
    for w, full in ((wo, wof), (wu, wuf), (wd, wdf)):
        rows = w.shape[0] // 2
        part = pl.ds(pl.multiple_of(c * rows, rows), rows)
        to_x = cps.to(w.at[part], full.at[d, part], me.across_x)
        to_y = cps.to(w.at[part], full.at[d, part], me.across_y)
        heavy.append((full, rows, part, to_x, to_y))
    xn_top, yn_low = wrows(me.xn, 0, half), wrows(me.yn, half, half)
    wg_dy = cps.to(wgf.at[xn_top], wgf.at[xn_top], me.across_y)
    wg_dx = cps.to(wgf.at[yn_low], wgf.at[yn_low], me.across_x)
    wg_x0.wait_recv()
    begin(wg_dy)
    wg_y0.wait_recv()
    begin(wg_dx)
    for full, rows, part, to_x, to_y in heavy[:2]:
        begin(to_x, to_y)

    xs[rows_of(t), :] = x[mine]
    wgf[wrows(d, 0, shard), :] = wg[...]
    q3[...] = jnp.zeros_like(q3)
    fill_segments(segq, segk)
    keeps = []
    for i, (load, buf, full) in enumerate(zip(loads, (bo, bu, bd), (wof, wuf, wdf))):
        load.wait()
        keep = pltpu.make_async_copy(buf, full.at[d], local.at[3 + i])
        keep.start()
        keeps.append(keep)

    def project(unit):
        rows = pl.ds(pl.multiple_of(unit * 2 * tok, 2 * tok), 2 * tok)
        both = nn(xs[rows, :], wgf[...])
        qf, kf, vf = both[:, :256], both[:, 256:512], both[:, 512:]
        qn[rows, :] = qf.astype(BF16)
        kn[rows, :] = kf.astype(BF16)
        vn[rows, :] = vf.astype(BF16)
        qt[:, rows] = qf.T.astype(BF16)
        kt[:, rows] = kf.T.astype(BF16)
        vt[:, rows] = vf.T.astype(BF16)
        xst[:, rows] = xs[rows, :].astype(F32).T.astype(BF16)

    wg_x1.wait_recv()
    wg_y1.wait_recv()
    wg_dy.wait_recv()
    wg_dx.wait_recv()
    give.wait_recv()
    near.wait_recv()
    near_rows = rows_of(2 * me.pair_z + c)
    pass_near = cps.to(xs.at[near_rows], xs.at[near_rows], me.partner)
    begin(pass_near)
    relays, onwards = [], []
    for j in range(2):
        src_rows = rows_of(2 * (2 * other + j) + c)
        relays.append(
            pltpu.make_async_remote_copy(
                src_ref=xs.at[src_rows], dst_ref=xs.at[src_rows], send_sem=xsend.at[1 + j],
                recv_sem=xrecv.at[j], device_id=me.at_z(me.pair_z), device_id_type=MESH,
            )
        )
        onwards.append(cps.to(xs.at[src_rows], xs.at[src_rows], me.partner))

    def forward_x(j):
        relays[j].wait_recv()
        pl.when(is_middle)(relays[j].start)
        begin(onwards[j])

    tail = []
    for full, rows, part, to_x, to_y in heavy:
        quarter = rows // 2
        lo = pl.ds(pl.multiple_of(c * rows, quarter), quarter)
        hi = pl.ds(pl.multiple_of(c * rows + quarter, quarter), quarter)
        tail.append(
            (
                to_x, to_y,
                cps.to(full.at[me.xn, lo], full.at[me.xn, lo], me.across_y),
                cps.to(full.at[me.xn, part], full.at[me.xn, part], me.partner),
                cps.to(full.at[me.yn, hi], full.at[me.yn, hi], me.across_x),
                cps.to(full.at[me.yn, part], full.at[me.yn, part], me.partner),
                cps.to(full.at[me.diag, part], full.at[me.diag, part], me.partner),
            )
        )

    def relay_weights(k):
        to_x, to_y, dy, px, dx, py, pd = tail[k]
        to_x.wait_recv()
        begin(dy, px)
        to_y.wait_recv()
        begin(dx, py)

    def relay_diag(k):
        to_x, to_y, dy, px, dx, py, pd = tail[k]
        dy.wait_recv()
        dx.wait_recv()
        begin(pd)

    def arrive(k):
        if k == 0:
            forward_x(0)
            relay_weights(0)
            begin(heavy[2][3], heavy[2][4])
        if k == 1:
            forward_x(1)
            pass_near.wait_recv()
        if k == 2:
            onwards[0].wait_recv()
        if k == 3:
            onwards[1].wait_recv()

    def project_step(k, carry):
        for i in range(4):
            pl.when(k == i)(functools.partial(arrive, i))
        unit = jnp.where(k < 2, 2 * mine + lax.rem(lax.rem(z, 2) + k, 2), 2 * other + k - 2)
        project(unit)
        return carry

    lax.fori_loop(0, 4, project_step, 0)
    saves = [
        pltpu.make_async_copy(src, dst, local.at[6 + i])
        for i, (src, dst) in enumerate(
            ((segk, segk_o), (qn, qn_o), (kn, kn_o), (vn, vn_o), (qt, qt_o), (kt, kt_o), (xst, xst_o), (wgf, wgf_o))
        )
    ]
    for save in saves:
        save.start()

    homes = []
    for u in range(4):
        unit = unit_place(me, u)
        for o in range(1 if u == 3 else 0, 2):
            to = 2 * unit + (c if o == 0 else 1 - c)
            homes.append((u, cps.to(att.at[rows_of(to)], home.at[t], (d, to))))

    def send_home(u):
        for v, move in homes:
            if u == v:
                move.start()

    def between(i):
        if i == 2:
            relay_weights(1)
        if i == per_unit:
            send_home(0)
        if i == per_unit + 1:
            relay_diag(0)
        if i == 2 * per_unit:
            send_home(1)
        if i == 3 * per_unit:
            send_home(2)
        if i == 3 * per_unit + 1:
            relay_weights(2)

    def tile_step(i, carry):
        for point in (2, per_unit, per_unit + 1, 2 * per_unit, 3 * per_unit, 3 * per_unit + 1):
            pl.when(i == point)(functools.partial(between, point))
        tile = unit_place(me, i // per_unit) * per_unit + lax.rem(i, per_unit)
        forward_tile(tile, rand, segq, segk, qt, kn, vt, q3, tbuf, att, otile, lse)
        return carry

    lax.fori_loop(0, steps, tile_step, 0)
    send_home(3)
    last = [
        pltpu.make_async_copy(src, dst, local.at[14 + i])
        for i, (src, dst) in enumerate(((otile, otile_o), (lse, lse_o)))
    ]
    for save in last:
        save.start()
    home[t] = att[rows_of(t), :]
    for u, move in homes:
        move.wait()
    for s in range(2):
        pieces = [home[4 * s + g].astype(F32) for g in range(4)]
        att_out[tok * s : tok * (s + 1), :] = jnp.concatenate(pieces, axis=1).astype(BF16)
    relay_diag(1)
    relay_diag(2)
    for to_x, to_y, dy, px, dx, py, pd in tail:
        px.wait_recv()
        py.wait_recv()
        pd.wait_recv()
    for cp in sent:
        cp.wait_send()

    @pl.when(is_middle)
    def _():
        for relay in relays:
            relay.wait_send()

    for copy in keeps + saves + last:
        copy.wait()


def forward_half(x, wg, wo, wu, wd, rand, segq):
    dp = lax.axis_size("dp")
    seq = lax.axis_size("seq")
    tok, features = x.shape[1:]
    length = seq * tok
    steps = length // TILE
    nat, tra = (length, 256), (256, length)
    stacked = lambda w: jax.ShapeDtypeStruct((dp,) + w.shape, BF16)
    low = lambda *shape: jax.ShapeDtypeStruct(shape, BF16)
    full = lambda *shape: jax.ShapeDtypeStruct(shape, F32)
    return pl.pallas_call(
        forward_kernel,
        in_specs=[VMEMSPACE] * 2 + [ANYSPACE] * 3 + [VMEMSPACE] * 2,
        out_specs=[ANYSPACE] * 3 + [VMEMSPACE] + [ANYSPACE] * 10,
        out_shape=[
            stacked(wo), stacked(wu), stacked(wd), low(2 * tok, features),
            full(steps, NH * HEAD, TILE), full(steps, 1, NH * TILE),
            jax.ShapeDtypeStruct((length, TILE), jnp.int32),
            low(*nat), low(*nat), low(*nat), low(*tra), low(*tra),
            low(features, length), low(features, 768),
        ],
        scratch_shapes=[
            pltpu.VMEM((length, features), BF16),
            pltpu.VMEM((features, 768), BF16),
            pltpu.VMEM(wo.shape, BF16),
            pltpu.VMEM(wu.shape, BF16),
            pltpu.VMEM(wd.shape, BF16),
            pltpu.VMEM((length, NH * HEAD), BF16),
            pltpu.VMEM((seq, tok, NH * HEAD), BF16),
            pltpu.VMEM((steps, NH * HEAD, TILE), F32),
            pltpu.VMEM((steps, 1, NH * TILE), F32),
            pltpu.VMEM((length, TILE), jnp.int32),
            pltpu.VMEM(nat, BF16),
            pltpu.VMEM(nat, BF16),
            pltpu.VMEM(nat, BF16),
            pltpu.VMEM(tra, BF16),
            pltpu.VMEM(tra, BF16),
            pltpu.VMEM(tra, BF16),
            pltpu.VMEM((features, length), BF16),
            pltpu.VMEM((256, NH * TILE), BF16),
            pltpu.VMEM((length, NH * TILE), F32),
            pltpu.SemaphoreType.DMA((90,)),
            pltpu.SemaphoreType.DMA((90,)),
            pltpu.SemaphoreType.DMA((3,)),
            pltpu.SemaphoreType.DMA((2,)),
            pltpu.SemaphoreType.DMA((16,)),
        ],
        compiler_params=pltpu.CompilerParams(
            collective_id=0, has_side_effects=True, vmem_limit_bytes=62 * 1024 * 1024
        ),
        name="forward_half",
    )(x, wg, wo, wu, wd, rand, segq)


def each(count, body):
    def run(i, carry):
        body(i)
        return carry

    lax.fori_loop(0, count, run, 0)


def plus(a, b):
    return a.astype(F32) + b.astype(F32)


def backward_tile(
    tile, dat, qn, qt, otile, lse, rand, segq, segk, kn, vn, kt, dqkv, q3t, d3t, q3, d3, dk, dv
):
    chunks = kn.shape[0] // CH
    on, off, seg = tile_tables(tile, rand, segq, kn.shape[0] // BLOCK)
    here = pl.ds(pl.multiple_of(tile * TILE, TILE), TILE)
    dat_f = dat[here, :].astype(F32)
    dat_t = dat_f.T
    lane = lax.broadcasted_iota(jnp.int32, (TILE, NH * HEAD), 1) // HEAD
    qblk = qn[here, : NH * HEAD].astype(F32)
    delta = []
    for h in range(NH):
        hr = slice(HEAD * h, HEAD * (h + 1))
        hc = slice(TILE * h, TILE * (h + 1))
        q3t[hr, hc] = qt[hr, here]
        d3t[hr, hc] = dat_t[hr].astype(BF16)
        q3[hc, :] = jnp.where(lane == h, qblk, 0.0).astype(BF16)
        d3[hc, :] = jnp.where(lane == h, dat_f, 0.0).astype(BF16)
        delta.append(jnp.sum(dat_t[hr] * otile[tile, hr, :], axis=0, keepdims=True))
    delta = jnp.concatenate(delta, axis=1)
    norm = lse[tile]
    dq = jnp.zeros((256, NH * TILE), F32)
    for j in range(chunks):
        rows = slice(CH * j, CH * (j + 1))
        s = nn(kn[rows, :], q3t[...])
        dp = nn(vn[rows, :], d3t[...])
        t = biased(s, segk[rows, :] == seg, on, off, CH // BLOCK * j)
        p = jnp.exp2(t - norm)
        ds = (p * (dp - delta)).astype(BF16)
        dv[rows, :] += nn(p.astype(BF16), d3[...])
        dk[rows, :] += nn(ds, q3[...])
        dq = dq + nn(kt[:, rows], ds)
    heads = [dq[HEAD * h : HEAD * (h + 1), TILE * h : TILE * (h + 1)] for h in range(NH)]
    merged = jnp.concatenate(heads, axis=0).T * HEAD ** (-0.5)
    dqkv[here, : NH * HEAD] = merged.astype(BF16)


def backward_kernel(*refs):
    (src, stats, g0, g1, g2), refs = refs[:5], refs[5:]
    (rand, segq), refs = refs[:2], refs[2:]
    saved, refs = refs[:10], refs[10:]
    (o0, o1, o2, stats_out, ig, wq), refs = refs[:6], refs[6:]
    bufs, refs = refs[:18], refs[18:]
    held, refs = refs[:10], refs[10:]
    kn, vn, kt, segk, qn, qt, otile, lse, xst, wg = held
    (dat, dqkv, q3t, d3t, q3, d3, dk, dv), refs = refs[:8], refs[8:]
    (part, own_p, rp, ra_p, rb_p, ro, dwg, wb1, wb2, wc, wr), refs = refs[:11], refs[11:]
    nsend, nrecv, send, recv, local = refs
    me = Place()
    c, z, x, y, t = me.c, me.z, me.x, me.y, me.t
    mine, other = me.half, 1 - me.half
    is_middle = z == 1 + me.half
    is_outer = z != 1 + me.half
    z_step = [lax.rem(z + k, 4) for k in (1, 2, 3)]
    tok = src.shape[1]
    loads = [
        pltpu.make_async_copy(from_hbm, to_vmem, local.at[4 + i])
        for i, (from_hbm, to_vmem) in enumerate(zip(saved, held))
    ]
    for load in loads:
        load.start()
    meet([me.across_x, me.across_y] + [(me.d, lax.rem(t + k, 8)) for k in range(1, 8)])
    cps = Copies(send, recv)

    def rows_of(index):
        return pl.ds(pl.multiple_of(index * tok, tok), tok)

    dat_moves = []
    for u in range(4):
        place = unit_place(me, 3 - u)
        for o in range(1 if u == 0 else 0, 2):
            to = 2 * place + (c if o == 0 else 1 - c)
            dat_moves.append((u, cps.to(src.at[to], dat.at[rows_of(t)], (me.d, to))))
    for u, move in dat_moves:
        move.start()
    keep = pltpu.make_async_copy(src.at[t], dat.at[rows_of(t)], local.at[3])
    keep.start()

    works = []
    for i, (g, o) in enumerate(((g2, o2), (g1, o1), (g0, o0))):
        own, ra, rb1, rb2, rc, rd = bufs[6 * i : 6 * i + 6]
        swap_core = cps.to(g.at[:, :, :, 1 - c], ra, me.partner)
        swap_core.start()
        load = pltpu.make_async_copy(g.at[:, :, :, c], own, local.at[i])
        load.start()
        moves = (
            swap_core,
            load,
            cps.to(own.at[:, 1 - x, 0:2], rb1, me.across_x),
            cps.to(own.at[1 - y, :, 2:4], rb2, me.across_y),
            cps.to(rb1.at[1 - y], rc.at[0:2], me.across_y),
            cps.to(rb2.at[1 - x], rc.at[2:4], me.across_x),
            [cps.to(rc.at[k], rd.at[j], me.at_z(k)) for j, k in enumerate(z_step)],
        )
        works.append(((o, own, ra, rb1, rb2, rc, rd), moves))
    stat_to = [me.partner, me.across_x, me.across_y, me.at_z(me.pair_z), me.at_z(lax.rem(z + 2, 4))]
    stat_all = [cps.to(nsend.at[k], nrecv.at[k], stat_to[k]) for k in range(5)]

    def stat_step(k):
        if k == 0:
            nsend[0] = stats[...]
        else:
            stat_all[k - 1].wait_recv()
            nsend[k] = nsend[k - 1] + nrecv[k - 1]
        stat_all[k].start()

    sent = []

    def begin(*copies):
        for cp in copies:
            cp.start()
            sent.append(cp)

    def stage_a(work):
        (o, own, ra, rb1, rb2, rc, rd), (swap_core, load, bx, by, cy, cx, ds) = work
        load.wait()
        swap_core.wait_recv()

        def fold(i):
            yy, xx, zz = i // 8, lax.rem(i // 4, 2), lax.rem(i, 4)
            own[yy, xx, zz] = plus(own[yy, xx, zz], ra[yy, xx, zz]).astype(BF16)

        each(16, fold)

    def cross(work):
        begin(work[1][2], work[1][3])

    def stage_b(work):
        (o, own, ra, rb1, rb2, rc, rd), (swap_core, load, bx, by, cy, cx, ds) = work
        bx.wait_recv()

        def fold_x(i):
            yy, zz = i // 2, lax.rem(i, 2)
            rb1[yy, zz] = plus(own[yy, x, zz], rb1[yy, zz]).astype(BF16)

        each(4, fold_x)
        begin(cy)
        by.wait_recv()

        def fold_y(i):
            xx, zz = i // 2, lax.rem(i, 2)
            rb2[xx, zz] = plus(own[y, xx, 2 + zz], rb2[xx, zz]).astype(BF16)

        each(4, fold_y)
        begin(cx)

    def stage_c(work):
        (o, own, ra, rb1, rb2, rc, rd), (swap_core, load, bx, by, cy, cx, ds) = work
        cy.wait_recv()
        cx.wait_recv()
        for zz in range(2):
            rc[zz] = plus(rb1[y, zz], rc[zz]).astype(BF16)
            rc[2 + zz] = plus(rb2[x, zz], rc[2 + zz]).astype(BF16)
        begin(*ds)

    def stage_d(work):
        (o, own, ra, rb1, rb2, rc, rd), (swap_core, load, bx, by, cy, cx, ds) = work
        for cp in ds:
            cp.wait_recv()
        o[...] = plus(rc[z], rd[0]) + plus(rd[1], rd[2])

    q3t[...] = jnp.zeros_like(q3t)
    d3t[...] = jnp.zeros_like(d3t)
    dk[...] = jnp.zeros_like(dk)
    dv[...] = jnp.zeros_like(dv)
    gap = jnp.zeros((dqkv.shape[0], 256 - NH * HEAD), BF16)
    for g in range(3):
        dqkv[:, 256 * g + NH * HEAD : 256 * (g + 1)] = gap
    stat_step(0)
    for load in loads[:8]:
        load.wait()
    keep.wait()
    per_unit = 2 * tok // TILE
    steps = dqkv.shape[0] // TILE

    def unit_arrives(u):
        for v, move in dat_moves:
            if u == v:
                move.wait_recv()

    def step_one():
        stage_a(works[0])
        cross(works[0])

    def step_two():
        stage_a(works[1])
        stat_step(1)

    def step_seven():
        stage_b(works[0])
        cross(works[1])
        cross(works[2])

    events = {
        1: [step_one],
        2: [step_two],
        4: [functools.partial(stage_a, works[2]), functools.partial(stat_step, 2)],
        7: [step_seven],
        8: [functools.partial(stat_step, 3)],
        10: [functools.partial(stage_c, works[0])],
    }
    for u in range(4):
        events.setdefault(u * per_unit, []).append(functools.partial(unit_arrives, u))

    def tile_step(i, carry):
        for point, actions in sorted(events.items()):

            @pl.when(i == point)
            def _():
                for action in actions:
                    action()

        tile = unit_place(me, 3 - i // per_unit) * per_unit + lax.rem(i, per_unit)
        backward_tile(
            tile, dat, qn, qt, otile, lse, rand, segq, segk, kn, vn, kt, dqkv,
            q3t, d3t, q3, d3, dk, dv,
        )
        return carry

    lax.fori_loop(0, steps, tile_step, 0)
    stat_step(4)
    loads[9].wait()

    dqkv[:, 256 : 256 + NH * HEAD] = (dk[...] * HEAD ** (-0.5)).astype(BF16)
    dqkv[:, 512 : 512 + NH * HEAD] = dv[...].astype(BF16)
    order = [2 * other, 2 * other + 1, me.pair_z, z]
    cores = []
    for zz in order:
        rows = pl.ds(pl.multiple_of(zz * 2 * tok, 2 * tok), 2 * tok)
        grad = nt(dqkv[rows, :], wg[...]).astype(BF16)
        part[zz, 0] = grad[:tok]
        part[zz, 1] = grad[tok:]
        core = cps.to(part.at[zz, 1 - c], rp.at[zz], me.partner)
        begin(core)
        cores.append(core)
    stage_b(works[1])
    stage_b(works[2])

    up = [cps.to(own_p.at[2 * other + j], rb_p.at[j], me.at_z(me.pair_z)) for j in range(2)]
    near = cps.to(own_p.at[me.pair_z], ra_p, me.at_z(me.pair_z))
    for k, zz in enumerate(order):
        cores[k].wait_recv()
        own_p[zz] = plus(part[zz, c], rp[zz]).astype(BF16)
        if k < 2:
            pl.when(is_outer)(up[k].start)
        if k == 2:
            begin(near)
    loads[8].wait()
    half_rows = xst.shape[0] // 2
    for yy in range(2):
        grad = nn(xst[half_rows * yy : half_rows * (yy + 1), :], dqkv[...]).astype(BF16)
        dwg[yy] = grad.reshape(dwg.shape[1:])
    bx = cps.to(dwg.at[:, 1 - x, 0:4], wb1, me.across_x)
    by = cps.to(dwg.at[1 - y, :, 4:8], wb2, me.across_y)
    begin(bx, by)
    down_send, down_recv = cps.used, cps.used
    cps.used += 2
    down = [
        pltpu.make_async_remote_copy(
            src_ref=own_p.at[2 * other + j], dst_ref=ro, send_sem=send.at[down_send + j],
            recv_sem=recv.at[down_recv], device_id=me.at_z(2 * other + j), device_id_type=MESH,
        )
        for j in range(2)
    ]

    @pl.when(is_middle)
    def _():
        for j in range(2):
            up[j].wait_recv()
            own_p[2 * other + j] = plus(own_p[2 * other + j], rb_p[j]).astype(BF16)
            down[j].start()

    stage_c(works[1])
    stage_c(works[2])
    bx.wait_recv()

    def fold_x(i):
        yy, tt = i // 4, lax.rem(i, 4)
        wb1[yy, tt] = plus(dwg[yy, x, tt], wb1[yy, tt]).astype(BF16)

    each(8, fold_x)
    cy = cps.to(wb1.at[1 - y], wc.at[0:4], me.across_y)
    begin(cy)
    by.wait_recv()

    def fold_y(i):
        xx, tt = i // 4, lax.rem(i, 4)
        wb2[xx, tt] = plus(dwg[y, xx, 4 + tt], wb2[xx, tt]).astype(BF16)

    each(8, fold_y)
    cx = cps.to(wb2.at[1 - x], wc.at[4:8], me.across_x)
    begin(cx)
    stat_all[-1].wait_recv()
    stats_out[...] = nsend[4] + nrecv[4]
    cy.wait_recv()
    cx.wait_recv()

    def fold_c(i):
        wc[i] = plus(wb1[y, i], wc[i]).astype(BF16)
        wc[4 + i] = plus(wb2[x, i], wc[4 + i]).astype(BF16)

    each(4, fold_c)
    moves = []
    for k in range(1, 8):
        peer = lax.rem(t + k, 8)
        moves.append(cps.to(wc.at[peer], wr.at[t], (me.d, peer)))
    begin(*moves)
    near.wait_recv()
    ig[mine] = plus(own_p[z], ra_p[...])
    down[0].wait_recv()
    ig[other] = ro[...].astype(F32)
    for work in works:
        stage_d(work)
    wr[t] = wc[t]
    for move in moves:
        move.wait_recv()
    for g in range(4):
        wq[g] = plus(wr[g], wr[4 + g])
    for cp in sent + stat_all + [move for u, move in dat_moves] + [moves[0] for refs, moves in works]:
        cp.wait_send()

    @pl.when(is_outer)
    def _():
        for cp in up:
            cp.wait_send()

    @pl.when(is_middle)
    def _():
        for cp in down:
            cp.wait_send()


def backward_half(src, stats, grads, rand, segq, saved):
    dims = [g.shape[-2:] for g in grads]
    tok = src.shape[1]
    features, length = saved[8].shape
    bufs = []
    for rows, cols in dims[::-1]:
        bufs += [
            pltpu.VMEM((2, 2, 4, rows, cols), BF16),
            pltpu.VMEM((2, 2, 4, rows, cols), BF16),
            pltpu.VMEM((2, 2, rows, cols), BF16),
            pltpu.VMEM((2, 2, rows, cols), BF16),
            pltpu.VMEM((4, rows, cols), BF16),
            pltpu.VMEM((3, rows, cols), BF16),
        ]
    wrows = features // 32
    return pl.pallas_call(
        backward_kernel,
        in_specs=[VMEMSPACE] * 2 + [ANYSPACE] * 3 + [VMEMSPACE] * 2 + [ANYSPACE] * 10,
        out_specs=[VMEMSPACE] * 6,
        out_shape=[jax.ShapeDtypeStruct(dim, F32) for dim in dims]
        + [
            jax.ShapeDtypeStruct(stats.shape, F32),
            jax.ShapeDtypeStruct((2, tok, features), F32),
            jax.ShapeDtypeStruct((4, wrows, 768), F32),
        ],
        scratch_shapes=bufs
        + [pltpu.VMEM(a.shape, a.dtype) for a in saved]
        + [
            pltpu.VMEM((length, NH * HEAD), BF16),
            pltpu.VMEM((length, 768), BF16),
            pltpu.VMEM((256, NH * TILE), BF16),
            pltpu.VMEM((256, NH * TILE), BF16),
            pltpu.VMEM((NH * TILE, NH * HEAD), BF16),
            pltpu.VMEM((NH * TILE, NH * HEAD), BF16),
            pltpu.VMEM((length, NH * HEAD), F32),
            pltpu.VMEM((length, NH * HEAD), F32),
            pltpu.VMEM((4, 2, tok, features), BF16),
            pltpu.VMEM((4, tok, features), BF16),
            pltpu.VMEM((4, tok, features), BF16),
            pltpu.VMEM((tok, features), BF16),
            pltpu.VMEM((2, tok, features), BF16),
            pltpu.VMEM((tok, features), BF16),
            pltpu.VMEM((2, 2, 8, wrows, 768), BF16),
            pltpu.VMEM((2, 4, wrows, 768), BF16),
            pltpu.VMEM((2, 4, wrows, 768), BF16),
            pltpu.VMEM((8, wrows, 768), BF16),
            pltpu.VMEM((8, wrows, 768), BF16),
            pltpu.VMEM((5,) + stats.shape, F32),
            pltpu.VMEM((5,) + stats.shape, F32),
            pltpu.SemaphoreType.DMA((90,)),
            pltpu.SemaphoreType.DMA((90,)),
            pltpu.SemaphoreType.DMA((14,)),
        ],
        compiler_params=pltpu.CompilerParams(
            collective_id=3, has_side_effects=True, vmem_limit_bytes=62 * 1024 * 1024
        ),
        name="backward_half",
    )(src, stats, *grads, rand, segq, *saved)


def head_layout(
    inputs, segments, rand_blocks, w_qkv, w_out, w_up, w_down, norm_gain, norm_bias, out_grad
):
    seqs, tok, features = inputs.shape
    seq = lax.axis_size("seq")
    t = lax.axis_index("seq")
    groups = seq // seqs
    my_seq, my_group = t // groups, lax.rem(t, groups)
    width = features // groups
    shard = w_qkv.reshape(w_qkv.shape[0], 3, groups, width)
    shard = lax.dynamic_index_in_dim(shard, my_group, 2, keepdims=False)
    shard = jnp.pad(shard, ((0, 0), (0, 0), (0, 256 - width))).reshape(w_qkv.shape[0], 768)
    steps = seq * tok // TILE
    rand = lax.dynamic_slice_in_dim(
        lax.dynamic_index_in_dim(rand_blocks, my_seq, 0, keepdims=False), my_group * NH, NH, 1
    )
    rand = rand.reshape(steps, TILE // BLOCK, NH, 3).transpose(0, 3, 2, 1)
    rand = jnp.broadcast_to(rand[..., None], rand.shape + (BLOCK,)).reshape(steps, 3, NH * TILE)
    seg = lax.dynamic_index_in_dim(segments, my_seq, 0, keepdims=False)
    segq = seg.reshape(steps, 1, TILE)
    wof, wuf, wdf, att_flat, otile, lse, segk, qn, kn, vn, qt, kt, xst, wgf = forward_half(
        inputs, shard, w_out, w_up, w_down, rand, segq
    )
    full_out = wof.reshape(features, features)
    full_up = wuf.reshape(features, -1)
    full_down = wdf.reshape(-1, features)
    tokens_flat = inputs.reshape(seqs * tok, features)
    resid_one = tokens_flat.astype(F32) + product(att_flat, full_out)
    hidden_one, normed_one, inv_one = norm_forward(resid_one, norm_gain[0], norm_bias[0])
    hidden_low = hidden_one.astype(BF16)
    pre_act = product(hidden_low, full_up)
    activated = gelu_value(pre_act).astype(BF16)
    resid_two = hidden_one + product(activated, full_down)
    result, normed_two, inv_two = norm_forward(resid_two, norm_gain[1], norm_bias[1])
    grad_rows = out_grad.reshape(seqs * tok, features).astype(F32)
    grad_resid_two, gain_two, shift_two = norm_backward(
        grad_rows, normed_two, inv_two, norm_gain[1]
    )
    grad_branch = grad_resid_two.astype(BF16)
    grad_down_w = product_tn(activated, grad_branch).astype(BF16)
    grad_pre = (product_nt(grad_branch, full_down) * gelu_slope(pre_act)).astype(BF16)
    grad_up_w = product_tn(hidden_low, grad_pre).astype(BF16)
    grad_hidden = grad_resid_two + product_nt(grad_pre, full_up)
    grad_resid_one, gain_one, shift_one = norm_backward(
        grad_hidden, normed_one, inv_one, norm_gain[0]
    )
    grad_mix = grad_resid_one.astype(BF16)
    grad_out_w = product_tn(att_flat, grad_mix).astype(BF16)
    grad_att = product_nt(grad_mix, full_out).astype(BF16)
    grad_att = grad_att.reshape(seqs, tok, groups, width).transpose(0, 2, 1, 3)
    src = grad_att.reshape(seq, tok, width)
    stats = jnp.stack([gain_one, gain_two, shift_one, shift_two])
    cut = lambda g: g.reshape(2, 2, 4, 2, g.shape[0] // 32, g.shape[1])
    out_sum, up_sum, down_sum, stats, ig, wq = backward_half(
        src, stats, [cut(grad_out_w), cut(grad_up_w), cut(grad_down_w)], rand, segq,
        (kn, vn, kt, segk, qn, qt, otile, lse, xst, wgf),
    )
    wq = wq.reshape(groups, features // 32, 3, 256)[..., :width].transpose(1, 2, 0, 3)
    mine = lax.axis_index("dp") * seq + t
    stats = lax.dynamic_slice_in_dim(stats, mine * (features // 32), features // 32, 1)
    return (
        result.astype(BF16).reshape(seqs, tok, features),
        ig + grad_resid_one.reshape(seqs, tok, features),
        wq.reshape(features // 32, 3 * features),
        out_sum,
        up_sum,
        down_sum,
        stats[:2],
        stats[2:],
    )


def solution(mesh):
    in_specs = (
        P("dp", "seq", None),
        P("dp", None),
        P("dp", None, None, None),
        P("dp", None),
        P("dp", None),
        P("dp", None),
        P("dp", None),
        P(),
        P(),
        P("dp", "seq", None),
    )
    out_specs = (
        P("dp", "seq", None),
        P("dp", "seq", None),
        P(("dp", "seq"), None),
        P(("dp", "seq"), None),
        P(("dp", "seq"), None),
        P(("dp", "seq"), None),
        P(None, ("dp", "seq")),
        P(None, ("dp", "seq")),
    )
    fits = mesh.shape["dp"] == 4 and mesh.shape["seq"] == 8
    return jax.shard_map(
        head_layout if fits else per_device, mesh=mesh, in_specs=in_specs, out_specs=out_specs, check_vma=False
    )
```

```python
import functools
import jax
import jax.numpy as jnp
import numpy as np
from jax import lax
from jax.experimental import pallas as pl
from jax.experimental.pallas import tpu as pltpu
from jax.sharding import PartitionSpec as P

H = 12
HEAD = 64
BLOCK = 64
R = 3
MICRO = 2


norm_eps = 1e-05
masked_score = -1e30
root_half = 0.7071067811865476
inv_root_two_pi = 0.3989422804014327


def padded(cells, sides, width):
    for axis, dim in sides:
        count = lax.axis_size(axis)
        ends = count - 1
        head = lax.slice_in_dim(cells, 0, width, axis=dim)
        tail = lax.slice_in_dim(cells, cells.shape[dim] - width, cells.shape[dim], axis=dim)
        cells = jnp.concatenate(
            [
                lax.ppermute(tail, axis, [(i, (i + 1) % count) for i in range(ends)]),
                cells,
                lax.ppermute(head, axis, [((i + 1) % count, i) for i in range(ends)]),
            ],
            axis=dim,
        )
    return cells


def from_root(x, axis, root):
    mine = lax.axis_index(axis) == root
    return lax.psum(jnp.where(mine, x, jnp.zeros_like(x)), axis)


def merged(x, axis, combine):
    everything = jax.tree.map(lambda part: lax.all_gather(part, axis), x)
    initial = jax.tree.map(lambda part: part[0], everything)

    def step(k, so_far):
        return combine(so_far, jax.tree.map(lambda part: part[k], everything))

    return lax.fori_loop(1, lax.axis_size(axis), step, initial)


def product(left_side, right_side):
    return jnp.dot(left_side, right_side, preferred_element_type=jnp.float32)


def product_tn(left_side, right_side):
    return lax.dot_general(
        left_side, right_side, (((0,), (0,)), ((), ())), preferred_element_type=jnp.float32
    )


def product_nt(left_side, right_side):
    return lax.dot_general(
        left_side, right_side, (((1,), (1,)), ((), ())), preferred_element_type=jnp.float32
    )


def gelu_value(pre_act):
    return 0.5 * pre_act * (1.0 + lax.erf(pre_act * root_half))


def gelu_slope(pre_act):
    return (
        0.5 * (1.0 + lax.erf(pre_act * root_half))
        + pre_act * jnp.exp(-0.5 * pre_act * pre_act) * inv_root_two_pi
    )


def norm_forward(residual, gain_row, shift_row):
    mean_row = jnp.mean(residual, axis=-1, keepdims=True)
    centred = residual - mean_row
    variance = jnp.mean(centred * centred, axis=-1, keepdims=True)
    inv_std = lax.rsqrt(variance + norm_eps)
    normed = centred * inv_std
    return (normed * gain_row + shift_row, normed, inv_std)


def norm_backward(grad_rows, normed, inv_std, gain_row):
    scaled = grad_rows * gain_row
    back_rows = inv_std * (
        scaled
        - jnp.mean(scaled, axis=-1, keepdims=True)
        - normed * jnp.mean(scaled * normed, axis=-1, keepdims=True)
    )
    return (back_rows, jnp.sum(grad_rows * normed, axis=0), jnp.sum(grad_rows, axis=0))


def merge_stats(first_pair, second_pair):
    joint_max = jnp.maximum(first_pair[0], second_pair[0])
    joint_sum = first_pair[1] * jnp.exp(first_pair[0] - joint_max) + second_pair[1] * jnp.exp(
        second_pair[0] - joint_max
    )
    return (joint_max, joint_sum)


def local_scores(query_heads, shared_keys, random_keys, shared_ok, random_ok, scale_factor):
    part_shared = jnp.einsum(
        "sbqhd,sbkhd->sbhqk", query_heads, shared_keys, preferred_element_type=jnp.float32
    )
    part_random = jnp.einsum(
        "sbqhd,sbhkd->sbhqk", query_heads, random_keys, preferred_element_type=jnp.float32
    )
    scores = jnp.concatenate([part_shared, part_random], axis=4) * scale_factor
    allowed = jnp.concatenate(
        [jnp.broadcast_to(shared_ok[:, :, None], part_shared.shape), random_ok], axis=4
    )
    return jnp.where(allowed, scores, masked_score)


def per_device(
    inputs, segments, rand_blocks, w_qkv, w_out, w_up, w_down, norm_gain, norm_bias, out_grad
):
    seq_total, tok_dev, features = inputs.shape
    devices = lax.axis_size("seq")
    my_index = lax.axis_index("seq")
    blocks_dev = tok_dev // BLOCK
    blocks_all = blocks_dev * devices
    entries = blocks_dev * H * R
    capacity = max(2, entries // devices + 1)
    per_micro = seq_total // MICRO
    glob_rows = 2 * BLOCK
    shared_count = 5 * BLOCK
    scale_factor = HEAD ** (-0.5)
    token_rows = per_micro * tok_dev
    owner_flag = (my_index == 0).astype(jnp.float32)
    row_global = my_index * tok_dev + jnp.arange(tok_dev, dtype=jnp.int32) < glob_rows
    window_index = np.arange(blocks_dev)[:, None] + np.arange(3)[None, :]
    win_blocks = (
        my_index * blocks_dev
        + jnp.arange(blocks_dev, dtype=jnp.int32)[:, None]
        + jnp.arange(-1, 2, dtype=jnp.int32)[None, :]
    )
    win_inside = (win_blocks >= 0) & (win_blocks < blocks_all)
    win_clipped = jnp.clip(win_blocks, 0, blocks_all - 1)
    entry_heads = jnp.arange(entries, dtype=jnp.int32) // R % H
    slot_ids = jnp.arange(capacity, dtype=jnp.int32)
    earlier = jnp.arange(entries)[None, :] < jnp.arange(entries)[:, None]
    seq_ids = jnp.arange(per_micro, dtype=jnp.int32)
    grad_qkv_w = jnp.zeros((features, 3 * features), jnp.float32)
    grad_out_w = jnp.zeros((features, features), jnp.float32)
    grad_up_w = jnp.zeros((features, w_up.shape[1]), jnp.float32)
    grad_down_w = jnp.zeros((w_down.shape[0] * lax.axis_size("dp"), features), jnp.float32)
    gain_acc = jnp.zeros((2, features), jnp.float32)
    shift_acc = jnp.zeros((2, features), jnp.float32)
    output_parts = []
    input_parts = []
    for micro_step in range(MICRO):
        start_seq = micro_step * per_micro
        tokens_in = inputs[start_seq : start_seq + per_micro]
        seg_micro = segments[start_seq : start_seq + per_micro]
        rand_micro = rand_blocks[start_seq : start_seq + per_micro]
        cotangent = out_grad[start_seq : start_seq + per_micro]
        full_qkv, full_out, full_up, full_down = (
            lax.all_gather(w_qkv, "dp", axis=0, tiled=True),
            lax.all_gather(w_out, "dp", axis=0, tiled=True),
            lax.all_gather(w_up, "dp", axis=0, tiled=True),
            lax.all_gather(w_down, "dp", axis=0, tiled=True),
        )
        tokens_flat = tokens_in.reshape(token_rows, features)
        qkv_rows = (
            product(tokens_flat, full_qkv)
            .astype(jnp.bfloat16)
            .reshape(per_micro, tok_dev, 3 * features)
        )
        queries = qkv_rows[..., :features]
        keyvals = qkv_rows[..., features:]
        extended = padded(keyvals, (("seq", 1),), BLOCK)
        global_block = from_root(qkv_rows[:, :glob_rows], "seq", 0)
        requests = rand_micro.reshape(per_micro, devices, entries)
        owners = requests // blocks_dev
        local_block = requests % blocks_dev
        same_owner = owners[:, :, :, None] == owners[:, :, None, :]
        slot_rank = jnp.sum(same_owner & earlier[None, None], axis=3)
        slot_hit = ((owners == my_index)[..., None] & (slot_rank[..., None] == slot_ids)).astype(
            jnp.int32
        )
        slot_live = jnp.sum(slot_hit, axis=2)
        slot_piece = jnp.sum(slot_hit * (local_block * H + entry_heads)[..., None], axis=2)
        piece_index = jnp.transpose(slot_piece, (1, 2, 0))
        live_mask = jnp.transpose(slot_live, (1, 2, 0))
        pieces = (
            keyvals.reshape(per_micro, blocks_dev, BLOCK, 2, H, HEAD)
            .transpose(0, 1, 4, 2, 3, 5)
            .reshape(per_micro, blocks_dev * H, BLOCK, 2 * HEAD)
        )
        outgoing = pieces[seq_ids[None, None, :], piece_index]
        outgoing = jnp.where(live_mask[..., None, None] > 0, outgoing, jnp.zeros((), jnp.bfloat16))
        outgoing = outgoing.reshape(devices * capacity, per_micro, BLOCK, 2 * HEAD)
        incoming = lax.all_to_all(outgoing, "seq", split_axis=0, concat_axis=0, tiled=True)
        my_owner = jnp.take(owners, my_index, axis=1)
        my_rank = jnp.take(slot_rank, my_index, axis=1)
        my_request = jnp.take(requests, my_index, axis=1)
        positions = my_owner * capacity + my_rank
        fetched = incoming[positions, seq_ids[:, None]].reshape(
            per_micro, blocks_dev, H, R, BLOCK, 2, HEAD
        )
        random_keys = fetched[..., 0, :].reshape(per_micro, blocks_dev, H, R * BLOCK, HEAD)
        random_vals = fetched[..., 1, :].reshape(per_micro, blocks_dev, H, R * BLOCK, HEAD)
        seg_blocks = seg_micro.reshape(per_micro, blocks_all, BLOCK)
        query_seg = lax.dynamic_slice_in_dim(seg_micro, my_index * tok_dev, tok_dev, 1).reshape(
            per_micro, blocks_dev, BLOCK
        )
        window_seg = seg_blocks[:, win_clipped].reshape(per_micro, blocks_dev, 3 * BLOCK)
        window_ok = (query_seg[..., :, None] == window_seg[:, :, None, :]) & jnp.repeat(
            win_inside, BLOCK, axis=1
        )[None, :, None, :]
        shared_ok = jnp.concatenate(
            [window_ok, jnp.ones((per_micro, blocks_dev, BLOCK, glob_rows), bool)], axis=3
        )
        random_seg = seg_blocks[seq_ids[:, None], my_request].reshape(
            per_micro, blocks_dev, H, R * BLOCK
        )
        random_ok = query_seg[:, :, None, :, None] == random_seg[:, :, :, None, :]
        ext_blocks = extended.reshape(per_micro, blocks_dev + 2, BLOCK, 2 * features)
        window_kv = ext_blocks[:, window_index].reshape(
            per_micro, blocks_dev, 3 * BLOCK, 2 * features
        )
        glob_kv = jnp.broadcast_to(
            global_block[:, None, :, features:], (per_micro, blocks_dev, glob_rows, 2 * features)
        )
        shared_kv = jnp.concatenate([window_kv, glob_kv], axis=2)
        shared_keys = shared_kv[..., :features].reshape(
            per_micro, blocks_dev, shared_count, H, HEAD
        )
        shared_vals = shared_kv[..., features:].reshape(
            per_micro, blocks_dev, shared_count, H, HEAD
        )
        query_heads = queries.reshape(per_micro, blocks_dev, BLOCK, H, HEAD)
        scores = local_scores(
            query_heads, shared_keys, random_keys, shared_ok, random_ok, scale_factor
        )
        row_max = jnp.max(scores, axis=4, keepdims=True)
        exp_terms = jnp.exp(scores - row_max)
        row_sum = jnp.sum(exp_terms, axis=4, keepdims=True)
        local_probs = exp_terms / row_sum
        log_norm = row_max + jnp.log(row_sum)
        local_weights = local_probs.astype(jnp.bfloat16)
        local_att = jnp.einsum(
            "sbhqk,sbkhd->sbqhd",
            local_weights[..., :shared_count],
            shared_vals,
            preferred_element_type=jnp.float32,
        )
        local_att = local_att + jnp.einsum(
            "sbhqk,sbhkd->sbqhd",
            local_weights[..., shared_count:],
            random_vals,
            preferred_element_type=jnp.float32,
        )
        local_att = local_att.reshape(per_micro, tok_dev, features)
        glob_query = global_block[..., :features].reshape(per_micro, glob_rows, H, HEAD)
        local_keys = keyvals[..., :features].reshape(per_micro, tok_dev, H, HEAD)
        local_vals = keyvals[..., features:].reshape(per_micro, tok_dev, H, HEAD)
        glob_scores = (
            jnp.einsum(
                "sqhd,skhd->shqk", glob_query, local_keys, preferred_element_type=jnp.float32
            )
            * scale_factor
        )
        part_max = jnp.max(glob_scores, axis=3)
        part_sum = jnp.sum(jnp.exp(glob_scores - part_max[..., None]), axis=3)
        glob_max, glob_sum = merged((part_max, part_sum), "seq", merge_stats)
        glob_lse = glob_max + jnp.log(glob_sum)
        glob_probs = jnp.exp(glob_scores - glob_lse[..., None])
        glob_weights = glob_probs.astype(jnp.bfloat16)
        glob_part = jnp.einsum(
            "shqk,skhd->sqhd", glob_weights, local_vals, preferred_element_type=jnp.float32
        ).reshape(per_micro, glob_rows, features)
        glob_out = lax.psum(glob_part, "seq")
        glob_full = jnp.concatenate(
            [glob_out, jnp.zeros((per_micro, tok_dev - glob_rows, features), jnp.float32)], axis=1
        )
        attention = jnp.where(row_global[None, :, None], glob_full, local_att).astype(jnp.bfloat16)
        att_flat = attention.reshape(token_rows, features)
        resid_one = tokens_flat.astype(jnp.float32) + product(att_flat, full_out)
        hidden_one, normed_one, inv_one = norm_forward(resid_one, norm_gain[0], norm_bias[0])
        hidden_low = hidden_one.astype(jnp.bfloat16)
        pre_act = product(hidden_low, full_up)
        activated = gelu_value(pre_act).astype(jnp.bfloat16)
        resid_two = hidden_one + product(activated, full_down)
        result, normed_two, inv_two = norm_forward(resid_two, norm_gain[1], norm_bias[1])
        output_parts.append(result.astype(jnp.bfloat16).reshape(per_micro, tok_dev, features))
        grad_rows = cotangent.reshape(token_rows, features).astype(jnp.float32)
        grad_resid_two, gain_two, shift_two = norm_backward(
            grad_rows, normed_two, inv_two, norm_gain[1]
        )
        grad_branch = grad_resid_two.astype(jnp.bfloat16)
        grad_down_w = grad_down_w + product_tn(activated, grad_branch)
        grad_pre = (product_nt(grad_branch, full_down) * gelu_slope(pre_act)).astype(jnp.bfloat16)
        grad_up_w = grad_up_w + product_tn(hidden_low, grad_pre)
        grad_hidden = grad_resid_two + product_nt(grad_pre, full_up)
        grad_resid_one, gain_one, shift_one = norm_backward(
            grad_hidden, normed_one, inv_one, norm_gain[0]
        )
        grad_mix = grad_resid_one.astype(jnp.bfloat16)
        grad_out_w = grad_out_w + product_tn(att_flat, grad_mix)
        grad_att = (
            product_nt(grad_mix, full_out)
            .astype(jnp.bfloat16)
            .reshape(per_micro, tok_dev, features)
        )
        gain_acc = gain_acc + jnp.stack([gain_one, gain_two])
        shift_acc = shift_acc + jnp.stack([shift_one, shift_two])
        grad_local = jnp.where(
            row_global[None, :, None], jnp.zeros((), jnp.bfloat16), grad_att
        ).reshape(per_micro, blocks_dev, BLOCK, H, HEAD)
        scores = local_scores(
            query_heads, shared_keys, random_keys, shared_ok, random_ok, scale_factor
        )
        local_probs = jnp.exp(scores - log_norm)
        local_weights = local_probs.astype(jnp.bfloat16)
        grad_prob = jnp.concatenate(
            [
                jnp.einsum(
                    "sbqhd,sbkhd->sbhqk",
                    grad_local,
                    shared_vals,
                    preferred_element_type=jnp.float32,
                ),
                jnp.einsum(
                    "sbqhd,sbhkd->sbhqk",
                    grad_local,
                    random_vals,
                    preferred_element_type=jnp.float32,
                ),
            ],
            axis=4,
        )
        row_delta = jnp.sum(local_probs * grad_prob, axis=4, keepdims=True)
        grad_score = (local_probs * (grad_prob - row_delta)).astype(jnp.bfloat16)
        grad_query = jnp.einsum(
            "sbhqk,sbkhd->sbqhd",
            grad_score[..., :shared_count],
            shared_keys,
            preferred_element_type=jnp.float32,
        )
        grad_query = (
            grad_query
            + jnp.einsum(
                "sbhqk,sbhkd->sbqhd",
                grad_score[..., shared_count:],
                random_keys,
                preferred_element_type=jnp.float32,
            )
        ) * scale_factor
        grad_key_shared = (
            jnp.einsum(
                "sbhqk,sbqhd->sbkhd",
                grad_score[..., :shared_count],
                query_heads,
                preferred_element_type=jnp.float32,
            )
            * scale_factor
        )
        grad_val_shared = jnp.einsum(
            "sbhqk,sbqhd->sbkhd",
            local_weights[..., :shared_count],
            grad_local,
            preferred_element_type=jnp.float32,
        )
        grad_key_random = (
            jnp.einsum(
                "sbhqk,sbqhd->sbhkd",
                grad_score[..., shared_count:],
                query_heads,
                preferred_element_type=jnp.float32,
            )
            * scale_factor
        )
        grad_val_random = jnp.einsum(
            "sbhqk,sbqhd->sbhkd",
            local_weights[..., shared_count:],
            grad_local,
            preferred_element_type=jnp.float32,
        )
        grad_shared = jnp.concatenate(
            [
                grad_key_shared.reshape(per_micro, blocks_dev, shared_count, features),
                grad_val_shared.reshape(per_micro, blocks_dev, shared_count, features),
            ],
            axis=3,
        )
        grad_window = grad_shared[:, :, : 3 * BLOCK].reshape(
            per_micro, blocks_dev, 3, BLOCK, 2 * features
        )
        ext_grad = jnp.zeros((per_micro, blocks_dev + 2, BLOCK, 2 * features), jnp.float32)
        for offset in range(3):
            ext_grad = ext_grad.at[:, offset : offset + blocks_dev].add(grad_window[:, :, offset])
        grad_glob_keys = jnp.sum(grad_shared[:, :, 3 * BLOCK :], axis=1)
        grad_random = jnp.stack([grad_key_random, grad_val_random], axis=4).reshape(
            per_micro, entries, BLOCK, 2 * HEAD
        )
        returned = (
            jnp.zeros((devices * capacity, per_micro, BLOCK, 2 * HEAD), jnp.float32)
            .at[positions, seq_ids[:, None]]
            .set(grad_random)
        )
        arrived = lax.all_to_all(
            returned.astype(jnp.bfloat16), "seq", split_axis=0, concat_axis=0, tiled=True
        ).astype(returned.dtype)
        arrived = arrived.reshape(devices, capacity, per_micro, BLOCK, 2 * HEAD) * live_mask[
            ..., None, None
        ].astype(jnp.float32)
        piece_grad = (
            jnp.zeros((per_micro, blocks_dev * H, BLOCK, 2 * HEAD), jnp.float32)
            .at[seq_ids[None, None, :], piece_index]
            .add(arrived)
        )
        piece_grad = (
            piece_grad.reshape(per_micro, blocks_dev, H, BLOCK, 2, HEAD)
            .transpose(0, 1, 3, 4, 2, 5)
            .reshape(per_micro, tok_dev, 2 * features)
        )
        rim_pair = jnp.concatenate([ext_grad[:, 0], ext_grad[:, blocks_dev + 1]], axis=1)
        rim_back = padded(rim_pair.astype(jnp.bfloat16), (("seq", 1),), BLOCK).astype(
            rim_pair.dtype
        )
        grad_kv = (
            ext_grad[:, 1 : blocks_dev + 1].reshape(per_micro, tok_dev, 2 * features) + piece_grad
        )
        grad_kv = grad_kv.at[:, :BLOCK].add(rim_back[:, :BLOCK])
        grad_kv = grad_kv.at[:, tok_dev - BLOCK :].add(rim_back[:, 3 * BLOCK :])
        grad_glob = from_root(grad_att[:, :glob_rows], "seq", 0)
        grad_glob_heads = grad_glob.reshape(per_micro, glob_rows, H, HEAD)
        glob_scores = (
            jnp.einsum(
                "sqhd,skhd->shqk", glob_query, local_keys, preferred_element_type=jnp.float32
            )
            * scale_factor
        )
        glob_probs = jnp.exp(glob_scores - glob_lse[..., None])
        glob_weights = glob_probs.astype(jnp.bfloat16)
        glob_grad_prob = jnp.einsum(
            "sqhd,skhd->shqk", grad_glob_heads, local_vals, preferred_element_type=jnp.float32
        )
        glob_delta = lax.psum(jnp.sum(glob_probs * glob_grad_prob, axis=3), "seq")
        glob_grad_score = (glob_probs * (glob_grad_prob - glob_delta[..., None])).astype(
            jnp.bfloat16
        )
        glob_grad_query = (
            jnp.einsum(
                "shqk,skhd->sqhd", glob_grad_score, local_keys, preferred_element_type=jnp.float32
            )
            * scale_factor
        )
        glob_grad_key = (
            jnp.einsum(
                "shqk,sqhd->skhd", glob_grad_score, glob_query, preferred_element_type=jnp.float32
            )
            * scale_factor
        )
        glob_grad_val = jnp.einsum(
            "shqk,sqhd->skhd", glob_weights, grad_glob_heads, preferred_element_type=jnp.float32
        )
        grad_kv = grad_kv + jnp.concatenate(
            [
                glob_grad_key.reshape(per_micro, tok_dev, features),
                glob_grad_val.reshape(per_micro, tok_dev, features),
            ],
            axis=2,
        )
        summed_query, summed_keys = lax.psum(
            (glob_grad_query.reshape(per_micro, glob_rows, features), grad_glob_keys), "seq"
        )
        grad_kv = grad_kv.at[:, :glob_rows].add(owner_flag * summed_keys)
        grad_queries = (
            grad_query.reshape(per_micro, tok_dev, features)
            .at[:, :glob_rows]
            .add(owner_flag * summed_query)
        )
        grad_qkv_rows = (
            jnp.concatenate([grad_queries, grad_kv], axis=2)
            .astype(jnp.bfloat16)
            .reshape(token_rows, 3 * features)
        )
        grad_qkv_w = grad_qkv_w + product_tn(tokens_flat, grad_qkv_rows)
        input_rows = grad_resid_one + product_nt(grad_qkv_rows, full_qkv)
        input_parts.append(input_rows.reshape(per_micro, tok_dev, features))
    summed = (
        lax.psum_scatter(grad_qkv_w, ("dp", "seq"), scatter_dimension=0, tiled=True),
        lax.psum_scatter(grad_out_w, ("dp", "seq"), scatter_dimension=0, tiled=True),
        lax.psum_scatter(grad_up_w, ("dp", "seq"), scatter_dimension=0, tiled=True),
        lax.psum_scatter(grad_down_w, ("dp", "seq"), scatter_dimension=0, tiled=True),
        lax.psum_scatter(gain_acc, ("dp", "seq"), scatter_dimension=1, tiled=True),
        lax.psum_scatter(shift_acc, ("dp", "seq"), scatter_dimension=1, tiled=True),
    )
    return (
        jnp.concatenate(output_parts, axis=0),
        jnp.concatenate(input_parts, axis=0),
        summed[0],
        summed[1],
        summed[2],
        summed[3],
        summed[4],
        summed[5],
    )


TILE = 128
NH = 3
CH = 256
LOG2E = 1.4426950408889634
SCALE2 = HEAD ** (-0.5) * LOG2E
NEG = -1e30
F32 = jnp.float32
BF16 = jnp.bfloat16


def nt(a, b):
    return lax.dot_general(a, b, (((1,), (1,)), ((), ())), preferred_element_type=F32)


def nn(a, b):
    return jnp.dot(a, b, preferred_element_type=F32)


MESH = pl.DeviceIdType.MESH
ANYSPACE = pl.BlockSpec(memory_space=pl.ANY)
VMEMSPACE = pl.BlockSpec(memory_space=pltpu.VMEM)


class Copies:
    def __init__(self, send, recv):
        self.send = send
        self.recv = recv
        self.used = 0

    def to(self, src, dst, device):
        index = self.used
        self.used += 1
        return pltpu.make_async_remote_copy(
            src_ref=src, dst_ref=dst, send_sem=self.send.at[index], recv_sem=self.recv.at[index],
            device_id=device, device_id_type=MESH,
        )


class Place:
    def __init__(self):
        self.d = lax.axis_index("dp")
        self.t = lax.axis_index("seq")
        self.x = lax.rem(self.d, 2)
        self.y = self.d // 2
        self.c = lax.rem(self.t, 2)
        self.z = self.t // 2
        self.half = self.z // 2
        self.xn = self.d + 1 - 2 * self.x
        self.yn = self.d + 2 - 4 * self.y
        self.diag = 3 - self.d
        self.pair_z = self.z + 1 - 2 * lax.rem(self.z, 2)
        self.across_x = (self.xn, self.t)
        self.across_y = (self.yn, self.t)
        self.partner = (self.d, self.t + 1 - 2 * self.c)

    def at_z(self, z):
        return (self.d, 2 * z + self.c)


def greet(devices):
    barrier = pltpu.get_barrier_semaphore()
    for device in devices:
        pl.semaphore_signal(barrier, inc=1, device_id=device, device_id_type=MESH)


def met(devices):
    pl.semaphore_wait(pltpu.get_barrier_semaphore(), len(devices))


def meet(devices):
    greet(devices)
    met(devices)


def tile_tables(tile, rand_ref, segq_ref, blocks):
    wide = NH * TILE
    key = lax.broadcasted_iota(jnp.int32, (blocks, wide), 0)
    lane = lax.broadcasted_iota(jnp.int32, (blocks, wide), 1)
    query = tile * (TILE // BLOCK) + lax.rem(lane, TILE) // BLOCK
    near = (key - query) * (key - query) <= 1
    hits = near.astype(F32)
    for r in range(rand_ref.shape[1]):
        hits = hits + (rand_ref[tile, r : r + 1, :] == key).astype(F32)
    fixed = jnp.logical_or(query < 2, key < 2)
    count = jnp.where(query < 2, 0.0, hits) + fixed.astype(F32)
    on = jnp.where(count > 0.0, jnp.log2(jnp.maximum(count, 1.0)), NEG)
    off = jnp.where(fixed, 0.0, NEG)
    return on, off, segq_ref[tile]


def biased(s, mask, on, off, first_block):
    rows = []
    for j in range(s.shape[0] // BLOCK):
        kb = first_block + j
        m3 = jnp.concatenate([mask[BLOCK * j : BLOCK * (j + 1)]] * NH, axis=1)
        bias = jnp.where(m3, on[kb : kb + 1, :], off[kb : kb + 1, :])
        rows.append(s[BLOCK * j : BLOCK * (j + 1)] * SCALE2 + bias)
    return jnp.concatenate(rows, axis=0)


def fill_segments(segq, segk):
    steps = segq.shape[0]
    for i in range(steps):
        column = jnp.broadcast_to(segq[i].astype(F32), (8, TILE)).T[:, :1]
        segk[TILE * i : TILE * (i + 1), :] = jnp.broadcast_to(column, (TILE, TILE)).astype(jnp.int32)


def forward_tile(tile, rand, segq, segk, qt, kn, vt, q3, tbuf, att, otile, lse):
    length = kn.shape[0]
    chunks = length // CH
    here = pl.ds(pl.multiple_of(tile * TILE, TILE), TILE)
    on, off, seg = tile_tables(tile, rand, segq, length // BLOCK)
    for h in range(NH):
        q3[HEAD * h : HEAD * (h + 1), TILE * h : TILE * (h + 1)] = qt[
            HEAD * h : HEAD * (h + 1), here
        ]
    top = jnp.full((8, NH * TILE), NEG, F32)
    for j in range(chunks):
        rows = slice(CH * j, CH * (j + 1))
        s = nn(kn[rows, :], q3[...])
        t = biased(s, segk[rows, :] == seg, on, off, CH // BLOCK * j)
        tbuf[rows, :] = t
        top = jnp.maximum(top, jnp.max(t.reshape(CH // 8, 8, NH * TILE), axis=0))
    peak = jnp.max(top, axis=0, keepdims=True)
    total = jnp.zeros((8, NH * TILE), F32)
    out = jnp.zeros((256, NH * TILE), F32)
    for j in range(chunks):
        rows = slice(CH * j, CH * (j + 1))
        p = jnp.exp2(tbuf[rows, :] - peak)
        total = total + jnp.sum(p.reshape(CH // 8, 8, NH * TILE), axis=0)
        out = out + nn(vt[:, rows], p.astype(BF16))
    weight = jnp.sum(total, axis=0, keepdims=True)
    lse[tile] = peak + jnp.log2(weight)
    inv = 1.0 / weight
    heads = [
        out[HEAD * h : HEAD * (h + 1), TILE * h : TILE * (h + 1)] * inv[:, TILE * h : TILE * (h + 1)]
        for h in range(NH)
    ]
    merged = jnp.concatenate(heads, axis=0)
    otile[tile] = merged
    att[here, :] = merged.T.astype(BF16)


def unit_place(me, u):
    low = lax.rem(me.z, 2)
    return 2 * lax.rem(me.half + 1 + u // 2, 2) + lax.rem(low + 1 + u, 2)


def forward_kernel(*refs):
    (x, wg, wo, wu, wd, rand, segq), refs = refs[:7], refs[7:]
    outs, refs = refs[:14], refs[14:]
    wof, wuf, wdf, att_out, otile_o, lse_o, segk_o, qn_o, kn_o, vn_o, qt_o, kt_o, xst_o, wgf_o = outs
    (xs, wgf, bo, bu, bd, att, home, otile, lse, segk), refs = refs[:10], refs[10:]
    (qn, kn, vn, qt, kt, vt, xst, q3, tbuf), refs = refs[:9], refs[9:]
    send, recv, xsend, xrecv, local = refs
    me = Place()
    d, t, c, z = me.d, me.t, me.c, me.z
    mine, other = me.half, 1 - me.half
    is_middle = z == 1 + me.half
    tok = x.shape[1]
    length = xs.shape[0]
    steps = length // TILE
    per_unit = 2 * tok // TILE
    loads = [
        pltpu.make_async_copy(src, dst, local.at[i])
        for i, (src, dst) in enumerate(((wo, bo), (wu, bu), (wd, bd)))
    ]
    for load in loads:
        load.start()
    meet([me.across_x, me.across_y] + [(d, lax.rem(t + k, 8)) for k in range(1, 8)])
    cps = Copies(send, recv)
    sent = []

    def begin(*copies):
        for cp in copies:
            cp.start()
            sent.append(cp)

    def rows_of(index):
        return pl.ds(pl.multiple_of(index * tok, tok), tok)

    shard = wg.shape[0]
    wrows = lambda index, start, size: pl.ds(pl.multiple_of(index * shard + start, size), size)
    half = shard // 2
    top_half, low_half = pl.ds(0, half), pl.ds(half, half)
    my_top, my_low = wrows(d, 0, half), wrows(d, half, half)
    wg_x0 = cps.to(wg.at[top_half], wgf.at[my_top], me.across_x)
    wg_x1 = cps.to(wg.at[low_half], wgf.at[my_low], me.across_x)
    wg_y0 = cps.to(wg.at[low_half], wgf.at[my_low], me.across_y)
    wg_y1 = cps.to(wg.at[top_half], wgf.at[my_top], me.across_y)
    near = cps.to(x.at[mine], xs.at[rows_of(t)], me.at_z(me.pair_z))
    give = cps.to(x.at[mine], xs.at[rows_of(t)], me.partner)
    far = pltpu.make_async_remote_copy(
        src_ref=x.at[other], dst_ref=xs.at[rows_of(t)], send_sem=xsend.at[0],
        recv_sem=xrecv.at[lax.rem(z, 2)], device_id=me.at_z(2 - me.half), device_id_type=MESH,
    )
    begin(wg_x0, wg_y0, far, wg_x1, wg_y1, near, give)
    heavy = []
    for w, full in ((wo, wof), (wu, wuf), (wd, wdf)):
        rows = w.shape[0] // 2
        part = pl.ds(pl.multiple_of(c * rows, rows), rows)
        to_x = cps.to(w.at[part], full.at[d, part], me.across_x)
        to_y = cps.to(w.at[part], full.at[d, part], me.across_y)
        heavy.append((full, rows, part, to_x, to_y))
    xn_top, yn_low = wrows(me.xn, 0, half), wrows(me.yn, half, half)
    wg_dy = cps.to(wgf.at[xn_top], wgf.at[xn_top], me.across_y)
    wg_dx = cps.to(wgf.at[yn_low], wgf.at[yn_low], me.across_x)
    wg_x0.wait_recv()
    begin(wg_dy)
    wg_y0.wait_recv()
    begin(wg_dx)
    for full, rows, part, to_x, to_y in heavy[:2]:
        begin(to_x, to_y)

    xs[rows_of(t), :] = x[mine]
    wgf[wrows(d, 0, shard), :] = wg[...]
    q3[...] = jnp.zeros_like(q3)
    fill_segments(segq, segk)
    keeps = []
    for i, (load, buf, full) in enumerate(zip(loads, (bo, bu, bd), (wof, wuf, wdf))):
        load.wait()
        keep = pltpu.make_async_copy(buf, full.at[d], local.at[3 + i])
        keep.start()
        keeps.append(keep)

    def project(unit):
        rows = pl.ds(pl.multiple_of(unit * 2 * tok, 2 * tok), 2 * tok)
        both = nn(xs[rows, :], wgf[...])
        qf, kf, vf = both[:, :256], both[:, 256:512], both[:, 512:]
        qn[rows, :] = qf.astype(BF16)
        kn[rows, :] = kf.astype(BF16)
        vn[rows, :] = vf.astype(BF16)
        qt[:, rows] = qf.T.astype(BF16)
        kt[:, rows] = kf.T.astype(BF16)
        vt[:, rows] = vf.T.astype(BF16)
        xst[:, rows] = xs[rows, :].astype(F32).T.astype(BF16)

    wg_x1.wait_recv()
    wg_y1.wait_recv()
    wg_dy.wait_recv()
    wg_dx.wait_recv()
    give.wait_recv()
    near.wait_recv()
    near_rows = rows_of(2 * me.pair_z + c)
    pass_near = cps.to(xs.at[near_rows], xs.at[near_rows], me.partner)
    begin(pass_near)
    relays, onwards = [], []
    for j in range(2):
        src_rows = rows_of(2 * (2 * other + j) + c)
        relays.append(
            pltpu.make_async_remote_copy(
                src_ref=xs.at[src_rows], dst_ref=xs.at[src_rows], send_sem=xsend.at[1 + j],
                recv_sem=xrecv.at[j], device_id=me.at_z(me.pair_z), device_id_type=MESH,
            )
        )
        onwards.append(cps.to(xs.at[src_rows], xs.at[src_rows], me.partner))

    def forward_x(j):
        relays[j].wait_recv()
        pl.when(is_middle)(relays[j].start)
        begin(onwards[j])

    tail = []
    for full, rows, part, to_x, to_y in heavy:
        quarter = rows // 2
        lo = pl.ds(pl.multiple_of(c * rows, quarter), quarter)
        hi = pl.ds(pl.multiple_of(c * rows + quarter, quarter), quarter)
        tail.append(
            (
                to_x, to_y,
                cps.to(full.at[me.xn, lo], full.at[me.xn, lo], me.across_y),
                cps.to(full.at[me.xn, part], full.at[me.xn, part], me.partner),
                cps.to(full.at[me.yn, hi], full.at[me.yn, hi], me.across_x),
                cps.to(full.at[me.yn, part], full.at[me.yn, part], me.partner),
                cps.to(full.at[me.diag, part], full.at[me.diag, part], me.partner),
            )
        )

    def relay_weights(k):
        to_x, to_y, dy, px, dx, py, pd = tail[k]
        to_x.wait_recv()
        begin(dy, px)
        to_y.wait_recv()
        begin(dx, py)

    def relay_diag(k):
        to_x, to_y, dy, px, dx, py, pd = tail[k]
        dy.wait_recv()
        dx.wait_recv()
        begin(pd)

    def arrive(k):
        if k == 0:
            forward_x(0)
            relay_weights(0)
            begin(heavy[2][3], heavy[2][4])
        if k == 1:
            forward_x(1)
            pass_near.wait_recv()
        if k == 2:
            onwards[0].wait_recv()
        if k == 3:
            onwards[1].wait_recv()

    def project_step(k, carry):
        for i in range(4):
            pl.when(k == i)(functools.partial(arrive, i))
        unit = jnp.where(k < 2, 2 * mine + lax.rem(lax.rem(z, 2) + k, 2), 2 * other + k - 2)
        project(unit)
        return carry

    lax.fori_loop(0, 4, project_step, 0)
    saves = [
        pltpu.make_async_copy(src, dst, local.at[6 + i])
        for i, (src, dst) in enumerate(
            ((segk, segk_o), (qn, qn_o), (kn, kn_o), (vn, vn_o), (qt, qt_o), (kt, kt_o), (xst, xst_o), (wgf, wgf_o))
        )
    ]
    for save in saves:
        save.start()

    homes = []
    for u in range(4):
        unit = unit_place(me, u)
        for o in range(1 if u == 3 else 0, 2):
            to = 2 * unit + (c if o == 0 else 1 - c)
            homes.append((u, cps.to(att.at[rows_of(to)], home.at[t], (d, to))))

    def send_home(u):
        for v, move in homes:
            if u == v:
                move.start()

    def between(i):
        if i == 2:
            relay_weights(1)
        if i == per_unit:
            send_home(0)
        if i == per_unit + 1:
            relay_diag(0)
        if i == 2 * per_unit:
            send_home(1)
        if i == 3 * per_unit:
            send_home(2)
        if i == 3 * per_unit + 1:
            relay_weights(2)

    def tile_step(i, carry):
        for point in (2, per_unit, per_unit + 1, 2 * per_unit, 3 * per_unit, 3 * per_unit + 1):
            pl.when(i == point)(functools.partial(between, point))
        tile = unit_place(me, i // per_unit) * per_unit + lax.rem(i, per_unit)
        forward_tile(tile, rand, segq, segk, qt, kn, vt, q3, tbuf, att, otile, lse)
        return carry

    lax.fori_loop(0, steps, tile_step, 0)
    send_home(3)
    last = [
        pltpu.make_async_copy(src, dst, local.at[14 + i])
        for i, (src, dst) in enumerate(((otile, otile_o), (lse, lse_o)))
    ]
    for save in last:
        save.start()
    home[t] = att[rows_of(t), :]
    for u, move in homes:
        move.wait()
    for s in range(2):
        pieces = [home[4 * s + g].astype(F32) for g in range(4)]
        att_out[tok * s : tok * (s + 1), :] = jnp.concatenate(pieces, axis=1).astype(BF16)
    relay_diag(1)
    relay_diag(2)
    for to_x, to_y, dy, px, dx, py, pd in tail:
        px.wait_recv()
        py.wait_recv()
        pd.wait_recv()
    for cp in sent:
        cp.wait_send()

    @pl.when(is_middle)
    def _():
        for relay in relays:
            relay.wait_send()

    for copy in keeps + saves + last:
        copy.wait()


def forward_half(x, wg, wo, wu, wd, rand, segq):
    dp = lax.axis_size("dp")
    seq = lax.axis_size("seq")
    tok, features = x.shape[1:]
    length = seq * tok
    steps = length // TILE
    nat, tra = (length, 256), (256, length)
    stacked = lambda w: jax.ShapeDtypeStruct((dp,) + w.shape, BF16)
    low = lambda *shape: jax.ShapeDtypeStruct(shape, BF16)
    full = lambda *shape: jax.ShapeDtypeStruct(shape, F32)
    return pl.pallas_call(
        forward_kernel,
        in_specs=[VMEMSPACE] * 2 + [ANYSPACE] * 3 + [VMEMSPACE] * 2,
        out_specs=[ANYSPACE] * 3 + [VMEMSPACE] + [ANYSPACE] * 10,
        out_shape=[
            stacked(wo), stacked(wu), stacked(wd), low(2 * tok, features),
            full(steps, NH * HEAD, TILE), full(steps, 1, NH * TILE),
            jax.ShapeDtypeStruct((length, TILE), jnp.int32),
            low(*nat), low(*nat), low(*nat), low(*tra), low(*tra),
            low(features, length), low(features, 768),
        ],
        scratch_shapes=[
            pltpu.VMEM((length, features), BF16),
            pltpu.VMEM((features, 768), BF16),
            pltpu.VMEM(wo.shape, BF16),
            pltpu.VMEM(wu.shape, BF16),
            pltpu.VMEM(wd.shape, BF16),
            pltpu.VMEM((length, NH * HEAD), BF16),
            pltpu.VMEM((seq, tok, NH * HEAD), BF16),
            pltpu.VMEM((steps, NH * HEAD, TILE), F32),
            pltpu.VMEM((steps, 1, NH * TILE), F32),
            pltpu.VMEM((length, TILE), jnp.int32),
            pltpu.VMEM(nat, BF16),
            pltpu.VMEM(nat, BF16),
            pltpu.VMEM(nat, BF16),
            pltpu.VMEM(tra, BF16),
            pltpu.VMEM(tra, BF16),
            pltpu.VMEM(tra, BF16),
            pltpu.VMEM((features, length), BF16),
            pltpu.VMEM((256, NH * TILE), BF16),
            pltpu.VMEM((length, NH * TILE), F32),
            pltpu.SemaphoreType.DMA((90,)),
            pltpu.SemaphoreType.DMA((90,)),
            pltpu.SemaphoreType.DMA((3,)),
            pltpu.SemaphoreType.DMA((2,)),
            pltpu.SemaphoreType.DMA((16,)),
        ],
        compiler_params=pltpu.CompilerParams(
            collective_id=0, has_side_effects=True, vmem_limit_bytes=62 * 1024 * 1024
        ),
        name="forward_half",
    )(x, wg, wo, wu, wd, rand, segq)


def each(count, body):
    def run(i, carry):
        body(i)
        return carry

    lax.fori_loop(0, count, run, 0)


def plus(a, b):
    return a.astype(F32) + b.astype(F32)


def backward_tile(
    tile, dat, qn, qt, otile, lse, rand, segq, segk, kn, vn, kt, dqkv, q3t, d3t, q3, d3, dk, dv
):
    chunks = kn.shape[0] // CH
    on, off, seg = tile_tables(tile, rand, segq, kn.shape[0] // BLOCK)
    here = pl.ds(pl.multiple_of(tile * TILE, TILE), TILE)
    dat_f = dat[here, :].astype(F32)
    dat_t = dat_f.T
    lane = lax.broadcasted_iota(jnp.int32, (TILE, NH * HEAD), 1) // HEAD
    qblk = qn[here, : NH * HEAD].astype(F32)
    delta = []
    for h in range(NH):
        hr = slice(HEAD * h, HEAD * (h + 1))
        hc = slice(TILE * h, TILE * (h + 1))
        q3t[hr, hc] = qt[hr, here]
        d3t[hr, hc] = dat_t[hr].astype(BF16)
        q3[hc, :] = jnp.where(lane == h, qblk, 0.0).astype(BF16)
        d3[hc, :] = jnp.where(lane == h, dat_f, 0.0).astype(BF16)
        delta.append(jnp.sum(dat_t[hr] * otile[tile, hr, :], axis=0, keepdims=True))
    delta = jnp.concatenate(delta, axis=1)
    norm = lse[tile]
    dq = jnp.zeros((256, NH * TILE), F32)
    for j in range(chunks):
        rows = slice(CH * j, CH * (j + 1))
        s = nn(kn[rows, :], q3t[...])
        dp = nn(vn[rows, :], d3t[...])
        t = biased(s, segk[rows, :] == seg, on, off, CH // BLOCK * j)
        p = jnp.exp2(t - norm)
        ds = (p * (dp - delta)).astype(BF16)
        dv[rows, :] += nn(p.astype(BF16), d3[...])
        dk[rows, :] += nn(ds, q3[...])
        dq = dq + nn(kt[:, rows], ds)
    heads = [dq[HEAD * h : HEAD * (h + 1), TILE * h : TILE * (h + 1)] for h in range(NH)]
    merged = jnp.concatenate(heads, axis=0).T * HEAD ** (-0.5)
    dqkv[here, : NH * HEAD] = merged.astype(BF16)


def backward_kernel(*refs):
    (da, stats, g2), refs = refs[:3], refs[3:]
    (rand, segq), refs = refs[:2], refs[2:]
    extra, refs = refs[:5], refs[5:]
    saved, refs = refs[:10], refs[10:]
    (o0, o1, o2, stats_out, ig, wq), refs = refs[:6], refs[6:]
    bufs, refs = refs[:18], refs[18:]
    held, refs = refs[:10], refs[10:]
    kn, vn, kt, segk, qn, qt, otile, lse, xst, wg = held
    more, refs = refs[:5], refs[5:]
    wo, hb, dpre, at, resid = more
    (src, rows_t), refs = refs[:2], refs[2:]
    (dat, dqkv, q3t, d3t, q3, d3, dk, dv), refs = refs[:8], refs[8:]
    (part, own_p, rp, ra_p, rb_p, ro, dwg, wb1, wb2, wc, wr), refs = refs[:11], refs[11:]
    nsend, nrecv, send, recv, local = refs
    me = Place()
    c, z, x, y, t = me.c, me.z, me.x, me.y, me.t
    mine, other = me.half, 1 - me.half
    is_middle = z == 1 + me.half
    is_outer = z != 1 + me.half
    z_step = [lax.rem(z + k, 4) for k in (1, 2, 3)]
    tok = src.shape[1]
    loads = [
        pltpu.make_async_copy(from_hbm, to_vmem, local.at[4 + i])
        for i, (from_hbm, to_vmem) in enumerate(zip(saved, held))
    ]
    more_loads = [
        pltpu.make_async_copy(from_hbm, to_vmem, local.at[14 + i])
        for i, (from_hbm, to_vmem) in enumerate(zip(extra, more))
    ]
    friends = [me.across_x, me.across_y] + [(me.d, lax.rem(t + k, 8)) for k in range(1, 8)]
    greet(friends)
    for load in more_loads[:4] + loads + more_loads[4:]:
        load.start()
    more_loads[0].wait()
    for g in range(4):
        both = nt(da[...], wo[g]).astype(BF16)
        src[g] = both[:tok]
        src[4 + g] = both[tok:]
    met(friends)
    cps = Copies(send, recv)

    def rows_of(index):
        return pl.ds(pl.multiple_of(index * tok, tok), tok)

    dat_moves = []
    for u in range(4):
        place = unit_place(me, 3 - u)
        for o in range(1 if u == 0 else 0, 2):
            to = 2 * place + (c if o == 0 else 1 - c)
            dat_moves.append((u, cps.to(src.at[to], dat.at[rows_of(t)], (me.d, to))))
    for u, move in dat_moves:
        move.start()
    keep = pltpu.make_async_copy(src.at[t], dat.at[rows_of(t)], local.at[3])
    keep.start()

    works = []
    for i, o in enumerate((o2, o1, o0)):
        own, ra, rb1, rb2, rc, rd = bufs[6 * i : 6 * i + 6]
        if i == 0:
            away = g2.at[:, :, :, 1 - c]
            load = pltpu.make_async_copy(g2.at[:, :, :, c], own, local.at[0])
        else:
            away, own, load = own.at[:, :, :, 1 - c], own.at[:, :, :, c], None
        swap_core = cps.to(away, ra, me.partner)
        moves = (
            swap_core,
            load,
            cps.to(own.at[:, 1 - x, 0:2], rb1, me.across_x),
            cps.to(own.at[1 - y, :, 2:4], rb2, me.across_y),
            cps.to(rb1.at[1 - y], rc.at[0:2], me.across_y),
            cps.to(rb2.at[1 - x], rc.at[2:4], me.across_x),
            [cps.to(rc.at[k], rd.at[j], me.at_z(k)) for j, k in enumerate(z_step)],
        )
        works.append(((o, own, ra, rb1, rb2, rc, rd), moves))
    stat_to = [me.partner, me.across_x, me.across_y, me.at_z(me.pair_z), me.at_z(lax.rem(z + 2, 4))]
    stat_all = [cps.to(nsend.at[k], nrecv.at[k], stat_to[k]) for k in range(5)]

    def stat_step(k):
        if k == 0:
            nsend[0] = stats[...]
        else:
            stat_all[k - 1].wait_recv()
            nsend[k] = nsend[k - 1] + nrecv[k - 1]
        stat_all[k].start()

    sent = []

    def begin(*copies):
        for cp in copies:
            cp.start()
            sent.append(cp)

    def stage_a(work):
        (o, own, ra, rb1, rb2, rc, rd), (swap_core, load, bx, by, cy, cx, ds) = work
        if load is not None:
            load.wait()
        swap_core.wait_recv()

        def fold(i):
            yy, xx, zz = i // 8, lax.rem(i // 4, 2), lax.rem(i, 4)
            own[yy, xx, zz] = plus(own[yy, xx, zz], ra[yy, xx, zz]).astype(BF16)

        each(16, fold)

    def cross(work):
        begin(work[1][2], work[1][3])

    def stage_b(work):
        (o, own, ra, rb1, rb2, rc, rd), (swap_core, load, bx, by, cy, cx, ds) = work
        bx.wait_recv()

        def fold_x(i):
            yy, zz = i // 2, lax.rem(i, 2)
            rb1[yy, zz] = plus(own[yy, x, zz], rb1[yy, zz]).astype(BF16)

        each(4, fold_x)
        begin(cy)
        by.wait_recv()

        def fold_y(i):
            xx, zz = i // 2, lax.rem(i, 2)
            rb2[xx, zz] = plus(own[y, xx, 2 + zz], rb2[xx, zz]).astype(BF16)

        each(4, fold_y)
        begin(cx)

    def stage_c(work):
        (o, own, ra, rb1, rb2, rc, rd), (swap_core, load, bx, by, cy, cx, ds) = work
        cy.wait_recv()
        cx.wait_recv()
        for zz in range(2):
            rc[zz] = plus(rb1[y, zz], rc[zz]).astype(BF16)
            rc[2 + zz] = plus(rb2[x, zz], rc[2 + zz]).astype(BF16)
        begin(*ds)

    def stage_d(work):
        (o, own, ra, rb1, rb2, rc, rd), (swap_core, load, bx, by, cy, cx, ds) = work
        for cp in ds:
            cp.wait_recv()
        o[...] = plus(rc[z], rd[0]) + plus(rd[1], rd[2])

    stat_step(0)
    down_work, up_work, out_work = works
    down_work[1][0].start()
    down_work[1][1].start()

    def weight_grad(tokens, cotangent, total):
        rows_t[...] = tokens[...].astype(F32).T.astype(BF16)
        size, wide = rows_t.shape[0] // 4, 768
        count = cotangent.shape[1] // wide

        def block(i):
            r, k = i // count, lax.rem(i, count)
            cols = pl.ds(pl.multiple_of(k * wide, wide), wide)
            grad = nn(rows_t[pl.ds(pl.multiple_of(r * size, size), size), :], cotangent[:, cols])
            total[r // 2, lax.rem(r, 2), :, :, :, cols] = grad.astype(BF16).reshape(
                total.shape[2:5] + (wide,)
            )

        each(4 * count, block)

    for load in more_loads[1:4]:
        load.wait()
    weight_grad(at, da, bufs[12])
    out_work[1][0].start()
    weight_grad(hb, dpre, bufs[6])
    up_work[1][0].start()
    q3t[...] = jnp.zeros_like(q3t)
    d3t[...] = jnp.zeros_like(d3t)
    dk[...] = jnp.zeros_like(dk)
    dv[...] = jnp.zeros_like(dv)
    gap = jnp.zeros((dqkv.shape[0], 256 - NH * HEAD), BF16)
    for g in range(3):
        dqkv[:, 256 * g + NH * HEAD : 256 * (g + 1)] = gap
    for load in loads[:8]:
        load.wait()
    keep.wait()
    per_unit = 2 * tok // TILE
    steps = dqkv.shape[0] // TILE

    def unit_arrives(u):
        for v, move in dat_moves:
            if u == v:
                move.wait_recv()

    def step_one():
        stat_step(1)
        stage_a(out_work)
        cross(out_work)

    def step_two():
        stat_step(2)
        stage_a(down_work)
        cross(down_work)

    events = {
        1: [step_one],
        2: [step_two],
        5: [functools.partial(stage_a, up_work)],
        7: [functools.partial(stage_b, out_work)],
        10: [functools.partial(stat_step, 3)],
    }
    for u in range(4):
        events.setdefault(u * per_unit, []).append(functools.partial(unit_arrives, u))

    def tile_step(i, carry):
        for point, actions in sorted(events.items()):

            @pl.when(i == point)
            def _():
                for action in actions:
                    action()

        tile = unit_place(me, 3 - i // per_unit) * per_unit + lax.rem(i, per_unit)
        backward_tile(
            tile, dat, qn, qt, otile, lse, rand, segq, segk, kn, vn, kt, dqkv,
            q3t, d3t, q3, d3, dk, dv,
        )
        return carry

    lax.fori_loop(0, steps, tile_step, 0)
    stat_step(4)
    loads[9].wait()

    dqkv[:, 256 : 256 + NH * HEAD] = (dk[...] * HEAD ** (-0.5)).astype(BF16)
    dqkv[:, 512 : 512 + NH * HEAD] = dv[...].astype(BF16)
    order = [2 * other, 2 * other + 1, me.pair_z, z]
    cores = []

    def partial_grad(k):
        zz = order[k]
        rows = pl.ds(pl.multiple_of(zz * 2 * tok, 2 * tok), 2 * tok)
        grad = nt(dqkv[rows, :], wg[...]).astype(BF16)
        part[zz, 0] = grad[:tok]
        part[zz, 1] = grad[tok:]
        core = cps.to(part.at[zz, 1 - c], rp.at[zz], me.partner)
        begin(core)
        cores.append(core)

    def merge_cores(k):
        zz = order[k]
        cores[k].wait_recv()
        own_p[zz] = plus(part[zz, c], rp[zz]).astype(BF16)

    up = [cps.to(own_p.at[2 * other + j], rb_p.at[j], me.at_z(me.pair_z)) for j in range(2)]
    near = cps.to(own_p.at[me.pair_z], ra_p, me.at_z(me.pair_z))
    down_send, down_recv = cps.used, cps.used
    cps.used += 2
    down = [
        pltpu.make_async_remote_copy(
            src_ref=own_p.at[2 * other + j], dst_ref=ro, send_sem=send.at[down_send + j],
            recv_sem=recv.at[down_recv], device_id=me.at_z(2 * other + j), device_id_type=MESH,
        )
        for j in range(2)
    ]

    partial_grad(0)
    partial_grad(1)
    merge_cores(0)
    pl.when(is_outer)(up[0].start)
    partial_grad(2)
    merge_cores(1)
    pl.when(is_outer)(up[1].start)
    partial_grad(3)
    stage_b(down_work)
    cross(up_work)
    merge_cores(2)
    begin(near)
    merge_cores(3)
    stage_c(out_work)
    loads[8].wait()
    half_rows = xst.shape[0] // 2
    for yy in range(2):
        grad = nn(xst[half_rows * yy : half_rows * (yy + 1), :], dqkv[...]).astype(BF16)
        dwg[yy] = grad.reshape(dwg.shape[1:])
    bx = cps.to(dwg.at[:, 1 - x, 0:4], wb1, me.across_x)
    by = cps.to(dwg.at[1 - y, :, 4:8], wb2, me.across_y)
    begin(bx, by)

    @pl.when(is_middle)
    def _():
        for j in range(2):
            up[j].wait_recv()
            own_p[2 * other + j] = plus(own_p[2 * other + j], rb_p[j]).astype(BF16)
            down[j].start()

    stage_c(down_work)
    stage_b(up_work)
    bx.wait_recv()

    def fold_x(i):
        yy, tt = i // 4, lax.rem(i, 4)
        wb1[yy, tt] = plus(dwg[yy, x, tt], wb1[yy, tt]).astype(BF16)

    each(8, fold_x)
    cy = cps.to(wb1.at[1 - y], wc.at[0:4], me.across_y)
    begin(cy)
    by.wait_recv()

    def fold_y(i):
        xx, tt = i // 4, lax.rem(i, 4)
        wb2[xx, tt] = plus(dwg[y, xx, 4 + tt], wb2[xx, tt]).astype(BF16)

    each(8, fold_y)
    cx = cps.to(wb2.at[1 - x], wc.at[4:8], me.across_x)
    begin(cx)
    stage_c(up_work)
    cy.wait_recv()
    cx.wait_recv()

    def fold_c(i):
        wc[i] = plus(wb1[y, i], wc[i]).astype(BF16)
        wc[4 + i] = plus(wb2[x, i], wc[4 + i]).astype(BF16)

    each(4, fold_c)
    moves = []
    for k in range(1, 8):
        peer = lax.rem(t + k, 8)
        moves.append(cps.to(wc.at[peer], wr.at[t], (me.d, peer)))
    begin(*moves)
    stat_all[-1].wait_recv()
    stats_out[...] = nsend[4] + nrecv[4]
    near.wait_recv()
    more_loads[4].wait()
    ig[mine] = resid[mine] + plus(own_p[z], ra_p[...])
    down[0].wait_recv()
    ig[other] = resid[other] + ro[...].astype(F32)
    stage_d(out_work)
    stage_d(down_work)
    wr[t] = wc[t]
    for move in moves:
        move.wait_recv()
    for g in range(4):
        wq[g] = plus(wr[g], wr[4 + g])
    stage_d(up_work)
    for cp in sent + stat_all + [move for u, move in dat_moves] + [moves[0] for refs, moves in works]:
        cp.wait_send()

    @pl.when(is_outer)
    def _():
        for cp in up:
            cp.wait_send()

    @pl.when(is_middle)
    def _():
        for cp in down:
            cp.wait_send()


def backward_half(da, stats, down_grad, rand, segq, extra, saved):
    features, length = saved[8].shape
    wide = extra[2].shape[1]
    dims = [(features // 32, features), (features // 32, wide), (wide // 32, features)]
    tok = da.shape[0] // 2
    bufs = []
    for i, (rows, cols) in enumerate(dims[::-1]):
        bufs += [
            pltpu.VMEM(((2, 2, 4, 2) if i else (2, 2, 4)) + (rows, cols), BF16),
            pltpu.VMEM((2, 2, 4, rows, cols), BF16),
            pltpu.VMEM((2, 2, rows, cols), BF16),
            pltpu.VMEM((2, 2, rows, cols), BF16),
            pltpu.VMEM((4, rows, cols), BF16),
            pltpu.VMEM((3, rows, cols), BF16),
        ]
    wrows = features // 32
    return pl.pallas_call(
        backward_kernel,
        in_specs=[VMEMSPACE] * 2 + [ANYSPACE] + [VMEMSPACE] * 2 + [ANYSPACE] * 15,
        out_specs=[VMEMSPACE] * 6,
        out_shape=[jax.ShapeDtypeStruct(dim, F32) for dim in dims]
        + [
            jax.ShapeDtypeStruct(stats.shape, F32),
            jax.ShapeDtypeStruct((2, tok, features), F32),
            jax.ShapeDtypeStruct((4, wrows, 768), F32),
        ],
        scratch_shapes=bufs
        + [pltpu.VMEM(a.shape, a.dtype) for a in saved + extra]
        + [
            pltpu.VMEM((8, tok, NH * HEAD), BF16),
            pltpu.VMEM((features, 2 * tok), BF16),
            pltpu.VMEM((length, NH * HEAD), BF16),
            pltpu.VMEM((length, 768), BF16),
            pltpu.VMEM((256, NH * TILE), BF16),
            pltpu.VMEM((256, NH * TILE), BF16),
            pltpu.VMEM((NH * TILE, NH * HEAD), BF16),
            pltpu.VMEM((NH * TILE, NH * HEAD), BF16),
            pltpu.VMEM((length, NH * HEAD), F32),
            pltpu.VMEM((length, NH * HEAD), F32),
            pltpu.VMEM((4, 2, tok, features), BF16),
            pltpu.VMEM((4, tok, features), BF16),
            pltpu.VMEM((4, tok, features), BF16),
            pltpu.VMEM((tok, features), BF16),
            pltpu.VMEM((2, tok, features), BF16),
            pltpu.VMEM((tok, features), BF16),
            pltpu.VMEM((2, 2, 8, wrows, 768), BF16),
            pltpu.VMEM((2, 4, wrows, 768), BF16),
            pltpu.VMEM((2, 4, wrows, 768), BF16),
            pltpu.VMEM((8, wrows, 768), BF16),
            pltpu.VMEM((8, wrows, 768), BF16),
            pltpu.VMEM((5,) + stats.shape, F32),
            pltpu.VMEM((5,) + stats.shape, F32),
            pltpu.SemaphoreType.DMA((90,)),
            pltpu.SemaphoreType.DMA((90,)),
            pltpu.SemaphoreType.DMA((19,)),
        ],
        compiler_params=pltpu.CompilerParams(
            collective_id=3, has_side_effects=True, vmem_limit_bytes=62 * 1024 * 1024
        ),
        name="backward_half",
    )(da, stats, down_grad, rand, segq, *extra, *saved)


def head_layout(
    inputs, segments, rand_blocks, w_qkv, w_out, w_up, w_down, norm_gain, norm_bias, out_grad
):
    seqs, tok, features = inputs.shape
    seq = lax.axis_size("seq")
    t = lax.axis_index("seq")
    groups = seq // seqs
    my_seq, my_group = t // groups, lax.rem(t, groups)
    width = features // groups
    shard = w_qkv.reshape(w_qkv.shape[0], 3, groups, width)
    shard = lax.dynamic_index_in_dim(shard, my_group, 2, keepdims=False)
    shard = jnp.pad(shard, ((0, 0), (0, 0), (0, 256 - width))).reshape(w_qkv.shape[0], 768)
    steps = seq * tok // TILE
    rand = lax.dynamic_slice_in_dim(
        lax.dynamic_index_in_dim(rand_blocks, my_seq, 0, keepdims=False), my_group * NH, NH, 1
    )
    rand = rand.reshape(steps, TILE // BLOCK, NH, 3).transpose(0, 3, 2, 1)
    rand = jnp.broadcast_to(rand[..., None], rand.shape + (BLOCK,)).reshape(steps, 3, NH * TILE)
    seg = lax.dynamic_index_in_dim(segments, my_seq, 0, keepdims=False)
    segq = seg.reshape(steps, 1, TILE)
    wof, wuf, wdf, att_flat, otile, lse, segk, qn, kn, vn, qt, kt, xst, wgf = forward_half(
        inputs, shard, w_out, w_up, w_down, rand, segq
    )
    full_out = wof.reshape(features, features)
    full_up = wuf.reshape(features, -1)
    full_down = wdf.reshape(-1, features)
    tokens_flat = inputs.reshape(seqs * tok, features)
    resid_one = tokens_flat.astype(F32) + product(att_flat, full_out)
    hidden_one, normed_one, inv_one = norm_forward(resid_one, norm_gain[0], norm_bias[0])
    hidden_low = hidden_one.astype(BF16)
    pre_act = product(hidden_low, full_up)
    activated = gelu_value(pre_act).astype(BF16)
    resid_two = hidden_one + product(activated, full_down)
    result, normed_two, inv_two = norm_forward(resid_two, norm_gain[1], norm_bias[1])
    grad_rows = out_grad.reshape(seqs * tok, features).astype(F32)
    grad_resid_two, gain_two, shift_two = norm_backward(
        grad_rows, normed_two, inv_two, norm_gain[1]
    )
    grad_branch = grad_resid_two.astype(BF16)
    grad_down_w = product_tn(activated, grad_branch).astype(BF16)
    grad_pre = (product_nt(grad_branch, full_down) * gelu_slope(pre_act)).astype(BF16)
    grad_hidden = grad_resid_two + product_nt(grad_pre, full_up)
    grad_resid_one, gain_one, shift_one = norm_backward(
        grad_hidden, normed_one, inv_one, norm_gain[0]
    )
    grad_mix = grad_resid_one.astype(BF16)
    stats = jnp.stack([gain_one, gain_two, shift_one, shift_two])
    grad_down_w = grad_down_w.reshape(2, 2, 4, 2, grad_down_w.shape[0] // 32, features)
    out_sum, up_sum, down_sum, stats, ig, wq = backward_half(
        grad_mix, stats, grad_down_w, rand, segq,
        (wof, hidden_low, grad_pre, att_flat, grad_resid_one.reshape(seqs, tok, features)),
        (kn, vn, kt, segk, qn, qt, otile, lse, xst, wgf),
    )
    wq = wq.reshape(groups, features // 32, 3, 256)[..., :width].transpose(1, 2, 0, 3)
    mine = lax.axis_index("dp") * seq + t
    stats = lax.dynamic_slice_in_dim(stats, mine * (features // 32), features // 32, 1)
    return (
        result.astype(BF16).reshape(seqs, tok, features),
        ig,
        wq.reshape(features // 32, 3 * features),
        out_sum,
        up_sum,
        down_sum,
        stats[:2],
        stats[2:],
    )


def solution(mesh):
    in_specs = (
        P("dp", "seq", None),
        P("dp", None),
        P("dp", None, None, None),
        P("dp", None),
        P("dp", None),
        P("dp", None),
        P("dp", None),
        P(),
        P(),
        P("dp", "seq", None),
    )
    out_specs = (
        P("dp", "seq", None),
        P("dp", "seq", None),
        P(("dp", "seq"), None),
        P(("dp", "seq"), None),
        P(("dp", "seq"), None),
        P(("dp", "seq"), None),
        P(None, ("dp", "seq")),
        P(None, ("dp", "seq")),
    )
    fits = mesh.shape["dp"] == 4 and mesh.shape["seq"] == 8
    return jax.shard_map(
        head_layout if fits else per_device, mesh=mesh, in_specs=in_specs, out_specs=out_specs, check_vma=False
    )
```

```python
import functools
import jax
import jax.numpy as jnp
import numpy as np
from jax import lax
from jax.experimental import pallas as pl
from jax.experimental.pallas import tpu as pltpu
from jax.sharding import PartitionSpec as P

H = 12
HEAD = 64
BLOCK = 64
R = 3
MICRO = 2


norm_eps = 1e-05
masked_score = -1e30
root_half = 0.7071067811865476
inv_root_two_pi = 0.3989422804014327


def padded(cells, sides, width):
    for axis, dim in sides:
        count = lax.axis_size(axis)
        ends = count - 1
        head = lax.slice_in_dim(cells, 0, width, axis=dim)
        tail = lax.slice_in_dim(cells, cells.shape[dim] - width, cells.shape[dim], axis=dim)
        cells = jnp.concatenate(
            [
                lax.ppermute(tail, axis, [(i, (i + 1) % count) for i in range(ends)]),
                cells,
                lax.ppermute(head, axis, [((i + 1) % count, i) for i in range(ends)]),
            ],
            axis=dim,
        )
    return cells


def from_root(x, axis, root):
    mine = lax.axis_index(axis) == root
    return lax.psum(jnp.where(mine, x, jnp.zeros_like(x)), axis)


def merged(x, axis, combine):
    everything = jax.tree.map(lambda part: lax.all_gather(part, axis), x)
    initial = jax.tree.map(lambda part: part[0], everything)

    def step(k, so_far):
        return combine(so_far, jax.tree.map(lambda part: part[k], everything))

    return lax.fori_loop(1, lax.axis_size(axis), step, initial)


def product(left_side, right_side):
    return jnp.dot(left_side, right_side, preferred_element_type=jnp.float32)


def product_tn(left_side, right_side):
    return lax.dot_general(
        left_side, right_side, (((0,), (0,)), ((), ())), preferred_element_type=jnp.float32
    )


def product_nt(left_side, right_side):
    return lax.dot_general(
        left_side, right_side, (((1,), (1,)), ((), ())), preferred_element_type=jnp.float32
    )


def gelu_value(pre_act):
    return 0.5 * pre_act * (1.0 + lax.erf(pre_act * root_half))


def gelu_slope(pre_act):
    return (
        0.5 * (1.0 + lax.erf(pre_act * root_half))
        + pre_act * jnp.exp(-0.5 * pre_act * pre_act) * inv_root_two_pi
    )


def norm_forward(residual, gain_row, shift_row):
    mean_row = jnp.mean(residual, axis=-1, keepdims=True)
    centred = residual - mean_row
    variance = jnp.mean(centred * centred, axis=-1, keepdims=True)
    inv_std = lax.rsqrt(variance + norm_eps)
    normed = centred * inv_std
    return (normed * gain_row + shift_row, normed, inv_std)


def norm_backward(grad_rows, normed, inv_std, gain_row):
    scaled = grad_rows * gain_row
    back_rows = inv_std * (
        scaled
        - jnp.mean(scaled, axis=-1, keepdims=True)
        - normed * jnp.mean(scaled * normed, axis=-1, keepdims=True)
    )
    return (back_rows, jnp.sum(grad_rows * normed, axis=0), jnp.sum(grad_rows, axis=0))


def merge_stats(first_pair, second_pair):
    joint_max = jnp.maximum(first_pair[0], second_pair[0])
    joint_sum = first_pair[1] * jnp.exp(first_pair[0] - joint_max) + second_pair[1] * jnp.exp(
        second_pair[0] - joint_max
    )
    return (joint_max, joint_sum)


def local_scores(query_heads, shared_keys, random_keys, shared_ok, random_ok, scale_factor):
    part_shared = jnp.einsum(
        "sbqhd,sbkhd->sbhqk", query_heads, shared_keys, preferred_element_type=jnp.float32
    )
    part_random = jnp.einsum(
        "sbqhd,sbhkd->sbhqk", query_heads, random_keys, preferred_element_type=jnp.float32
    )
    scores = jnp.concatenate([part_shared, part_random], axis=4) * scale_factor
    allowed = jnp.concatenate(
        [jnp.broadcast_to(shared_ok[:, :, None], part_shared.shape), random_ok], axis=4
    )
    return jnp.where(allowed, scores, masked_score)


def per_device(
    inputs, segments, rand_blocks, w_qkv, w_out, w_up, w_down, norm_gain, norm_bias, out_grad
):
    seq_total, tok_dev, features = inputs.shape
    devices = lax.axis_size("seq")
    my_index = lax.axis_index("seq")
    blocks_dev = tok_dev // BLOCK
    blocks_all = blocks_dev * devices
    entries = blocks_dev * H * R
    capacity = max(2, entries // devices + 1)
    per_micro = seq_total // MICRO
    glob_rows = 2 * BLOCK
    shared_count = 5 * BLOCK
    scale_factor = HEAD ** (-0.5)
    token_rows = per_micro * tok_dev
    owner_flag = (my_index == 0).astype(jnp.float32)
    row_global = my_index * tok_dev + jnp.arange(tok_dev, dtype=jnp.int32) < glob_rows
    window_index = np.arange(blocks_dev)[:, None] + np.arange(3)[None, :]
    win_blocks = (
        my_index * blocks_dev
        + jnp.arange(blocks_dev, dtype=jnp.int32)[:, None]
        + jnp.arange(-1, 2, dtype=jnp.int32)[None, :]
    )
    win_inside = (win_blocks >= 0) & (win_blocks < blocks_all)
    win_clipped = jnp.clip(win_blocks, 0, blocks_all - 1)
    entry_heads = jnp.arange(entries, dtype=jnp.int32) // R % H
    slot_ids = jnp.arange(capacity, dtype=jnp.int32)
    earlier = jnp.arange(entries)[None, :] < jnp.arange(entries)[:, None]
    seq_ids = jnp.arange(per_micro, dtype=jnp.int32)
    grad_qkv_w = jnp.zeros((features, 3 * features), jnp.float32)
    grad_out_w = jnp.zeros((features, features), jnp.float32)
    grad_up_w = jnp.zeros((features, w_up.shape[1]), jnp.float32)
    grad_down_w = jnp.zeros((w_down.shape[0] * lax.axis_size("dp"), features), jnp.float32)
    gain_acc = jnp.zeros((2, features), jnp.float32)
    shift_acc = jnp.zeros((2, features), jnp.float32)
    output_parts = []
    input_parts = []
    for micro_step in range(MICRO):
        start_seq = micro_step * per_micro
        tokens_in = inputs[start_seq : start_seq + per_micro]
        seg_micro = segments[start_seq : start_seq + per_micro]
        rand_micro = rand_blocks[start_seq : start_seq + per_micro]
        cotangent = out_grad[start_seq : start_seq + per_micro]
        full_qkv, full_out, full_up, full_down = (
            lax.all_gather(w_qkv, "dp", axis=0, tiled=True),
            lax.all_gather(w_out, "dp", axis=0, tiled=True),
            lax.all_gather(w_up, "dp", axis=0, tiled=True),
            lax.all_gather(w_down, "dp", axis=0, tiled=True),
        )
        tokens_flat = tokens_in.reshape(token_rows, features)
        qkv_rows = (
            product(tokens_flat, full_qkv)
            .astype(jnp.bfloat16)
            .reshape(per_micro, tok_dev, 3 * features)
        )
        queries = qkv_rows[..., :features]
        keyvals = qkv_rows[..., features:]
        extended = padded(keyvals, (("seq", 1),), BLOCK)
        global_block = from_root(qkv_rows[:, :glob_rows], "seq", 0)
        requests = rand_micro.reshape(per_micro, devices, entries)
        owners = requests // blocks_dev
        local_block = requests % blocks_dev
        same_owner = owners[:, :, :, None] == owners[:, :, None, :]
        slot_rank = jnp.sum(same_owner & earlier[None, None], axis=3)
        slot_hit = ((owners == my_index)[..., None] & (slot_rank[..., None] == slot_ids)).astype(
            jnp.int32
        )
        slot_live = jnp.sum(slot_hit, axis=2)
        slot_piece = jnp.sum(slot_hit * (local_block * H + entry_heads)[..., None], axis=2)
        piece_index = jnp.transpose(slot_piece, (1, 2, 0))
        live_mask = jnp.transpose(slot_live, (1, 2, 0))
        pieces = (
            keyvals.reshape(per_micro, blocks_dev, BLOCK, 2, H, HEAD)
            .transpose(0, 1, 4, 2, 3, 5)
            .reshape(per_micro, blocks_dev * H, BLOCK, 2 * HEAD)
        )
        outgoing = pieces[seq_ids[None, None, :], piece_index]
        outgoing = jnp.where(live_mask[..., None, None] > 0, outgoing, jnp.zeros((), jnp.bfloat16))
        outgoing = outgoing.reshape(devices * capacity, per_micro, BLOCK, 2 * HEAD)
        incoming = lax.all_to_all(outgoing, "seq", split_axis=0, concat_axis=0, tiled=True)
        my_owner = jnp.take(owners, my_index, axis=1)
        my_rank = jnp.take(slot_rank, my_index, axis=1)
        my_request = jnp.take(requests, my_index, axis=1)
        positions = my_owner * capacity + my_rank
        fetched = incoming[positions, seq_ids[:, None]].reshape(
            per_micro, blocks_dev, H, R, BLOCK, 2, HEAD
        )
        random_keys = fetched[..., 0, :].reshape(per_micro, blocks_dev, H, R * BLOCK, HEAD)
        random_vals = fetched[..., 1, :].reshape(per_micro, blocks_dev, H, R * BLOCK, HEAD)
        seg_blocks = seg_micro.reshape(per_micro, blocks_all, BLOCK)
        query_seg = lax.dynamic_slice_in_dim(seg_micro, my_index * tok_dev, tok_dev, 1).reshape(
            per_micro, blocks_dev, BLOCK
        )
        window_seg = seg_blocks[:, win_clipped].reshape(per_micro, blocks_dev, 3 * BLOCK)
        window_ok = (query_seg[..., :, None] == window_seg[:, :, None, :]) & jnp.repeat(
            win_inside, BLOCK, axis=1
        )[None, :, None, :]
        shared_ok = jnp.concatenate(
            [window_ok, jnp.ones((per_micro, blocks_dev, BLOCK, glob_rows), bool)], axis=3
        )
        random_seg = seg_blocks[seq_ids[:, None], my_request].reshape(
            per_micro, blocks_dev, H, R * BLOCK
        )
        random_ok = query_seg[:, :, None, :, None] == random_seg[:, :, :, None, :]
        ext_blocks = extended.reshape(per_micro, blocks_dev + 2, BLOCK, 2 * features)
        window_kv = ext_blocks[:, window_index].reshape(
            per_micro, blocks_dev, 3 * BLOCK, 2 * features
        )
        glob_kv = jnp.broadcast_to(
            global_block[:, None, :, features:], (per_micro, blocks_dev, glob_rows, 2 * features)
        )
        shared_kv = jnp.concatenate([window_kv, glob_kv], axis=2)
        shared_keys = shared_kv[..., :features].reshape(
            per_micro, blocks_dev, shared_count, H, HEAD
        )
        shared_vals = shared_kv[..., features:].reshape(
            per_micro, blocks_dev, shared_count, H, HEAD
        )
        query_heads = queries.reshape(per_micro, blocks_dev, BLOCK, H, HEAD)
        scores = local_scores(
            query_heads, shared_keys, random_keys, shared_ok, random_ok, scale_factor
        )
        row_max = jnp.max(scores, axis=4, keepdims=True)
        exp_terms = jnp.exp(scores - row_max)
        row_sum = jnp.sum(exp_terms, axis=4, keepdims=True)
        local_probs = exp_terms / row_sum
        log_norm = row_max + jnp.log(row_sum)
        local_weights = local_probs.astype(jnp.bfloat16)
        local_att = jnp.einsum(
            "sbhqk,sbkhd->sbqhd",
            local_weights[..., :shared_count],
            shared_vals,
            preferred_element_type=jnp.float32,
        )
        local_att = local_att + jnp.einsum(
            "sbhqk,sbhkd->sbqhd",
            local_weights[..., shared_count:],
            random_vals,
            preferred_element_type=jnp.float32,
        )
        local_att = local_att.reshape(per_micro, tok_dev, features)
        glob_query = global_block[..., :features].reshape(per_micro, glob_rows, H, HEAD)
        local_keys = keyvals[..., :features].reshape(per_micro, tok_dev, H, HEAD)
        local_vals = keyvals[..., features:].reshape(per_micro, tok_dev, H, HEAD)
        glob_scores = (
            jnp.einsum(
                "sqhd,skhd->shqk", glob_query, local_keys, preferred_element_type=jnp.float32
            )
            * scale_factor
        )
        part_max = jnp.max(glob_scores, axis=3)
        part_sum = jnp.sum(jnp.exp(glob_scores - part_max[..., None]), axis=3)
        glob_max, glob_sum = merged((part_max, part_sum), "seq", merge_stats)
        glob_lse = glob_max + jnp.log(glob_sum)
        glob_probs = jnp.exp(glob_scores - glob_lse[..., None])
        glob_weights = glob_probs.astype(jnp.bfloat16)
        glob_part = jnp.einsum(
            "shqk,skhd->sqhd", glob_weights, local_vals, preferred_element_type=jnp.float32
        ).reshape(per_micro, glob_rows, features)
        glob_out = lax.psum(glob_part, "seq")
        glob_full = jnp.concatenate(
            [glob_out, jnp.zeros((per_micro, tok_dev - glob_rows, features), jnp.float32)], axis=1
        )
        attention = jnp.where(row_global[None, :, None], glob_full, local_att).astype(jnp.bfloat16)
        att_flat = attention.reshape(token_rows, features)
        resid_one = tokens_flat.astype(jnp.float32) + product(att_flat, full_out)
        hidden_one, normed_one, inv_one = norm_forward(resid_one, norm_gain[0], norm_bias[0])
        hidden_low = hidden_one.astype(jnp.bfloat16)
        pre_act = product(hidden_low, full_up)
        activated = gelu_value(pre_act).astype(jnp.bfloat16)
        resid_two = hidden_one + product(activated, full_down)
        result, normed_two, inv_two = norm_forward(resid_two, norm_gain[1], norm_bias[1])
        output_parts.append(result.astype(jnp.bfloat16).reshape(per_micro, tok_dev, features))
        grad_rows = cotangent.reshape(token_rows, features).astype(jnp.float32)
        grad_resid_two, gain_two, shift_two = norm_backward(
            grad_rows, normed_two, inv_two, norm_gain[1]
        )
        grad_branch = grad_resid_two.astype(jnp.bfloat16)
        grad_down_w = grad_down_w + product_tn(activated, grad_branch)
        grad_pre = (product_nt(grad_branch, full_down) * gelu_slope(pre_act)).astype(jnp.bfloat16)
        grad_up_w = grad_up_w + product_tn(hidden_low, grad_pre)
        grad_hidden = grad_resid_two + product_nt(grad_pre, full_up)
        grad_resid_one, gain_one, shift_one = norm_backward(
            grad_hidden, normed_one, inv_one, norm_gain[0]
        )
        grad_mix = grad_resid_one.astype(jnp.bfloat16)
        grad_out_w = grad_out_w + product_tn(att_flat, grad_mix)
        grad_att = (
            product_nt(grad_mix, full_out)
            .astype(jnp.bfloat16)
            .reshape(per_micro, tok_dev, features)
        )
        gain_acc = gain_acc + jnp.stack([gain_one, gain_two])
        shift_acc = shift_acc + jnp.stack([shift_one, shift_two])
        grad_local = jnp.where(
            row_global[None, :, None], jnp.zeros((), jnp.bfloat16), grad_att
        ).reshape(per_micro, blocks_dev, BLOCK, H, HEAD)
        scores = local_scores(
            query_heads, shared_keys, random_keys, shared_ok, random_ok, scale_factor
        )
        local_probs = jnp.exp(scores - log_norm)
        local_weights = local_probs.astype(jnp.bfloat16)
        grad_prob = jnp.concatenate(
            [
                jnp.einsum(
                    "sbqhd,sbkhd->sbhqk",
                    grad_local,
                    shared_vals,
                    preferred_element_type=jnp.float32,
                ),
                jnp.einsum(
                    "sbqhd,sbhkd->sbhqk",
                    grad_local,
                    random_vals,
                    preferred_element_type=jnp.float32,
                ),
            ],
            axis=4,
        )
        row_delta = jnp.sum(local_probs * grad_prob, axis=4, keepdims=True)
        grad_score = (local_probs * (grad_prob - row_delta)).astype(jnp.bfloat16)
        grad_query = jnp.einsum(
            "sbhqk,sbkhd->sbqhd",
            grad_score[..., :shared_count],
            shared_keys,
            preferred_element_type=jnp.float32,
        )
        grad_query = (
            grad_query
            + jnp.einsum(
                "sbhqk,sbhkd->sbqhd",
                grad_score[..., shared_count:],
                random_keys,
                preferred_element_type=jnp.float32,
            )
        ) * scale_factor
        grad_key_shared = (
            jnp.einsum(
                "sbhqk,sbqhd->sbkhd",
                grad_score[..., :shared_count],
                query_heads,
                preferred_element_type=jnp.float32,
            )
            * scale_factor
        )
        grad_val_shared = jnp.einsum(
            "sbhqk,sbqhd->sbkhd",
            local_weights[..., :shared_count],
            grad_local,
            preferred_element_type=jnp.float32,
        )
        grad_key_random = (
            jnp.einsum(
                "sbhqk,sbqhd->sbhkd",
                grad_score[..., shared_count:],
                query_heads,
                preferred_element_type=jnp.float32,
            )
            * scale_factor
        )
        grad_val_random = jnp.einsum(
            "sbhqk,sbqhd->sbhkd",
            local_weights[..., shared_count:],
            grad_local,
            preferred_element_type=jnp.float32,
        )
        grad_shared = jnp.concatenate(
            [
                grad_key_shared.reshape(per_micro, blocks_dev, shared_count, features),
                grad_val_shared.reshape(per_micro, blocks_dev, shared_count, features),
            ],
            axis=3,
        )
        grad_window = grad_shared[:, :, : 3 * BLOCK].reshape(
            per_micro, blocks_dev, 3, BLOCK, 2 * features
        )
        ext_grad = jnp.zeros((per_micro, blocks_dev + 2, BLOCK, 2 * features), jnp.float32)
        for offset in range(3):
            ext_grad = ext_grad.at[:, offset : offset + blocks_dev].add(grad_window[:, :, offset])
        grad_glob_keys = jnp.sum(grad_shared[:, :, 3 * BLOCK :], axis=1)
        grad_random = jnp.stack([grad_key_random, grad_val_random], axis=4).reshape(
            per_micro, entries, BLOCK, 2 * HEAD
        )
        returned = (
            jnp.zeros((devices * capacity, per_micro, BLOCK, 2 * HEAD), jnp.float32)
            .at[positions, seq_ids[:, None]]
            .set(grad_random)
        )
        arrived = lax.all_to_all(
            returned.astype(jnp.bfloat16), "seq", split_axis=0, concat_axis=0, tiled=True
        ).astype(returned.dtype)
        arrived = arrived.reshape(devices, capacity, per_micro, BLOCK, 2 * HEAD) * live_mask[
            ..., None, None
        ].astype(jnp.float32)
        piece_grad = (
            jnp.zeros((per_micro, blocks_dev * H, BLOCK, 2 * HEAD), jnp.float32)
            .at[seq_ids[None, None, :], piece_index]
            .add(arrived)
        )
        piece_grad = (
            piece_grad.reshape(per_micro, blocks_dev, H, BLOCK, 2, HEAD)
            .transpose(0, 1, 3, 4, 2, 5)
            .reshape(per_micro, tok_dev, 2 * features)
        )
        rim_pair = jnp.concatenate([ext_grad[:, 0], ext_grad[:, blocks_dev + 1]], axis=1)
        rim_back = padded(rim_pair.astype(jnp.bfloat16), (("seq", 1),), BLOCK).astype(
            rim_pair.dtype
        )
        grad_kv = (
            ext_grad[:, 1 : blocks_dev + 1].reshape(per_micro, tok_dev, 2 * features) + piece_grad
        )
        grad_kv = grad_kv.at[:, :BLOCK].add(rim_back[:, :BLOCK])
        grad_kv = grad_kv.at[:, tok_dev - BLOCK :].add(rim_back[:, 3 * BLOCK :])
        grad_glob = from_root(grad_att[:, :glob_rows], "seq", 0)
        grad_glob_heads = grad_glob.reshape(per_micro, glob_rows, H, HEAD)
        glob_scores = (
            jnp.einsum(
                "sqhd,skhd->shqk", glob_query, local_keys, preferred_element_type=jnp.float32
            )
            * scale_factor
        )
        glob_probs = jnp.exp(glob_scores - glob_lse[..., None])
        glob_weights = glob_probs.astype(jnp.bfloat16)
        glob_grad_prob = jnp.einsum(
            "sqhd,skhd->shqk", grad_glob_heads, local_vals, preferred_element_type=jnp.float32
        )
        glob_delta = lax.psum(jnp.sum(glob_probs * glob_grad_prob, axis=3), "seq")
        glob_grad_score = (glob_probs * (glob_grad_prob - glob_delta[..., None])).astype(
            jnp.bfloat16
        )
        glob_grad_query = (
            jnp.einsum(
                "shqk,skhd->sqhd", glob_grad_score, local_keys, preferred_element_type=jnp.float32
            )
            * scale_factor
        )
        glob_grad_key = (
            jnp.einsum(
                "shqk,sqhd->skhd", glob_grad_score, glob_query, preferred_element_type=jnp.float32
            )
            * scale_factor
        )
        glob_grad_val = jnp.einsum(
            "shqk,sqhd->skhd", glob_weights, grad_glob_heads, preferred_element_type=jnp.float32
        )
        grad_kv = grad_kv + jnp.concatenate(
            [
                glob_grad_key.reshape(per_micro, tok_dev, features),
                glob_grad_val.reshape(per_micro, tok_dev, features),
            ],
            axis=2,
        )
        summed_query, summed_keys = lax.psum(
            (glob_grad_query.reshape(per_micro, glob_rows, features), grad_glob_keys), "seq"
        )
        grad_kv = grad_kv.at[:, :glob_rows].add(owner_flag * summed_keys)
        grad_queries = (
            grad_query.reshape(per_micro, tok_dev, features)
            .at[:, :glob_rows]
            .add(owner_flag * summed_query)
        )
        grad_qkv_rows = (
            jnp.concatenate([grad_queries, grad_kv], axis=2)
            .astype(jnp.bfloat16)
            .reshape(token_rows, 3 * features)
        )
        grad_qkv_w = grad_qkv_w + product_tn(tokens_flat, grad_qkv_rows)
        input_rows = grad_resid_one + product_nt(grad_qkv_rows, full_qkv)
        input_parts.append(input_rows.reshape(per_micro, tok_dev, features))
    summed = (
        lax.psum_scatter(grad_qkv_w, ("dp", "seq"), scatter_dimension=0, tiled=True),
        lax.psum_scatter(grad_out_w, ("dp", "seq"), scatter_dimension=0, tiled=True),
        lax.psum_scatter(grad_up_w, ("dp", "seq"), scatter_dimension=0, tiled=True),
        lax.psum_scatter(grad_down_w, ("dp", "seq"), scatter_dimension=0, tiled=True),
        lax.psum_scatter(gain_acc, ("dp", "seq"), scatter_dimension=1, tiled=True),
        lax.psum_scatter(shift_acc, ("dp", "seq"), scatter_dimension=1, tiled=True),
    )
    return (
        jnp.concatenate(output_parts, axis=0),
        jnp.concatenate(input_parts, axis=0),
        summed[0],
        summed[1],
        summed[2],
        summed[3],
        summed[4],
        summed[5],
    )


TILE = 128
NH = 3
CH = 256
LOG2E = 1.4426950408889634
SCALE2 = HEAD ** (-0.5) * LOG2E
NEG = -1e30
F32 = jnp.float32
BF16 = jnp.bfloat16


def nt(a, b):
    return lax.dot_general(a, b, (((1,), (1,)), ((), ())), preferred_element_type=F32)


def nn(a, b):
    return jnp.dot(a, b, preferred_element_type=F32)


MESH = pl.DeviceIdType.MESH
ANYSPACE = pl.BlockSpec(memory_space=pl.ANY)
VMEMSPACE = pl.BlockSpec(memory_space=pltpu.VMEM)


class Copies:
    def __init__(self, send, recv):
        self.send = send
        self.recv = recv
        self.used = 0

    def to(self, src, dst, device):
        index = self.used
        self.used += 1
        return pltpu.make_async_remote_copy(
            src_ref=src, dst_ref=dst, send_sem=self.send.at[index], recv_sem=self.recv.at[index],
            device_id=device, device_id_type=MESH,
        )


class Place:
    def __init__(self):
        self.d = lax.axis_index("dp")
        self.t = lax.axis_index("seq")
        self.x = lax.rem(self.d, 2)
        self.y = self.d // 2
        self.c = lax.rem(self.t, 2)
        self.z = self.t // 2
        self.half = self.z // 2
        self.xn = self.d + 1 - 2 * self.x
        self.yn = self.d + 2 - 4 * self.y
        self.diag = 3 - self.d
        self.pair_z = self.z + 1 - 2 * lax.rem(self.z, 2)
        self.across_x = (self.xn, self.t)
        self.across_y = (self.yn, self.t)
        self.partner = (self.d, self.t + 1 - 2 * self.c)

    def at_z(self, z):
        return (self.d, 2 * z + self.c)


def greet(devices):
    barrier = pltpu.get_barrier_semaphore()
    for device in devices:
        pl.semaphore_signal(barrier, inc=1, device_id=device, device_id_type=MESH)


def met(devices):
    pl.semaphore_wait(pltpu.get_barrier_semaphore(), len(devices))


def tile_tables(tile, rand_ref, segq_ref, blocks):
    wide = NH * TILE
    key = lax.broadcasted_iota(jnp.int32, (blocks, wide), 0)
    lane = lax.broadcasted_iota(jnp.int32, (blocks, wide), 1)
    query = tile * (TILE // BLOCK) + lax.rem(lane, TILE) // BLOCK
    near = (key - query) * (key - query) <= 1
    hits = near.astype(F32)
    for r in range(rand_ref.shape[1]):
        hits = hits + (rand_ref[tile, r : r + 1, :] == key).astype(F32)
    fixed = jnp.logical_or(query < 2, key < 2)
    count = jnp.where(query < 2, 0.0, hits) + fixed.astype(F32)
    on = jnp.where(count > 0.0, jnp.log2(jnp.maximum(count, 1.0)), NEG)
    off = jnp.where(fixed, 0.0, NEG)
    return on, off, segq_ref[tile]


def biased(s, mask, on, off, first_block):
    rows = []
    for j in range(s.shape[0] // BLOCK):
        kb = first_block + j
        m3 = jnp.concatenate([mask[BLOCK * j : BLOCK * (j + 1)]] * NH, axis=1)
        bias = jnp.where(m3, on[kb : kb + 1, :], off[kb : kb + 1, :])
        rows.append(s[BLOCK * j : BLOCK * (j + 1)] * SCALE2 + bias)
    return jnp.concatenate(rows, axis=0)


def fill_segments(segq, segk):
    steps = segq.shape[0]
    for i in range(steps):
        column = jnp.broadcast_to(segq[i].astype(F32), (8, TILE)).T[:, :1]
        segk[TILE * i : TILE * (i + 1), :] = jnp.broadcast_to(column, (TILE, TILE)).astype(jnp.int32)


def fill_requests(requests, rand, half, group):
    row = lax.broadcasted_iota(jnp.int32, (32, TILE), 0)
    entry = lax.broadcasted_iota(jnp.int32, (32, TILE), 1)
    slot = lax.rem(row, 8)
    pick = jnp.logical_and(slot < 3, entry == 9 * group + 3 * (row // 8) + slot)
    chosen = jnp.where(half == 0, requests[0], requests[1])
    mine = nn(pick.astype(F32).astype(BF16), chosen)
    steps = rand.shape[0]
    block = lax.broadcasted_iota(jnp.int32, (TILE, steps * TILE), 0)
    token = lax.broadcasted_iota(jnp.int32, (TILE, steps * TILE), 1)
    spread = nn(mine.astype(BF16), (token // BLOCK == block).astype(F32).astype(BF16))
    for i in range(steps):
        for h in range(NH):
            rand[i, :, TILE * h : TILE * (h + 1)] = spread[
                8 * h : 8 * h + 3, TILE * i : TILE * (i + 1)
            ].astype(jnp.int32)


def forward_tile(tile, rand, segq, segk, qt, kn, vt, q3, tbuf, att, otile, lse):
    length = kn.shape[0]
    chunks = length // CH
    here = pl.ds(pl.multiple_of(tile * TILE, TILE), TILE)
    on, off, seg = tile_tables(tile, rand, segq, length // BLOCK)
    for h in range(NH):
        q3[HEAD * h : HEAD * (h + 1), TILE * h : TILE * (h + 1)] = qt[
            HEAD * h : HEAD * (h + 1), here
        ]
    top = jnp.full((8, NH * TILE), NEG, F32)
    for j in range(chunks):
        rows = slice(CH * j, CH * (j + 1))
        s = nn(kn[rows, :], q3[...])
        t = biased(s, segk[rows, :] == seg, on, off, CH // BLOCK * j)
        tbuf[rows, :] = t
        top = jnp.maximum(top, jnp.max(t.reshape(CH // 8, 8, NH * TILE), axis=0))
    peak = jnp.max(top, axis=0, keepdims=True)
    total = jnp.zeros((8, NH * TILE), F32)
    out = jnp.zeros((256, NH * TILE), F32)
    for j in range(chunks):
        rows = slice(CH * j, CH * (j + 1))
        p = jnp.exp2(tbuf[rows, :] - peak)
        total = total + jnp.sum(p.reshape(CH // 8, 8, NH * TILE), axis=0)
        out = out + nn(vt[:, rows], p.astype(BF16))
    weight = jnp.sum(total, axis=0, keepdims=True)
    lse[tile] = peak + jnp.log2(weight)
    inv = 1.0 / weight
    heads = [
        out[HEAD * h : HEAD * (h + 1), TILE * h : TILE * (h + 1)] * inv[:, TILE * h : TILE * (h + 1)]
        for h in range(NH)
    ]
    merged = jnp.concatenate(heads, axis=0)
    otile[tile] = merged
    att[here, :] = merged.T.astype(BF16)


def unit_place(me, u):
    low = lax.rem(me.z, 2)
    return 2 * lax.rem(me.half + 1 + u // 2, 2) + lax.rem(low + 1 + u, 2)


def forward_kernel(*refs):
    (x, w, wo, wu, wd, requests, seg), refs = refs[:7], refs[7:]
    outs, refs = refs[:14], refs[14:]
    (rand, segq), refs = refs[:2], refs[2:]
    wof, wuf, wdf, att_out, otile_o, lse_o, segk_o, qn_o, kn_o, vn_o, qt_o, kt_o, xst_o, wgf_o = outs
    (xs, wgf, bo, bu, bd, att, home, otile, lse, segk), refs = refs[:10], refs[10:]
    (qn, kn, vn, qt, kt, vt, xst, q3, tbuf), refs = refs[:9], refs[9:]
    send, recv, xsend, xrecv, local = refs
    me = Place()
    d, t, c, z = me.d, me.t, me.c, me.z
    mine, other = me.half, 1 - me.half
    is_middle = z == 1 + me.half
    tok = x.shape[1]
    length = xs.shape[0]
    steps = length // TILE
    per_unit = 2 * tok // TILE
    loads = [
        pltpu.make_async_copy(src, dst, local.at[i])
        for i, (src, dst) in enumerate(((wo, bo), (wu, bu), (wd, bd)))
    ]
    for load in loads:
        load.start()
    friends = [me.across_x, me.across_y] + [(d, lax.rem(t + k, 8)) for k in range(1, 8)]
    greet(friends)
    shard = w.shape[0]
    wrows = lambda index, start, size: pl.ds(pl.multiple_of(index * shard + start, size), size)
    lane = lax.broadcasted_iota(jnp.int32, (shard, 256), 1)
    for k in range(3):
        first = w.shape[1] // 3 * k + 2 * NH * HEAD * lax.rem(z, 2) + TILE * c
        window = w[:, pl.ds(pl.multiple_of(first, TILE), 256)].astype(F32)
        moved = jnp.concatenate([window[:, HEAD:], window[:, :HEAD]], axis=1)
        mine_k = jnp.where(lane < NH * HEAD, jnp.where(c == 0, window, moved), 0.0)
        wgf[wrows(d, 0, shard), 256 * k : 256 * (k + 1)] = mine_k.astype(BF16)
    met(friends)
    cps = Copies(send, recv)
    sent = []

    def begin(*copies):
        for cp in copies:
            cp.start()
            sent.append(cp)

    def rows_of(index):
        return pl.ds(pl.multiple_of(index * tok, tok), tok)

    half = shard // 2
    my_top, my_low = wrows(d, 0, half), wrows(d, half, half)
    wg_x0 = cps.to(wgf.at[my_top], wgf.at[my_top], me.across_x)
    wg_x1 = cps.to(wgf.at[my_low], wgf.at[my_low], me.across_x)
    wg_y0 = cps.to(wgf.at[my_low], wgf.at[my_low], me.across_y)
    wg_y1 = cps.to(wgf.at[my_top], wgf.at[my_top], me.across_y)
    near = cps.to(x.at[mine], xs.at[rows_of(t)], me.at_z(me.pair_z))
    give = cps.to(x.at[mine], xs.at[rows_of(t)], me.partner)
    far = pltpu.make_async_remote_copy(
        src_ref=x.at[other], dst_ref=xs.at[rows_of(t)], send_sem=xsend.at[0],
        recv_sem=xrecv.at[lax.rem(z, 2)], device_id=me.at_z(2 - me.half), device_id_type=MESH,
    )
    begin(wg_x0, wg_y0, far, wg_x1, wg_y1, near, give)
    heavy = []
    for w, full in ((wo, wof), (wu, wuf), (wd, wdf)):
        rows = w.shape[0] // 2
        part = pl.ds(pl.multiple_of(c * rows, rows), rows)
        to_x = cps.to(w.at[part], full.at[d, part], me.across_x)
        to_y = cps.to(w.at[part], full.at[d, part], me.across_y)
        heavy.append((full, rows, part, to_x, to_y))
    xn_top, yn_low = wrows(me.xn, 0, half), wrows(me.yn, half, half)
    wg_dy = cps.to(wgf.at[xn_top], wgf.at[xn_top], me.across_y)
    wg_dx = cps.to(wgf.at[yn_low], wgf.at[yn_low], me.across_x)
    wg_x0.wait_recv()
    begin(wg_dy)
    wg_y0.wait_recv()
    begin(wg_dx)
    for full, rows, part, to_x, to_y in heavy[:2]:
        begin(to_x, to_y)

    xs[rows_of(t), :] = x[mine]
    q3[...] = jnp.zeros_like(q3)
    seg_row = jnp.where(me.half == 0, seg[0:1, :], seg[1:2, :])
    for i in range(steps):
        segq[i] = seg_row[:, TILE * i : TILE * (i + 1)]
    fill_segments(segq, segk)
    fill_requests(requests, rand, me.half, lax.rem(t, 4))
    keeps = []
    for i, (load, buf, full) in enumerate(zip(loads, (bo, bu, bd), (wof, wuf, wdf))):
        load.wait()
        keep = pltpu.make_async_copy(buf, full.at[d], local.at[3 + i])
        keep.start()
        keeps.append(keep)

    def project(unit):
        rows = pl.ds(pl.multiple_of(unit * 2 * tok, 2 * tok), 2 * tok)
        both = nn(xs[rows, :], wgf[...])
        qf, kf, vf = both[:, :256], both[:, 256:512], both[:, 512:]
        qn[rows, :] = qf.astype(BF16)
        kn[rows, :] = kf.astype(BF16)
        vn[rows, :] = vf.astype(BF16)
        qt[:, rows] = qf.T.astype(BF16)
        kt[:, rows] = kf.T.astype(BF16)
        vt[:, rows] = vf.T.astype(BF16)
        xst[:, rows] = xs[rows, :].astype(F32).T.astype(BF16)

    wg_x1.wait_recv()
    wg_y1.wait_recv()
    wg_dy.wait_recv()
    wg_dx.wait_recv()
    give.wait_recv()
    near.wait_recv()
    near_rows = rows_of(2 * me.pair_z + c)
    pass_near = cps.to(xs.at[near_rows], xs.at[near_rows], me.partner)
    begin(pass_near)
    relays, onwards = [], []
    for j in range(2):
        src_rows = rows_of(2 * (2 * other + j) + c)
        relays.append(
            pltpu.make_async_remote_copy(
                src_ref=xs.at[src_rows], dst_ref=xs.at[src_rows], send_sem=xsend.at[1 + j],
                recv_sem=xrecv.at[j], device_id=me.at_z(me.pair_z), device_id_type=MESH,
            )
        )
        onwards.append(cps.to(xs.at[src_rows], xs.at[src_rows], me.partner))

    def forward_x(j):
        relays[j].wait_recv()
        pl.when(is_middle)(relays[j].start)
        begin(onwards[j])

    tail = []
    for full, rows, part, to_x, to_y in heavy:
        quarter = rows // 2
        lo = pl.ds(pl.multiple_of(c * rows, quarter), quarter)
        hi = pl.ds(pl.multiple_of(c * rows + quarter, quarter), quarter)
        tail.append(
            (
                to_x, to_y,
                cps.to(full.at[me.xn, lo], full.at[me.xn, lo], me.across_y),
                cps.to(full.at[me.xn, part], full.at[me.xn, part], me.partner),
                cps.to(full.at[me.yn, hi], full.at[me.yn, hi], me.across_x),
                cps.to(full.at[me.yn, part], full.at[me.yn, part], me.partner),
                cps.to(full.at[me.diag, part], full.at[me.diag, part], me.partner),
            )
        )

    def relay_weights(k):
        to_x, to_y, dy, px, dx, py, pd = tail[k]
        to_x.wait_recv()
        begin(dy, px)
        to_y.wait_recv()
        begin(dx, py)

    def relay_diag(k):
        to_x, to_y, dy, px, dx, py, pd = tail[k]
        dy.wait_recv()
        dx.wait_recv()
        begin(pd)

    def arrive(k):
        if k == 0:
            forward_x(0)
            relay_weights(0)
            begin(heavy[2][3], heavy[2][4])
        if k == 1:
            forward_x(1)
            pass_near.wait_recv()
        if k == 2:
            onwards[0].wait_recv()
        if k == 3:
            onwards[1].wait_recv()

    def project_step(k, carry):
        for i in range(4):
            pl.when(k == i)(functools.partial(arrive, i))
        unit = jnp.where(k < 2, 2 * mine + lax.rem(lax.rem(z, 2) + k, 2), 2 * other + k - 2)
        project(unit)
        return carry

    lax.fori_loop(0, 4, project_step, 0)
    saves = [
        pltpu.make_async_copy(src, dst, local.at[6 + i])
        for i, (src, dst) in enumerate(
            ((segk, segk_o), (qn, qn_o), (kn, kn_o), (vn, vn_o), (qt, qt_o), (kt, kt_o), (xst, xst_o), (wgf, wgf_o))
        )
    ]
    for save in saves:
        save.start()

    homes = []
    for u in range(4):
        unit = unit_place(me, u)
        for o in range(1 if u == 3 else 0, 2):
            to = 2 * unit + (c if o == 0 else 1 - c)
            homes.append((u, cps.to(att.at[rows_of(to)], home.at[t], (d, to))))

    def send_home(u):
        for v, move in homes:
            if u == v:
                move.start()

    def between(i):
        if i == 2:
            relay_weights(1)
        if i == per_unit:
            send_home(0)
        if i == per_unit + 1:
            relay_diag(0)
        if i == 2 * per_unit:
            send_home(1)
        if i == 3 * per_unit:
            send_home(2)
        if i == 3 * per_unit + 1:
            relay_weights(2)

    def tile_step(i, carry):
        for point in (2, per_unit, per_unit + 1, 2 * per_unit, 3 * per_unit, 3 * per_unit + 1):
            pl.when(i == point)(functools.partial(between, point))
        tile = unit_place(me, i // per_unit) * per_unit + lax.rem(i, per_unit)
        forward_tile(tile, rand, segq, segk, qt, kn, vt, q3, tbuf, att, otile, lse)
        return carry

    lax.fori_loop(0, steps, tile_step, 0)
    send_home(3)
    last = [
        pltpu.make_async_copy(src, dst, local.at[14 + i])
        for i, (src, dst) in enumerate(((otile, otile_o), (lse, lse_o)))
    ]
    for save in last:
        save.start()
    home[t] = att[rows_of(t), :]
    for u, move in homes:
        move.wait()
    for s in range(2):
        pieces = [home[4 * s + g].astype(F32) for g in range(4)]
        att_out[tok * s : tok * (s + 1), :] = jnp.concatenate(pieces, axis=1).astype(BF16)
    relay_diag(1)
    relay_diag(2)
    for to_x, to_y, dy, px, dx, py, pd in tail:
        px.wait_recv()
        py.wait_recv()
        pd.wait_recv()
    for cp in sent:
        cp.wait_send()

    @pl.when(is_middle)
    def _():
        for relay in relays:
            relay.wait_send()

    for copy in keeps + saves + last:
        copy.wait()


def forward_half(x, w, wo, wu, wd, requests, seg):
    dp = lax.axis_size("dp")
    seq = lax.axis_size("seq")
    tok, features = x.shape[1:]
    length = seq * tok
    steps = length // TILE
    nat, tra = (length, 256), (256, length)
    stacked = lambda w: jax.ShapeDtypeStruct((dp,) + w.shape, BF16)
    low = lambda *shape: jax.ShapeDtypeStruct(shape, BF16)
    full = lambda *shape: jax.ShapeDtypeStruct(shape, F32)
    return pl.pallas_call(
        forward_kernel,
        in_specs=[VMEMSPACE] * 2 + [ANYSPACE] * 3 + [VMEMSPACE] * 2,
        out_specs=[ANYSPACE] * 3 + [VMEMSPACE] + [ANYSPACE] * 10 + [VMEMSPACE] * 2,
        out_shape=[
            stacked(wo), stacked(wu), stacked(wd), low(2 * tok, features),
            full(steps, NH * HEAD, TILE), full(steps, 1, NH * TILE),
            jax.ShapeDtypeStruct((length, TILE), jnp.int32),
            low(*nat), low(*nat), low(*nat), low(*tra), low(*tra),
            low(features, length), low(features, 768),
            jax.ShapeDtypeStruct((steps, 3, NH * TILE), jnp.int32),
            jax.ShapeDtypeStruct((steps, 1, TILE), jnp.int32),
        ],
        scratch_shapes=[
            pltpu.VMEM((length, features), BF16),
            pltpu.VMEM((features, 768), BF16),
            pltpu.VMEM(wo.shape, BF16),
            pltpu.VMEM(wu.shape, BF16),
            pltpu.VMEM(wd.shape, BF16),
            pltpu.VMEM((length, NH * HEAD), BF16),
            pltpu.VMEM((seq, tok, NH * HEAD), BF16),
            pltpu.VMEM((steps, NH * HEAD, TILE), F32),
            pltpu.VMEM((steps, 1, NH * TILE), F32),
            pltpu.VMEM((length, TILE), jnp.int32),
            pltpu.VMEM(nat, BF16),
            pltpu.VMEM(nat, BF16),
            pltpu.VMEM(nat, BF16),
            pltpu.VMEM(tra, BF16),
            pltpu.VMEM(tra, BF16),
            pltpu.VMEM(tra, BF16),
            pltpu.VMEM((features, length), BF16),
            pltpu.VMEM((256, NH * TILE), BF16),
            pltpu.VMEM((length, NH * TILE), F32),
            pltpu.SemaphoreType.DMA((90,)),
            pltpu.SemaphoreType.DMA((90,)),
            pltpu.SemaphoreType.DMA((3,)),
            pltpu.SemaphoreType.DMA((2,)),
            pltpu.SemaphoreType.DMA((16,)),
        ],
        compiler_params=pltpu.CompilerParams(
            collective_id=0, has_side_effects=True, vmem_limit_bytes=62 * 1024 * 1024
        ),
        name="forward_half",
    )(x, w, wo, wu, wd, requests, seg)


def each(count, body):
    def run(i, carry):
        body(i)
        return carry

    lax.fori_loop(0, count, run, 0)


def plus(a, b):
    return a.astype(F32) + b.astype(F32)


def backward_tile(
    tile, dat, qn, qt, otile, lse, rand, segq, segk, kn, vn, kt, dqkv, q3t, d3t, q3, d3, dk, dv
):
    chunks = kn.shape[0] // CH
    on, off, seg = tile_tables(tile, rand, segq, kn.shape[0] // BLOCK)
    here = pl.ds(pl.multiple_of(tile * TILE, TILE), TILE)
    dat_f = dat[here, :].astype(F32)
    dat_t = dat_f.T
    lane = lax.broadcasted_iota(jnp.int32, (TILE, NH * HEAD), 1) // HEAD
    qblk = qn[here, : NH * HEAD].astype(F32)
    delta = []
    for h in range(NH):
        hr = slice(HEAD * h, HEAD * (h + 1))
        hc = slice(TILE * h, TILE * (h + 1))
        q3t[hr, hc] = qt[hr, here]
        d3t[hr, hc] = dat_t[hr].astype(BF16)
        q3[hc, :] = jnp.where(lane == h, qblk, 0.0).astype(BF16)
        d3[hc, :] = jnp.where(lane == h, dat_f, 0.0).astype(BF16)
        delta.append(jnp.sum(dat_t[hr] * otile[tile, hr, :], axis=0, keepdims=True))
    delta = jnp.concatenate(delta, axis=1)
    norm = lse[tile]
    dq = jnp.zeros((256, NH * TILE), F32)
    for j in range(chunks):
        rows = slice(CH * j, CH * (j + 1))
        s = nn(kn[rows, :], q3t[...])
        dp = nn(vn[rows, :], d3t[...])
        t = biased(s, segk[rows, :] == seg, on, off, CH // BLOCK * j)
        p = jnp.exp2(t - norm)
        ds = (p * (dp - delta)).astype(BF16)
        dv[rows, :] += nn(p.astype(BF16), d3[...])
        dk[rows, :] += nn(ds, q3[...])
        dq = dq + nn(kt[:, rows], ds)
    heads = [dq[HEAD * h : HEAD * (h + 1), TILE * h : TILE * (h + 1)] for h in range(NH)]
    merged = jnp.concatenate(heads, axis=0).T * HEAD ** (-0.5)
    dqkv[here, : NH * HEAD] = merged.astype(BF16)


def backward_kernel(*refs):
    (da, stats, g2), refs = refs[:3], refs[3:]
    (rand, segq), refs = refs[:2], refs[2:]
    extra, refs = refs[:5], refs[5:]
    saved, refs = refs[:10], refs[10:]
    (o0, o1, o2, stats_out, ig, wq), refs = refs[:6], refs[6:]
    bufs, refs = refs[:18], refs[18:]
    held, refs = refs[:10], refs[10:]
    kn, vn, kt, segk, qn, qt, otile, lse, xst, wg = held
    more, refs = refs[:5], refs[5:]
    wo, hb, dpre, at, resid = more
    (src, rows_t), refs = refs[:2], refs[2:]
    (dat, dqkv, q3t, d3t, q3, d3, dk, dv), refs = refs[:8], refs[8:]
    (part, own_p, rp, ra_p, rb_p, ro, dwg, wb1, wb2, wc, wr), refs = refs[:11], refs[11:]
    nsend, nrecv, send, recv, local = refs
    me = Place()
    c, z, x, y, t = me.c, me.z, me.x, me.y, me.t
    mine, other = me.half, 1 - me.half
    z_step = [lax.rem(z + k, 4) for k in (1, 2, 3)]
    tok = src.shape[1]
    loads = [
        pltpu.make_async_copy(from_hbm, to_vmem, local.at[4 + i])
        for i, (from_hbm, to_vmem) in enumerate(zip(saved, held))
    ]
    more_loads = [
        pltpu.make_async_copy(from_hbm, to_vmem, local.at[14 + i])
        for i, (from_hbm, to_vmem) in enumerate(zip(extra, more))
    ]
    friends = [me.across_x, me.across_y] + [(me.d, lax.rem(t + k, 8)) for k in range(1, 8)]
    greet(friends)
    for load in more_loads[:4] + loads + more_loads[4:]:
        load.start()
    more_loads[0].wait()
    for g in range(4):
        both = nt(da[...], wo[g]).astype(BF16)
        src[g] = both[:tok]
        src[4 + g] = both[tok:]
    met(friends)
    cps = Copies(send, recv)

    def rows_of(index):
        return pl.ds(pl.multiple_of(index * tok, tok), tok)

    dat_moves = []
    for u in range(4):
        place = unit_place(me, 3 - u)
        for o in range(1 if u == 0 else 0, 2):
            to = 2 * place + (c if o == 0 else 1 - c)
            dat_moves.append((u, cps.to(src.at[to], dat.at[rows_of(t)], (me.d, to))))
    for u, move in dat_moves:
        move.start()
    keep = pltpu.make_async_copy(src.at[t], dat.at[rows_of(t)], local.at[3])
    keep.start()

    works = []
    for i, o in enumerate((o2, o1, o0)):
        own, ra, rb1, rb2, rc, rd = bufs[6 * i : 6 * i + 6]
        if i == 0:
            away = g2.at[:, :, :, 1 - c]
            load = pltpu.make_async_copy(g2.at[:, :, :, c], own, local.at[0])
        else:
            away, own, load = own.at[:, :, :, 1 - c], own.at[:, :, :, c], None
        swap_core = cps.to(away, ra, me.partner)
        moves = (
            swap_core,
            load,
            cps.to(own.at[:, 1 - x, 0:2], rb1, me.across_x),
            cps.to(own.at[1 - y, :, 2:4], rb2, me.across_y),
            cps.to(rb1.at[1 - y], rc.at[0:2], me.across_y),
            cps.to(rb2.at[1 - x], rc.at[2:4], me.across_x),
            [cps.to(rc.at[k], rd.at[j], me.at_z(k)) for j, k in enumerate(z_step)],
        )
        works.append(((o, own, ra, rb1, rb2, rc, rd), moves))
    stat_to = [me.partner, me.across_x, me.across_y, me.at_z(me.pair_z), me.at_z(lax.rem(z + 2, 4))]
    stat_all = [cps.to(nsend.at[k], nrecv.at[k], stat_to[k]) for k in range(5)]

    def stat_step(k):
        if k == 0:
            nsend[0] = stats[...]
        else:
            stat_all[k - 1].wait_recv()
            nsend[k] = nsend[k - 1] + nrecv[k - 1]
        stat_all[k].start()

    sent = []

    def begin(*copies):
        for cp in copies:
            cp.start()
            sent.append(cp)

    def stage_a(work):
        (o, own, ra, rb1, rb2, rc, rd), (swap_core, load, bx, by, cy, cx, ds) = work
        if load is not None:
            load.wait()
        swap_core.wait_recv()

        def fold(i):
            yy, xx, zz = i // 8, lax.rem(i // 4, 2), lax.rem(i, 4)
            own[yy, xx, zz] = plus(own[yy, xx, zz], ra[yy, xx, zz]).astype(BF16)

        each(16, fold)

    def cross(work):
        begin(work[1][2], work[1][3])

    def stage_b(work):
        (o, own, ra, rb1, rb2, rc, rd), (swap_core, load, bx, by, cy, cx, ds) = work
        bx.wait_recv()

        def fold_x(i):
            yy, zz = i // 2, lax.rem(i, 2)
            rb1[yy, zz] = plus(own[yy, x, zz], rb1[yy, zz]).astype(BF16)

        each(4, fold_x)
        begin(cy)
        by.wait_recv()

        def fold_y(i):
            xx, zz = i // 2, lax.rem(i, 2)
            rb2[xx, zz] = plus(own[y, xx, 2 + zz], rb2[xx, zz]).astype(BF16)

        each(4, fold_y)
        begin(cx)

    def stage_c(work):
        (o, own, ra, rb1, rb2, rc, rd), (swap_core, load, bx, by, cy, cx, ds) = work
        cy.wait_recv()
        cx.wait_recv()
        for zz in range(2):
            rc[zz] = plus(rb1[y, zz], rc[zz]).astype(BF16)
            rc[2 + zz] = plus(rb2[x, zz], rc[2 + zz]).astype(BF16)
        begin(*ds)

    def stage_d(work):
        (o, own, ra, rb1, rb2, rc, rd), (swap_core, load, bx, by, cy, cx, ds) = work
        for cp in ds:
            cp.wait_recv()
        o[...] = plus(rc[z], rd[0]) + plus(rd[1], rd[2])

    stat_step(0)
    down_work, up_work, out_work = works
    down_work[1][0].start()
    down_work[1][1].start()

    def weight_grad(tokens, cotangent, total):
        rows_t[...] = tokens[...].astype(F32).T.astype(BF16)
        size, wide = rows_t.shape[0] // 4, 768
        count = cotangent.shape[1] // wide

        def block(i):
            r, k = i // count, lax.rem(i, count)
            cols = pl.ds(pl.multiple_of(k * wide, wide), wide)
            grad = nn(rows_t[pl.ds(pl.multiple_of(r * size, size), size), :], cotangent[:, cols])
            total[r // 2, lax.rem(r, 2), :, :, :, cols] = grad.astype(BF16).reshape(
                total.shape[2:5] + (wide,)
            )

        each(4 * count, block)

    for load in more_loads[1:4]:
        load.wait()
    weight_grad(at, da, bufs[12])
    out_work[1][0].start()
    weight_grad(hb, dpre, bufs[6])
    up_work[1][0].start()
    q3t[...] = jnp.zeros_like(q3t)
    d3t[...] = jnp.zeros_like(d3t)
    dk[...] = jnp.zeros_like(dk)
    dv[...] = jnp.zeros_like(dv)
    gap = jnp.zeros((dqkv.shape[0], 256 - NH * HEAD), BF16)
    for g in range(3):
        dqkv[:, 256 * g + NH * HEAD : 256 * (g + 1)] = gap
    for load in loads[:8]:
        load.wait()
    keep.wait()
    per_unit = 2 * tok // TILE
    steps = dqkv.shape[0] // TILE

    def unit_arrives(u):
        for v, move in dat_moves:
            if u == v:
                move.wait_recv()

    def step_one():
        stat_step(1)
        stage_a(out_work)
        cross(out_work)

    def step_two():
        stat_step(2)
        stage_a(down_work)
        cross(down_work)

    events = {
        1: [step_one],
        2: [step_two],
        4: [functools.partial(stage_a, up_work), functools.partial(cross, up_work)],
        7: [functools.partial(stage_b, out_work)],
        10: [functools.partial(stat_step, 3)],
    }
    for u in range(4):
        events.setdefault(u * per_unit, []).append(functools.partial(unit_arrives, u))

    def tile_step(i, carry):
        for point, actions in sorted(events.items()):

            @pl.when(i == point)
            def _():
                for action in actions:
                    action()

        tile = unit_place(me, 3 - i // per_unit) * per_unit + lax.rem(i, per_unit)
        backward_tile(
            tile, dat, qn, qt, otile, lse, rand, segq, segk, kn, vn, kt, dqkv,
            q3t, d3t, q3, d3, dk, dv,
        )
        return carry

    lax.fori_loop(0, steps, tile_step, 0)
    stat_step(4)
    loads[9].wait()

    dqkv[:, 256 : 256 + NH * HEAD] = (dk[...] * HEAD ** (-0.5)).astype(BF16)
    dqkv[:, 512 : 512 + NH * HEAD] = dv[...].astype(BF16)
    facing = 3 - z
    order = [3 - me.pair_z, facing, me.pair_z, z]
    cores = []

    def partial_grad(k):
        zz = order[k]
        rows = pl.ds(pl.multiple_of(zz * 2 * tok, 2 * tok), 2 * tok)
        grad = nt(dqkv[rows, :], wg[...]).astype(BF16)
        part[zz, 0] = grad[:tok]
        part[zz, 1] = grad[tok:]
        core = cps.to(part.at[zz, 1 - c], rp.at[zz], me.partner)
        begin(core)
        cores.append(core)

    def merge_cores(k):
        zz = order[k]
        cores[k].wait_recv()
        own_p[zz] = plus(part[zz, c], rp[zz]).astype(BF16)

    up = cps.to(own_p.at[3 - me.pair_z], rb_p, me.at_z(me.pair_z))
    near = cps.to(own_p.at[me.pair_z], ra_p, me.at_z(me.pair_z))
    over = cps.to(own_p.at[facing], ro, me.at_z(facing))

    partial_grad(0)
    partial_grad(1)
    merge_cores(0)
    begin(up)
    stage_b(down_work)
    loads[8].wait()
    half_rows = xst.shape[0] // 2
    for yy in range(2):
        grad = nn(xst[half_rows * yy : half_rows * (yy + 1), :], dqkv[...]).astype(BF16)
        dwg[yy] = grad.reshape(dwg.shape[1:])
    bx = cps.to(dwg.at[:, 1 - x, 0:4], wb1, me.across_x)
    by = cps.to(dwg.at[1 - y, :, 4:8], wb2, me.across_y)
    begin(bx, by)
    stage_b(up_work)
    partial_grad(2)
    merge_cores(1)
    stage_c(out_work)
    partial_grad(3)
    merge_cores(2)
    begin(near)
    merge_cores(3)
    stage_c(down_work)
    up.wait_recv()
    own_p[facing] = plus(own_p[facing], rb_p[...]).astype(BF16)
    begin(over)
    bx.wait_recv()

    def fold_x(i):
        yy, tt = i // 4, lax.rem(i, 4)
        wb1[yy, tt] = plus(dwg[yy, x, tt], wb1[yy, tt]).astype(BF16)

    each(8, fold_x)
    cy = cps.to(wb1.at[1 - y], wc.at[0:4], me.across_y)
    begin(cy)
    by.wait_recv()

    def fold_y(i):
        xx, tt = i // 4, lax.rem(i, 4)
        wb2[xx, tt] = plus(dwg[y, xx, 4 + tt], wb2[xx, tt]).astype(BF16)

    each(8, fold_y)
    cx = cps.to(wb2.at[1 - x], wc.at[4:8], me.across_x)
    begin(cx)
    stage_c(up_work)
    cy.wait_recv()
    cx.wait_recv()

    def fold_c(i):
        wc[i] = plus(wb1[y, i], wc[i]).astype(BF16)
        wc[4 + i] = plus(wb2[x, i], wc[4 + i]).astype(BF16)

    each(4, fold_c)
    moves = []
    for k in range(1, 8):
        peer = lax.rem(t + k, 8)
        moves.append(cps.to(wc.at[peer], wr.at[t], (me.d, peer)))
    begin(*moves)
    stat_all[-1].wait_recv()
    stats_out[...] = nsend[4] + nrecv[4]
    near.wait_recv()
    more_loads[4].wait()
    ig[mine] = resid[mine] + plus(own_p[z], ra_p[...])
    over.wait_recv()
    ig[other] = resid[other] + ro[...].astype(F32)
    stage_d(out_work)
    stage_d(down_work)
    wr[t] = wc[t]
    for move in moves:
        move.wait_recv()
    sums = [plus(wr[g], wr[4 + g]) for g in range(4)]
    width = NH * HEAD
    for k in range(3):
        part_k = [total[:, 256 * k : 256 * k + width] for total in sums]
        wq[:, 4 * width * k : 4 * width * (k + 1)] = jnp.concatenate(part_k, axis=1)
    stage_d(up_work)
    for cp in sent + stat_all + [move for u, move in dat_moves] + [moves[0] for refs, moves in works]:
        cp.wait_send()


def backward_half(da, stats, down_grad, rand, segq, extra, saved):
    features, length = saved[8].shape
    wide = extra[2].shape[1]
    dims = [(features // 32, features), (features // 32, wide), (wide // 32, features)]
    tok = da.shape[0] // 2
    bufs = []
    for i, (rows, cols) in enumerate(dims[::-1]):
        bufs += [
            pltpu.VMEM(((2, 2, 4, 2) if i else (2, 2, 4)) + (rows, cols), BF16),
            pltpu.VMEM((2, 2, 4, rows, cols), BF16),
            pltpu.VMEM((2, 2, rows, cols), BF16),
            pltpu.VMEM((2, 2, rows, cols), BF16),
            pltpu.VMEM((4, rows, cols), BF16),
            pltpu.VMEM((3, rows, cols), BF16),
        ]
    wrows = features // 32
    return pl.pallas_call(
        backward_kernel,
        in_specs=[VMEMSPACE] * 2 + [ANYSPACE] + [VMEMSPACE] * 2 + [ANYSPACE] * 15,
        out_specs=[VMEMSPACE] * 6,
        out_shape=[jax.ShapeDtypeStruct(dim, F32) for dim in dims]
        + [
            jax.ShapeDtypeStruct(stats.shape, F32),
            jax.ShapeDtypeStruct((2, tok, features), F32),
            jax.ShapeDtypeStruct((wrows, 3 * features), F32),
        ],
        scratch_shapes=bufs
        + [pltpu.VMEM(a.shape, a.dtype) for a in saved + extra]
        + [
            pltpu.VMEM((8, tok, NH * HEAD), BF16),
            pltpu.VMEM((features, 2 * tok), BF16),
            pltpu.VMEM((length, NH * HEAD), BF16),
            pltpu.VMEM((length, 768), BF16),
            pltpu.VMEM((256, NH * TILE), BF16),
            pltpu.VMEM((256, NH * TILE), BF16),
            pltpu.VMEM((NH * TILE, NH * HEAD), BF16),
            pltpu.VMEM((NH * TILE, NH * HEAD), BF16),
            pltpu.VMEM((length, NH * HEAD), F32),
            pltpu.VMEM((length, NH * HEAD), F32),
            pltpu.VMEM((4, 2, tok, features), BF16),
            pltpu.VMEM((4, tok, features), BF16),
            pltpu.VMEM((4, tok, features), BF16),
            pltpu.VMEM((tok, features), BF16),
            pltpu.VMEM((tok, features), BF16),
            pltpu.VMEM((tok, features), BF16),
            pltpu.VMEM((2, 2, 8, wrows, 768), BF16),
            pltpu.VMEM((2, 4, wrows, 768), BF16),
            pltpu.VMEM((2, 4, wrows, 768), BF16),
            pltpu.VMEM((8, wrows, 768), BF16),
            pltpu.VMEM((8, wrows, 768), BF16),
            pltpu.VMEM((5,) + stats.shape, F32),
            pltpu.VMEM((5,) + stats.shape, F32),
            pltpu.SemaphoreType.DMA((90,)),
            pltpu.SemaphoreType.DMA((90,)),
            pltpu.SemaphoreType.DMA((19,)),
        ],
        compiler_params=pltpu.CompilerParams(
            collective_id=3, has_side_effects=True, vmem_limit_bytes=62 * 1024 * 1024
        ),
        name="backward_half",
    )(da, stats, down_grad, rand, segq, *extra, *saved)


def head_layout(
    inputs, segments, rand_blocks, w_qkv, w_out, w_up, w_down, norm_gain, norm_bias, out_grad
):
    seqs, tok, features = inputs.shape
    seq = lax.axis_size("seq")
    t = lax.axis_index("seq")
    requests = rand_blocks.transpose(0, 2, 3, 1).reshape(seqs, H * R, -1).astype(BF16)
    requests = jnp.pad(
        requests, ((0, 0), (0, TILE - requests.shape[1]), (0, TILE - requests.shape[2]))
    )
    wof, wuf, wdf, att_flat, otile, lse, segk, qn, kn, vn, qt, kt, xst, wgf, rand, segq = forward_half(
        inputs, w_qkv, w_out, w_up, w_down, requests, segments
    )
    full_out = wof.reshape(features, features)
    full_up = wuf.reshape(features, -1)
    full_down = wdf.reshape(-1, features)
    tokens_flat = inputs.reshape(seqs * tok, features)
    resid_one = tokens_flat.astype(F32) + product(att_flat, full_out)
    hidden_one, normed_one, inv_one = norm_forward(resid_one, norm_gain[0], norm_bias[0])
    hidden_low = hidden_one.astype(BF16)
    pre_act = product(hidden_low, full_up)
    activated = gelu_value(pre_act).astype(BF16)
    resid_two = hidden_one + product(activated, full_down)
    result, normed_two, inv_two = norm_forward(resid_two, norm_gain[1], norm_bias[1])
    grad_rows = out_grad.reshape(seqs * tok, features).astype(F32)
    grad_resid_two, gain_two, shift_two = norm_backward(
        grad_rows, normed_two, inv_two, norm_gain[1]
    )
    grad_branch = grad_resid_two.astype(BF16)
    grad_down_w = product_tn(activated, grad_branch).astype(BF16)
    grad_pre = (product_nt(grad_branch, full_down) * gelu_slope(pre_act)).astype(BF16)
    grad_hidden = grad_resid_two + product_nt(grad_pre, full_up)
    grad_resid_one, gain_one, shift_one = norm_backward(
        grad_hidden, normed_one, inv_one, norm_gain[0]
    )
    grad_mix = grad_resid_one.astype(BF16)
    stats = jnp.stack([gain_one, gain_two, shift_one, shift_two])
    grad_down_w = grad_down_w.reshape(2, 2, 4, 2, grad_down_w.shape[0] // 32, features)
    out_sum, up_sum, down_sum, stats, ig, wq = backward_half(
        grad_mix, stats, grad_down_w, rand, segq,
        (wof, hidden_low, grad_pre, att_flat, grad_resid_one.reshape(seqs, tok, features)),
        (kn, vn, kt, segk, qn, qt, otile, lse, xst, wgf),
    )
    mine = lax.axis_index("dp") * seq + t
    stats = lax.dynamic_slice_in_dim(stats, mine * (features // 32), features // 32, 1)
    return (
        result.astype(BF16).reshape(seqs, tok, features),
        ig,
        wq,
        out_sum,
        up_sum,
        down_sum,
        stats[:2],
        stats[2:],
    )


def solution(mesh):
    in_specs = (
        P("dp", "seq", None),
        P("dp", None),
        P("dp", None, None, None),
        P("dp", None),
        P("dp", None),
        P("dp", None),
        P("dp", None),
        P(),
        P(),
        P("dp", "seq", None),
    )
    out_specs = (
        P("dp", "seq", None),
        P("dp", "seq", None),
        P(("dp", "seq"), None),
        P(("dp", "seq"), None),
        P(("dp", "seq"), None),
        P(("dp", "seq"), None),
        P(None, ("dp", "seq")),
        P(None, ("dp", "seq")),
    )
    fits = mesh.shape["dp"] == 4 and mesh.shape["seq"] == 8
    return jax.shard_map(
        head_layout if fits else per_device, mesh=mesh, in_specs=in_specs, out_specs=out_specs, check_vma=False
    )
```

```python
import functools
import jax
import jax.numpy as jnp
import numpy as np
from jax import lax
from jax.experimental import pallas as pl
from jax.experimental.pallas import tpu as pltpu
from jax.sharding import PartitionSpec as P

H = 12
HEAD = 64
BLOCK = 64
R = 3
MICRO = 2


norm_eps = 1e-05
masked_score = -1e30
root_half = 0.7071067811865476
inv_root_two_pi = 0.3989422804014327


def padded(cells, sides, width):
    for axis, dim in sides:
        count = lax.axis_size(axis)
        ends = count - 1
        head = lax.slice_in_dim(cells, 0, width, axis=dim)
        tail = lax.slice_in_dim(cells, cells.shape[dim] - width, cells.shape[dim], axis=dim)
        cells = jnp.concatenate(
            [
                lax.ppermute(tail, axis, [(i, (i + 1) % count) for i in range(ends)]),
                cells,
                lax.ppermute(head, axis, [((i + 1) % count, i) for i in range(ends)]),
            ],
            axis=dim,
        )
    return cells


def from_root(x, axis, root):
    mine = lax.axis_index(axis) == root
    return lax.psum(jnp.where(mine, x, jnp.zeros_like(x)), axis)


def merged(x, axis, combine):
    everything = jax.tree.map(lambda part: lax.all_gather(part, axis), x)
    initial = jax.tree.map(lambda part: part[0], everything)

    def step(k, so_far):
        return combine(so_far, jax.tree.map(lambda part: part[k], everything))

    return lax.fori_loop(1, lax.axis_size(axis), step, initial)


def product(left_side, right_side):
    return jnp.dot(left_side, right_side, preferred_element_type=jnp.float32)


def product_tn(left_side, right_side):
    return lax.dot_general(
        left_side, right_side, (((0,), (0,)), ((), ())), preferred_element_type=jnp.float32
    )


def product_nt(left_side, right_side):
    return lax.dot_general(
        left_side, right_side, (((1,), (1,)), ((), ())), preferred_element_type=jnp.float32
    )


def gelu_value(pre_act):
    return 0.5 * pre_act * (1.0 + lax.erf(pre_act * root_half))


def gelu_slope(pre_act):
    return (
        0.5 * (1.0 + lax.erf(pre_act * root_half))
        + pre_act * jnp.exp(-0.5 * pre_act * pre_act) * inv_root_two_pi
    )


def norm_forward(residual, gain_row, shift_row):
    mean_row = jnp.mean(residual, axis=-1, keepdims=True)
    centred = residual - mean_row
    variance = jnp.mean(centred * centred, axis=-1, keepdims=True)
    inv_std = lax.rsqrt(variance + norm_eps)
    normed = centred * inv_std
    return (normed * gain_row + shift_row, normed, inv_std)


def norm_backward(grad_rows, normed, inv_std, gain_row):
    scaled = grad_rows * gain_row
    back_rows = inv_std * (
        scaled
        - jnp.mean(scaled, axis=-1, keepdims=True)
        - normed * jnp.mean(scaled * normed, axis=-1, keepdims=True)
    )
    return (back_rows, jnp.sum(grad_rows * normed, axis=0), jnp.sum(grad_rows, axis=0))


def merge_stats(first_pair, second_pair):
    joint_max = jnp.maximum(first_pair[0], second_pair[0])
    joint_sum = first_pair[1] * jnp.exp(first_pair[0] - joint_max) + second_pair[1] * jnp.exp(
        second_pair[0] - joint_max
    )
    return (joint_max, joint_sum)


def local_scores(query_heads, shared_keys, random_keys, shared_ok, random_ok, scale_factor):
    part_shared = jnp.einsum(
        "sbqhd,sbkhd->sbhqk", query_heads, shared_keys, preferred_element_type=jnp.float32
    )
    part_random = jnp.einsum(
        "sbqhd,sbhkd->sbhqk", query_heads, random_keys, preferred_element_type=jnp.float32
    )
    scores = jnp.concatenate([part_shared, part_random], axis=4) * scale_factor
    allowed = jnp.concatenate(
        [jnp.broadcast_to(shared_ok[:, :, None], part_shared.shape), random_ok], axis=4
    )
    return jnp.where(allowed, scores, masked_score)


def per_device(
    inputs, segments, rand_blocks, w_qkv, w_out, w_up, w_down, norm_gain, norm_bias, out_grad
):
    seq_total, tok_dev, features = inputs.shape
    devices = lax.axis_size("seq")
    my_index = lax.axis_index("seq")
    blocks_dev = tok_dev // BLOCK
    blocks_all = blocks_dev * devices
    entries = blocks_dev * H * R
    capacity = max(2, entries // devices + 1)
    per_micro = seq_total // MICRO
    glob_rows = 2 * BLOCK
    shared_count = 5 * BLOCK
    scale_factor = HEAD ** (-0.5)
    token_rows = per_micro * tok_dev
    owner_flag = (my_index == 0).astype(jnp.float32)
    row_global = my_index * tok_dev + jnp.arange(tok_dev, dtype=jnp.int32) < glob_rows
    window_index = np.arange(blocks_dev)[:, None] + np.arange(3)[None, :]
    win_blocks = (
        my_index * blocks_dev
        + jnp.arange(blocks_dev, dtype=jnp.int32)[:, None]
        + jnp.arange(-1, 2, dtype=jnp.int32)[None, :]
    )
    win_inside = (win_blocks >= 0) & (win_blocks < blocks_all)
    win_clipped = jnp.clip(win_blocks, 0, blocks_all - 1)
    entry_heads = jnp.arange(entries, dtype=jnp.int32) // R % H
    slot_ids = jnp.arange(capacity, dtype=jnp.int32)
    earlier = jnp.arange(entries)[None, :] < jnp.arange(entries)[:, None]
    seq_ids = jnp.arange(per_micro, dtype=jnp.int32)
    grad_qkv_w = jnp.zeros((features, 3 * features), jnp.float32)
    grad_out_w = jnp.zeros((features, features), jnp.float32)
    grad_up_w = jnp.zeros((features, w_up.shape[1]), jnp.float32)
    grad_down_w = jnp.zeros((w_down.shape[0] * lax.axis_size("dp"), features), jnp.float32)
    gain_acc = jnp.zeros((2, features), jnp.float32)
    shift_acc = jnp.zeros((2, features), jnp.float32)
    output_parts = []
    input_parts = []
    for micro_step in range(MICRO):
        start_seq = micro_step * per_micro
        tokens_in = inputs[start_seq : start_seq + per_micro]
        seg_micro = segments[start_seq : start_seq + per_micro]
        rand_micro = rand_blocks[start_seq : start_seq + per_micro]
        cotangent = out_grad[start_seq : start_seq + per_micro]
        full_qkv, full_out, full_up, full_down = (
            lax.all_gather(w_qkv, "dp", axis=0, tiled=True),
            lax.all_gather(w_out, "dp", axis=0, tiled=True),
            lax.all_gather(w_up, "dp", axis=0, tiled=True),
            lax.all_gather(w_down, "dp", axis=0, tiled=True),
        )
        tokens_flat = tokens_in.reshape(token_rows, features)
        qkv_rows = (
            product(tokens_flat, full_qkv)
            .astype(jnp.bfloat16)
            .reshape(per_micro, tok_dev, 3 * features)
        )
        queries = qkv_rows[..., :features]
        keyvals = qkv_rows[..., features:]
        extended = padded(keyvals, (("seq", 1),), BLOCK)
        global_block = from_root(qkv_rows[:, :glob_rows], "seq", 0)
        requests = rand_micro.reshape(per_micro, devices, entries)
        owners = requests // blocks_dev
        local_block = requests % blocks_dev
        same_owner = owners[:, :, :, None] == owners[:, :, None, :]
        slot_rank = jnp.sum(same_owner & earlier[None, None], axis=3)
        slot_hit = ((owners == my_index)[..., None] & (slot_rank[..., None] == slot_ids)).astype(
            jnp.int32
        )
        slot_live = jnp.sum(slot_hit, axis=2)
        slot_piece = jnp.sum(slot_hit * (local_block * H + entry_heads)[..., None], axis=2)
        piece_index = jnp.transpose(slot_piece, (1, 2, 0))
        live_mask = jnp.transpose(slot_live, (1, 2, 0))
        pieces = (
            keyvals.reshape(per_micro, blocks_dev, BLOCK, 2, H, HEAD)
            .transpose(0, 1, 4, 2, 3, 5)
            .reshape(per_micro, blocks_dev * H, BLOCK, 2 * HEAD)
        )
        outgoing = pieces[seq_ids[None, None, :], piece_index]
        outgoing = jnp.where(live_mask[..., None, None] > 0, outgoing, jnp.zeros((), jnp.bfloat16))
        outgoing = outgoing.reshape(devices * capacity, per_micro, BLOCK, 2 * HEAD)
        incoming = lax.all_to_all(outgoing, "seq", split_axis=0, concat_axis=0, tiled=True)
        my_owner = jnp.take(owners, my_index, axis=1)
        my_rank = jnp.take(slot_rank, my_index, axis=1)
        my_request = jnp.take(requests, my_index, axis=1)
        positions = my_owner * capacity + my_rank
        fetched = incoming[positions, seq_ids[:, None]].reshape(
            per_micro, blocks_dev, H, R, BLOCK, 2, HEAD
        )
        random_keys = fetched[..., 0, :].reshape(per_micro, blocks_dev, H, R * BLOCK, HEAD)
        random_vals = fetched[..., 1, :].reshape(per_micro, blocks_dev, H, R * BLOCK, HEAD)
        seg_blocks = seg_micro.reshape(per_micro, blocks_all, BLOCK)
        query_seg = lax.dynamic_slice_in_dim(seg_micro, my_index * tok_dev, tok_dev, 1).reshape(
            per_micro, blocks_dev, BLOCK
        )
        window_seg = seg_blocks[:, win_clipped].reshape(per_micro, blocks_dev, 3 * BLOCK)
        window_ok = (query_seg[..., :, None] == window_seg[:, :, None, :]) & jnp.repeat(
            win_inside, BLOCK, axis=1
        )[None, :, None, :]
        shared_ok = jnp.concatenate(
            [window_ok, jnp.ones((per_micro, blocks_dev, BLOCK, glob_rows), bool)], axis=3
        )
        random_seg = seg_blocks[seq_ids[:, None], my_request].reshape(
            per_micro, blocks_dev, H, R * BLOCK
        )
        random_ok = query_seg[:, :, None, :, None] == random_seg[:, :, :, None, :]
        ext_blocks = extended.reshape(per_micro, blocks_dev + 2, BLOCK, 2 * features)
        window_kv = ext_blocks[:, window_index].reshape(
            per_micro, blocks_dev, 3 * BLOCK, 2 * features
        )
        glob_kv = jnp.broadcast_to(
            global_block[:, None, :, features:], (per_micro, blocks_dev, glob_rows, 2 * features)
        )
        shared_kv = jnp.concatenate([window_kv, glob_kv], axis=2)
        shared_keys = shared_kv[..., :features].reshape(
            per_micro, blocks_dev, shared_count, H, HEAD
        )
        shared_vals = shared_kv[..., features:].reshape(
            per_micro, blocks_dev, shared_count, H, HEAD
        )
        query_heads = queries.reshape(per_micro, blocks_dev, BLOCK, H, HEAD)
        scores = local_scores(
            query_heads, shared_keys, random_keys, shared_ok, random_ok, scale_factor
        )
        row_max = jnp.max(scores, axis=4, keepdims=True)
        exp_terms = jnp.exp(scores - row_max)
        row_sum = jnp.sum(exp_terms, axis=4, keepdims=True)
        local_probs = exp_terms / row_sum
        log_norm = row_max + jnp.log(row_sum)
        local_weights = local_probs.astype(jnp.bfloat16)
        local_att = jnp.einsum(
            "sbhqk,sbkhd->sbqhd",
            local_weights[..., :shared_count],
            shared_vals,
            preferred_element_type=jnp.float32,
        )
        local_att = local_att + jnp.einsum(
            "sbhqk,sbhkd->sbqhd",
            local_weights[..., shared_count:],
            random_vals,
            preferred_element_type=jnp.float32,
        )
        local_att = local_att.reshape(per_micro, tok_dev, features)
        glob_query = global_block[..., :features].reshape(per_micro, glob_rows, H, HEAD)
        local_keys = keyvals[..., :features].reshape(per_micro, tok_dev, H, HEAD)
        local_vals = keyvals[..., features:].reshape(per_micro, tok_dev, H, HEAD)
        glob_scores = (
            jnp.einsum(
                "sqhd,skhd->shqk", glob_query, local_keys, preferred_element_type=jnp.float32
            )
            * scale_factor
        )
        part_max = jnp.max(glob_scores, axis=3)
        part_sum = jnp.sum(jnp.exp(glob_scores - part_max[..., None]), axis=3)
        glob_max, glob_sum = merged((part_max, part_sum), "seq", merge_stats)
        glob_lse = glob_max + jnp.log(glob_sum)
        glob_probs = jnp.exp(glob_scores - glob_lse[..., None])
        glob_weights = glob_probs.astype(jnp.bfloat16)
        glob_part = jnp.einsum(
            "shqk,skhd->sqhd", glob_weights, local_vals, preferred_element_type=jnp.float32
        ).reshape(per_micro, glob_rows, features)
        glob_out = lax.psum(glob_part, "seq")
        glob_full = jnp.concatenate(
            [glob_out, jnp.zeros((per_micro, tok_dev - glob_rows, features), jnp.float32)], axis=1
        )
        attention = jnp.where(row_global[None, :, None], glob_full, local_att).astype(jnp.bfloat16)
        att_flat = attention.reshape(token_rows, features)
        resid_one = tokens_flat.astype(jnp.float32) + product(att_flat, full_out)
        hidden_one, normed_one, inv_one = norm_forward(resid_one, norm_gain[0], norm_bias[0])
        hidden_low = hidden_one.astype(jnp.bfloat16)
        pre_act = product(hidden_low, full_up)
        activated = gelu_value(pre_act).astype(jnp.bfloat16)
        resid_two = hidden_one + product(activated, full_down)
        result, normed_two, inv_two = norm_forward(resid_two, norm_gain[1], norm_bias[1])
        output_parts.append(result.astype(jnp.bfloat16).reshape(per_micro, tok_dev, features))
        grad_rows = cotangent.reshape(token_rows, features).astype(jnp.float32)
        grad_resid_two, gain_two, shift_two = norm_backward(
            grad_rows, normed_two, inv_two, norm_gain[1]
        )
        grad_branch = grad_resid_two.astype(jnp.bfloat16)
        grad_down_w = grad_down_w + product_tn(activated, grad_branch)
        grad_pre = (product_nt(grad_branch, full_down) * gelu_slope(pre_act)).astype(jnp.bfloat16)
        grad_up_w = grad_up_w + product_tn(hidden_low, grad_pre)
        grad_hidden = grad_resid_two + product_nt(grad_pre, full_up)
        grad_resid_one, gain_one, shift_one = norm_backward(
            grad_hidden, normed_one, inv_one, norm_gain[0]
        )
        grad_mix = grad_resid_one.astype(jnp.bfloat16)
        grad_out_w = grad_out_w + product_tn(att_flat, grad_mix)
        grad_att = (
            product_nt(grad_mix, full_out)
            .astype(jnp.bfloat16)
            .reshape(per_micro, tok_dev, features)
        )
        gain_acc = gain_acc + jnp.stack([gain_one, gain_two])
        shift_acc = shift_acc + jnp.stack([shift_one, shift_two])
        grad_local = jnp.where(
            row_global[None, :, None], jnp.zeros((), jnp.bfloat16), grad_att
        ).reshape(per_micro, blocks_dev, BLOCK, H, HEAD)
        scores = local_scores(
            query_heads, shared_keys, random_keys, shared_ok, random_ok, scale_factor
        )
        local_probs = jnp.exp(scores - log_norm)
        local_weights = local_probs.astype(jnp.bfloat16)
        grad_prob = jnp.concatenate(
            [
                jnp.einsum(
                    "sbqhd,sbkhd->sbhqk",
                    grad_local,
                    shared_vals,
                    preferred_element_type=jnp.float32,
                ),
                jnp.einsum(
                    "sbqhd,sbhkd->sbhqk",
                    grad_local,
                    random_vals,
                    preferred_element_type=jnp.float32,
                ),
            ],
            axis=4,
        )
        row_delta = jnp.sum(local_probs * grad_prob, axis=4, keepdims=True)
        grad_score = (local_probs * (grad_prob - row_delta)).astype(jnp.bfloat16)
        grad_query = jnp.einsum(
            "sbhqk,sbkhd->sbqhd",
            grad_score[..., :shared_count],
            shared_keys,
            preferred_element_type=jnp.float32,
        )
        grad_query = (
            grad_query
            + jnp.einsum(
                "sbhqk,sbhkd->sbqhd",
                grad_score[..., shared_count:],
                random_keys,
                preferred_element_type=jnp.float32,
            )
        ) * scale_factor
        grad_key_shared = (
            jnp.einsum(
                "sbhqk,sbqhd->sbkhd",
                grad_score[..., :shared_count],
                query_heads,
                preferred_element_type=jnp.float32,
            )
            * scale_factor
        )
        grad_val_shared = jnp.einsum(
            "sbhqk,sbqhd->sbkhd",
            local_weights[..., :shared_count],
            grad_local,
            preferred_element_type=jnp.float32,
        )
        grad_key_random = (
            jnp.einsum(
                "sbhqk,sbqhd->sbhkd",
                grad_score[..., shared_count:],
                query_heads,
                preferred_element_type=jnp.float32,
            )
            * scale_factor
        )
        grad_val_random = jnp.einsum(
            "sbhqk,sbqhd->sbhkd",
            local_weights[..., shared_count:],
            grad_local,
            preferred_element_type=jnp.float32,
        )
        grad_shared = jnp.concatenate(
            [
                grad_key_shared.reshape(per_micro, blocks_dev, shared_count, features),
                grad_val_shared.reshape(per_micro, blocks_dev, shared_count, features),
            ],
            axis=3,
        )
        grad_window = grad_shared[:, :, : 3 * BLOCK].reshape(
            per_micro, blocks_dev, 3, BLOCK, 2 * features
        )
        ext_grad = jnp.zeros((per_micro, blocks_dev + 2, BLOCK, 2 * features), jnp.float32)
        for offset in range(3):
            ext_grad = ext_grad.at[:, offset : offset + blocks_dev].add(grad_window[:, :, offset])
        grad_glob_keys = jnp.sum(grad_shared[:, :, 3 * BLOCK :], axis=1)
        grad_random = jnp.stack([grad_key_random, grad_val_random], axis=4).reshape(
            per_micro, entries, BLOCK, 2 * HEAD
        )
        returned = (
            jnp.zeros((devices * capacity, per_micro, BLOCK, 2 * HEAD), jnp.float32)
            .at[positions, seq_ids[:, None]]
            .set(grad_random)
        )
        arrived = lax.all_to_all(
            returned.astype(jnp.bfloat16), "seq", split_axis=0, concat_axis=0, tiled=True
        ).astype(returned.dtype)
        arrived = arrived.reshape(devices, capacity, per_micro, BLOCK, 2 * HEAD) * live_mask[
            ..., None, None
        ].astype(jnp.float32)
        piece_grad = (
            jnp.zeros((per_micro, blocks_dev * H, BLOCK, 2 * HEAD), jnp.float32)
            .at[seq_ids[None, None, :], piece_index]
            .add(arrived)
        )
        piece_grad = (
            piece_grad.reshape(per_micro, blocks_dev, H, BLOCK, 2, HEAD)
            .transpose(0, 1, 3, 4, 2, 5)
            .reshape(per_micro, tok_dev, 2 * features)
        )
        rim_pair = jnp.concatenate([ext_grad[:, 0], ext_grad[:, blocks_dev + 1]], axis=1)
        rim_back = padded(rim_pair.astype(jnp.bfloat16), (("seq", 1),), BLOCK).astype(
            rim_pair.dtype
        )
        grad_kv = (
            ext_grad[:, 1 : blocks_dev + 1].reshape(per_micro, tok_dev, 2 * features) + piece_grad
        )
        grad_kv = grad_kv.at[:, :BLOCK].add(rim_back[:, :BLOCK])
        grad_kv = grad_kv.at[:, tok_dev - BLOCK :].add(rim_back[:, 3 * BLOCK :])
        grad_glob = from_root(grad_att[:, :glob_rows], "seq", 0)
        grad_glob_heads = grad_glob.reshape(per_micro, glob_rows, H, HEAD)
        glob_scores = (
            jnp.einsum(
                "sqhd,skhd->shqk", glob_query, local_keys, preferred_element_type=jnp.float32
            )
            * scale_factor
        )
        glob_probs = jnp.exp(glob_scores - glob_lse[..., None])
        glob_weights = glob_probs.astype(jnp.bfloat16)
        glob_grad_prob = jnp.einsum(
            "sqhd,skhd->shqk", grad_glob_heads, local_vals, preferred_element_type=jnp.float32
        )
        glob_delta = lax.psum(jnp.sum(glob_probs * glob_grad_prob, axis=3), "seq")
        glob_grad_score = (glob_probs * (glob_grad_prob - glob_delta[..., None])).astype(
            jnp.bfloat16
        )
        glob_grad_query = (
            jnp.einsum(
                "shqk,skhd->sqhd", glob_grad_score, local_keys, preferred_element_type=jnp.float32
            )
            * scale_factor
        )
        glob_grad_key = (
            jnp.einsum(
                "shqk,sqhd->skhd", glob_grad_score, glob_query, preferred_element_type=jnp.float32
            )
            * scale_factor
        )
        glob_grad_val = jnp.einsum(
            "shqk,sqhd->skhd", glob_weights, grad_glob_heads, preferred_element_type=jnp.float32
        )
        grad_kv = grad_kv + jnp.concatenate(
            [
                glob_grad_key.reshape(per_micro, tok_dev, features),
                glob_grad_val.reshape(per_micro, tok_dev, features),
            ],
            axis=2,
        )
        summed_query, summed_keys = lax.psum(
            (glob_grad_query.reshape(per_micro, glob_rows, features), grad_glob_keys), "seq"
        )
        grad_kv = grad_kv.at[:, :glob_rows].add(owner_flag * summed_keys)
        grad_queries = (
            grad_query.reshape(per_micro, tok_dev, features)
            .at[:, :glob_rows]
            .add(owner_flag * summed_query)
        )
        grad_qkv_rows = (
            jnp.concatenate([grad_queries, grad_kv], axis=2)
            .astype(jnp.bfloat16)
            .reshape(token_rows, 3 * features)
        )
        grad_qkv_w = grad_qkv_w + product_tn(tokens_flat, grad_qkv_rows)
        input_rows = grad_resid_one + product_nt(grad_qkv_rows, full_qkv)
        input_parts.append(input_rows.reshape(per_micro, tok_dev, features))
    summed = (
        lax.psum_scatter(grad_qkv_w, ("dp", "seq"), scatter_dimension=0, tiled=True),
        lax.psum_scatter(grad_out_w, ("dp", "seq"), scatter_dimension=0, tiled=True),
        lax.psum_scatter(grad_up_w, ("dp", "seq"), scatter_dimension=0, tiled=True),
        lax.psum_scatter(grad_down_w, ("dp", "seq"), scatter_dimension=0, tiled=True),
        lax.psum_scatter(gain_acc, ("dp", "seq"), scatter_dimension=1, tiled=True),
        lax.psum_scatter(shift_acc, ("dp", "seq"), scatter_dimension=1, tiled=True),
    )
    return (
        jnp.concatenate(output_parts, axis=0),
        jnp.concatenate(input_parts, axis=0),
        summed[0],
        summed[1],
        summed[2],
        summed[3],
        summed[4],
        summed[5],
    )


TILE = 128
NH = 3
CH = 512
LOG2E = 1.4426950408889634
SCALE2 = HEAD ** (-0.5) * LOG2E
NEG = -1e30
F32 = jnp.float32
BF16 = jnp.bfloat16


def nt(a, b):
    return lax.dot_general(a, b, (((1,), (1,)), ((), ())), preferred_element_type=F32)


def nn(a, b):
    return jnp.dot(a, b, preferred_element_type=F32)


MESH = pl.DeviceIdType.MESH
ANYSPACE = pl.BlockSpec(memory_space=pl.ANY)
VMEMSPACE = pl.BlockSpec(memory_space=pltpu.VMEM)


class Copies:
    def __init__(self, send, recv):
        self.send = send
        self.recv = recv
        self.used = 0

    def to(self, src, dst, device):
        index = self.used
        self.used += 1
        return pltpu.make_async_remote_copy(
            src_ref=src, dst_ref=dst, send_sem=self.send.at[index], recv_sem=self.recv.at[index],
            device_id=device, device_id_type=MESH,
        )


class Place:
    def __init__(self):
        self.d = lax.axis_index("dp")
        self.t = lax.axis_index("seq")
        self.x = lax.rem(self.d, 2)
        self.y = self.d // 2
        self.c = lax.rem(self.t, 2)
        self.z = self.t // 2
        self.half = self.z // 2
        self.xn = self.d + 1 - 2 * self.x
        self.yn = self.d + 2 - 4 * self.y
        self.diag = 3 - self.d
        self.pair_z = self.z + 1 - 2 * lax.rem(self.z, 2)
        self.across_x = (self.xn, self.t)
        self.across_y = (self.yn, self.t)
        self.partner = (self.d, self.t + 1 - 2 * self.c)

    def at_z(self, z):
        return (self.d, 2 * z + self.c)


def greet(devices):
    barrier = pltpu.get_barrier_semaphore()
    for device in devices:
        pl.semaphore_signal(barrier, inc=1, device_id=device, device_id_type=MESH)


def met(devices):
    pl.semaphore_wait(pltpu.get_barrier_semaphore(), len(devices))


def tile_tables(tile, rand_ref, segq_ref, blocks):
    wide = NH * TILE
    key = lax.broadcasted_iota(jnp.int32, (blocks, wide), 0)
    lane = lax.broadcasted_iota(jnp.int32, (blocks, wide), 1)
    query = tile * (TILE // BLOCK) + lax.rem(lane, TILE) // BLOCK
    near = (key - query) * (key - query) <= 1
    hits = near.astype(F32)
    for r in range(rand_ref.shape[1]):
        hits = hits + (rand_ref[tile, r : r + 1, :] == key).astype(F32)
    fixed = jnp.logical_or(query < 2, key < 2)
    count = jnp.where(query < 2, 0.0, hits) + fixed.astype(F32)
    on = jnp.where(count > 0.0, jnp.log2(jnp.maximum(count, 1.0)), NEG)
    off = jnp.where(fixed, 0.0, NEG)
    return on, off, segq_ref[tile]


def biased(s, mask, on, off, first_block):
    rows = []
    for j in range(s.shape[0] // BLOCK):
        kb = first_block + j
        m3 = jnp.concatenate([mask[BLOCK * j : BLOCK * (j + 1)]] * NH, axis=1)
        bias = jnp.where(m3, on[kb : kb + 1, :], off[kb : kb + 1, :])
        rows.append(s[BLOCK * j : BLOCK * (j + 1)] * SCALE2 + bias)
    return jnp.concatenate(rows, axis=0)


def fill_segments(segq, segk):
    steps = segq.shape[0]
    for i in range(steps):
        column = jnp.broadcast_to(segq[i].astype(F32), (8, TILE)).T[:, :1]
        segk[TILE * i : TILE * (i + 1), :] = jnp.broadcast_to(column, (TILE, TILE)).astype(jnp.int32)


def fill_requests(requests, rand, half, group):
    row = lax.broadcasted_iota(jnp.int32, (32, TILE), 0)
    entry = lax.broadcasted_iota(jnp.int32, (32, TILE), 1)
    slot = lax.rem(row, 8)
    pick = jnp.logical_and(slot < 3, entry == 9 * group + 3 * (row // 8) + slot)
    chosen = jnp.where(half == 0, requests[0], requests[1])
    mine = nn(pick.astype(F32).astype(BF16), chosen)
    steps = rand.shape[0]
    block = lax.broadcasted_iota(jnp.int32, (TILE, steps * TILE), 0)
    token = lax.broadcasted_iota(jnp.int32, (TILE, steps * TILE), 1)
    spread = nn(mine.astype(BF16), (token // BLOCK == block).astype(F32).astype(BF16))
    for i in range(steps):
        for h in range(NH):
            rand[i, :, TILE * h : TILE * (h + 1)] = spread[
                8 * h : 8 * h + 3, TILE * i : TILE * (i + 1)
            ].astype(jnp.int32)


def forward_tile(tile, rand, segq, segk, qt, kn, vt, q3, tbuf, att, otile, lse):
    length = kn.shape[0]
    chunks = length // CH
    here = pl.ds(pl.multiple_of(tile * TILE, TILE), TILE)
    on, off, seg = tile_tables(tile, rand, segq, length // BLOCK)
    for h in range(NH):
        q3[HEAD * h : HEAD * (h + 1), TILE * h : TILE * (h + 1)] = qt[
            HEAD * h : HEAD * (h + 1), here
        ]
    top = jnp.full((8, NH * TILE), NEG, F32)
    for j in range(chunks):
        rows = slice(CH * j, CH * (j + 1))
        s = nn(kn[rows, :], q3[...])
        t = biased(s, segk[rows, :] == seg, on, off, CH // BLOCK * j)
        tbuf[rows, :] = t
        top = jnp.maximum(top, jnp.max(t.reshape(CH // 8, 8, NH * TILE), axis=0))
    peak = jnp.max(top, axis=0, keepdims=True)
    total = jnp.zeros((8, NH * TILE), F32)
    out = jnp.zeros((256, NH * TILE), F32)
    for j in range(chunks):
        rows = slice(CH * j, CH * (j + 1))
        p = jnp.exp2(tbuf[rows, :] - peak)
        total = total + jnp.sum(p.reshape(CH // 8, 8, NH * TILE), axis=0)
        out = out + nn(vt[:, rows], p.astype(BF16))
    weight = jnp.sum(total, axis=0, keepdims=True)
    lse[tile] = peak + jnp.log2(weight)
    inv = 1.0 / weight
    heads = [
        out[HEAD * h : HEAD * (h + 1), TILE * h : TILE * (h + 1)] * inv[:, TILE * h : TILE * (h + 1)]
        for h in range(NH)
    ]
    merged = jnp.concatenate(heads, axis=0)
    otile[tile] = merged
    att[here, :] = merged.T.astype(BF16)


def unit_place(me, u):
    low = lax.rem(me.z, 2)
    return 2 * lax.rem(me.half + 1 + u // 2, 2) + lax.rem(low + 1 + u, 2)


def forward_kernel(*refs):
    (x, w, wo, wu, wd, requests, seg), refs = refs[:7], refs[7:]
    outs, refs = refs[:14], refs[14:]
    (rand, segq), refs = refs[:2], refs[2:]
    wof, wuf, wdf, att_out, otile_o, lse_o, segk_o, qn_o, kn_o, vn_o, qt_o, kt_o, xst_o, wgf_o = outs
    (xs, wgf, bo, bu, bd, att, home, otile, lse, segk), refs = refs[:10], refs[10:]
    (qn, kn, vn, qt, kt, vt, xst, q3, tbuf), refs = refs[:9], refs[9:]
    send, recv, xsend, xrecv, local = refs
    me = Place()
    d, t, c, z = me.d, me.t, me.c, me.z
    mine, other = me.half, 1 - me.half
    is_middle = z == 1 + me.half
    tok = x.shape[1]
    length = xs.shape[0]
    steps = length // TILE
    per_unit = 2 * tok // TILE
    loads = [
        pltpu.make_async_copy(src, dst, local.at[i])
        for i, (src, dst) in enumerate(((wo, bo), (wu, bu), (wd, bd)))
    ]
    for load in loads:
        load.start()
    friends = [me.across_x, me.across_y] + [(d, lax.rem(t + k, 8)) for k in range(1, 8)]
    greet(friends)
    shard = w.shape[0]
    wrows = lambda index, start, size: pl.ds(pl.multiple_of(index * shard + start, size), size)
    lane = lax.broadcasted_iota(jnp.int32, (shard, 256), 1)
    for k in range(3):
        first = w.shape[1] // 3 * k + 2 * NH * HEAD * lax.rem(z, 2) + TILE * c
        window = w[:, pl.ds(pl.multiple_of(first, TILE), 256)].astype(F32)
        moved = jnp.concatenate([window[:, HEAD:], window[:, :HEAD]], axis=1)
        mine_k = jnp.where(lane < NH * HEAD, jnp.where(c == 0, window, moved), 0.0)
        wgf[wrows(d, 0, shard), 256 * k : 256 * (k + 1)] = mine_k.astype(BF16)
    met(friends)
    cps = Copies(send, recv)
    sent = []

    def begin(*copies):
        for cp in copies:
            cp.start()
            sent.append(cp)

    def rows_of(index):
        return pl.ds(pl.multiple_of(index * tok, tok), tok)

    half = shard // 2
    my_top, my_low = wrows(d, 0, half), wrows(d, half, half)
    wg_x0 = cps.to(wgf.at[my_top], wgf.at[my_top], me.across_x)
    wg_x1 = cps.to(wgf.at[my_low], wgf.at[my_low], me.across_x)
    wg_y0 = cps.to(wgf.at[my_low], wgf.at[my_low], me.across_y)
    wg_y1 = cps.to(wgf.at[my_top], wgf.at[my_top], me.across_y)
    near = cps.to(x.at[mine], xs.at[rows_of(t)], me.at_z(me.pair_z))
    give = cps.to(x.at[mine], xs.at[rows_of(t)], me.partner)
    far = pltpu.make_async_remote_copy(
        src_ref=x.at[other], dst_ref=xs.at[rows_of(t)], send_sem=xsend.at[0],
        recv_sem=xrecv.at[lax.rem(z, 2)], device_id=me.at_z(2 - me.half), device_id_type=MESH,
    )
    begin(wg_x0, wg_y0, far, wg_x1, wg_y1, near, give)
    heavy = []
    for w, full in ((wo, wof), (wu, wuf), (wd, wdf)):
        rows = w.shape[0] // 2
        part = pl.ds(pl.multiple_of(c * rows, rows), rows)
        to_x = cps.to(w.at[part], full.at[d, part], me.across_x)
        to_y = cps.to(w.at[part], full.at[d, part], me.across_y)
        heavy.append((full, rows, part, to_x, to_y))
    xn_top, yn_low = wrows(me.xn, 0, half), wrows(me.yn, half, half)
    wg_dy = cps.to(wgf.at[xn_top], wgf.at[xn_top], me.across_y)
    wg_dx = cps.to(wgf.at[yn_low], wgf.at[yn_low], me.across_x)
    wg_x0.wait_recv()
    begin(wg_dy)
    wg_y0.wait_recv()
    begin(wg_dx)
    for full, rows, part, to_x, to_y in heavy[:2]:
        begin(to_x, to_y)

    xs[rows_of(t), :] = x[mine]
    q3[...] = jnp.zeros_like(q3)
    seg_row = jnp.where(me.half == 0, seg[0:1, :], seg[1:2, :])
    for i in range(steps):
        segq[i] = seg_row[:, TILE * i : TILE * (i + 1)]
    fill_segments(segq, segk)
    fill_requests(requests, rand, me.half, lax.rem(t, 4))
    keeps = []
    for i, (load, buf, full) in enumerate(zip(loads, (bo, bu, bd), (wof, wuf, wdf))):
        load.wait()
        keep = pltpu.make_async_copy(buf, full.at[d], local.at[3 + i])
        keep.start()
        keeps.append(keep)

    def project(unit):
        rows = pl.ds(pl.multiple_of(unit * 2 * tok, 2 * tok), 2 * tok)
        both = nn(xs[rows, :], wgf[...])
        qf, kf, vf = both[:, :256], both[:, 256:512], both[:, 512:]
        qn[rows, :] = qf.astype(BF16)
        kn[rows, :] = kf.astype(BF16)
        vn[rows, :] = vf.astype(BF16)
        qt[:, rows] = qf.T.astype(BF16)
        kt[:, rows] = kf.T.astype(BF16)
        vt[:, rows] = vf.T.astype(BF16)
        xst[:, rows] = xs[rows, :].astype(F32).T.astype(BF16)

    wg_x1.wait_recv()
    wg_y1.wait_recv()
    wg_dy.wait_recv()
    wg_dx.wait_recv()
    give.wait_recv()
    near.wait_recv()
    near_rows = rows_of(2 * me.pair_z + c)
    pass_near = cps.to(xs.at[near_rows], xs.at[near_rows], me.partner)
    begin(pass_near)
    relays, onwards = [], []
    for j in range(2):
        src_rows = rows_of(2 * (2 * other + j) + c)
        relays.append(
            pltpu.make_async_remote_copy(
                src_ref=xs.at[src_rows], dst_ref=xs.at[src_rows], send_sem=xsend.at[1 + j],
                recv_sem=xrecv.at[j], device_id=me.at_z(me.pair_z), device_id_type=MESH,
            )
        )
        onwards.append(cps.to(xs.at[src_rows], xs.at[src_rows], me.partner))

    def forward_x(j):
        relays[j].wait_recv()
        pl.when(is_middle)(relays[j].start)
        begin(onwards[j])

    tail = []
    for full, rows, part, to_x, to_y in heavy:
        quarter = rows // 2
        lo = pl.ds(pl.multiple_of(c * rows, quarter), quarter)
        hi = pl.ds(pl.multiple_of(c * rows + quarter, quarter), quarter)
        tail.append(
            (
                to_x, to_y,
                cps.to(full.at[me.xn, lo], full.at[me.xn, lo], me.across_y),
                cps.to(full.at[me.xn, part], full.at[me.xn, part], me.partner),
                cps.to(full.at[me.yn, hi], full.at[me.yn, hi], me.across_x),
                cps.to(full.at[me.yn, part], full.at[me.yn, part], me.partner),
                cps.to(full.at[me.diag, part], full.at[me.diag, part], me.partner),
            )
        )

    def relay_weights(k):
        to_x, to_y, dy, px, dx, py, pd = tail[k]
        to_x.wait_recv()
        begin(dy, px)
        to_y.wait_recv()
        begin(dx, py)

    def relay_diag(k):
        to_x, to_y, dy, px, dx, py, pd = tail[k]
        dy.wait_recv()
        dx.wait_recv()
        begin(pd)

    def arrive(k):
        if k == 0:
            forward_x(0)
            relay_weights(0)
            begin(heavy[2][3], heavy[2][4])
        if k == 1:
            forward_x(1)
            pass_near.wait_recv()
        if k == 2:
            onwards[0].wait_recv()
        if k == 3:
            onwards[1].wait_recv()

    def project_step(k, carry):
        for i in range(4):
            pl.when(k == i)(functools.partial(arrive, i))
        unit = jnp.where(k < 2, 2 * mine + lax.rem(lax.rem(z, 2) + k, 2), 2 * other + k - 2)
        project(unit)
        return carry

    lax.fori_loop(0, 4, project_step, 0)
    saves = [
        pltpu.make_async_copy(src, dst, local.at[6 + i])
        for i, (src, dst) in enumerate(
            ((segk, segk_o), (qn, qn_o), (kn, kn_o), (vn, vn_o), (qt, qt_o), (kt, kt_o), (xst, xst_o), (wgf, wgf_o))
        )
    ]
    for save in saves:
        save.start()

    homes = []
    for u in range(4):
        unit = unit_place(me, u)
        for o in range(1 if u == 3 else 0, 2):
            to = 2 * unit + (c if o == 0 else 1 - c)
            homes.append((u, cps.to(att.at[rows_of(to)], home.at[t], (d, to))))

    def send_home(u):
        for v, move in homes:
            if u == v:
                move.start()

    def between(i):
        if i == 2:
            relay_weights(1)
        if i == per_unit:
            send_home(0)
        if i == per_unit + 1:
            relay_diag(0)
        if i == 2 * per_unit:
            send_home(1)
        if i == 3 * per_unit:
            send_home(2)
        if i == 3 * per_unit + 1:
            relay_weights(2)

    def tile_step(i, carry):
        for point in (2, per_unit, per_unit + 1, 2 * per_unit, 3 * per_unit, 3 * per_unit + 1):
            pl.when(i == point)(functools.partial(between, point))
        tile = unit_place(me, i // per_unit) * per_unit + lax.rem(i, per_unit)
        forward_tile(tile, rand, segq, segk, qt, kn, vt, q3, tbuf, att, otile, lse)
        return carry

    lax.fori_loop(0, steps, tile_step, 0)
    send_home(3)
    last = [
        pltpu.make_async_copy(src, dst, local.at[14 + i])
        for i, (src, dst) in enumerate(((otile, otile_o), (lse, lse_o)))
    ]
    for save in last:
        save.start()
    home[t] = att[rows_of(t), :]
    for u, move in homes:
        move.wait()
    for s in range(2):
        pieces = [home[4 * s + g].astype(F32) for g in range(4)]
        att_out[tok * s : tok * (s + 1), :] = jnp.concatenate(pieces, axis=1).astype(BF16)
    relay_diag(1)
    relay_diag(2)
    for to_x, to_y, dy, px, dx, py, pd in tail:
        px.wait_recv()
        py.wait_recv()
        pd.wait_recv()
    for cp in sent:
        cp.wait_send()

    @pl.when(is_middle)
    def _():
        for relay in relays:
            relay.wait_send()

    for copy in keeps + saves + last:
        copy.wait()


def forward_half(x, w, wo, wu, wd, requests, seg):
    dp = lax.axis_size("dp")
    seq = lax.axis_size("seq")
    tok, features = x.shape[1:]
    length = seq * tok
    steps = length // TILE
    nat, tra = (length, 256), (256, length)
    stacked = lambda w: jax.ShapeDtypeStruct((dp,) + w.shape, BF16)
    low = lambda *shape: jax.ShapeDtypeStruct(shape, BF16)
    full = lambda *shape: jax.ShapeDtypeStruct(shape, F32)
    return pl.pallas_call(
        forward_kernel,
        in_specs=[VMEMSPACE] * 2 + [ANYSPACE] * 3 + [VMEMSPACE] * 2,
        out_specs=[ANYSPACE] * 3 + [VMEMSPACE] + [ANYSPACE] * 10 + [VMEMSPACE] * 2,
        out_shape=[
            stacked(wo), stacked(wu), stacked(wd), low(2 * tok, features),
            full(steps, NH * HEAD, TILE), full(steps, 1, NH * TILE),
            jax.ShapeDtypeStruct((length, TILE), jnp.int32),
            low(*nat), low(*nat), low(*nat), low(*tra), low(*tra),
            low(features, length), low(features, 768),
            jax.ShapeDtypeStruct((steps, 3, NH * TILE), jnp.int32),
            jax.ShapeDtypeStruct((steps, 1, TILE), jnp.int32),
        ],
        scratch_shapes=[
            pltpu.VMEM((length, features), BF16),
            pltpu.VMEM((features, 768), BF16),
            pltpu.VMEM(wo.shape, BF16),
            pltpu.VMEM(wu.shape, BF16),
            pltpu.VMEM(wd.shape, BF16),
            pltpu.VMEM((length, NH * HEAD), BF16),
            pltpu.VMEM((seq, tok, NH * HEAD), BF16),
            pltpu.VMEM((steps, NH * HEAD, TILE), F32),
            pltpu.VMEM((steps, 1, NH * TILE), F32),
            pltpu.VMEM((length, TILE), jnp.int32),
            pltpu.VMEM(nat, BF16),
            pltpu.VMEM(nat, BF16),
            pltpu.VMEM(nat, BF16),
            pltpu.VMEM(tra, BF16),
            pltpu.VMEM(tra, BF16),
            pltpu.VMEM(tra, BF16),
            pltpu.VMEM((features, length), BF16),
            pltpu.VMEM((256, NH * TILE), BF16),
            pltpu.VMEM((length, NH * TILE), F32),
            pltpu.SemaphoreType.DMA((90,)),
            pltpu.SemaphoreType.DMA((90,)),
            pltpu.SemaphoreType.DMA((3,)),
            pltpu.SemaphoreType.DMA((2,)),
            pltpu.SemaphoreType.DMA((16,)),
        ],
        compiler_params=pltpu.CompilerParams(
            collective_id=0, has_side_effects=True, vmem_limit_bytes=62 * 1024 * 1024
        ),
        name="forward_half",
    )(x, w, wo, wu, wd, requests, seg)


def each(count, body):
    def run(i, carry):
        body(i)
        return carry

    lax.fori_loop(0, count, run, 0)


def plus(a, b):
    return a.astype(F32) + b.astype(F32)


def backward_tile(
    tile, dat, qn, qt, otile, lse, rand, segq, segk, kn, vn, kt, dqkv, q3t, d3t, q3, d3, dk, dv
):
    chunks = kn.shape[0] // CH
    on, off, seg = tile_tables(tile, rand, segq, kn.shape[0] // BLOCK)
    here = pl.ds(pl.multiple_of(tile * TILE, TILE), TILE)
    dat_f = dat[here, :].astype(F32)
    dat_t = dat_f.T
    lane = lax.broadcasted_iota(jnp.int32, (TILE, NH * HEAD), 1) // HEAD
    qblk = qn[here, : NH * HEAD].astype(F32)
    delta = []
    for h in range(NH):
        hr = slice(HEAD * h, HEAD * (h + 1))
        hc = slice(TILE * h, TILE * (h + 1))
        q3t[hr, hc] = qt[hr, here]
        d3t[hr, hc] = dat_t[hr].astype(BF16)
        q3[hc, :] = jnp.where(lane == h, qblk, 0.0).astype(BF16)
        d3[hc, :] = jnp.where(lane == h, dat_f, 0.0).astype(BF16)
        delta.append(jnp.sum(dat_t[hr] * otile[tile, hr, :], axis=0, keepdims=True))
    delta = jnp.concatenate(delta, axis=1)
    norm = lse[tile]
    dq = jnp.zeros((256, NH * TILE), F32)
    for j in range(chunks):
        rows = slice(CH * j, CH * (j + 1))
        s = nn(kn[rows, :], q3t[...])
        dp = nn(vn[rows, :], d3t[...])
        t = biased(s, segk[rows, :] == seg, on, off, CH // BLOCK * j)
        p = jnp.exp2(t - norm)
        ds = (p * (dp - delta)).astype(BF16)
        dv[rows, :] += nn(p.astype(BF16), d3[...])
        dk[rows, :] += nn(ds, q3[...])
        dq = dq + nn(kt[:, rows], ds)
    heads = [dq[HEAD * h : HEAD * (h + 1), TILE * h : TILE * (h + 1)] for h in range(NH)]
    merged = jnp.concatenate(heads, axis=0).T * HEAD ** (-0.5)
    dqkv[here, : NH * HEAD] = merged.astype(BF16)


def backward_kernel(*refs):
    (da, stats, g2), refs = refs[:3], refs[3:]
    (rand, segq), refs = refs[:2], refs[2:]
    extra, refs = refs[:5], refs[5:]
    saved, refs = refs[:10], refs[10:]
    (o0, o1, o2, stats_out, ig, wq), refs = refs[:6], refs[6:]
    bufs, refs = refs[:18], refs[18:]
    held, refs = refs[:10], refs[10:]
    kn, vn, kt, segk, qn, qt, otile, lse, xst, wg = held
    more, refs = refs[:5], refs[5:]
    wo, hb, dpre, at, resid = more
    (src, rows_t), refs = refs[:2], refs[2:]
    (dat, dqkv, q3t, d3t, q3, d3, dk, dv), refs = refs[:8], refs[8:]
    (part, own_p, rp, ra_p, rb_p, ro, dwg, wb1, wb2, wc, wr), refs = refs[:11], refs[11:]
    nsend, nrecv, send, recv, local = refs
    me = Place()
    c, z, x, y, t = me.c, me.z, me.x, me.y, me.t
    mine, other = me.half, 1 - me.half
    z_step = [lax.rem(z + k, 4) for k in (1, 2, 3)]
    tok = src.shape[1]
    loads = [
        pltpu.make_async_copy(from_hbm, to_vmem, local.at[4 + i])
        for i, (from_hbm, to_vmem) in enumerate(zip(saved, held))
    ]
    more_loads = [
        pltpu.make_async_copy(from_hbm, to_vmem, local.at[14 + i])
        for i, (from_hbm, to_vmem) in enumerate(zip(extra, more))
    ]
    friends = [me.across_x, me.across_y] + [(me.d, lax.rem(t + k, 8)) for k in range(1, 8)]
    greet(friends)
    for load in more_loads[:4] + loads + more_loads[4:]:
        load.start()
    more_loads[0].wait()
    for g in range(4):
        both = nt(da[...], wo[g]).astype(BF16)
        src[g] = both[:tok]
        src[4 + g] = both[tok:]
    met(friends)
    cps = Copies(send, recv)

    def rows_of(index):
        return pl.ds(pl.multiple_of(index * tok, tok), tok)

    dat_moves = []
    for u in range(4):
        place = unit_place(me, 3 - u)
        for o in range(1 if u == 0 else 0, 2):
            to = 2 * place + (c if o == 0 else 1 - c)
            dat_moves.append((u, cps.to(src.at[to], dat.at[rows_of(t)], (me.d, to))))
    for u, move in dat_moves:
        move.start()
    keep = pltpu.make_async_copy(src.at[t], dat.at[rows_of(t)], local.at[3])
    keep.start()

    works = []
    for i, o in enumerate((o2, o1, o0)):
        own, ra, rb1, rb2, rc, rd = bufs[6 * i : 6 * i + 6]
        if i == 0:
            away = g2.at[:, :, :, 1 - c]
            load = pltpu.make_async_copy(g2.at[:, :, :, c], own, local.at[0])
        else:
            away, own, load = own.at[:, :, :, 1 - c], own.at[:, :, :, c], None
        swap_core = cps.to(away, ra, me.partner)
        moves = (
            swap_core,
            load,
            cps.to(own.at[:, 1 - x, 0:2], rb1, me.across_x),
            cps.to(own.at[1 - y, :, 2:4], rb2, me.across_y),
            cps.to(rb1.at[1 - y], rc.at[0:2], me.across_y),
            cps.to(rb2.at[1 - x], rc.at[2:4], me.across_x),
            [cps.to(rc.at[k], rd.at[j], me.at_z(k)) for j, k in enumerate(z_step)],
        )
        works.append(((o, own, ra, rb1, rb2, rc, rd), moves))
    stat_to = [me.partner, me.across_x, me.across_y, me.at_z(me.pair_z), me.at_z(lax.rem(z + 2, 4))]
    stat_all = [cps.to(nsend.at[k], nrecv.at[k], stat_to[k]) for k in range(5)]

    def stat_step(k):
        if k == 0:
            nsend[0] = stats[...]
        else:
            stat_all[k - 1].wait_recv()
            nsend[k] = nsend[k - 1] + nrecv[k - 1]
        stat_all[k].start()

    sent = []

    def begin(*copies):
        for cp in copies:
            cp.start()
            sent.append(cp)

    def stage_a(work):
        (o, own, ra, rb1, rb2, rc, rd), (swap_core, load, bx, by, cy, cx, ds) = work
        if load is not None:
            load.wait()
        swap_core.wait_recv()

        def fold(i):
            yy, xx, zz = i // 8, lax.rem(i // 4, 2), lax.rem(i, 4)
            own[yy, xx, zz] = plus(own[yy, xx, zz], ra[yy, xx, zz]).astype(BF16)

        each(16, fold)

    def cross(work):
        begin(work[1][2], work[1][3])

    def stage_b(work):
        (o, own, ra, rb1, rb2, rc, rd), (swap_core, load, bx, by, cy, cx, ds) = work
        bx.wait_recv()

        def fold_x(i):
            yy, zz = i // 2, lax.rem(i, 2)
            rb1[yy, zz] = plus(own[yy, x, zz], rb1[yy, zz]).astype(BF16)

        each(4, fold_x)
        begin(cy)
        by.wait_recv()

        def fold_y(i):
            xx, zz = i // 2, lax.rem(i, 2)
            rb2[xx, zz] = plus(own[y, xx, 2 + zz], rb2[xx, zz]).astype(BF16)

        each(4, fold_y)
        begin(cx)

    def stage_c(work):
        (o, own, ra, rb1, rb2, rc, rd), (swap_core, load, bx, by, cy, cx, ds) = work
        cy.wait_recv()
        cx.wait_recv()
        for zz in range(2):
            rc[zz] = plus(rb1[y, zz], rc[zz]).astype(BF16)
            rc[2 + zz] = plus(rb2[x, zz], rc[2 + zz]).astype(BF16)
        begin(*ds)

    def stage_d(work):
        (o, own, ra, rb1, rb2, rc, rd), (swap_core, load, bx, by, cy, cx, ds) = work
        for cp in ds:
            cp.wait_recv()
        o[...] = plus(rc[z], rd[0]) + plus(rd[1], rd[2])

    stat_step(0)
    down_work, up_work, out_work = works
    down_work[1][0].start()
    down_work[1][1].start()

    def weight_grad(tokens, cotangent, total):
        rows_t[...] = tokens[...].astype(F32).T.astype(BF16)
        size, wide = rows_t.shape[0] // 4, 768
        count = cotangent.shape[1] // wide

        def block(i):
            r, k = i // count, lax.rem(i, count)
            cols = pl.ds(pl.multiple_of(k * wide, wide), wide)
            grad = nn(rows_t[pl.ds(pl.multiple_of(r * size, size), size), :], cotangent[:, cols])
            total[r // 2, lax.rem(r, 2), :, :, :, cols] = grad.astype(BF16).reshape(
                total.shape[2:5] + (wide,)
            )

        each(4 * count, block)

    for load in more_loads[1:4]:
        load.wait()
    weight_grad(at, da, bufs[12])
    out_work[1][0].start()
    weight_grad(hb, dpre, bufs[6])
    up_work[1][0].start()
    q3t[...] = jnp.zeros_like(q3t)
    d3t[...] = jnp.zeros_like(d3t)
    dk[...] = jnp.zeros_like(dk)
    dv[...] = jnp.zeros_like(dv)
    gap = jnp.zeros((dqkv.shape[0], 256 - NH * HEAD), BF16)
    for g in range(3):
        dqkv[:, 256 * g + NH * HEAD : 256 * (g + 1)] = gap
    for load in loads[:8]:
        load.wait()
    keep.wait()
    per_unit = 2 * tok // TILE
    steps = dqkv.shape[0] // TILE

    def unit_arrives(u):
        for v, move in dat_moves:
            if u == v:
                move.wait_recv()

    def step_one():
        stat_step(1)
        stage_a(out_work)
        cross(out_work)

    def step_two():
        stat_step(2)
        stage_a(down_work)
        cross(down_work)

    events = {
        1: [step_one],
        2: [step_two],
        4: [functools.partial(stage_a, up_work), functools.partial(cross, up_work)],
        7: [functools.partial(stage_b, out_work)],
        10: [functools.partial(stat_step, 3)],
    }
    for u in range(4):
        events.setdefault(u * per_unit, []).append(functools.partial(unit_arrives, u))

    def tile_step(i, carry):
        for point, actions in sorted(events.items()):

            @pl.when(i == point)
            def _():
                for action in actions:
                    action()

        tile = unit_place(me, 3 - i // per_unit) * per_unit + lax.rem(i, per_unit)
        backward_tile(
            tile, dat, qn, qt, otile, lse, rand, segq, segk, kn, vn, kt, dqkv,
            q3t, d3t, q3, d3, dk, dv,
        )
        return carry

    lax.fori_loop(0, steps, tile_step, 0)
    stat_step(4)
    loads[9].wait()

    dqkv[:, 256 : 256 + NH * HEAD] = (dk[...] * HEAD ** (-0.5)).astype(BF16)
    dqkv[:, 512 : 512 + NH * HEAD] = dv[...].astype(BF16)
    facing = 3 - z
    order = [3 - me.pair_z, facing, me.pair_z, z]
    cores = []

    def partial_grad(k):
        zz = order[k]
        rows = pl.ds(pl.multiple_of(zz * 2 * tok, 2 * tok), 2 * tok)
        grad = nt(dqkv[rows, :], wg[...]).astype(BF16)
        part[zz, 0] = grad[:tok]
        part[zz, 1] = grad[tok:]
        core = cps.to(part.at[zz, 1 - c], rp.at[zz], me.partner)
        begin(core)
        cores.append(core)

    def merge_cores(k):
        zz = order[k]
        cores[k].wait_recv()
        own_p[zz] = plus(part[zz, c], rp[zz]).astype(BF16)

    up = cps.to(own_p.at[3 - me.pair_z], rb_p, me.at_z(me.pair_z))
    near = cps.to(own_p.at[me.pair_z], ra_p, me.at_z(me.pair_z))
    over = cps.to(own_p.at[facing], ro, me.at_z(facing))

    partial_grad(0)
    partial_grad(1)
    merge_cores(0)
    begin(up)
    stage_b(down_work)
    loads[8].wait()
    half_rows = xst.shape[0] // 2
    for yy in range(2):
        grad = nn(xst[half_rows * yy : half_rows * (yy + 1), :], dqkv[...]).astype(BF16)
        dwg[yy] = grad.reshape(dwg.shape[1:])
    bx = cps.to(dwg.at[:, 1 - x, 0:4], wb1, me.across_x)
    by = cps.to(dwg.at[1 - y, :, 4:8], wb2, me.across_y)
    begin(bx, by)
    stage_b(up_work)
    partial_grad(2)
    merge_cores(1)
    stage_c(out_work)
    partial_grad(3)
    merge_cores(2)
    begin(near)
    merge_cores(3)
    stage_c(down_work)
    up.wait_recv()
    own_p[facing] = plus(own_p[facing], rb_p[...]).astype(BF16)
    begin(over)
    bx.wait_recv()

    def fold_x(i):
        yy, tt = i // 4, lax.rem(i, 4)
        wb1[yy, tt] = plus(dwg[yy, x, tt], wb1[yy, tt]).astype(BF16)

    each(8, fold_x)
    cy = cps.to(wb1.at[1 - y], wc.at[0:4], me.across_y)
    begin(cy)
    by.wait_recv()

    def fold_y(i):
        xx, tt = i // 4, lax.rem(i, 4)
        wb2[xx, tt] = plus(dwg[y, xx, 4 + tt], wb2[xx, tt]).astype(BF16)

    each(8, fold_y)
    cx = cps.to(wb2.at[1 - x], wc.at[4:8], me.across_x)
    begin(cx)
    stage_c(up_work)
    cy.wait_recv()
    cx.wait_recv()

    def fold_c(i):
        wc[i] = plus(wb1[y, i], wc[i]).astype(BF16)
        wc[4 + i] = plus(wb2[x, i], wc[4 + i]).astype(BF16)

    each(4, fold_c)
    moves = []
    for k in range(1, 8):
        peer = lax.rem(t + k, 8)
        moves.append(cps.to(wc.at[peer], wr.at[t], (me.d, peer)))
    begin(*moves)
    stat_all[-1].wait_recv()
    stats_out[...] = nsend[4] + nrecv[4]
    near.wait_recv()
    more_loads[4].wait()
    ig[mine] = resid[mine] + plus(own_p[z], ra_p[...])
    over.wait_recv()
    ig[other] = resid[other] + ro[...].astype(F32)
    stage_d(out_work)
    stage_d(down_work)
    wr[t] = wc[t]
    for move in moves:
        move.wait_recv()
    sums = [plus(wr[g], wr[4 + g]) for g in range(4)]
    width = NH * HEAD
    for k in range(3):
        part_k = [total[:, 256 * k : 256 * k + width] for total in sums]
        wq[:, 4 * width * k : 4 * width * (k + 1)] = jnp.concatenate(part_k, axis=1)
    stage_d(up_work)
    for cp in sent + stat_all + [move for u, move in dat_moves] + [moves[0] for refs, moves in works]:
        cp.wait_send()


def backward_half(da, stats, down_grad, rand, segq, extra, saved):
    features, length = saved[8].shape
    wide = extra[2].shape[1]
    dims = [(features // 32, features), (features // 32, wide), (wide // 32, features)]
    tok = da.shape[0] // 2
    bufs = []
    for i, (rows, cols) in enumerate(dims[::-1]):
        bufs += [
            pltpu.VMEM(((2, 2, 4, 2) if i else (2, 2, 4)) + (rows, cols), BF16),
            pltpu.VMEM((2, 2, 4, rows, cols), BF16),
            pltpu.VMEM((2, 2, rows, cols), BF16),
            pltpu.VMEM((2, 2, rows, cols), BF16),
            pltpu.VMEM((4, rows, cols), BF16),
            pltpu.VMEM((3, rows, cols), BF16),
        ]
    wrows = features // 32
    return pl.pallas_call(
        backward_kernel,
        in_specs=[VMEMSPACE] * 2 + [ANYSPACE] + [VMEMSPACE] * 2 + [ANYSPACE] * 15,
        out_specs=[VMEMSPACE] * 6,
        out_shape=[jax.ShapeDtypeStruct(dim, F32) for dim in dims]
        + [
            jax.ShapeDtypeStruct(stats.shape, F32),
            jax.ShapeDtypeStruct((2, tok, features), F32),
            jax.ShapeDtypeStruct((wrows, 3 * features), F32),
        ],
        scratch_shapes=bufs
        + [pltpu.VMEM(a.shape, a.dtype) for a in saved + extra]
        + [
            pltpu.VMEM((8, tok, NH * HEAD), BF16),
            pltpu.VMEM((features, 2 * tok), BF16),
            pltpu.VMEM((length, NH * HEAD), BF16),
            pltpu.VMEM((length, 768), BF16),
            pltpu.VMEM((256, NH * TILE), BF16),
            pltpu.VMEM((256, NH * TILE), BF16),
            pltpu.VMEM((NH * TILE, NH * HEAD), BF16),
            pltpu.VMEM((NH * TILE, NH * HEAD), BF16),
            pltpu.VMEM((length, NH * HEAD), F32),
            pltpu.VMEM((length, NH * HEAD), F32),
            pltpu.VMEM((4, 2, tok, features), BF16),
            pltpu.VMEM((4, tok, features), BF16),
            pltpu.VMEM((4, tok, features), BF16),
            pltpu.VMEM((tok, features), BF16),
            pltpu.VMEM((tok, features), BF16),
            pltpu.VMEM((tok, features), BF16),
            pltpu.VMEM((2, 2, 8, wrows, 768), BF16),
            pltpu.VMEM((2, 4, wrows, 768), BF16),
            pltpu.VMEM((2, 4, wrows, 768), BF16),
            pltpu.VMEM((8, wrows, 768), BF16),
            pltpu.VMEM((8, wrows, 768), BF16),
            pltpu.VMEM((5,) + stats.shape, F32),
            pltpu.VMEM((5,) + stats.shape, F32),
            pltpu.SemaphoreType.DMA((90,)),
            pltpu.SemaphoreType.DMA((90,)),
            pltpu.SemaphoreType.DMA((19,)),
        ],
        compiler_params=pltpu.CompilerParams(
            collective_id=3, has_side_effects=True, vmem_limit_bytes=62 * 1024 * 1024
        ),
        name="backward_half",
    )(da, stats, down_grad, rand, segq, *extra, *saved)


def head_layout(
    inputs, segments, rand_blocks, w_qkv, w_out, w_up, w_down, norm_gain, norm_bias, out_grad
):
    seqs, tok, features = inputs.shape
    seq = lax.axis_size("seq")
    t = lax.axis_index("seq")
    requests = rand_blocks.transpose(0, 2, 3, 1).reshape(seqs, H * R, -1).astype(BF16)
    requests = jnp.pad(
        requests, ((0, 0), (0, TILE - requests.shape[1]), (0, TILE - requests.shape[2]))
    )
    wof, wuf, wdf, att_flat, otile, lse, segk, qn, kn, vn, qt, kt, xst, wgf, rand, segq = forward_half(
        inputs, w_qkv, w_out, w_up, w_down, requests, segments
    )
    full_out = wof.reshape(features, features)
    full_up = wuf.reshape(features, -1)
    full_down = wdf.reshape(-1, features)
    tokens_flat = inputs.reshape(seqs * tok, features)
    resid_one = tokens_flat.astype(F32) + product(att_flat, full_out)
    hidden_one, normed_one, inv_one = norm_forward(resid_one, norm_gain[0], norm_bias[0])
    hidden_low = hidden_one.astype(BF16)
    pre_act = product(hidden_low, full_up)
    activated = gelu_value(pre_act).astype(BF16)
    resid_two = hidden_one + product(activated, full_down)
    result, normed_two, inv_two = norm_forward(resid_two, norm_gain[1], norm_bias[1])
    grad_rows = out_grad.reshape(seqs * tok, features).astype(F32)
    grad_resid_two, gain_two, shift_two = norm_backward(
        grad_rows, normed_two, inv_two, norm_gain[1]
    )
    grad_branch = grad_resid_two.astype(BF16)
    grad_down_w = product_tn(activated, grad_branch).astype(BF16)
    grad_pre = (product_nt(grad_branch, full_down) * gelu_slope(pre_act)).astype(BF16)
    grad_hidden = grad_resid_two + product_nt(grad_pre, full_up)
    grad_resid_one, gain_one, shift_one = norm_backward(
        grad_hidden, normed_one, inv_one, norm_gain[0]
    )
    grad_mix = grad_resid_one.astype(BF16)
    stats = jnp.stack([gain_one, gain_two, shift_one, shift_two])
    grad_down_w = grad_down_w.reshape(2, 2, 4, 2, grad_down_w.shape[0] // 32, features)
    out_sum, up_sum, down_sum, stats, ig, wq = backward_half(
        grad_mix, stats, grad_down_w, rand, segq,
        (wof, hidden_low, grad_pre, att_flat, grad_resid_one.reshape(seqs, tok, features)),
        (kn, vn, kt, segk, qn, qt, otile, lse, xst, wgf),
    )
    mine = lax.axis_index("dp") * seq + t
    stats = lax.dynamic_slice_in_dim(stats, mine * (features // 32), features // 32, 1)
    return (
        result.astype(BF16).reshape(seqs, tok, features),
        ig,
        wq,
        out_sum,
        up_sum,
        down_sum,
        stats[:2],
        stats[2:],
    )


def solution(mesh):
    in_specs = (
        P("dp", "seq", None),
        P("dp", None),
        P("dp", None, None, None),
        P("dp", None),
        P("dp", None),
        P("dp", None),
        P("dp", None),
        P(),
        P(),
        P("dp", "seq", None),
    )
    out_specs = (
        P("dp", "seq", None),
        P("dp", "seq", None),
        P(("dp", "seq"), None),
        P(("dp", "seq"), None),
        P(("dp", "seq"), None),
        P(("dp", "seq"), None),
        P(None, ("dp", "seq")),
        P(None, ("dp", "seq")),
    )
    fits = mesh.shape["dp"] == 4 and mesh.shape["seq"] == 8
    return jax.shard_map(
        head_layout if fits else per_device, mesh=mesh, in_specs=in_specs, out_specs=out_specs, check_vma=False
    )
```
